32 devices in a mesh: row: 4 (over y, x), col: 8 (over z, core).
Axes of the slice: x: 2, y: 2, z: 4, core: 2. Of those that a mesh axis runs over, the one named last changes fastest.
Arguments:
- tokens: bfloat16 [10240, 2048], P('col', 'row'), may hold values from -6 to 6
- cotangent: bfloat16 [10240, 2048], P('col', 'row'), may hold values from -6 to 6
- query_weight: bfloat16 [2048, 2048], P('col', 'row'), may hold values from -0.125 to 0.125
- key_weight: bfloat16 [2048, 2048], P('col', 'row'), may hold values from -0.125 to 0.125
- value_weight: bfloat16 [2048, 4096], P('col', 'row'), may hold values from -0.125 to 0.125
- gate_weight: bfloat16 [2048, 4096], P('col', 'row'), may hold values from -0.125 to 0.125
- out_weight: bfloat16 [4096, 2048], P('row', 'col'), may hold values from -0.1875 to 0.1875
- up_weight: bfloat16 [2048, 4096], P('col', 'row'), may hold values from -0.125 to 0.125
- down_weight: bfloat16 [4096, 2048], P('row', 'col'), may hold values from -0.09375 to 0.09375
- first_gain: float32 [2048], P('row'), may hold values from 0.5 to 1.5
- first_bias: float32 [2048], P('row'), may hold values from -1 to 1
- group_gain: float32 [4096], P('row'), may hold values from 0.5 to 1.5
- group_bias: float32 [4096], P('row'), may hold values from -1 to 1
- second_gain: float32 [2048], P('row'), may hold values from 0.5 to 1.5
- second_bias: float32 [2048], P('row'), may hold values from -1 to 1
- up_bias: float32 [4096], P('row'), may hold values from -1 to 1
- down_bias: float32 [2048], P('row'), may hold values from -1 to 1
- segment_lengths: int32 [1, 13], replicated, may hold values from 128 to 4096, as said below
- leaf_parents: int32 [1, 8], replicated, may hold values from 0 to 3
Outputs:
- block_out: bfloat16 [10240, 2048], P('col', 'row')
- tokens_grad: float32 [10240, 2048], P('col', 'row')
- query_grad: float32 [2048, 2048], P('col', 'row')
- key_grad: float32 [2048, 2048], P('col', 'row')
- value_grad: float32 [2048, 4096], P('col', 'row')
- gate_grad: float32 [2048, 4096], P('col', 'row')
- out_grad: float32 [4096, 2048], P('row', 'col')
- up_grad: float32 [2048, 4096], P('col', 'row')
- down_grad: float32 [4096, 2048], P('row', 'col')
- first_gain_grad: float32 [2048], P(('row', 'col'))
- first_bias_grad: float32 [2048], P(('row', 'col'))
- group_gain_grad: float32 [4096], P(('row', 'col'))
- group_bias_grad: float32 [4096], P(('row', 'col'))
- second_gain_grad: float32 [2048], P(('row', 'col'))
- second_bias_grad: float32 [2048], P(('row', 'col'))
- up_bias_grad: float32 [4096], P(('row', 'col'))
- down_bias_grad: float32 [2048], P(('row', 'col'))
- norm_values: float32 [3], replicated
The draws below stay inside these ranges and needn't reach their ends.
Inputs may be any that keep to these rules, and one draw needn't show every extreme that they name: segment_lengths[t, 0] is tree t's trunk length, at most 4096; entries 1 to 4 are its branches' and 5 to 12 its leaves' lengths, each at most 512; every entry is at least a quarter of its slot; in tree 0 the trunk, the first branch and the first leaf fill their slots. leaf_parents[t, j] names the branch of tree t on which leaf j hangs.
All inputs are finite; a program needn't handle non-finite values.
Results may differ from the reference program's by a relative error of at most 0.014.
Values may be sent and summed in bfloat16 or wider, within the bound.
A program may use at most 256 MiB of HBM per device.

```python
import jax
import jax.numpy as jnp
from jax import lax

D = 2048
HEADS = 8
QK = 256
HV = 512
FF = 4096
TRUNK = 4096
SEG = 512
QD = 2048
VAL = 4096
TREE_LEN = 10240
TREES = 1
TOKENS = 10240


def draw_segment_lengths(key, part):
    slot_sizes = jnp.where(jnp.arange(13) == 0, TRUNK, SEG).astype(jnp.int32)
    full_key, short_key = jax.random.split(key)
    chosen = jax.random.randint(full_key, (TREES, 13), 0, 4) == 0
    shortfall = jax.random.randint(short_key, (TREES, 13), 0, 3 * slot_sizes // 4 + 1)
    columns = jnp.arange(13)[None, :]
    forced = (jnp.arange(TREES)[:, None] == 0) & ((columns == 0) | (columns == 1) | (columns == 5))
    lengths = slot_sizes[None, :] - jnp.where(chosen | forced, 0, shortfall)
    return lengths.astype(jnp.int32)


def plant(entries, own_key, low, high):
    longest = entries.shape.index(max(entries.shape))
    spots = []
    for shift in (0, 1):
        where = [jax.random.randint(jax.random.fold_in(own_key, axis), (), 0, length) for axis, length in enumerate(entries.shape)]
        where[longest] = (where[longest] + shift) % entries.shape[longest]
        spots.append(tuple(where))
    return entries.at[spots[0]].set(low).at[spots[1]].set(high)


def shard_levels(own_key, extent, cuts, low, high):
    loudness, own = 1.0, jax.random.fold_in(own_key, 6)
    for dim, blocks in cuts:
        draws = jnp.exp(jax.random.uniform(jax.random.fold_in(own, dim), (blocks,), jnp.float32, low / len(cuts), high / len(cuts)))
        loudness = loudness * jnp.repeat(draws, extent[dim] // blocks).reshape([-1 if axis == dim else 1 for axis in range(len(extent))])
    return loudness


def normal_values(key, dims, width, reach, cuts=(), kind=jnp.bfloat16):
    gain = shard_levels(key, dims, cuts, -0.22, 0.18) if cuts else 1.0
    drawn = jax.random.normal(key, dims, jnp.float32) * width * gain
    return jnp.minimum(jnp.maximum(drawn, -reach), reach).astype(kind)


def setup_inputs(seed: int = 0) -> dict:
    key_list = jax.random.split(jax.random.key(seed), 20)
    return {
        "tokens": normal_values(key_list[0], (TOKENS, D), 1.0, 6.0, ((0, 8), (1, 4))),
        "cotangent": normal_values(key_list[1], (TOKENS, D), 1.0, 6.0, ((0, 8), (1, 4))),
        "query_weight": normal_values(key_list[2], (D, QD), D ** -0.5, 0.125, ((0, 8), (1, 4))),
        "key_weight": normal_values(key_list[3], (D, QD), D ** -0.5, 0.125, ((0, 8), (1, 4))),
        "value_weight": normal_values(key_list[4], (D, VAL), D ** -0.5, 0.125, ((0, 8), (1, 4))),
        "gate_weight": normal_values(key_list[5], (D, VAL), D ** -0.5, 0.125, ((0, 8), (1, 4))),
        "out_weight": normal_values(key_list[6], (VAL, D), (VAL // 4) ** -0.5, 0.1875, ((0, 4), (1, 8))),
        "up_weight": normal_values(key_list[7], (D, FF), D ** -0.5, 0.125, ((0, 8), (1, 4))),
        "down_weight": normal_values(key_list[8], (FF, D), FF ** -0.5, 0.09375, ((0, 4), (1, 8))),
        "first_gain": jnp.clip(1.0 + 0.1 * jax.random.normal(key_list[9], (D,), jnp.float32), 0.5, 1.5),
        "first_bias": normal_values(key_list[10], (D,), 0.2, 1.0, ((0, 4),), jnp.float32),
        "group_gain": jnp.clip(1.0 + 0.1 * jax.random.normal(key_list[11], (VAL,), jnp.float32), 0.5, 1.5),
        "group_bias": normal_values(key_list[12], (VAL,), 0.2, 1.0, ((0, 4),), jnp.float32),
        "second_gain": jnp.clip(1.0 + 0.1 * jax.random.normal(key_list[13], (D,), jnp.float32), 0.5, 1.5),
        "second_bias": normal_values(key_list[14], (D,), 0.2, 1.0, ((0, 4),), jnp.float32),
        "up_bias": normal_values(key_list[15], (FF,), 0.2, 1.0, ((0, 4),), jnp.float32),
        "down_bias": normal_values(key_list[16], (D,), 0.2, 1.0, ((0, 4),), jnp.float32),
        "segment_lengths": draw_segment_lengths(jax.random.fold_in(key_list[19], 71), 0),
        "leaf_parents": plant(jax.random.randint(key_list[18], (TREES, 8), 0, 4), jax.random.fold_in(key_list[18], 1), 0, 3).astype(jnp.int32),
    }


EPSILON = 1e-05

@jax.custom_vjp
def low(v):
    return lax.optimization_barrier(v.astype(jnp.bfloat16)).astype(jnp.float32)

@jax.custom_vjp
def low_back(v):
    return v

def low_keep(v):
    return (low(v), None)

def low_pass(kept, grad):
    return (grad,)

def back_keep(v):
    return (v, None)

def back_low(kept, grad):
    return (low(grad),)
low.defvjp(low_keep, low_pass)
low_back.defvjp(back_keep, back_low)

def lookup(values_table, positions):
    matches = positions[..., None] == jnp.arange(values_table.shape[0], dtype=jnp.int32)
    return lax.optimization_barrier(jnp.sum(jnp.where(matches, values_table, 0), axis=-1)).astype(jnp.int32)

def token_info(token_index, segment_lengths, leaf_parents):
    tree_count = segment_lengths.shape[0]
    tree_width = TRUNK + 12 * SEG
    tree_id = jnp.floor_divide(token_index, tree_width).astype(jnp.int32)
    inside = (tree_id >= 0) & (tree_id < tree_count)
    tree_safe = jnp.clip(tree_id, 0, tree_count - 1)
    offset_in = token_index - tree_id * tree_width
    in_trunk = offset_in < TRUNK
    beyond = jnp.maximum(offset_in - TRUNK, 0)
    segment = jnp.where(in_trunk, 0, 1 + beyond // SEG).astype(jnp.int32)
    position = jnp.where(in_trunk, offset_in, beyond % SEG).astype(jnp.int32)
    flat_lengths = segment_lengths.reshape(-1)
    own_length = lookup(flat_lengths, tree_safe * 13 + segment)
    trunk_length = lookup(flat_lengths, tree_safe * 13)
    leaf_slot = jnp.clip(segment - 5, 0, 7)
    branch = 1 + lookup(leaf_parents.reshape(-1), tree_safe * 8 + leaf_slot)
    parent = jnp.where(segment >= 5, branch, jnp.where(segment >= 1, 0, -1)).astype(jnp.int32)
    branch_length = lookup(flat_lengths, tree_safe * 13 + branch)
    path_depth = jnp.where(segment == 0, position, jnp.where(segment < 5, trunk_length + position, trunk_length + branch_length + position)).astype(jnp.int32)
    is_valid = inside & (position < own_length)
    return (jnp.where(inside, tree_id, -1).astype(jnp.int32), segment, position, path_depth, is_valid, parent)

def coefficients(query_info, key_info, log_decay):
    query_tree, query_segment, query_position, query_depth, query_valid, query_parent = query_info
    key_tree, key_segment, key_position, key_depth, key_valid, key_parent = key_info
    same_tree = (query_tree[:, None] == key_tree[None, :]) & key_valid[None, :]
    own_segment = (key_segment[None, :] == query_segment[:, None]) & (key_position[None, :] <= query_position[:, None])
    trunk_key = (key_segment[None, :] == 0) & (query_segment[:, None] > 0)
    parent_key = (query_segment[:, None] >= 5) & (key_segment[None, :] == query_parent[:, None])
    visible = same_tree & (own_segment | trunk_key | parent_key)
    distance = jnp.maximum(query_depth[:, None] - key_depth[None, :], 0).astype(jnp.float32)
    decayed = jnp.exp(distance[None, :, :] * log_decay[:, None, None]) * QK ** (-0.5)
    return (jnp.where(visible[None, :, :], decayed, 0.0).astype(jnp.float32), jnp.any(visible))

def rotation_tables(path_depth):
    half_width = QK // 2
    frequency = 10000.0 ** (-jnp.arange(half_width, dtype=jnp.float32) / (half_width - 1))
    angles = path_depth.astype(jnp.float32)[:, None] * frequency[None, :]
    return (jnp.cos(angles)[:, None, :], jnp.sin(angles)[:, None, :])

def rotate(values, cosine_table, sine_table):
    half_width = values.shape[-1] // 2
    leading = values[..., :half_width]
    trailing = values[..., half_width:]
    return jnp.concatenate([leading * cosine_table - trailing * sine_table, trailing * cosine_table + leading * sine_table], axis=-1)

def matmul(left, right):
    return jnp.dot(left, right, precision=lax.Precision.HIGHEST)

def layer_norm(values, gain_vector, bias_vector):
    average = lax.optimization_barrier(jnp.mean(values, axis=-1, keepdims=True))
    spread = lax.optimization_barrier(jnp.mean(values * values, axis=-1, keepdims=True)) - average * average
    return (values - average) * lax.rsqrt(spread + EPSILON) * gain_vector + bias_vector

def gate_piece(retained, gate_raw, gain_vector, bias_vector):
    average = lax.optimization_barrier(jnp.mean(retained, axis=-1, keepdims=True))
    centred = retained - average
    spread = lax.optimization_barrier(jnp.mean(centred * centred, axis=-1, keepdims=True))
    normed = (centred * lax.rsqrt(spread + EPSILON)).reshape(retained.shape[0], -1) * gain_vector + bias_vector
    return normed * jax.nn.silu(gate_raw)

def retention(queries, keys, values_in, segment_lengths, leaf_parents, log_decay):
    block_rows = 512 if TREE_LEN % 512 == 0 else TREE_LEN

    def one_tree(tree_number):
        begin = (tree_number * TREE_LEN).astype(jnp.int32)
        tree_keys = lax.dynamic_slice_in_dim(keys, begin, TREE_LEN, 0)
        tree_values = lax.dynamic_slice_in_dim(values_in, begin, TREE_LEN, 0)
        key_info = token_info(begin + jnp.arange(TREE_LEN, dtype=jnp.int32), segment_lengths, leaf_parents)

        def one_block(block_number):
            first_index = (begin + block_number * block_rows).astype(jnp.int32)
            block_queries = lax.dynamic_slice_in_dim(queries, first_index, block_rows, 0)
            query_info = token_info(first_index + jnp.arange(block_rows, dtype=jnp.int32), segment_lengths, leaf_parents)
            weights, any_seen = coefficients(query_info, key_info, log_decay)
            products = jnp.einsum('qhd,khd->hqk', block_queries, tree_keys, precision=lax.Precision.HIGHEST)
            scores = low(low_back(products) * weights)
            return jnp.einsum('hqk,khe->qhe', scores, tree_values, precision=lax.Precision.HIGHEST)
        outputs = lax.map(jax.checkpoint(one_block), jnp.arange(TREE_LEN // block_rows, dtype=jnp.int32))
        return outputs.reshape(TREE_LEN, HEADS, HV)
    result = lax.map(one_tree, jnp.arange(TREES, dtype=jnp.int32))
    return result.reshape(TOKENS, HEADS, HV)

def layer(params, cosine_table, sine_table, log_decay, segment_lengths, leaf_parents):
    tokens, query_weight, key_weight, value_weight, gate_weight, out_weight, up_weight, down_weight, first_gain, first_bias, group_gain, group_bias, second_gain, second_bias, up_bias, down_bias = params
    first_low = low(layer_norm(tokens, first_gain, first_bias))
    queries = low(rotate(low_back(matmul(first_low, query_weight)).reshape(TOKENS, HEADS, QK), cosine_table, sine_table))
    keys = low(rotate(low_back(matmul(first_low, key_weight)).reshape(TOKENS, HEADS, QK), cosine_table, sine_table))
    values_in = low(low_back(matmul(first_low, value_weight))).reshape(TOKENS, HEADS, HV)
    gate_raw = low_back(matmul(first_low, gate_weight))
    retained = low_back(retention(queries, keys, values_in, segment_lengths, leaf_parents, log_decay))
    gated_out = low(gate_piece(retained, gate_raw, group_gain, group_bias))
    attended = low_back(matmul(gated_out, out_weight))
    middle = tokens + attended
    second = low(layer_norm(middle, second_gain, second_bias))
    before = low_back(matmul(second, up_weight) + up_bias)
    hidden = low(jax.nn.gelu(before, approximate=False))
    fed_out = low_back(matmul(hidden, down_weight) + down_bias)
    return (middle + fed_out, (attended, fed_out))

def reference(tokens, cotangent, query_weight, key_weight, value_weight, gate_weight, out_weight, up_weight, down_weight, first_gain, first_bias, group_gain, group_bias, second_gain, second_bias, up_bias, down_bias, segment_lengths, leaf_parents):
    info = token_info(jnp.arange(TOKENS, dtype=jnp.int32), segment_lengths, leaf_parents)
    valid_rows = info[4].astype(jnp.float32)
    cosine_table, sine_table = rotation_tables(info[3])
    log_decay = jnp.log(1.0 - 2.0 ** (-5.0 - jnp.arange(HEADS, dtype=jnp.float32)))
    primals = tuple((argument.astype(jnp.float32) for argument in (tokens, query_weight, key_weight, value_weight, gate_weight, out_weight, up_weight, down_weight, first_gain, first_bias, group_gain, group_bias, second_gain, second_bias, up_bias, down_bias)))

    def forward(*params):
        return layer(params, cosine_table, sine_table, log_decay, segment_lengths, leaf_parents)
    layer_out, pullback, branches = jax.vjp(forward, *primals, has_aux=True)
    gradients = pullback(cotangent.astype(jnp.float32) * valid_rows[:, None])
    attended, fed_out = branches
    valid_count = jnp.sum(segment_lengths).astype(jnp.float32) * D
    column = valid_rows[:, None]
    norm_values = jnp.sqrt(jnp.stack([jnp.sum(column * layer_out * layer_out), jnp.sum(column * attended * attended), jnp.sum(column * fed_out * fed_out)]) / valid_count)
    return (layer_out.astype(jnp.bfloat16), gradients[0], gradients[1], gradients[2], gradients[3], gradients[4], gradients[5], gradients[6], gradients[7], gradients[8], gradients[9], gradients[10], gradients[11], gradients[12], gradients[13], gradients[14], gradients[15], norm_values)
```

```python
import functools

import jax
import jax.numpy as jnp
from jax import lax
from jax.experimental import pallas as pl
from jax.experimental.pallas import tpu as pltpu
from jax.sharding import PartitionSpec as P

D = 2048
QK = 256
HV = 512
TRUNK = 4096
SEG = 512
TREE_LEN = TRUNK + 12 * SEG
CHUNK = 256
TRUNK_CHUNKS = TRUNK // CHUNK
SLOTS = 8

EPSILON = 1e-05
SCALE = QK**-0.5
F32 = jnp.float32
BF16 = jnp.bfloat16

X_PAIRS = [(0, 1), (1, 0), (2, 3), (3, 2)]
Y_PAIRS = [(0, 2), (2, 0), (1, 3), (3, 1)]
D_PAIRS = [(0, 3), (3, 0), (1, 2), (2, 1)]


def mm(a, b):
    return lax.dot_general(a, b, (((1,), (0,)), ((), ())), preferred_element_type=F32)


def mm_nt(a, b):
    return lax.dot_general(a, b, (((1,), (1,)), ((), ())), preferred_element_type=F32)


def mm_tn(a, b):
    return lax.dot_general(a, b, (((0,), (0,)), ((), ())), preferred_element_type=F32)


def params(semantics, limit=None):
    return pltpu.CompilerParams(
        dimension_semantics=semantics, vmem_limit_bytes=limit or 60 * 1024 * 1024
    )


def smem():
    return pl.BlockSpec(memory_space=pltpu.SMEM)


class Chunk:
    def __init__(self, meta, index):
        in_trunk = index < TRUNK_CHUNKS
        beyond = jnp.maximum(index - TRUNK_CHUNKS, 0)
        self.in_trunk = in_trunk
        self.segment = jnp.where(in_trunk, 0, 1 + beyond // 2)
        self.first = jnp.where(in_trunk, index * CHUNK, (beyond % 2) * CHUNK)
        length = meta[self.segment]
        trunk_length = meta[0]
        self.trunk_length = trunk_length
        self.length = length
        self.is_leaf = self.segment >= 5
        self.parent = meta[13 + jnp.clip(self.segment - 5, 0, 7)]
        parent_length = meta[1 + self.parent]
        self.start = jnp.where(
            in_trunk,
            self.first,
            trunk_length + self.first + jnp.where(self.is_leaf, parent_length, 0),
        )
        self.count = jnp.clip(length - self.first, 0, CHUNK)
        self.end = self.start + self.count
        self.continues = jnp.where(in_trunk, index + 1 < TRUNK_CHUNKS, beyond % 2 == 0)


def trunk_reference(meta, place, rows):
    return jnp.minimum(meta[0], jnp.minimum(rows * (place + 1), TRUNK))


def slot_branch(slot):
    return (slot - 4 + 2) % 4


def power(rate, exponent, width):
    return jnp.exp(jnp.full((1, width), exponent.astype(F32), F32) * rate)


def column_power(rate, exponents):
    return jnp.exp(exponents.astype(F32) * rate)


def token_column(width=1):
    return lax.broadcasted_iota(jnp.int32, (CHUNK, width), 0)


def decay_matrix(rate, count):
    t = lax.broadcasted_iota(jnp.int32, (CHUNK, CHUNK), 0)
    u = lax.broadcasted_iota(jnp.int32, (CHUNK, CHUNK), 1)
    seen = (u <= t) & (u < count)
    return jnp.where(seen, jnp.exp((t - u).astype(F32) * rate) * SCALE, 0.0)


def key_decay(rate, count):
    j = token_column()
    return jnp.where(j < count, column_power(rate, jnp.maximum(count - j, 0)), 0.0)


def export_terms(meta, chunk, local, chunks, place, slot, rows):
    if slot == 0:
        is_shift = ((place == 4) | (place == 6)) & (local == chunks - 1)
        exponent = jnp.where(
            chunk.in_trunk,
            jnp.maximum(trunk_reference(meta, place, rows) - chunk.end, 0),
            0,
        )
        return chunk.in_trunk | is_shift, exponent
    wanted = (place == 3) | (place == 4)
    mine = (chunk.segment % 2 == 1) if slot == 1 else (chunk.segment % 2 == 0)
    is_branch = (chunk.segment >= 1) & (chunk.segment < 5)
    exponent = jnp.where(is_branch, jnp.maximum(chunk.length - chunk.first - chunk.count, 0), 0)
    return wanted & mine & is_branch, exponent


def import_terms(meta, chunk, place, slot, rows):
    if slot < 4:
        sees = jnp.logical_not(chunk.in_trunk) | (place > slot)
        return sees, jnp.maximum(chunk.start - trunk_reference(meta, jnp.int32(slot), rows), 0)
    sees = chunk.is_leaf & (chunk.parent == slot_branch(slot))
    return sees, chunk.first


def shift_in(meta, place, chunks):
    previous = Chunk(meta, jnp.maximum(place * chunks - 1, 0))
    return (place == 5) | (place == 7), CHUNK - previous.count


def states_kernel(rows, chunks, meta, rates, key, value, out, acc):
    local = pl.program_id(1)
    rate = rates[pl.program_id(0)]
    place = meta[21]
    chunk = Chunk(meta, place * chunks + local)
    weighted = (key[...].astype(F32) * key_decay(rate, chunk.count)).astype(BF16)
    state = mm_tn(weighted, value[...])

    @pl.when(local == 0)
    def _():
        acc[...] = jnp.zeros_like(acc)

    for slot in range(3):
        on, exponent = export_terms(meta, chunk, local, chunks, place, slot, rows)

        @pl.when(on)
        def _():
            acc[slot] += state * power(rate, exponent, HV)

    @pl.when(local == chunks - 1)
    def _():
        out[:, 0] = acc[...].astype(BF16)


def make_states(meta, rates, key, value):
    rows = key.shape[0]
    heads = key.shape[1] // QK
    chunks = rows // CHUNK
    return pl.pallas_call(
        functools.partial(states_kernel, rows, chunks),
        grid=(heads, chunks),
        in_specs=[
            smem(),
            smem(),
            pl.BlockSpec((CHUNK, QK), lambda h, c: (c, h)),
            pl.BlockSpec((CHUNK, HV), lambda h, c: (c, h)),
        ],
        out_specs=pl.BlockSpec((3, 1, QK, HV), lambda h, c: (0, h, 0, 0)),
        out_shape=jax.ShapeDtypeStruct((3, heads, QK, HV), BF16),
        scratch_shapes=[pltpu.VMEM((3, QK, HV), F32)],
        compiler_params=params(("arbitrary", "arbitrary")),
        name="chunk_states",
        cost_estimate=pl.CostEstimate(
            flops=2 * rows * heads * QK * HV, bytes_accessed=rows * heads * 1536, transcendentals=0
        ),
    )(meta, rates, key, value)


def retain_kernel(
    rows, chunks, meta, rates, query, key, value, gate, shared, shifted, gain, bias,
    gated_out, normal_out, inverse_out, state_out, running,
):
    local = pl.program_id(1)
    rate = rates[pl.program_id(0)]
    place = meta[21]
    chunk = Chunk(meta, place * chunks + local)

    @pl.when(local == 0)
    def _():
        running[...] = jnp.zeros_like(running)
        on, exponent = shift_in(meta, place, chunks)

        @pl.when(on)
        def _():
            running[...] = shifted[0].astype(F32) * power(rate, exponent, HV)

    incoming = running[...]
    state_ref = state_out.at[0, 0]
    running_total = incoming
    for slot in range(SLOTS):
        on, exponent = import_terms(meta, chunk, place, slot, rows)
        scale = jnp.where(on, power(rate, exponent, HV), 0.0)
        running_total = running_total + shared[slot, 0].astype(F32) * scale
    state = running_total.astype(BF16)
    state_ref[...] = state

    q, k, v = query[...], key[...], value[...]
    scores = (mm_nt(q, k) * decay_matrix(rate, chunk.count)).astype(BF16)
    own = token_column()
    reach = column_power(rate, own) * SCALE
    retained = mm(scores, v) + mm(q, state) * reach

    j = token_column()
    ahead = jnp.where(j < chunk.count, column_power(rate, CHUNK - j), 0.0)
    fresh = mm_tn((k.astype(F32) * ahead).astype(BF16), v)
    keep = jnp.where(chunk.continues, 1.0, 0.0)
    running[...] = (incoming * power(rate, jnp.int32(CHUNK), HV) + fresh) * keep

    average = jnp.mean(retained, axis=1, keepdims=True)
    centred = retained - average
    inverse = lax.rsqrt(jnp.mean(centred * centred, axis=1, keepdims=True) + EPSILON)
    normal = centred * inverse
    gate_value = gate[...].astype(F32)
    gated = (normal * gain[...] + bias[...]) * (gate_value / (1.0 + jnp.exp(-gate_value)))
    gated_out[...] = gated.astype(BF16)
    normal_out[...] = normal.astype(BF16)
    inverse_out[0] = jnp.broadcast_to(inverse, (CHUNK, 128))


def retain(meta, rates, query, key, value, gate, shared, shifted, gain, bias):
    rows = key.shape[0]
    heads = key.shape[1] // QK
    chunks = rows // CHUNK
    wide = pl.BlockSpec((CHUNK, HV), lambda h, c: (c, h))
    narrow = pl.BlockSpec((CHUNK, QK), lambda h, c: (c, h))
    vector = pl.BlockSpec((1, HV), lambda h, c: (0, h))
    return pl.pallas_call(
        functools.partial(retain_kernel, rows, chunks),
        grid=(heads, chunks),
        in_specs=[
            smem(), smem(), narrow, narrow, wide, wide,
            pl.BlockSpec((SLOTS, 1, QK, HV), lambda h, c: (0, h, 0, 0)),
            pl.BlockSpec((1, QK, HV), lambda h, c: (h, 0, 0)),
            vector, vector,
        ],
        out_specs=[
            wide, wide,
            pl.BlockSpec((1, CHUNK, 128), lambda h, c: (h, c, 0)),
            pl.BlockSpec((1, 1, QK, HV), lambda h, c: (h, c, 0, 0)),
        ],
        out_shape=[
            jax.ShapeDtypeStruct((rows, heads * HV), BF16),
            jax.ShapeDtypeStruct((rows, heads * HV), BF16),
            jax.ShapeDtypeStruct((heads, rows, 128), F32),
            jax.ShapeDtypeStruct((heads, chunks, QK, HV), BF16),
        ],
        scratch_shapes=[pltpu.VMEM((QK, HV), F32)],
        compiler_params=params(("arbitrary", "arbitrary")),
        name="retention_forward",
        cost_estimate=pl.CostEstimate(
            flops=2 * rows * heads * (CHUNK * 768 + 2 * QK * HV),
            bytes_accessed=rows * heads * 8192,
            transcendentals=rows * heads * 768,
        ),
    )(meta, rates, query, key, value, gate, shared, shifted, gain[None, :], bias[None, :])


def gate_back_kernel(
    rows, chunks, meta, rates, wide, weight, gate, normal_in, inverse_in, query, gain, bias,
    gate_out, retained_out, gain_out, bias_out, exports, first_out, acc,
):
    local = pl.program_id(1)
    rate = rates[pl.program_id(0)]
    place = meta[21]
    chunk = Chunk(meta, place * chunks + local)
    grad_gated = mm(wide[...], weight[...])
    gate_value = gate[...].astype(F32)
    normal = normal_in[...].astype(F32)
    sigmoid = 1.0 / (1.0 + jnp.exp(-gate_value))
    normed = normal * gain[...] + bias[...]
    grad_gate = grad_gated * normed * (sigmoid * (1.0 + gate_value * (1.0 - sigmoid)))
    gate_out[...] = grad_gate.astype(BF16)
    grad_normed = grad_gated * (gate_value * sigmoid)

    @pl.when(local == 0)
    def _():
        gain_out[...] = jnp.zeros_like(gain_out)
        bias_out[...] = jnp.zeros_like(bias_out)
        acc[...] = jnp.zeros_like(acc)

    gain_out[...] += jnp.sum(grad_normed * normal, axis=0, keepdims=True)
    bias_out[...] += jnp.sum(grad_normed, axis=0, keepdims=True)
    scaled = grad_normed * gain[...]
    grad = inverse_in[0][:, :1] * (
        scaled
        - jnp.mean(scaled, axis=1, keepdims=True)
        - normal * jnp.mean(scaled * normal, axis=1, keepdims=True)
    )
    grad = grad.astype(BF16)
    retained_out[...] = grad
    reach = column_power(rate, token_column()) * SCALE
    state = mm_tn((query[...].astype(F32) * reach).astype(BF16), grad)
    for slot in range(SLOTS):
        on, exponent = import_terms(meta, chunk, place, slot, rows)

        @pl.when(on)
        def _():
            acc[slot] += state * power(rate, exponent, HV)

    @pl.when(local == 0)
    def _():
        on, exponent = shift_in(meta, place, chunks)
        scale = jnp.where(on, power(rate, exponent, HV), 0.0)
        first_out[0] = (state * scale).astype(BF16)

    @pl.when(local == chunks - 1)
    def _():
        exports[:, 0] = acc[...].astype(BF16)


def gate_back(meta, rates, wide, weight, gate, normal, inverse, query, gain, bias):
    rows = query.shape[0]
    heads = query.shape[1] // QK
    chunks = rows // CHUNK
    block = pl.BlockSpec((CHUNK, HV), lambda h, c: (c, h))
    vector = pl.BlockSpec((1, HV), lambda h, c: (0, h))
    return pl.pallas_call(
        functools.partial(gate_back_kernel, rows, chunks),
        grid=(heads, chunks),
        in_specs=[
            smem(), smem(),
            pl.BlockSpec((CHUNK, D), lambda h, c: (c, 0)),
            pl.BlockSpec((D, HV), lambda h, c: (0, h)),
            block, block,
            pl.BlockSpec((1, CHUNK, 128), lambda h, c: (h, c, 0)),
            pl.BlockSpec((CHUNK, QK), lambda h, c: (c, h)),
            vector, vector,
        ],
        out_specs=[
            block, block, vector, vector,
            pl.BlockSpec((SLOTS, 1, QK, HV), lambda h, c: (0, h, 0, 0)),
            pl.BlockSpec((1, QK, HV), lambda h, c: (h, 0, 0)),
        ],
        out_shape=[
            jax.ShapeDtypeStruct((rows, heads * HV), BF16),
            jax.ShapeDtypeStruct((rows, heads * HV), BF16),
            jax.ShapeDtypeStruct((1, heads * HV), F32),
            jax.ShapeDtypeStruct((1, heads * HV), F32),
            jax.ShapeDtypeStruct((SLOTS, heads, QK, HV), BF16),
            jax.ShapeDtypeStruct((heads, QK, HV), BF16),
        ],
        scratch_shapes=[pltpu.VMEM((SLOTS, QK, HV), F32)],
        compiler_params=params(("arbitrary", "arbitrary")),
        name="gate_backward",
        cost_estimate=pl.CostEstimate(
            flops=2 * rows * heads * HV * (D + QK),
            bytes_accessed=rows * heads * 12288,
            transcendentals=rows * heads * HV,
        ),
    )(meta, rates, wide, weight, gate, normal, inverse, query, gain[None, :], bias[None, :])


def retain_back_kernel(
    rows, chunks, meta, rates, query, key, value, grad, state_in, cosine, sine, own0, own1, own2,
    query_out, key_out, value_out, running,
):
    step = pl.program_id(1)
    local = chunks - 1 - step
    rate = rates[pl.program_id(0)]
    place = meta[21]
    chunk = Chunk(meta, place * chunks + local)
    before = Chunk(meta, jnp.maximum(place * chunks + local - 1, 0))

    @pl.when(step == 0)
    def _():
        running[...] = jnp.zeros_like(running)

    later = running[...]
    total = later
    for slot, ref in ((0, own0), (1, own1), (2, own2)):
        on, exponent = export_terms(meta, chunk, local, chunks, place, slot, rows)
        total = total + ref[0].astype(F32) * jnp.where(on, power(rate, exponent, HV), 0.0)
    total = total.astype(BF16)

    q, k, v, g = query[...], key[...], value[...], grad[...]
    decay = decay_matrix(rate, chunk.count)
    scores = (mm_nt(q, k) * decay).astype(BF16)
    slopes = (mm_nt(g, v) * decay).astype(BF16)
    reach = column_power(rate, token_column()) * SCALE
    toward = key_decay(rate, chunk.count)
    grad_query = mm(slopes, k) + mm_nt(g, state_in[0, 0]) * reach
    grad_key = mm_tn(slopes, q) + mm_nt(v, total) * toward
    grad_value = mm_tn(scores, g) + mm(k, total) * toward
    value_out[...] = grad_value.astype(BF16)
    cos, sin = cosine[...], sine[...]
    half = QK // 2
    for out, val in ((query_out, grad_query), (key_out, grad_key)):
        a, b = val[:, :half], val[:, half:]
        out[:, :half] = (a * cos + b * sin).astype(BF16)
        out[:, half:] = (b * cos - a * sin).astype(BF16)

    fresh = mm_tn((q.astype(F32) * reach).astype(BF16), g)
    carried = fresh + later * power(rate, chunk.count, HV)
    keep = jnp.where((local > 0) & before.continues, 1.0, 0.0)
    running[...] = carried * power(rate, CHUNK - before.count, HV) * keep


def retain_back(meta, rates, query, key, value, grad, states, cosine, sine, own):
    rows = query.shape[0]
    heads = query.shape[1] // QK
    chunks = rows // CHUNK
    last = chunks - 1
    wide = pl.BlockSpec((CHUNK, HV), lambda h, s: (last - s, h))
    narrow = pl.BlockSpec((CHUNK, QK), lambda h, s: (last - s, h))
    table = pl.BlockSpec((CHUNK, QK // 2), lambda h, s: (last - s, 0))
    state = pl.BlockSpec((1, QK, HV), lambda h, s: (h, 0, 0))
    return pl.pallas_call(
        functools.partial(retain_back_kernel, rows, chunks),
        grid=(heads, chunks),
        in_specs=[
            smem(), smem(), narrow, narrow, wide, wide,
            pl.BlockSpec((1, 1, QK, HV), lambda h, s: (h, last - s, 0, 0)),
            table, table, state, state, state,
        ],
        out_specs=[narrow, narrow, wide],
        out_shape=[
            jax.ShapeDtypeStruct((rows, heads * QK), BF16),
            jax.ShapeDtypeStruct((rows, heads * QK), BF16),
            jax.ShapeDtypeStruct((rows, heads * HV), BF16),
        ],
        scratch_shapes=[pltpu.VMEM((QK, HV), F32)],
        compiler_params=params(("arbitrary", "arbitrary")),
        name="retention_backward",
        cost_estimate=pl.CostEstimate(
            flops=2 * rows * heads * (CHUNK * 1792 + 4 * QK * HV),
            bytes_accessed=rows * heads * 6144,
            transcendentals=rows * heads * 256,
        ),
    )(meta, rates, query, key, value, grad, states, cosine, sine, *own)


def norm_kernel(values, gain, bias, out, average_out, inverse_out):
    x = values[...].astype(F32)
    average = jnp.mean(x, axis=1, keepdims=True)
    inverse = lax.rsqrt(jnp.mean(x * x, axis=1, keepdims=True) - average * average + EPSILON)
    out[...] = ((x - average) * inverse * gain[...] + bias[...]).astype(BF16)
    average_out[...] = jnp.broadcast_to(average, average_out.shape)
    inverse_out[...] = jnp.broadcast_to(inverse, inverse_out.shape)


def norm_wide(values, gain, bias):
    rows = values.shape[0]
    block = pl.BlockSpec((CHUNK, D), lambda i: (i, 0))
    vector = pl.BlockSpec((1, D), lambda i: (0, 0))
    stat = pl.BlockSpec((CHUNK, 128), lambda i: (i, 0))
    return pl.pallas_call(
        norm_kernel,
        grid=(rows // CHUNK,),
        in_specs=[block, vector, vector],
        out_specs=[block, stat, stat],
        out_shape=[
            jax.ShapeDtypeStruct((rows, D), BF16),
            jax.ShapeDtypeStruct((rows, 128), F32),
            jax.ShapeDtypeStruct((rows, 128), F32),
        ],
        compiler_params=params(("arbitrary",)),
        name="layer_norm",
        cost_estimate=pl.CostEstimate(
            flops=8 * rows * D, bytes_accessed=4 * rows * D, transcendentals=rows
        ),
    )(values, gain[None, :], bias[None, :])


def rotate_kernel(heads, values, weight, cosine, sine, out):
    raw = mm(values[...], weight[...])
    cos, sin = cosine[...], sine[...]
    half = QK // 2
    for head in range(heads):
        a = raw[:, head * QK : head * QK + half]
        b = raw[:, head * QK + half : (head + 1) * QK]
        out[:, head * QK : head * QK + half] = (a * cos - b * sin).astype(BF16)
        out[:, head * QK + half : (head + 1) * QK] = (b * cos + a * sin).astype(BF16)


def project_rotated(values, weight, cosine, sine):
    rows, width = values.shape[0], weight.shape[1]
    table = pl.BlockSpec((CHUNK, QK // 2), lambda i: (i, 0))
    return pl.pallas_call(
        functools.partial(rotate_kernel, width // QK),
        grid=(rows // CHUNK,),
        in_specs=[
            pl.BlockSpec((CHUNK, D), lambda i: (i, 0)),
            pl.BlockSpec((D, width), lambda i: (0, 0)),
            table, table,
        ],
        out_specs=pl.BlockSpec((CHUNK, width), lambda i: (i, 0)),
        out_shape=jax.ShapeDtypeStruct((rows, width), BF16),
        compiler_params=params(("arbitrary",)),
        name="project_rotated",
        cost_estimate=pl.CostEstimate(
            flops=2 * rows * D * width, bytes_accessed=2 * (rows + width) * D, transcendentals=0
        ),
    )(values, weight, cosine, sine)


def up_kernel(values, weight, bias, grad_hidden, hidden_out, grad_out, bias_out):
    before = mm(values[...], weight[...]) + bias[...]
    phi = 0.5 * (1.0 + lax.erf(before * (0.5**0.5)))
    hidden_out[...] = (before * phi).astype(BF16)
    density = jnp.exp(-0.5 * before * before) * 0.3989422804014327
    grad = (grad_hidden[...].astype(F32) * (phi + before * density)).astype(BF16)
    grad_out[...] = grad

    @pl.when(pl.program_id(0) == 0)
    def _():
        bias_out[...] = jnp.zeros_like(bias_out)

    bias_out[...] += jnp.sum(grad.astype(F32), axis=0, keepdims=True)


def feed_up(values, weight, bias, grad_hidden):
    rows, width = values.shape[0], weight.shape[1]
    block = pl.BlockSpec((CHUNK, width), lambda i: (i, 0))
    vector = pl.BlockSpec((1, width), lambda i: (0, 0))
    return pl.pallas_call(
        up_kernel,
        grid=(rows // CHUNK,),
        in_specs=[
            pl.BlockSpec((CHUNK, D), lambda i: (i, 0)),
            pl.BlockSpec((D, width), lambda i: (0, 0)),
            vector, block,
        ],
        out_specs=[block, block, vector],
        out_shape=[
            jax.ShapeDtypeStruct((rows, width), BF16),
            jax.ShapeDtypeStruct((rows, width), BF16),
            jax.ShapeDtypeStruct((1, width), F32),
        ],
        compiler_params=params(("arbitrary",)),
        name="feed_up",
        cost_estimate=pl.CostEstimate(
            flops=2 * rows * D * width,
            bytes_accessed=2 * (rows + width) * D + 8 * rows * width,
            transcendentals=2 * rows * width,
        ),
    )(values, weight, bias[None, :], grad_hidden)


PARTIAL_FLIP = (1, 3, 2, 3, 2, 1, 0, 0)
PARTIAL_HALF = (0, 0, 1, 1, 0, 1, 0, 1)


def table_lookup(table, step):
    result = jnp.int32(table[0])
    for index in range(1, len(table)):
        result = jnp.where(step == index, table[index], result)
    return result


def partial_kernel(count, row, *refs):
    values, weights = refs[:count], refs[count : 2 * count]
    outs = refs[2 * count :]
    step = pl.program_id(0)
    total = mm_nt(values[0][...], weights[0][...])
    for x, w in zip(values[1:], weights[1:]):
        total = total + mm_nt(x[...], w[...])
    for index, out in enumerate(outs):

        @pl.when(step // 2 == index)
        def _():
            out[0] = total.astype(out.dtype)


def partial_blocks(values, weights, row):
    rows = values[0].shape[0]
    half, block = rows // 2, D // 4
    count = len(values)

    def value_spec(x):
        return pl.BlockSpec((half, x.shape[1]), lambda s, r: (table_lookup(PARTIAL_HALF, s), 0))

    def weight_spec(w):
        return pl.BlockSpec(
            (block, w.shape[1]), lambda s, r: (r[0] ^ table_lookup(PARTIAL_FLIP, s), 0)
        )

    def out_spec(index):
        return pl.BlockSpec(
            (1, half, block), lambda s, r: (jnp.clip(s - 2 * index, 0, 1), 0, 0)
        )

    depth = sum(x.shape[1] for x in values)
    return pl.pallas_call(
        functools.partial(partial_kernel, count),
        grid_spec=pltpu.PrefetchScalarGridSpec(
            num_scalar_prefetch=1,
            grid=(8,),
            in_specs=[value_spec(x) for x in values] + [weight_spec(w) for w in weights],
            out_specs=[out_spec(index) for index in range(4)],
        ),
        out_shape=[
            jax.ShapeDtypeStruct((2, half, block), BF16 if index < 3 else F32) for index in range(4)
        ],
        compiler_params=params(("arbitrary",)),
        name="partial_blocks",
        cost_estimate=pl.CostEstimate(
            flops=2 * rows * D * depth,
            bytes_accessed=2 * (2 * rows + 2 * D) * depth + 4 * rows * D,
            transcendentals=0,
        ),
    )(row, *values, *weights)


def permute_row(value, pairs):
    return lax.ppermute(value, "row", pairs)


def reduce_row(values, weights, row):
    if lax.axis_size("row") != 4:
        total = sum(mm_nt(x, w) for x, w in zip(values, weights)).astype(BF16)
        return lax.psum_scatter(total, "row", scatter_dimension=1, tiled=True).astype(F32)
    send_x, send_y, keep, own = partial_blocks(values, weights, row)
    from_x = permute_row(send_x, X_PAIRS)
    from_y = permute_row(send_y, Y_PAIRS)
    next_y = (keep[0].astype(F32) + from_x[1].astype(F32)).astype(BF16)
    next_x = (keep[1].astype(F32) + from_y[1].astype(F32)).astype(BF16)
    last_y = permute_row(next_y, Y_PAIRS)
    last_x = permute_row(next_x, X_PAIRS)
    first_half = own[0] + from_x[0].astype(F32) + last_y.astype(F32)
    second_half = own[1] + from_y[0].astype(F32) + last_x.astype(F32)
    return jnp.concatenate([first_half, second_half], axis=0)


def gather_row(value):
    if lax.axis_size("row") != 4:
        return lax.all_gather(value, "row", axis=1, tiled=True)
    row = lax.axis_index("row")
    rows, block = value.shape
    half = rows // 2
    from_x = permute_row(value, X_PAIRS)
    from_y = permute_row(value, Y_PAIRS)
    far_a = permute_row(from_x[:half], Y_PAIRS)
    far_b = permute_row(from_y[half:], X_PAIRS)
    out = jnp.zeros((rows, 4 * block), value.dtype)
    zero = jnp.int32(0)
    out = lax.dynamic_update_slice(out, value, (zero, row * block))
    out = lax.dynamic_update_slice(out, from_x, (zero, (row ^ 1) * block))
    out = lax.dynamic_update_slice(out, from_y, (zero, (row ^ 2) * block))
    out = lax.dynamic_update_slice(out, far_a, (zero, (row ^ 3) * block))
    return lax.dynamic_update_slice(out, far_b, (jnp.int32(half), (row ^ 3) * block))


def gather_row_small(value):
    if lax.axis_size("row") != 4:
        return lax.all_gather(value, "row", axis=1, tiled=True)
    row = lax.axis_index("row")
    pieces = jnp.stack(
        [value] + [permute_row(value, pairs) for pairs in (X_PAIRS, Y_PAIRS, D_PAIRS)]
    )
    ordered = [
        lax.dynamic_index_in_dim(pieces, row ^ place, 0, keepdims=False) for place in range(4)
    ]
    return jnp.concatenate(ordered, axis=1)


def sum_row_small(value):
    if lax.axis_size("row") != 4:
        return lax.psum(value, "row")
    first = value + permute_row(value, X_PAIRS)
    return first + permute_row(first, Y_PAIRS)


def norm_backward(grad_out, normal, inverse, gain_vector):
    scaled = grad_out * gain_vector
    sums = sum_row_small(jnp.stack([jnp.sum(scaled, axis=1), jnp.sum(scaled * normal, axis=1)]))
    means = sums / D
    grad_in = inverse * (scaled - means[0][:, None] - normal * means[1][:, None])
    return (grad_in, jnp.sum(grad_out * normal, axis=0), jnp.sum(grad_out, axis=0))


def gather_col(weight):
    return lax.all_gather(weight, "col", axis=0, tiled=True)


def scatter_col(grad):
    return lax.psum_scatter(grad, "col", scatter_dimension=0, tiled=True).astype(F32)


def permute_col(value, pairs, place_count):
    size = lax.axis_size("col")
    all_pairs = [
        (base + a, base + b) for base in range(0, size, place_count) for a, b in pairs
    ]
    return lax.ppermute(value, "col", all_pairs)


def share_states(exports, place, tree):
    from_b0 = permute_col(exports[1], [(3, 6)], SLOTS)
    from_b = permute_col(exports[2], [(3, 7), (4, 5)], SLOTS)
    shifted = permute_col(exports[0], [(4, 5), (6, 7)], SLOTS)
    mine = jnp.where(
        place < 4,
        exports[0],
        jnp.where(place == 4, exports[1], jnp.where(place == 6, from_b0, from_b)),
    )
    shared = lax.all_gather(mine, "col", axis=0)
    if shared.shape[0] != SLOTS:
        shared = lax.dynamic_slice_in_dim(shared, tree * SLOTS, SLOTS, 0)
    return shared, shifted


def return_states(exports, first_state, place, tree):
    size = lax.axis_size("col")
    if size != SLOTS:
        full = jnp.zeros((size,) + exports.shape[1:], exports.dtype)
        zero = jnp.int32(0)
        exports = lax.dynamic_update_slice(full, exports, (tree * SLOTS, zero, zero, zero))
    mine = lax.psum_scatter(exports, "col", scatter_dimension=0, tiled=True)[0]
    to_b0 = permute_col(mine, [(6, 3)], SLOTS)
    to_b = permute_col(mine, [(7, 3), (5, 4)], SLOTS)
    shifted = permute_col(first_state, [(5, 4), (7, 6)], SLOTS)
    own0 = jnp.where(place < 4, mine, shifted)
    own1 = jnp.where(place == 4, mine, to_b0)
    return own0, own1, to_b


def sum_col_vectors(vectors, extra=None):
    col = lax.axis_index("col")
    size = lax.axis_size("col")
    parts = list(vectors) + ([extra] if extra is not None else [])
    total = jnp.sum(lax.all_gather(jnp.concatenate(parts), "col", axis=0), axis=0)
    results, first = [], 0
    for vector in vectors:
        width = vector.shape[0] // size
        results.append(lax.dynamic_slice_in_dim(total, first + col * width, width, 0))
        first += vector.shape[0]
    return results, total[first:]


def token_tables(place, rows, lengths, parents):
    index = place * rows + jnp.arange(rows, dtype=jnp.int32)
    in_trunk = index < TRUNK
    beyond = jnp.maximum(index - TRUNK, 0)
    segment = jnp.where(in_trunk, 0, 1 + beyond // SEG)
    position = jnp.where(in_trunk, index, beyond % SEG)

    def lookup(table, spots):
        hits = spots[:, None] == jnp.arange(table.shape[0], dtype=jnp.int32)
        return jnp.sum(jnp.where(hits, table, 0), axis=1)

    branch = 1 + lookup(parents, jnp.clip(segment - 5, 0, 7))
    parent_length = lookup(lengths, branch)
    depth = position + jnp.where(segment >= 1, lengths[0], 0)
    depth = depth + jnp.where(segment >= 5, parent_length, 0)
    valid = (position < lookup(lengths, segment)).astype(F32)
    half = QK // 2
    frequency = 10000.0 ** (-jnp.arange(half, dtype=F32) / (half - 1))
    angles = depth.astype(F32)[:, None] * frequency[None, :]
    return valid, jnp.cos(angles), jnp.sin(angles)


def body(
    tokens,
    cotangent,
    query_weight,
    key_weight,
    value_weight,
    gate_weight,
    out_weight,
    up_weight,
    down_weight,
    first_gain,
    first_bias,
    group_gain,
    group_bias,
    second_gain,
    second_bias,
    up_bias,
    down_bias,
    segment_lengths,
    leaf_parents,
):
    rows = tokens.shape[0]
    col = lax.axis_index("col")
    row = lax.axis_index("row")
    row_ref = row.astype(jnp.int32)[None]
    place = (col % SLOTS).astype(jnp.int32)
    tree = (col // SLOTS).astype(jnp.int32)
    lengths = lax.dynamic_index_in_dim(segment_lengths, tree, 0, keepdims=False)
    parents = lax.dynamic_index_in_dim(leaf_parents, tree, 0, keepdims=False)
    meta = jnp.concatenate([lengths, parents, place[None]]).astype(jnp.int32)
    heads = query_weight.shape[1] // QK
    head_numbers = (row * heads + jnp.arange(heads, dtype=jnp.int32)).astype(F32)
    rates = jnp.log(1.0 - 2.0 ** (-5.0 - head_numbers))

    query_full = gather_col(query_weight)
    key_full = gather_col(key_weight)
    value_full = gather_col(value_weight)
    gate_full = gather_col(gate_weight)
    out_full = gather_col(out_weight.T)
    up_full = gather_col(up_weight)
    down_full = gather_col(down_weight.T)

    valid, cosine, sine = token_tables(place, rows, lengths, parents)
    column = valid[:, None]
    gains = gather_row_small(jnp.stack([first_gain, first_bias, second_gain, second_bias]))
    token_wide = gather_row(tokens)
    fed_low = (cotangent.astype(F32) * column).astype(BF16)
    fed_wide = gather_row(fed_low)

    first_wide, first_average, first_inverse = norm_wide(token_wide, gains[0], gains[1])
    query_rot = project_rotated(first_wide, query_full, cosine, sine)
    key_rot = project_rotated(first_wide, key_full, cosine, sine)
    value_low = mm(first_wide, value_full).astype(BF16)
    exports = make_states(meta, rates, key_rot, value_low)
    shared, shifted = share_states(exports, place, tree)
    gate_raw = mm(first_wide, gate_full)
    gated, normal, inverse, states = retain(
        meta, rates, query_rot, key_rot, value_low, gate_raw, shared, shifted, group_gain, group_bias
    )

    attended = reduce_row([gated], [out_full], row_ref)
    middle = tokens.astype(F32) + attended
    middle_wide = gather_row(middle.astype(BF16))
    second_wide, second_average, second_inverse = norm_wide(middle_wide, gains[2], gains[3])
    grad_hidden = mm(fed_wide, down_full).astype(BF16)
    hidden, grad_before, up_bias_grad = feed_up(second_wide, up_full, up_bias, grad_hidden)
    second_back = reduce_row([grad_before], [up_full], row_ref)
    fed_out = reduce_row([hidden], [down_full], row_ref) + down_bias
    layer_out = middle + fed_out
    grad_fed = fed_low.astype(F32)
    down_grad = scatter_col(mm_tn(fed_wide, hidden).astype(BF16))
    up_grad = scatter_col(mm_tn(second_wide, grad_before).astype(BF16))
    down_bias_grad = jnp.sum(grad_fed, axis=0)

    second_normal = (middle - second_average[:, :1]) * second_inverse[:, :1]
    grad_middle_norm, second_gain_grad, second_bias_grad = norm_backward(
        second_back, second_normal, second_inverse[:, :1], second_gain
    )
    grad_middle = grad_fed + grad_middle_norm
    grad_wide = gather_row(grad_middle.astype(BF16))
    grad_gate, grad_retained, group_gain_grad, group_bias_grad, returns, first_state = gate_back(
        meta, rates, grad_wide, out_full, gate_raw, normal, inverse, query_rot, group_gain, group_bias
    )
    out_grad = scatter_col(mm_tn(grad_wide, gated).astype(BF16))
    own = return_states(returns, first_state, place, tree)
    gate_grad = scatter_col(mm_tn(first_wide, grad_gate).astype(BF16))
    grad_query, grad_key, grad_value = retain_back(
        meta, rates, query_rot, key_rot, value_low, grad_retained, states, cosine, sine, own
    )
    first_back = reduce_row(
        [grad_query, grad_key, grad_value, grad_gate],
        [query_full, key_full, value_full, gate_full],
        row_ref,
    )
    value_grad = scatter_col(mm_tn(first_wide, grad_value).astype(BF16))
    query_grad = scatter_col(mm_tn(first_wide, grad_query).astype(BF16))
    key_grad = scatter_col(mm_tn(first_wide, grad_key).astype(BF16))

    first_normal = (tokens.astype(F32) - first_average[:, :1]) * first_inverse[:, :1]
    grad_first, first_gain_grad, first_bias_grad = norm_backward(
        first_back, first_normal, first_inverse[:, :1], first_gain
    )
    tokens_grad = grad_middle + grad_first

    squares = jnp.stack(
        [
            jnp.sum(column * layer_out * layer_out),
            jnp.sum(column * attended * attended),
            jnp.sum(column * fed_out * fed_out),
        ]
    )
    vectors, col_squares = sum_col_vectors(
        (
            group_gain_grad[0],
            group_bias_grad[0],
            second_gain_grad,
            second_bias_grad,
            up_bias_grad[0],
            down_bias_grad,
        ),
        jnp.concatenate([squares, jnp.zeros((125,), F32)]),
    )
    totals = sum_row_small(col_squares[None, :])[0, :3]
    last, _ = sum_col_vectors((first_gain_grad, first_bias_grad))
    valid_count = jnp.sum(segment_lengths).astype(F32) * D
    norm_values = jnp.sqrt(totals / valid_count)
    return (
        layer_out.astype(BF16),
        tokens_grad,
        query_grad,
        key_grad,
        value_grad,
        gate_grad,
        out_grad.T,
        up_grad,
        down_grad.T,
        last[0],
        last[1],
        vectors[0],
        vectors[1],
        vectors[2],
        vectors[3],
        vectors[4],
        vectors[5],
        norm_values,
    )


def solution(mesh):
    matrix, turned, vector = P("col", "row"), P("row", "col"), P("row")
    in_specs = (matrix,) * 6 + (turned, matrix, turned) + (vector,) * 8 + (P(), P())
    split = P(("row", "col"))
    out_specs = (matrix,) * 6 + (turned, matrix, turned) + (split,) * 8 + (P(),)
    return jax.shard_map(body, mesh=mesh, in_specs=in_specs, out_specs=out_specs, check_vma=False)
```

```python
import functools

import jax
import jax.numpy as jnp
from jax import lax
from jax.experimental import pallas as pl
from jax.experimental.pallas import tpu as pltpu
from jax.sharding import PartitionSpec as P

D = 2048
QK = 256
HV = 512
TRUNK = 4096
SEG = 512
TREE_LEN = TRUNK + 12 * SEG
CHUNK = 256
TRUNK_CHUNKS = TRUNK // CHUNK
SLOTS = 8

EPSILON = 1e-05
SCALE = QK**-0.5
F32 = jnp.float32
BF16 = jnp.bfloat16

X_PAIRS = [(0, 1), (1, 0), (2, 3), (3, 2)]
Y_PAIRS = [(0, 2), (2, 0), (1, 3), (3, 1)]
D_PAIRS = [(0, 3), (3, 0), (1, 2), (2, 1)]


def mm(a, b):
    return lax.dot_general(a, b, (((1,), (0,)), ((), ())), preferred_element_type=F32)


def mm_nt(a, b):
    return lax.dot_general(a, b, (((1,), (1,)), ((), ())), preferred_element_type=F32)


def mm_tn(a, b):
    return lax.dot_general(a, b, (((0,), (0,)), ((), ())), preferred_element_type=F32)


def params(semantics, limit=None):
    return pltpu.CompilerParams(
        dimension_semantics=semantics, vmem_limit_bytes=limit or 60 * 1024 * 1024
    )


def smem():
    return pl.BlockSpec(memory_space=pltpu.SMEM)


class Chunk:
    def __init__(self, meta, index):
        in_trunk = index < TRUNK_CHUNKS
        beyond = jnp.maximum(index - TRUNK_CHUNKS, 0)
        self.in_trunk = in_trunk
        self.segment = jnp.where(in_trunk, 0, 1 + beyond // 2)
        self.first = jnp.where(in_trunk, index * CHUNK, (beyond % 2) * CHUNK)
        length = meta[self.segment]
        trunk_length = meta[0]
        self.trunk_length = trunk_length
        self.length = length
        self.is_leaf = self.segment >= 5
        self.parent = meta[13 + jnp.clip(self.segment - 5, 0, 7)]
        parent_length = meta[1 + self.parent]
        self.start = jnp.where(
            in_trunk,
            self.first,
            trunk_length + self.first + jnp.where(self.is_leaf, parent_length, 0),
        )
        self.count = jnp.clip(length - self.first, 0, CHUNK)
        self.end = self.start + self.count
        self.continues = jnp.where(in_trunk, index + 1 < TRUNK_CHUNKS, beyond % 2 == 0)


def trunk_reference(meta, place, rows):
    return jnp.minimum(meta[0], jnp.minimum(rows * (place + 1), TRUNK))


def power(rate, exponent, width):
    return jnp.exp(jnp.full((1, width), exponent.astype(F32), F32) * rate)


def column_power(rate, exponents):
    return jnp.exp(exponents.astype(F32) * rate)


def token_column(width=1):
    return lax.broadcasted_iota(jnp.int32, (CHUNK, width), 0)


def decay_matrix(rate, count):
    t = lax.broadcasted_iota(jnp.int32, (CHUNK, CHUNK), 0)
    u = lax.broadcasted_iota(jnp.int32, (CHUNK, CHUNK), 1)
    seen = (u <= t) & (u < count)
    return jnp.where(seen, jnp.exp((t - u).astype(F32) * rate) * SCALE, 0.0)


def key_decay(rate, count):
    j = token_column()
    return jnp.where(j < count, column_power(rate, jnp.maximum(count - j, 0)), 0.0)


def export_terms(meta, chunk, local, chunks, place, slot, rows):
    if slot == 0:
        is_shift = ((place == 4) | (place == 6)) & (local == chunks - 1)
        exponent = jnp.where(
            chunk.in_trunk,
            jnp.maximum(trunk_reference(meta, place, rows) - chunk.end, 0),
            0,
        )
        return chunk.in_trunk | is_shift, exponent
    wanted = (place == 3) | (place == 4)
    mine = (chunk.segment % 2 == 1) if slot == 1 else (chunk.segment % 2 == 0)
    is_branch = (chunk.segment >= 1) & (chunk.segment < 5)
    exponent = jnp.where(is_branch, jnp.maximum(chunk.length - chunk.first - chunk.count, 0), 0)
    return wanted & mine & is_branch, exponent


def import_terms(meta, chunk, place, slot, rows):
    if slot < 4:
        sees = jnp.logical_not(chunk.in_trunk) | (place > slot)
        if slot < 3:
            sees = sees & (place < 4)
        return sees, jnp.maximum(chunk.start - trunk_reference(meta, jnp.int32(slot), rows), 0)
    sees = chunk.is_leaf & (chunk.parent == slot - 4)
    return sees, chunk.first


def shift_in(meta, place, chunks):
    previous = Chunk(meta, jnp.maximum(place * chunks - 1, 0))
    return (place == 5) | (place == 7), CHUNK - previous.count


def states_kernel(rows, chunks, meta, rates, key, value, out, acc):
    local = pl.program_id(1)
    rate = rates[pl.program_id(0)]
    place = meta[21]
    chunk = Chunk(meta, place * chunks + local)
    weighted = (key[...].astype(F32) * key_decay(rate, chunk.count)).astype(BF16)
    state = mm_tn(weighted, value[...])

    @pl.when(local == 0)
    def _():
        acc[...] = jnp.zeros_like(acc)

    for slot in range(3):
        on, exponent = export_terms(meta, chunk, local, chunks, place, slot, rows)

        @pl.when(on)
        def _():
            acc[slot] += state * power(rate, exponent, HV)

    @pl.when(local == chunks - 1)
    def _():
        out[:, 0] = acc[...].astype(BF16)


def make_states(meta, rates, key, value):
    rows = key.shape[0]
    heads = key.shape[1] // QK
    chunks = rows // CHUNK
    return pl.pallas_call(
        functools.partial(states_kernel, rows, chunks),
        grid=(heads, chunks),
        in_specs=[
            smem(),
            smem(),
            pl.BlockSpec((CHUNK, QK), lambda h, c: (c, h)),
            pl.BlockSpec((CHUNK, HV), lambda h, c: (c, h)),
        ],
        out_specs=pl.BlockSpec((3, 1, QK, HV), lambda h, c: (0, h, 0, 0)),
        out_shape=jax.ShapeDtypeStruct((3, heads, QK, HV), BF16),
        scratch_shapes=[pltpu.VMEM((3, QK, HV), F32)],
        compiler_params=params(("arbitrary", "arbitrary")),
        name="chunk_states",
        cost_estimate=pl.CostEstimate(
            flops=2 * rows * heads * QK * HV, bytes_accessed=rows * heads * 1536, transcendentals=0
        ),
    )(meta, rates, key, value)


def retain_kernel(
    rows, chunks, meta, rates, query, key, value, gate, shared, shifted, gain, bias,
    gated_out, normal_out, inverse_out, state_out, running, total,
):
    local = pl.program_id(1)
    rate = rates[pl.program_id(0)]
    place = meta[21]
    chunk = Chunk(meta, place * chunks + local)

    @pl.when(local == 0)
    def _():
        running[...] = jnp.zeros_like(running)
        on, exponent = shift_in(meta, place, chunks)

        @pl.when(on)
        def _():
            running[...] = shifted[0].astype(F32) * power(rate, exponent, HV)

    incoming = running[...]
    total[...] = incoming
    for slot in range(SLOTS):
        on, exponent = import_terms(meta, chunk, place, slot, rows)

        @pl.when(on)
        def _():
            total[...] += shared[slot, 0].astype(F32) * power(rate, exponent, HV)

    state = total[...].astype(BF16)
    state_out[0, 0] = state

    q, k, v = query[...], key[...], value[...]
    scores = (mm_nt(q, k) * decay_matrix(rate, chunk.count)).astype(BF16)
    own = token_column()
    reach = column_power(rate, own) * SCALE
    retained = mm(scores, v) + mm(q, state) * reach

    j = token_column()
    ahead = jnp.where(j < chunk.count, column_power(rate, CHUNK - j), 0.0)
    fresh = mm_tn((k.astype(F32) * ahead).astype(BF16), v)
    keep = jnp.where(chunk.continues, 1.0, 0.0)
    running[...] = (incoming * power(rate, jnp.int32(CHUNK), HV) + fresh) * keep

    average = jnp.mean(retained, axis=1, keepdims=True)
    centred = retained - average
    inverse = lax.rsqrt(jnp.mean(centred * centred, axis=1, keepdims=True) + EPSILON)
    normal = centred * inverse
    gate_value = gate[...].astype(F32)
    gated = (normal * gain[...] + bias[...]) * (gate_value / (1.0 + jnp.exp(-gate_value)))
    gated_out[...] = gated.astype(BF16)
    normal_out[...] = normal.astype(BF16)
    inverse_out[0] = jnp.broadcast_to(inverse, (CHUNK, 128))


def retain(meta, rates, query, key, value, gate, shared, shifted, gain, bias):
    rows = key.shape[0]
    heads = key.shape[1] // QK
    chunks = rows // CHUNK
    wide = pl.BlockSpec((CHUNK, HV), lambda h, c: (c, h))
    narrow = pl.BlockSpec((CHUNK, QK), lambda h, c: (c, h))
    vector = pl.BlockSpec((1, HV), lambda h, c: (0, h))
    return pl.pallas_call(
        functools.partial(retain_kernel, rows, chunks),
        grid=(heads, chunks),
        in_specs=[
            smem(), smem(), narrow, narrow, wide, wide,
            pl.BlockSpec((SLOTS, 1, QK, HV), lambda h, c: (0, h, 0, 0)),
            pl.BlockSpec((1, QK, HV), lambda h, c: (h, 0, 0)),
            vector, vector,
        ],
        out_specs=[
            wide, wide,
            pl.BlockSpec((1, CHUNK, 128), lambda h, c: (h, c, 0)),
            pl.BlockSpec((1, 1, QK, HV), lambda h, c: (h, c, 0, 0)),
        ],
        out_shape=[
            jax.ShapeDtypeStruct((rows, heads * HV), BF16),
            jax.ShapeDtypeStruct((rows, heads * HV), BF16),
            jax.ShapeDtypeStruct((heads, rows, 128), F32),
            jax.ShapeDtypeStruct((heads, chunks, QK, HV), BF16),
        ],
        scratch_shapes=[pltpu.VMEM((QK, HV), F32), pltpu.VMEM((QK, HV), F32)],
        compiler_params=params(("arbitrary", "arbitrary")),
        name="retention_forward",
        cost_estimate=pl.CostEstimate(
            flops=2 * rows * heads * (CHUNK * 768 + 2 * QK * HV),
            bytes_accessed=rows * heads * 8192,
            transcendentals=rows * heads * 768,
        ),
    )(meta, rates, query, key, value, gate, shared, shifted, gain[None, :], bias[None, :])


def gate_back_kernel(
    rows, chunks, meta, rates, wide, weight, gate, normal_in, inverse_in, query, gain, bias,
    gate_out, retained_out, gain_out, bias_out, exports, first_out, acc,
):
    local = pl.program_id(1)
    rate = rates[pl.program_id(0)]
    place = meta[21]
    chunk = Chunk(meta, place * chunks + local)
    grad_gated = mm(wide[...], weight[...])
    gate_value = gate[...].astype(F32)
    normal = normal_in[...].astype(F32)
    sigmoid = 1.0 / (1.0 + jnp.exp(-gate_value))
    normed = normal * gain[...] + bias[...]
    grad_gate = grad_gated * normed * (sigmoid * (1.0 + gate_value * (1.0 - sigmoid)))
    gate_out[...] = grad_gate.astype(BF16)
    grad_normed = grad_gated * (gate_value * sigmoid)

    @pl.when(local == 0)
    def _():
        gain_out[...] = jnp.zeros_like(gain_out)
        bias_out[...] = jnp.zeros_like(bias_out)
        acc[...] = jnp.zeros_like(acc)

    gain_out[...] += jnp.sum(grad_normed * normal, axis=0, keepdims=True)
    bias_out[...] += jnp.sum(grad_normed, axis=0, keepdims=True)
    scaled = grad_normed * gain[...]
    grad = inverse_in[0][:, :1] * (
        scaled
        - jnp.mean(scaled, axis=1, keepdims=True)
        - normal * jnp.mean(scaled * normal, axis=1, keepdims=True)
    )
    grad = grad.astype(BF16)
    retained_out[...] = grad
    reach = column_power(rate, token_column()) * SCALE
    state = mm_tn((query[...].astype(F32) * reach).astype(BF16), grad)
    for slot in range(SLOTS):
        on, exponent = import_terms(meta, chunk, place, slot, rows)

        @pl.when(on)
        def _():
            acc[slot] += state * power(rate, exponent, HV)

    @pl.when(local == 0)
    def _():
        on, exponent = shift_in(meta, place, chunks)
        scale = jnp.where(on, power(rate, exponent, HV), 0.0)
        first_out[0] = (state * scale).astype(BF16)

    @pl.when(local == chunks - 1)
    def _():
        exports[:, 0] = acc[...].astype(BF16)


def gate_back(meta, rates, wide, weight, gate, normal, inverse, query, gain, bias):
    array, width, number = weight
    first = number * (width // HV)
    rows = query.shape[0]
    heads = query.shape[1] // QK
    chunks = rows // CHUNK
    block = pl.BlockSpec((CHUNK, HV), lambda h, c: (c, h))
    vector = pl.BlockSpec((1, HV), lambda h, c: (0, h))
    return pl.pallas_call(
        functools.partial(gate_back_kernel, rows, chunks),
        grid=(heads, chunks),
        in_specs=[
            smem(), smem(),
            pl.BlockSpec((CHUNK, D), lambda h, c: (c, 0)),
            pl.BlockSpec((D, HV), lambda h, c: (0, first + h)),
            block, block,
            pl.BlockSpec((1, CHUNK, 128), lambda h, c: (h, c, 0)),
            pl.BlockSpec((CHUNK, QK), lambda h, c: (c, h)),
            vector, vector,
        ],
        out_specs=[
            block, block, vector, vector,
            pl.BlockSpec((SLOTS, 1, QK, HV), lambda h, c: (0, h, 0, 0)),
            pl.BlockSpec((1, QK, HV), lambda h, c: (h, 0, 0)),
        ],
        out_shape=[
            jax.ShapeDtypeStruct((rows, heads * HV), BF16),
            jax.ShapeDtypeStruct((rows, heads * HV), BF16),
            jax.ShapeDtypeStruct((1, heads * HV), F32),
            jax.ShapeDtypeStruct((1, heads * HV), F32),
            jax.ShapeDtypeStruct((SLOTS, heads, QK, HV), BF16),
            jax.ShapeDtypeStruct((heads, QK, HV), BF16),
        ],
        scratch_shapes=[pltpu.VMEM((SLOTS, QK, HV), F32)],
        compiler_params=params(("arbitrary", "arbitrary")),
        name="gate_backward",
        cost_estimate=pl.CostEstimate(
            flops=2 * rows * heads * HV * (D + QK),
            bytes_accessed=rows * heads * 12288,
            transcendentals=rows * heads * HV,
        ),
    )(meta, rates, wide, array, gate, normal, inverse, query, gain[None, :], bias[None, :])


def retain_back_kernel(
    rows, chunks, meta, rates, query, key, value, grad, state_in, cosine, sine, own0, own1, own2,
    query_out, key_out, value_out, running, total_ref,
):
    step = pl.program_id(1)
    local = chunks - 1 - step
    rate = rates[pl.program_id(0)]
    place = meta[21]
    chunk = Chunk(meta, place * chunks + local)
    before = Chunk(meta, jnp.maximum(place * chunks + local - 1, 0))

    @pl.when(step == 0)
    def _():
        running[...] = jnp.zeros_like(running)

    later = running[...]
    total_ref[...] = later
    for slot, ref in ((0, own0), (1, own1), (2, own2)):
        on, exponent = export_terms(meta, chunk, local, chunks, place, slot, rows)

        @pl.when(on)
        def _():
            total_ref[...] += ref[0].astype(F32) * power(rate, exponent, HV)

    total = total_ref[...].astype(BF16)

    q, k, v, g = query[...], key[...], value[...], grad[...]
    decay = decay_matrix(rate, chunk.count)
    scores = (mm_nt(q, k) * decay).astype(BF16)
    slopes = (mm_nt(g, v) * decay).astype(BF16)
    reach = column_power(rate, token_column()) * SCALE
    toward = key_decay(rate, chunk.count)
    grad_query = mm(slopes, k) + mm_nt(g, state_in[0, 0]) * reach
    grad_key = mm_tn(slopes, q) + mm_nt(v, total) * toward
    grad_value = mm_tn(scores, g) + mm(k, total) * toward
    value_out[...] = grad_value.astype(BF16)
    cos, sin = cosine[...], sine[...]
    half = QK // 2
    for out, val in ((query_out, grad_query), (key_out, grad_key)):
        a, b = val[:, :half], val[:, half:]
        out[:, :half] = (a * cos + b * sin).astype(BF16)
        out[:, half:] = (b * cos - a * sin).astype(BF16)

    fresh = mm_tn((q.astype(F32) * reach).astype(BF16), g)
    carried = fresh + later * power(rate, chunk.count, HV)
    keep = jnp.where((local > 0) & before.continues, 1.0, 0.0)
    running[...] = carried * power(rate, CHUNK - before.count, HV) * keep


def retain_back(meta, rates, query, key, value, grad, states, cosine, sine, own):
    rows = query.shape[0]
    heads = query.shape[1] // QK
    chunks = rows // CHUNK
    last = chunks - 1
    wide = pl.BlockSpec((CHUNK, HV), lambda h, s: (last - s, h))
    narrow = pl.BlockSpec((CHUNK, QK), lambda h, s: (last - s, h))
    table = pl.BlockSpec((CHUNK, QK // 2), lambda h, s: (last - s, 0))
    state = pl.BlockSpec((1, QK, HV), lambda h, s: (h, 0, 0))
    return pl.pallas_call(
        functools.partial(retain_back_kernel, rows, chunks),
        grid=(heads, chunks),
        in_specs=[
            smem(), smem(), narrow, narrow, wide, wide,
            pl.BlockSpec((1, 1, QK, HV), lambda h, s: (h, last - s, 0, 0)),
            table, table, state, state, state,
        ],
        out_specs=[narrow, narrow, wide],
        out_shape=[
            jax.ShapeDtypeStruct((rows, heads * QK), BF16),
            jax.ShapeDtypeStruct((rows, heads * QK), BF16),
            jax.ShapeDtypeStruct((rows, heads * HV), BF16),
        ],
        scratch_shapes=[pltpu.VMEM((QK, HV), F32), pltpu.VMEM((QK, HV), F32)],
        compiler_params=params(("arbitrary", "arbitrary")),
        name="retention_backward",
        cost_estimate=pl.CostEstimate(
            flops=2 * rows * heads * (CHUNK * 1792 + 4 * QK * HV),
            bytes_accessed=rows * heads * 6144,
            transcendentals=rows * heads * 256,
        ),
    )(meta, rates, query, key, value, grad, states, cosine, sine, *own)


def norm_kernel(values, gain, bias, out, average_out, inverse_out):
    x = values[...].astype(F32)
    average = jnp.mean(x, axis=1, keepdims=True)
    inverse = lax.rsqrt(jnp.mean(x * x, axis=1, keepdims=True) - average * average + EPSILON)
    out[...] = ((x - average) * inverse * gain[...] + bias[...]).astype(BF16)
    average_out[...] = jnp.broadcast_to(average, average_out.shape)
    inverse_out[...] = jnp.broadcast_to(inverse, inverse_out.shape)


def norm_wide(values, gain, bias):
    rows = values.shape[0]
    block = pl.BlockSpec((CHUNK, D), lambda i: (i, 0))
    vector = pl.BlockSpec((1, D), lambda i: (0, 0))
    stat = pl.BlockSpec((CHUNK, 128), lambda i: (i, 0))
    return pl.pallas_call(
        norm_kernel,
        grid=(rows // CHUNK,),
        in_specs=[block, vector, vector],
        out_specs=[block, stat, stat],
        out_shape=[
            jax.ShapeDtypeStruct((rows, D), BF16),
            jax.ShapeDtypeStruct((rows, 128), F32),
            jax.ShapeDtypeStruct((rows, 128), F32),
        ],
        compiler_params=params(("arbitrary",)),
        name="layer_norm",
        cost_estimate=pl.CostEstimate(
            flops=8 * rows * D, bytes_accessed=4 * rows * D, transcendentals=rows
        ),
    )(values, gain[None, :], bias[None, :])


def join_kernel(row, own, from_x, from_y, far_a, far_b, *refs, norm):
    block = own.shape[1]
    second = pl.program_id(0) >= pl.num_programs(0) // 2
    spots = [
        pl.ds(pl.multiple_of((row[0] ^ flip) * block, 128), block) for flip in range(4)
    ]
    pieces = [own[...], from_x[...], from_y[...], jnp.where(second, far_b[...], far_a[...])]
    if not norm:
        for spot, piece in zip(spots, pieces):
            refs[0][:, spot] = piece
        return
    gain, bias, out, average_out, inverse_out = refs
    pieces = [piece.astype(F32) for piece in pieces]
    average = sum(jnp.sum(piece, axis=1, keepdims=True) for piece in pieces) / D
    squares = sum(jnp.sum(piece * piece, axis=1, keepdims=True) for piece in pieces) / D
    inverse = lax.rsqrt(squares - average * average + EPSILON)
    for spot, piece in zip(spots, pieces):
        out[:, spot] = ((piece - average) * inverse * gain[:, spot] + bias[:, spot]).astype(BF16)
    average_out[...] = jnp.broadcast_to(average, average_out.shape)
    inverse_out[...] = jnp.broadcast_to(inverse, inverse_out.shape)


def join(pieces, row, gain=None, bias=None):
    norm = gain is not None
    if not isinstance(pieces, tuple):
        return norm_wide(pieces, gain, bias) if norm else pieces
    rows, block = pieces[0].shape
    steps = 4
    tile = rows // steps
    piece = pl.BlockSpec((tile, block), lambda i, r: (i, 0))
    far_a = pl.BlockSpec((tile, block), lambda i, r: (jnp.minimum(i, steps // 2 - 1), 0))
    far_b = pl.BlockSpec((tile, block), lambda i, r: (jnp.maximum(i - steps // 2, 0), 0))
    vector = pl.BlockSpec((1, D), lambda i, r: (0, 0))
    wide = pl.BlockSpec((tile, D), lambda i, r: (i, 0))
    stat = pl.BlockSpec((tile, 128), lambda i, r: (i, 0))
    wide_shape = jax.ShapeDtypeStruct((rows, D), BF16)
    stat_shape = jax.ShapeDtypeStruct((rows, 128), F32)
    return pl.pallas_call(
        functools.partial(join_kernel, norm=norm),
        grid_spec=pltpu.PrefetchScalarGridSpec(
            num_scalar_prefetch=1,
            grid=(steps,),
            in_specs=[piece] * 3 + [far_a, far_b] + ([vector] * 2 if norm else []),
            out_specs=[wide, stat, stat] if norm else wide,
        ),
        out_shape=[wide_shape, stat_shape, stat_shape] if norm else wide_shape,
        compiler_params=params(("arbitrary",)),
        name="join_norm" if norm else "join",
        cost_estimate=pl.CostEstimate(
            flops=8 * rows * D, bytes_accessed=4 * rows * D, transcendentals=0
        ),
    )(row, *pieces, *((gain[None, :], bias[None, :]) if norm else ()))


def project_kernel(heads, values, weight, cosine, sine, query_out, key_out, value_out):
    raw = mm(values[...], weight[...])
    cos, sin = cosine[...], sine[...]
    half = QK // 2
    for part, out in ((0, query_out), (1, key_out)):
        for head in range(heads):
            first = (part * heads + head) * QK
            a, b = raw[:, first : first + half], raw[:, first + half : first + QK]
            out[:, head * QK : head * QK + half] = (a * cos - b * sin).astype(BF16)
            out[:, head * QK + half : (head + 1) * QK] = (b * cos + a * sin).astype(BF16)
    value_out[...] = raw[:, 2 * heads * QK :].astype(BF16)


def project(values, weight, cosine, sine):
    rows, width = values.shape[0], weight.shape[1]
    heads = width // (2 * QK + HV)
    table = pl.BlockSpec((CHUNK, QK // 2), lambda i: (i, 0))
    widths = (heads * QK, heads * QK, heads * HV)
    return pl.pallas_call(
        functools.partial(project_kernel, heads),
        grid=(rows // CHUNK,),
        in_specs=[
            pl.BlockSpec((CHUNK, D), lambda i: (i, 0)),
            pl.BlockSpec((D, width), lambda i: (0, 0)),
            table, table,
        ],
        out_specs=[pl.BlockSpec((CHUNK, w), lambda i: (i, 0)) for w in widths],
        out_shape=[jax.ShapeDtypeStruct((rows, w), BF16) for w in widths],
        compiler_params=params(("arbitrary",)),
        name="project",
        cost_estimate=pl.CostEstimate(
            flops=2 * rows * D * width, bytes_accessed=2 * (rows + width) * D, transcendentals=0
        ),
    )(values, weight, cosine, sine)


def matmul_kernel(values, weight, out):
    out[...] = mm(values[...], weight[...]).astype(out.dtype)


def matmul(values, weight, kind):
    array, width, number = weight
    rows = values.shape[0]
    return pl.pallas_call(
        matmul_kernel,
        grid=(rows // CHUNK,),
        in_specs=[
            pl.BlockSpec((CHUNK, D), lambda i: (i, 0)),
            pl.BlockSpec((D, width), lambda i: (0, number)),
        ],
        out_specs=pl.BlockSpec((CHUNK, width), lambda i: (i, 0)),
        out_shape=jax.ShapeDtypeStruct((rows, width), kind),
        compiler_params=params(("arbitrary",)),
        name="matmul",
        cost_estimate=pl.CostEstimate(
            flops=2 * rows * D * width, bytes_accessed=2 * (rows + width) * D, transcendentals=0
        ),
    )(values, array)


def weight_grad_kernel(spans, *refs):
    count = len(spans)
    lefts, rights, out = refs[:count], refs[count : 2 * count], refs[2 * count]
    tile = pl.program_id(0)
    for left, right, (first, last) in zip(lefts, rights, spans):

        @pl.when((tile >= first) & (tile < last))
        def _():
            out[...] = mm_tn(left[...], right[...]).astype(BF16)


def weight_grads(pairs):
    rows = pairs[0][0].shape[0]
    wide = min(right.shape[1] for _, right in pairs)
    tall = 1024
    steps = D // tall
    spans, first = [], 0
    for _, right in pairs:
        spans.append((first, first + right.shape[1] // wide))
        first = spans[-1][1]

    def left_spec(span):
        return pl.BlockSpec(
            (rows, tall),
            lambda n, m: (
                0, jnp.where(n < span[0], 0, jnp.where(n < span[1], m, steps - 1)),
            ),
        )

    def right_spec(span):
        return pl.BlockSpec(
            (rows, wide), lambda n, m: (0, jnp.clip(n - span[0], 0, span[1] - span[0] - 1))
        )

    return pl.pallas_call(
        functools.partial(weight_grad_kernel, tuple(spans)),
        grid=(first, steps),
        in_specs=[left_spec(span) for span in spans] + [right_spec(span) for span in spans],
        out_specs=pl.BlockSpec((tall, wide), lambda n, m: (m, n)),
        out_shape=jax.ShapeDtypeStruct((D, first * wide), BF16),
        compiler_params=params(("arbitrary", "arbitrary")),
        name="weight_grads",
        cost_estimate=pl.CostEstimate(
            flops=2 * rows * D * first * wide,
            bytes_accessed=2 * D * first * wide + 4 * rows * D,
            transcendentals=0,
        ),
    )(*[left for left, _ in pairs], *[right for _, right in pairs])


def up_kernel(values, weight, bias, grad_hidden, hidden_out, grad_out, bias_out):
    before = mm(values[...], weight[...]) + bias[...]
    phi = 0.5 * (1.0 + lax.erf(before * (0.5**0.5)))
    hidden_out[...] = (before * phi).astype(BF16)
    density = jnp.exp(-0.5 * before * before) * 0.3989422804014327
    grad = (grad_hidden[...].astype(F32) * (phi + before * density)).astype(BF16)
    grad_out[...] = grad

    @pl.when(pl.program_id(0) == 0)
    def _():
        bias_out[...] = jnp.zeros_like(bias_out)

    bias_out[...] += jnp.sum(grad.astype(F32), axis=0, keepdims=True)


def feed_up(values, weight, bias, grad_hidden):
    array, width, number = weight
    rows = values.shape[0]
    block = pl.BlockSpec((CHUNK, width), lambda i: (i, 0))
    vector = pl.BlockSpec((1, width), lambda i: (0, 0))
    return pl.pallas_call(
        up_kernel,
        grid=(rows // CHUNK,),
        in_specs=[
            pl.BlockSpec((CHUNK, D), lambda i: (i, 0)),
            pl.BlockSpec((D, width), lambda i: (0, number)),
            vector, block,
        ],
        out_specs=[block, block, vector],
        out_shape=[
            jax.ShapeDtypeStruct((rows, width), BF16),
            jax.ShapeDtypeStruct((rows, width), BF16),
            jax.ShapeDtypeStruct((1, width), F32),
        ],
        compiler_params=params(("arbitrary",)),
        name="feed_up",
        cost_estimate=pl.CostEstimate(
            flops=2 * rows * D * width,
            bytes_accessed=2 * (rows + width) * D + 8 * rows * width,
            transcendentals=2 * rows * width,
        ),
    )(values, array, bias[None, :], grad_hidden)


PARTIAL_FLIP = (1, 3, 2, 3, 2, 1, 0, 0)
PARTIAL_HALF = (0, 0, 1, 1, 0, 1, 0, 1)


def table_lookup(table, step):
    result = jnp.int32(table[0])
    for index in range(1, len(table)):
        result = jnp.where(step == index, table[index], result)
    return result


def partial_kernel(count, row, *refs):
    values, weights = refs[:count], refs[count : 2 * count]
    outs = refs[2 * count :]
    step = pl.program_id(0)
    total = mm_nt(values[0][...], weights[0][...])
    for x, w in zip(values[1:], weights[1:]):
        total = total + mm_nt(x[...], w[...])
    for index, out in enumerate(outs):

        @pl.when(step // 2 == index)
        def _():
            out[0] = total.astype(out.dtype)


def partial_blocks(values, weights, row, first, kinds):
    rows = values[0].shape[0]
    half, block = rows // 2, D // 4
    count = len(values)
    flips = PARTIAL_FLIP[2 * first : 2 * (first + len(kinds))]
    halves = PARTIAL_HALF[2 * first : 2 * (first + len(kinds))]

    def value_spec(x):
        return pl.BlockSpec((half, x.shape[1]), lambda s, r: (table_lookup(halves, s), 0))

    def weight_spec(w):
        return pl.BlockSpec((block, w[1]), lambda s, r: (r[0] ^ table_lookup(flips, s), w[2]))

    def out_spec(index):
        return pl.BlockSpec((1, half, block), lambda s, r: (jnp.clip(s - 2 * index, 0, 1), 0, 0))

    depth = sum(x.shape[1] for x in values)
    return pl.pallas_call(
        functools.partial(partial_kernel, count),
        grid_spec=pltpu.PrefetchScalarGridSpec(
            num_scalar_prefetch=1,
            grid=(2 * len(kinds),),
            in_specs=[value_spec(x) for x in values] + [weight_spec(w) for w in weights],
            out_specs=[out_spec(index) for index in range(len(kinds))],
        ),
        out_shape=[jax.ShapeDtypeStruct((2, half, block), kind) for kind in kinds],
        compiler_params=params(("arbitrary",)),
        name="partial_blocks",
        cost_estimate=pl.CostEstimate(
            flops=rows * block * depth * 2 * len(kinds),
            bytes_accessed=(rows + D) * depth * 2 + 4 * rows * block * len(kinds),
            transcendentals=0,
        ),
    )(row, *values, *[w[0] for w in weights])


def permute_row(value, pairs):
    return lax.ppermute(value, "row", pairs)


def in_order(*values):
    return lax.optimization_barrier(values)


def reduce_row_start(values, weights, row):
    if lax.axis_size("row") != 4:
        columns = [array[:, n * width : (n + 1) * width] for array, width, n in weights]
        return sum(mm_nt(x, w) for x, w in zip(values, columns)).astype(BF16)
    return tuple(partial_blocks(values, weights, row, 0, (BF16, BF16)))


def reduce_row_finish(sends, values, weights, row, between=None):
    if lax.axis_size("row") != 4:
        total = lax.psum_scatter(sends, "row", scatter_dimension=1, tiled=True).astype(F32)
        return total, between() if between else None
    from_x = permute_row(sends[0], X_PAIRS)
    from_y = permute_row(sends[1], Y_PAIRS)
    extra = None
    if between is not None:
        extra = between()
        from_x, from_y, extra = in_order(from_x, from_y, extra)
    keep, own = partial_blocks(values, weights, row, 2, (BF16, F32))
    next_y = (keep[0].astype(F32) + from_x[1].astype(F32)).astype(BF16)
    next_x = (keep[1].astype(F32) + from_y[1].astype(F32)).astype(BF16)
    last_y = permute_row(next_y, Y_PAIRS)
    last_x = permute_row(next_x, X_PAIRS)
    first_half = own[0] + from_x[0].astype(F32) + last_y.astype(F32)
    second_half = own[1] + from_y[0].astype(F32) + last_x.astype(F32)
    return jnp.concatenate([first_half, second_half], axis=0), extra


def gather_row(value, between=None):
    if lax.axis_size("row") != 4:
        gathered = lax.all_gather(value, "row", axis=1, tiled=True)
        return gathered, between() if between else None
    half = value.shape[0] // 2
    from_x = permute_row(value, X_PAIRS)
    from_y = permute_row(value, Y_PAIRS)
    extra = None
    if between is not None:
        extra = between()
        from_x, from_y, extra = in_order(from_x, from_y, extra)
    far_a = permute_row(from_x[:half], Y_PAIRS)
    far_b = permute_row(from_y[half:], X_PAIRS)
    return (value, from_x, from_y, far_a, far_b), extra


def gather_row_small(value):
    if lax.axis_size("row") != 4:
        return lax.all_gather(value, "row", axis=1, tiled=True)
    row = lax.axis_index("row")
    pieces = jnp.stack(
        [value] + [permute_row(value, pairs) for pairs in (X_PAIRS, Y_PAIRS, D_PAIRS)]
    )
    ordered = [
        lax.dynamic_index_in_dim(pieces, row ^ place, 0, keepdims=False) for place in range(4)
    ]
    return jnp.concatenate(ordered, axis=1)


def sum_row_small(value):
    if lax.axis_size("row") != 4:
        return lax.psum(value, "row")
    first = value + permute_row(value, X_PAIRS)
    return first + permute_row(first, Y_PAIRS)


def norm_backward(grad_out, normal, inverse, gain_vector):
    scaled = grad_out * gain_vector
    sums = sum_row_small(jnp.stack([jnp.sum(scaled, axis=1), jnp.sum(scaled * normal, axis=1)]))
    means = sums / D
    grad_in = inverse * (scaled - means[0][:, None] - normal * means[1][:, None])
    return (grad_in, jnp.sum(grad_out * normal, axis=0), jnp.sum(grad_out, axis=0))


def gather_col(weight):
    return lax.all_gather(weight, "col", axis=0, tiled=True)


def scatter_col(grad):
    return lax.psum_scatter(grad, "col", scatter_dimension=0, tiled=True).astype(F32)


class Exchange:
    def __init__(self, messages, send_sem, recv_sem):
        col = lax.axis_index("col")
        self.base = (col // SLOTS) * SLOTS
        self.place = col % SLOTS
        self.messages, self.send_sem, self.recv_sem = messages, send_sem, recv_sem

    def copy(self, index):
        _, target, source, destination = self.messages[index]
        return pltpu.make_async_remote_copy(
            src_ref=source,
            dst_ref=destination,
            send_sem=self.send_sem.at[index],
            recv_sem=self.recv_sem.at[index],
            device_id={"col": self.base + target},
            device_id_type=pl.DeviceIdType.MESH,
        )

    def greet(self):
        barrier = pltpu.get_barrier_semaphore()
        for step in range(1, SLOTS):
            other = self.base + (self.place + step) % SLOTS
            pl.semaphore_signal(
                barrier, inc=1, device_id={"col": other}, device_id_type=pl.DeviceIdType.MESH
            )
        pl.semaphore_wait(barrier, SLOTS - 1)

    def run(self, programs):
        for place, program in enumerate(programs):

            @pl.when(self.place == place)
            def _():
                sent = []
                for action in program:
                    if callable(action):
                        action()
                    elif action >= 0:
                        self.copy(action).start()
                        sent.append(action)
                    else:
                        self.copy(~action).wait_recv()
                for index in sent:
                    self.copy(index).wait_send()


def scaled_add(meta, rates, target, terms, rows):
    heads = target.shape[0]
    for head in range(heads):
        total = None
        for term in terms:
            if isinstance(term, tuple):
                ref, slot = term
                exponent = jnp.maximum(
                    trunk_reference(meta, jnp.int32(3), rows)
                    - trunk_reference(meta, jnp.int32(slot), rows),
                    0,
                )
                value = ref[head].astype(F32) * power(rates[head], exponent, HV)
            else:
                value = term[head].astype(F32)
            total = value if total is None else total + value
        target[head] = total.astype(BF16)


def share_kernel(rows, meta, rates, ex, sh, shift, tot, send_sem, recv_sem):
    messages = [
        (0, 2, ex.at[0], sh.at[0]),
        (0, 1, ex.at[0], sh.at[0]),
        (1, 3, ex.at[0], sh.at[1]),
        (2, 3, ex.at[0], sh.at[2]),
        (2, 3, sh.at[0], sh.at[0]),
        (3, 2, sh.at[1], sh.at[1]),
        (3, 4, ex.at[1], sh.at[4]),
        (3, 5, ex.at[2], sh.at[5]),
        (3, 4, tot, sh.at[3]),
        (4, 5, ex.at[1], sh.at[6]),
        (4, 6, ex.at[1], sh.at[6]),
        (4, 5, ex.at[2], sh.at[7]),
        (5, 7, sh.at[7], sh.at[7]),
        (4, 5, sh.at[4], sh.at[4]),
        (4, 6, sh.at[4], sh.at[4]),
        (5, 4, sh.at[5], sh.at[5]),
        (5, 7, sh.at[5], sh.at[5]),
        (4, 5, sh.at[3], sh.at[3]),
        (4, 6, sh.at[3], sh.at[3]),
        (6, 7, sh.at[6], sh.at[6]),
        (6, 7, sh.at[4], sh.at[4]),
        (6, 7, sh.at[3], sh.at[3]),
        (7, 6, sh.at[7], sh.at[7]),
        (7, 6, sh.at[5], sh.at[5]),
        (4, 5, ex.at[0], shift),
        (6, 7, ex.at[0], shift),
    ]
    exchange = Exchange(messages, send_sem, recv_sem)

    def keep_trunk():
        sh[3] = ex[0]

    def total_trunk():
        terms = [(sh.at[slot], slot) for slot in range(3)] + [ex.at[0]]
        scaled_add(meta, rates, tot, terms, rows)

    def keep_branches():
        sh[6] = ex[1]
        sh[7] = ex[2]

    exchange.greet()
    exchange.run(
        [
            [0, 1],
            [2, ~1],
            [3, ~0, 4, ~5],
            [6, 7, keep_trunk, ~2, 5, ~4, ~3, total_trunk, 8],
            [10, 11, 9, 24, keep_branches, ~6, 14, 13, ~15, ~8, 18, 17],
            [~11, 12, ~7, 16, 15, ~9, ~24, ~13, ~17],
            [25, ~10, 19, ~14, 20, ~22, ~23, ~18, 21],
            [~12, 22, ~16, 23, ~19, ~20, ~25, ~21],
        ]
    )


def vmem():
    return pl.BlockSpec(memory_space=pltpu.VMEM)


def share_states(meta, rates, exports, rows):
    heads = exports.shape[1]
    state = (heads, QK, HV)
    return pl.pallas_call(
        functools.partial(share_kernel, rows),
        in_specs=[smem(), smem(), vmem()],
        out_specs=[vmem(), vmem()],
        out_shape=[
            jax.ShapeDtypeStruct((SLOTS,) + state, BF16),
            jax.ShapeDtypeStruct(state, BF16),
        ],
        scratch_shapes=[
            pltpu.VMEM(state, BF16),
            pltpu.SemaphoreType.DMA((26,)),
            pltpu.SemaphoreType.DMA((26,)),
        ],
        compiler_params=pltpu.CompilerParams(
            collective_id=1, has_side_effects=True, vmem_limit_bytes=40 * 1024 * 1024
        ),
        name="share_states",
        cost_estimate=pl.CostEstimate(
            flops=0, bytes_accessed=100 * 1024 * 1024, transcendentals=0
        ),
    )(meta, rates, exports)


def return_kernel(rows, meta, rates, y, first, own0, own1, own2, rx, tx, send_sem, recv_sem):
    messages = [
        (7, 6, y.at[3], rx.at[0]),
        (7, 6, y.at[4], rx.at[1]),
        (7, 6, y.at[5], rx.at[2]),
        (6, 7, y.at[6], rx.at[0]),
        (6, 7, y.at[7], rx.at[1]),
        (7, 5, tx.at[0], rx.at[0]),
        (7, 5, tx.at[1], rx.at[1]),
        (6, 4, tx.at[0], rx.at[0]),
        (6, 4, tx.at[1], rx.at[1]),
        (6, 4, tx.at[2], rx.at[2]),
        (5, 4, y.at[3], rx.at[3]),
        (5, 4, y.at[4], rx.at[4]),
        (5, 4, y.at[5], rx.at[5]),
        (5, 4, tx.at[0], rx.at[6]),
        (5, 4, tx.at[1], rx.at[7]),
        (4, 3, tx.at[0], rx.at[0]),
        (4, 3, tx.at[1], own1),
        (4, 3, tx.at[2], own2),
        (2, 3, y.at[0], rx.at[1]),
        (2, 3, y.at[1], rx.at[2]),
        (3, 2, tx.at[2], own0),
        (3, 1, tx.at[1], own0),
        (3, 0, tx.at[0], rx.at[0]),
        (1, 0, y.at[0], rx.at[1]),
        (5, 4, first, own0),
        (7, 6, first, own0),
    ]
    exchange = Exchange(messages, send_sem, recv_sem)

    def add(target, *terms):
        return lambda: scaled_add(meta, rates, target, terms, rows)

    exchange.greet()
    exchange.run(
        [
            [~23, ~22, add(own0, rx.at[0], rx.at[1])],
            [23, ~21],
            [18, 19, ~20],
            [
                ~18, ~19, ~15,
                add(tx.at[0], y.at[0], rx.at[1], (rx.at[0], 0)), 22,
                add(tx.at[1], y.at[1], rx.at[2], (rx.at[0], 1)), 21,
                add(tx.at[2], y.at[2], (rx.at[0], 2)), 20,
                add(own0, rx.at[0], y.at[3]),
                ~16, ~17,
            ],
            [
                ~10, ~7, add(tx.at[0], y.at[3], rx.at[0], rx.at[3]), 15,
                ~11, ~8, add(tx.at[1], y.at[4], rx.at[1], rx.at[4]), 16,
                ~12, ~9, add(tx.at[2], y.at[5], rx.at[2], rx.at[5]), 17,
                ~13, add(own1, y.at[6], rx.at[6]),
                ~14, add(own2, y.at[7], rx.at[7]),
                ~24,
            ],
            [
                10, 11, 12, 24,
                ~5, add(tx.at[0], y.at[6], rx.at[0]), 13,
                ~6, add(tx.at[1], y.at[7], rx.at[1]), 14,
            ],
            [
                3, 4,
                ~0, add(tx.at[0], y.at[3], rx.at[0]), 7,
                ~1, add(tx.at[1], y.at[4], rx.at[1]), 8,
                ~2, add(tx.at[2], y.at[5], rx.at[2]), 9,
                ~25,
            ],
            [
                0, 1, 2, 25,
                ~3, add(tx.at[0], y.at[6], rx.at[0]), 5,
                ~4, add(tx.at[1], y.at[7], rx.at[1]), 6,
            ],
        ]
    )


def return_states(meta, rates, exports, first_state, rows):
    heads = exports.shape[1]
    state = (heads, QK, HV)
    return pl.pallas_call(
        functools.partial(return_kernel, rows),
        in_specs=[smem(), smem(), vmem(), vmem()],
        out_specs=[vmem()] * 3,
        out_shape=[jax.ShapeDtypeStruct(state, BF16)] * 3,
        scratch_shapes=[
            pltpu.VMEM((8,) + state, BF16),
            pltpu.VMEM((3,) + state, BF16),
            pltpu.SemaphoreType.DMA((26,)),
            pltpu.SemaphoreType.DMA((26,)),
        ],
        compiler_params=pltpu.CompilerParams(
            collective_id=2, has_side_effects=True, vmem_limit_bytes=40 * 1024 * 1024
        ),
        name="return_states",
        cost_estimate=pl.CostEstimate(
            flops=0, bytes_accessed=100 * 1024 * 1024, transcendentals=0
        ),
    )(meta, rates, exports, first_state)


def sum_col(value):
    size = lax.axis_size("col")
    if size != SLOTS:
        return lax.psum(value, "col")
    for flip in (1, 2, 4):
        value = value + lax.ppermute(value, "col", [(a, a ^ flip) for a in range(size)])
    return value


def sum_col_vectors(vectors, extra=None):
    col = lax.axis_index("col")
    size = lax.axis_size("col")
    parts = list(vectors) + ([extra] if extra is not None else [])
    total = sum_col(jnp.concatenate(parts).reshape(-1, 128)).reshape(-1)
    results, first = [], 0
    for vector in vectors:
        width = vector.shape[0] // size
        results.append(lax.dynamic_slice_in_dim(total, first + col * width, width, 0))
        first += vector.shape[0]
    return results, total[first:]


def token_tables(place, rows, lengths, parents):
    index = place * rows + jnp.arange(rows, dtype=jnp.int32)
    in_trunk = index < TRUNK
    beyond = jnp.maximum(index - TRUNK, 0)
    segment = jnp.where(in_trunk, 0, 1 + beyond // SEG)
    position = jnp.where(in_trunk, index, beyond % SEG)

    def lookup(table, spots):
        hits = spots[:, None] == jnp.arange(table.shape[0], dtype=jnp.int32)
        return jnp.sum(jnp.where(hits, table, 0), axis=1)

    branch = 1 + lookup(parents, jnp.clip(segment - 5, 0, 7))
    parent_length = lookup(lengths, branch)
    depth = position + jnp.where(segment >= 1, lengths[0], 0)
    depth = depth + jnp.where(segment >= 5, parent_length, 0)
    valid = (position < lookup(lengths, segment)).astype(F32)
    half = QK // 2
    frequency = 10000.0 ** (-jnp.arange(half, dtype=F32) / (half - 1))
    angles = depth.astype(F32)[:, None] * frequency[None, :]
    return valid, jnp.cos(angles), jnp.sin(angles)


def body(
    tokens,
    cotangent,
    query_weight,
    key_weight,
    value_weight,
    gate_weight,
    out_weight,
    up_weight,
    down_weight,
    first_gain,
    first_bias,
    group_gain,
    group_bias,
    second_gain,
    second_bias,
    up_bias,
    down_bias,
    segment_lengths,
    leaf_parents,
):
    rows = tokens.shape[0]
    col = lax.axis_index("col")
    row = lax.axis_index("row")
    row_ref = row.astype(jnp.int32)[None]
    place = (col % SLOTS).astype(jnp.int32)
    tree = (col // SLOTS).astype(jnp.int32)
    lengths = lax.dynamic_index_in_dim(segment_lengths, tree, 0, keepdims=False)
    parents = lax.dynamic_index_in_dim(leaf_parents, tree, 0, keepdims=False)
    meta = jnp.concatenate([lengths, parents, place[None]]).astype(jnp.int32)
    heads = query_weight.shape[1] // QK
    head_numbers = (row * heads + jnp.arange(heads, dtype=jnp.int32)).astype(F32)
    rates = jnp.log(1.0 - 2.0 ** (-5.0 - head_numbers))

    wide = heads * HV
    narrow = heads * QK
    project_full = gather_col(jnp.concatenate([query_weight, key_weight, value_weight], axis=1))
    mix_full = gather_col(jnp.concatenate([gate_weight, out_weight.T], axis=1))
    feed_full = gather_col(jnp.concatenate([down_weight.T, up_weight], axis=1))
    query_part, key_part = (project_full, narrow, 0), (project_full, narrow, 1)
    value_part = (project_full, wide, 1)
    gate_part, out_part = (mix_full, wide, 0), (mix_full, wide, 1)
    down_part, up_part = (feed_full, wide, 0), (feed_full, wide, 1)

    valid, cosine, sine = token_tables(place, rows, lengths, parents)
    column = valid[:, None]
    gains = gather_row_small(jnp.stack([first_gain, first_bias, second_gain, second_bias]))
    token_pieces, _ = gather_row(tokens)
    first_wide, first_average, first_inverse = join(token_pieces, row_ref, gains[0], gains[1])
    fed_low = (cotangent.astype(F32) * column).astype(BF16)
    fed_low, first_average = lax.optimization_barrier((fed_low, first_average))

    fed_pieces, projected = gather_row(
        fed_low, lambda: project(first_wide, project_full, cosine, sine)
    )
    query_rot, key_rot, value_low = projected
    exports = make_states(meta, rates, key_rot, value_low)
    shared, shifted = share_states(meta, rates, exports, rows)
    mix_full, shared = in_order(mix_full, shared)
    gate_part, out_part = (mix_full, wide, 0), (mix_full, wide, 1)
    gate_raw = matmul(first_wide, gate_part, F32)
    gate_raw, fed_pieces = in_order(gate_raw, fed_pieces)
    gated, normal, inverse, states = retain(
        meta, rates, query_rot, key_rot, value_low, gate_raw, shared, shifted, group_gain, group_bias
    )

    sends = reduce_row_start([gated], [out_part], row_ref)
    attended, _ = reduce_row_finish(sends, [gated], [out_part], row_ref)
    middle = tokens.astype(F32) + attended

    def feed_gradient():
        joined = join(fed_pieces, row_ref)
        return joined, matmul(joined, down_part, BF16)

    middle_pieces, (fed_wide, grad_hidden) = gather_row(middle.astype(BF16), feed_gradient)
    second_wide, second_average, second_inverse = join(middle_pieces, row_ref, gains[2], gains[3])
    hidden, grad_before, up_bias_grad = feed_up(second_wide, up_part, up_bias, grad_hidden)
    sends = reduce_row_start([grad_before], [up_part], row_ref)
    sends, hidden = in_order(sends, hidden)
    second_back, feed_partial = reduce_row_finish(
        sends,
        [grad_before],
        [up_part],
        row_ref,
        lambda: weight_grads([(fed_wide, hidden), (second_wide, grad_before)]),
    )
    feed_grad = scatter_col(feed_partial)
    grad_fed = fed_low.astype(F32)
    down_bias_grad = jnp.sum(grad_fed, axis=0)

    second_normal = (middle - second_average[:, :1]) * second_inverse[:, :1]
    grad_middle_norm, second_gain_grad, second_bias_grad = norm_backward(
        second_back, second_normal, second_inverse[:, :1], second_gain
    )
    grad_middle = grad_fed + grad_middle_norm
    grad_pieces, fed_sends = gather_row(
        grad_middle.astype(BF16), lambda: reduce_row_start([hidden], [down_part], row_ref)
    )
    grad_wide = join(grad_pieces, row_ref)
    out_partial = weight_grads([(grad_wide, gated)])
    out_partial, grad_wide, feed_grad, fed_sends = in_order(
        out_partial, grad_wide, feed_grad, fed_sends
    )
    out_grad = scatter_col(out_partial)
    fed_out, gate_results = reduce_row_finish(
        fed_sends,
        [hidden],
        [down_part],
        row_ref,
        lambda: gate_back(
            meta, rates, grad_wide, out_part, gate_raw, normal, inverse, query_rot, group_gain, group_bias
        ),
    )
    fed_out = fed_out + down_bias
    layer_out = middle + fed_out
    grad_gate, grad_retained, group_gain_grad, group_bias_grad, returns, first_state = gate_results
    own = return_states(meta, rates, returns, first_state, rows)
    grad_gate, own = in_order(grad_gate, own)
    gate_partial = weight_grads([(first_wide, grad_gate)])
    gate_partial, own, out_grad = in_order(gate_partial, own, out_grad)
    gate_grad = scatter_col(gate_partial)
    grad_query, grad_key, grad_value = retain_back(
        meta, rates, query_rot, key_rot, value_low, grad_retained, states, cosine, sine, own
    )
    back_values = [grad_query, grad_key, grad_value, grad_gate]
    back_weights = [query_part, key_part, value_part, gate_part]
    sends = reduce_row_start(back_values, back_weights, row_ref)
    sends, grad_value = in_order(sends, grad_value)
    first_back, project_partial = reduce_row_finish(
        sends,
        back_values,
        back_weights,
        row_ref,
        lambda: weight_grads(
            [(first_wide, grad_query), (first_wide, grad_key), (first_wide, grad_value)]
        ),
    )
    project_partial, gate_grad = in_order(project_partial, gate_grad)
    project_grad = scatter_col(project_partial)

    first_normal = (tokens.astype(F32) - first_average[:, :1]) * first_inverse[:, :1]
    grad_first, first_gain_grad, first_bias_grad = norm_backward(
        first_back, first_normal, first_inverse[:, :1], first_gain
    )
    tokens_grad = grad_middle + grad_first

    vectors, _ = sum_col_vectors(
        (
            group_gain_grad[0],
            group_bias_grad[0],
            second_gain_grad,
            second_bias_grad,
            up_bias_grad[0],
            down_bias_grad,
        )
    )
    squares = jnp.stack(
        [
            jnp.sum(column * layer_out * layer_out),
            jnp.sum(column * attended * attended),
            jnp.sum(column * fed_out * fed_out),
        ]
    )
    last, col_squares = sum_col_vectors(
        (first_gain_grad, first_bias_grad), jnp.concatenate([squares, jnp.zeros((125,), F32)])
    )
    totals = sum_row_small(col_squares[None, :])[0, :3]
    valid_count = jnp.sum(segment_lengths).astype(F32) * D
    norm_values = jnp.sqrt(totals / valid_count)
    return (
        layer_out.astype(BF16),
        tokens_grad,
        project_grad[:, :narrow],
        project_grad[:, narrow : 2 * narrow],
        project_grad[:, 2 * narrow :],
        gate_grad,
        out_grad.T,
        feed_grad[:, wide:],
        feed_grad[:, :wide].T,
        last[0],
        last[1],
        vectors[0],
        vectors[1],
        vectors[2],
        vectors[3],
        vectors[4],
        vectors[5],
        norm_values,
    )


def solution(mesh):
    matrix, turned, vector = P("col", "row"), P("row", "col"), P("row")
    in_specs = (matrix,) * 6 + (turned, matrix, turned) + (vector,) * 8 + (P(), P())
    split = P(("row", "col"))
    out_specs = (matrix,) * 6 + (turned, matrix, turned) + (split,) * 8 + (P(),)
    return jax.shard_map(body, mesh=mesh, in_specs=in_specs, out_specs=out_specs, check_vma=False)
```

```python
import functools

import jax
import jax.numpy as jnp
from jax import lax
from jax.experimental import pallas as pl
from jax.experimental.pallas import tpu as pltpu
from jax.sharding import PartitionSpec as P

D = 2048
QK = 256
HV = 512
TRUNK = 4096
SEG = 512
TREE_LEN = TRUNK + 12 * SEG
CHUNK = 256
TRUNK_CHUNKS = TRUNK // CHUNK
SLOTS = 8

EPSILON = 1e-05
SCALE = QK**-0.5
F32 = jnp.float32
BF16 = jnp.bfloat16

X_PAIRS = [(0, 1), (1, 0), (2, 3), (3, 2)]
Y_PAIRS = [(0, 2), (2, 0), (1, 3), (3, 1)]
D_PAIRS = [(0, 3), (3, 0), (1, 2), (2, 1)]


def mm(a, b):
    return lax.dot_general(a, b, (((1,), (0,)), ((), ())), preferred_element_type=F32)


def mm_nt(a, b):
    return lax.dot_general(a, b, (((1,), (1,)), ((), ())), preferred_element_type=F32)


def mm_tn(a, b):
    return lax.dot_general(a, b, (((0,), (0,)), ((), ())), preferred_element_type=F32)


def params(semantics, limit=None):
    return pltpu.CompilerParams(
        dimension_semantics=semantics, vmem_limit_bytes=limit or 60 * 1024 * 1024
    )


def smem():
    return pl.BlockSpec(memory_space=pltpu.SMEM)


class Chunk:
    def __init__(self, meta, index):
        in_trunk = index < TRUNK_CHUNKS
        beyond = jnp.maximum(index - TRUNK_CHUNKS, 0)
        self.in_trunk = in_trunk
        self.segment = jnp.where(in_trunk, 0, 1 + beyond // 2)
        self.first = jnp.where(in_trunk, index * CHUNK, (beyond % 2) * CHUNK)
        length = meta[self.segment]
        trunk_length = meta[0]
        self.trunk_length = trunk_length
        self.length = length
        self.is_leaf = self.segment >= 5
        self.parent = meta[13 + jnp.clip(self.segment - 5, 0, 7)]
        parent_length = meta[1 + self.parent]
        self.start = jnp.where(
            in_trunk,
            self.first,
            trunk_length + self.first + jnp.where(self.is_leaf, parent_length, 0),
        )
        self.count = jnp.clip(length - self.first, 0, CHUNK)
        self.end = self.start + self.count
        self.continues = jnp.where(in_trunk, index + 1 < TRUNK_CHUNKS, beyond % 2 == 0)


def trunk_reference(meta, place, rows):
    return jnp.minimum(meta[0], jnp.minimum(rows * (place + 1), TRUNK))


def power(rate, exponent, width):
    return jnp.exp(jnp.full((1, width), exponent.astype(F32), F32) * rate)


def column_power(rate, exponents):
    return jnp.exp(exponents.astype(F32) * rate)


def token_column(width=1):
    return lax.broadcasted_iota(jnp.int32, (CHUNK, width), 0)


def decay_matrix(rate):
    t = lax.broadcasted_iota(jnp.int32, (CHUNK, CHUNK), 0)
    u = lax.broadcasted_iota(jnp.int32, (CHUNK, CHUNK), 1)
    return jnp.where(u <= t, jnp.exp((t - u).astype(F32) * rate) * SCALE, 0.0)


def valid_decay(decay, count):
    u = lax.broadcasted_iota(jnp.int32, (1, CHUNK), 1)
    return decay[...] * jnp.where(u < count, 1.0, 0.0)


def key_decay(rate, count):
    j = token_column()
    return jnp.where(j < count, column_power(rate, jnp.maximum(count - j, 0)), 0.0)


def export_terms(meta, chunk, local, chunks, place, slot, rows):
    if slot == 0:
        is_shift = ((place == 4) | (place == 6)) & (local == chunks - 1)
        exponent = jnp.where(
            chunk.in_trunk,
            jnp.maximum(trunk_reference(meta, place, rows) - chunk.end, 0),
            0,
        )
        return chunk.in_trunk | is_shift, exponent
    wanted = (place == 3) | (place == 4)
    mine = (chunk.segment % 2 == 1) if slot == 1 else (chunk.segment % 2 == 0)
    is_branch = (chunk.segment >= 1) & (chunk.segment < 5)
    exponent = jnp.where(is_branch, jnp.maximum(chunk.length - chunk.first - chunk.count, 0), 0)
    return wanted & mine & is_branch, exponent


def import_terms(meta, chunk, place, slot, rows):
    if slot < 4:
        sees = jnp.logical_not(chunk.in_trunk) | (place > slot)
        if slot < 3:
            sees = sees & (place < 4)
        return sees, jnp.maximum(chunk.start - trunk_reference(meta, jnp.int32(slot), rows), 0)
    sees = chunk.is_leaf & (chunk.parent == slot - 4)
    return sees, chunk.first


def shift_in(meta, place, chunks):
    previous = Chunk(meta, jnp.maximum(place * chunks - 1, 0))
    return (place == 5) | (place == 7), CHUNK - previous.count


def retain_kernel(
    rows, chunks, meta, rates, query, key, value, wide, weight, shared, shifted, gain, bias,
    gate_out, gated_out, normal_out, inverse_out, state_out, running, total, decay,
):
    local = pl.program_id(1)
    rate = rates[pl.program_id(0)]
    place = meta[21]
    chunk = Chunk(meta, place * chunks + local)

    @pl.when(local == 0)
    def _():
        decay[...] = decay_matrix(rate)
        running[...] = jnp.zeros_like(running)
        on, exponent = shift_in(meta, place, chunks)

        @pl.when(on)
        def _():
            running[...] = shifted[0].astype(F32) * power(rate, exponent, HV)

    incoming = running[...]
    total[...] = incoming
    for slot in range(SLOTS):
        on, exponent = import_terms(meta, chunk, place, slot, rows)

        @pl.when(on)
        def _():
            total[...] += shared[slot, 0].astype(F32) * power(rate, exponent, HV)

    state = total[...].astype(BF16)
    state_out[0, 0] = state

    q, k, v = query[...], key[...], value[...]
    scores = (mm_nt(q, k) * valid_decay(decay, chunk.count)).astype(BF16)
    own = token_column()
    reach = column_power(rate, own) * SCALE
    retained = mm(scores, v) + mm(q, state) * reach

    j = token_column()
    ahead = jnp.where(j < chunk.count, column_power(rate, CHUNK - j), 0.0)
    fresh = mm_tn((k.astype(F32) * ahead).astype(BF16), v)
    keep = jnp.where(chunk.continues, 1.0, 0.0)
    running[...] = (incoming * power(rate, jnp.int32(CHUNK), HV) + fresh) * keep

    average = jnp.mean(retained, axis=1, keepdims=True)
    centred = retained - average
    inverse = lax.rsqrt(jnp.mean(centred * centred, axis=1, keepdims=True) + EPSILON)
    normal = centred * inverse
    gate_value = mm(wide[...], weight[...])
    gate_out[...] = gate_value
    gated = (normal * gain[...] + bias[...]) * (gate_value / (1.0 + jnp.exp(-gate_value)))
    gated_out[...] = gated.astype(BF16)
    normal_out[...] = normal.astype(BF16)
    inverse_out[0] = jnp.broadcast_to(inverse, (CHUNK, 128))


def retain(meta, rates, query, key, value, inputs, weight, shared, shifted, gain, bias):
    array, _, number = weight
    rows = key.shape[0]
    heads = key.shape[1] // QK
    chunks = rows // CHUNK
    wide = pl.BlockSpec((CHUNK, HV), lambda h, c: (c, h))
    narrow = pl.BlockSpec((CHUNK, QK), lambda h, c: (c, h))
    vector = pl.BlockSpec((1, HV), lambda h, c: (0, h))
    return pl.pallas_call(
        functools.partial(retain_kernel, rows, chunks),
        grid=(heads, chunks),
        in_specs=[
            smem(), smem(), narrow, narrow, wide,
            pl.BlockSpec((CHUNK, D), lambda h, c: (c, 0)),
            pl.BlockSpec((D, HV), lambda h, c: (0, number * heads + h)),
            pl.BlockSpec((SLOTS, 1, QK, HV), lambda h, c: (0, h, 0, 0)),
            pl.BlockSpec((1, QK, HV), lambda h, c: (h, 0, 0)),
            vector, vector,
        ],
        out_specs=[
            wide, wide, wide,
            pl.BlockSpec((1, CHUNK, 128), lambda h, c: (h, c, 0)),
            pl.BlockSpec((1, 1, QK, HV), lambda h, c: (h, c, 0, 0)),
        ],
        out_shape=[
            jax.ShapeDtypeStruct((rows, heads * HV), F32),
            jax.ShapeDtypeStruct((rows, heads * HV), BF16),
            jax.ShapeDtypeStruct((rows, heads * HV), BF16),
            jax.ShapeDtypeStruct((heads, rows, 128), F32),
            jax.ShapeDtypeStruct((heads, chunks, QK, HV), BF16),
        ],
        scratch_shapes=[
            pltpu.VMEM((QK, HV), F32), pltpu.VMEM((QK, HV), F32), pltpu.VMEM((CHUNK, CHUNK), F32)
        ],
        compiler_params=params(("arbitrary", "arbitrary")),
        name="retention_forward",
        cost_estimate=pl.CostEstimate(
            flops=2 * rows * heads * (CHUNK * 768 + 2 * QK * HV + D * HV),
            bytes_accessed=rows * heads * 8192,
            transcendentals=rows * heads * 768,
        ),
    )(meta, rates, query, key, value, inputs, array, shared, shifted, gain[None, :], bias[None, :])


def gate_back_kernel(
    rows, chunks, meta, rates, wide, weight, gate, normal_in, inverse_in, query, gain, bias,
    gate_out, retained_out, gain_out, bias_out, exports, first_out, acc,
):
    local = pl.program_id(1)
    rate = rates[pl.program_id(0)]
    place = meta[21]
    chunk = Chunk(meta, place * chunks + local)
    grad_gated = mm(wide[...], weight[...])
    gate_value = gate[...].astype(F32)
    normal = normal_in[...].astype(F32)
    sigmoid = 1.0 / (1.0 + jnp.exp(-gate_value))
    normed = normal * gain[...] + bias[...]
    grad_gate = grad_gated * normed * (sigmoid * (1.0 + gate_value * (1.0 - sigmoid)))
    gate_out[...] = grad_gate.astype(BF16)
    grad_normed = grad_gated * (gate_value * sigmoid)

    @pl.when(local == 0)
    def _():
        gain_out[...] = jnp.zeros_like(gain_out)
        bias_out[...] = jnp.zeros_like(bias_out)
        acc[...] = jnp.zeros_like(acc)

    gain_out[...] += jnp.sum(grad_normed * normal, axis=0, keepdims=True)
    bias_out[...] += jnp.sum(grad_normed, axis=0, keepdims=True)
    scaled = grad_normed * gain[...]
    grad = inverse_in[0][:, :1] * (
        scaled
        - jnp.mean(scaled, axis=1, keepdims=True)
        - normal * jnp.mean(scaled * normal, axis=1, keepdims=True)
    )
    grad = grad.astype(BF16)
    retained_out[...] = grad
    reach = column_power(rate, token_column()) * SCALE
    state = mm_tn((query[...].astype(F32) * reach).astype(BF16), grad)
    for slot in range(SLOTS):
        on, exponent = import_terms(meta, chunk, place, slot, rows)

        @pl.when(on)
        def _():
            acc[slot] += state * power(rate, exponent, HV)

    @pl.when(local == 0)
    def _():
        on, exponent = shift_in(meta, place, chunks)
        scale = jnp.where(on, power(rate, exponent, HV), 0.0)
        first_out[0] = (state * scale).astype(BF16)

    @pl.when(local == chunks - 1)
    def _():
        exports[:, 0] = acc[...].astype(BF16)


def gate_back(meta, rates, wide, weight, gate, normal, inverse, query, gain, bias):
    array, width, number = weight
    first = number * (width // HV)
    rows = query.shape[0]
    heads = query.shape[1] // QK
    chunks = rows // CHUNK
    block = pl.BlockSpec((CHUNK, HV), lambda h, c: (c, h))
    vector = pl.BlockSpec((1, HV), lambda h, c: (0, h))
    return pl.pallas_call(
        functools.partial(gate_back_kernel, rows, chunks),
        grid=(heads, chunks),
        in_specs=[
            smem(), smem(),
            pl.BlockSpec((CHUNK, D), lambda h, c: (c, 0)),
            pl.BlockSpec((D, HV), lambda h, c: (0, first + h)),
            block, block,
            pl.BlockSpec((1, CHUNK, 128), lambda h, c: (h, c, 0)),
            pl.BlockSpec((CHUNK, QK), lambda h, c: (c, h)),
            vector, vector,
        ],
        out_specs=[
            block, block, vector, vector,
            pl.BlockSpec((SLOTS, 1, QK, HV), lambda h, c: (0, h, 0, 0)),
            pl.BlockSpec((1, QK, HV), lambda h, c: (h, 0, 0)),
        ],
        out_shape=[
            jax.ShapeDtypeStruct((rows, heads * HV), BF16),
            jax.ShapeDtypeStruct((rows, heads * HV), BF16),
            jax.ShapeDtypeStruct((1, heads * HV), F32),
            jax.ShapeDtypeStruct((1, heads * HV), F32),
            jax.ShapeDtypeStruct((SLOTS, heads, QK, HV), BF16),
            jax.ShapeDtypeStruct((heads, QK, HV), BF16),
        ],
        scratch_shapes=[pltpu.VMEM((SLOTS, QK, HV), F32)],
        compiler_params=params(("arbitrary", "arbitrary")),
        name="gate_backward",
        cost_estimate=pl.CostEstimate(
            flops=2 * rows * heads * HV * (D + QK),
            bytes_accessed=rows * heads * 12288,
            transcendentals=rows * heads * HV,
        ),
    )(meta, rates, wide, array, gate, normal, inverse, query, gain[None, :], bias[None, :])


def retain_back_kernel(
    rows, chunks, meta, rates, query, key, value, grad, state_in, cosine, sine, own0, own1, own2,
    query_out, key_out, value_out, running, total_ref, decay_ref,
):
    step = pl.program_id(1)
    local = chunks - 1 - step
    rate = rates[pl.program_id(0)]
    place = meta[21]
    chunk = Chunk(meta, place * chunks + local)
    before = Chunk(meta, jnp.maximum(place * chunks + local - 1, 0))

    @pl.when(step == 0)
    def _():
        decay_ref[...] = decay_matrix(rate)
        running[...] = jnp.zeros_like(running)

    later = running[...]
    total_ref[...] = later
    for slot, ref in ((0, own0), (1, own1), (2, own2)):
        on, exponent = export_terms(meta, chunk, local, chunks, place, slot, rows)

        @pl.when(on)
        def _():
            total_ref[...] += ref[0].astype(F32) * power(rate, exponent, HV)

    total = total_ref[...].astype(BF16)

    q, k, v, g = query[...], key[...], value[...], grad[...]
    decay = valid_decay(decay_ref, chunk.count)
    scores = (mm_nt(q, k) * decay).astype(BF16)
    slopes = (mm_nt(g, v) * decay).astype(BF16)
    reach = column_power(rate, token_column()) * SCALE
    toward = key_decay(rate, chunk.count)
    grad_query = mm(slopes, k) + mm_nt(g, state_in[0, 0]) * reach
    grad_key = mm_tn(slopes, q) + mm_nt(v, total) * toward
    grad_value = mm_tn(scores, g) + mm(k, total) * toward
    value_out[...] = grad_value.astype(BF16)
    cos, sin = cosine[...], sine[...]
    half = QK // 2
    for out, val in ((query_out, grad_query), (key_out, grad_key)):
        a, b = val[:, :half], val[:, half:]
        out[:, :half] = (a * cos + b * sin).astype(BF16)
        out[:, half:] = (b * cos - a * sin).astype(BF16)

    fresh = mm_tn((q.astype(F32) * reach).astype(BF16), g)
    carried = fresh + later * power(rate, chunk.count, HV)
    keep = jnp.where((local > 0) & before.continues, 1.0, 0.0)
    running[...] = carried * power(rate, CHUNK - before.count, HV) * keep


def retain_back(meta, rates, query, key, value, grad, states, cosine, sine, own):
    rows = query.shape[0]
    heads = query.shape[1] // QK
    chunks = rows // CHUNK
    last = chunks - 1
    wide = pl.BlockSpec((CHUNK, HV), lambda h, s: (last - s, h))
    narrow = pl.BlockSpec((CHUNK, QK), lambda h, s: (last - s, h))
    table = pl.BlockSpec((CHUNK, QK // 2), lambda h, s: (last - s, 0))
    state = pl.BlockSpec((1, QK, HV), lambda h, s: (h, 0, 0))
    return pl.pallas_call(
        functools.partial(retain_back_kernel, rows, chunks),
        grid=(heads, chunks),
        in_specs=[
            smem(), smem(), narrow, narrow, wide, wide,
            pl.BlockSpec((1, 1, QK, HV), lambda h, s: (h, last - s, 0, 0)),
            table, table, state, state, state,
        ],
        out_specs=[narrow, narrow, wide],
        out_shape=[
            jax.ShapeDtypeStruct((rows, heads * QK), BF16),
            jax.ShapeDtypeStruct((rows, heads * QK), BF16),
            jax.ShapeDtypeStruct((rows, heads * HV), BF16),
        ],
        scratch_shapes=[
            pltpu.VMEM((QK, HV), F32), pltpu.VMEM((QK, HV), F32), pltpu.VMEM((CHUNK, CHUNK), F32)
        ],
        compiler_params=params(("arbitrary", "arbitrary")),
        name="retention_backward",
        cost_estimate=pl.CostEstimate(
            flops=2 * rows * heads * (CHUNK * 1792 + 4 * QK * HV),
            bytes_accessed=rows * heads * 6144,
            transcendentals=rows * heads * 256,
        ),
    )(meta, rates, query, key, value, grad, states, cosine, sine, *own)


def norm_kernel(values, gain, bias, out, average_out, inverse_out):
    x = values[...].astype(F32)
    average = jnp.mean(x, axis=1, keepdims=True)
    inverse = lax.rsqrt(jnp.mean(x * x, axis=1, keepdims=True) - average * average + EPSILON)
    out[...] = ((x - average) * inverse * gain[...] + bias[...]).astype(BF16)
    average_out[...] = jnp.broadcast_to(average, average_out.shape)
    inverse_out[...] = jnp.broadcast_to(inverse, inverse_out.shape)


def norm_wide(values, gain, bias):
    rows = values.shape[0]
    block = pl.BlockSpec((CHUNK, D), lambda i: (i, 0))
    vector = pl.BlockSpec((1, D), lambda i: (0, 0))
    stat = pl.BlockSpec((CHUNK, 128), lambda i: (i, 0))
    return pl.pallas_call(
        norm_kernel,
        grid=(rows // CHUNK,),
        in_specs=[block, vector, vector],
        out_specs=[block, stat, stat],
        out_shape=[
            jax.ShapeDtypeStruct((rows, D), BF16),
            jax.ShapeDtypeStruct((rows, 128), F32),
            jax.ShapeDtypeStruct((rows, 128), F32),
        ],
        compiler_params=params(("arbitrary",)),
        name="layer_norm",
        cost_estimate=pl.CostEstimate(
            flops=8 * rows * D, bytes_accessed=4 * rows * D, transcendentals=rows
        ),
    )(values, gain[None, :], bias[None, :])


def join_kernel(row, own, from_x, from_y, far_a, far_b, *refs, norm):
    block = own.shape[1]
    second = pl.program_id(0) >= pl.num_programs(0) // 2
    spots = [
        pl.ds(pl.multiple_of((row[0] ^ flip) * block, 128), block) for flip in range(4)
    ]
    pieces = [own[...], from_x[...], from_y[...], jnp.where(second, far_b[...], far_a[...])]
    if not norm:
        for spot, piece in zip(spots, pieces):
            refs[0][:, spot] = piece
        return
    gain, bias, out, average_out, inverse_out = refs
    pieces = [piece.astype(F32) for piece in pieces]
    average = sum(jnp.sum(piece, axis=1, keepdims=True) for piece in pieces) / D
    squares = sum(jnp.sum(piece * piece, axis=1, keepdims=True) for piece in pieces) / D
    inverse = lax.rsqrt(squares - average * average + EPSILON)
    for spot, piece in zip(spots, pieces):
        out[:, spot] = ((piece - average) * inverse * gain[:, spot] + bias[:, spot]).astype(BF16)
    average_out[...] = jnp.broadcast_to(average, average_out.shape)
    inverse_out[...] = jnp.broadcast_to(inverse, inverse_out.shape)


def join(pieces, row, gain=None, bias=None):
    norm = gain is not None
    if not isinstance(pieces, tuple):
        return norm_wide(pieces, gain, bias) if norm else pieces
    rows, block = pieces[0].shape
    steps = 4
    tile = rows // steps
    piece = pl.BlockSpec((tile, block), lambda i, r: (i, 0))
    far_a = pl.BlockSpec((tile, block), lambda i, r: (jnp.minimum(i, steps // 2 - 1), 0))
    far_b = pl.BlockSpec((tile, block), lambda i, r: (jnp.maximum(i - steps // 2, 0), 0))
    vector = pl.BlockSpec((1, D), lambda i, r: (0, 0))
    wide = pl.BlockSpec((tile, D), lambda i, r: (i, 0))
    stat = pl.BlockSpec((tile, 128), lambda i, r: (i, 0))
    wide_shape = jax.ShapeDtypeStruct((rows, D), BF16)
    stat_shape = jax.ShapeDtypeStruct((rows, 128), F32)
    return pl.pallas_call(
        functools.partial(join_kernel, norm=norm),
        grid_spec=pltpu.PrefetchScalarGridSpec(
            num_scalar_prefetch=1,
            grid=(steps,),
            in_specs=[piece] * 3 + [far_a, far_b] + ([vector] * 2 if norm else []),
            out_specs=[wide, stat, stat] if norm else wide,
        ),
        out_shape=[wide_shape, stat_shape, stat_shape] if norm else wide_shape,
        compiler_params=params(("arbitrary",)),
        name="join_norm" if norm else "join",
        cost_estimate=pl.CostEstimate(
            flops=8 * rows * D, bytes_accessed=4 * rows * D, transcendentals=0
        ),
    )(row, *pieces, *((gain[None, :], bias[None, :]) if norm else ()))


def project_kernel(
    heads, rows, chunks, meta, rates, values, weight, cosine, sine,
    query_out, key_out, value_out, exports, acc,
):
    local = pl.program_id(0)
    place = meta[21]
    chunk = Chunk(meta, place * chunks + local)
    raw = mm(values[...], weight[...])
    cos, sin = cosine[...], sine[...]
    half = QK // 2
    for part, out in ((0, query_out), (1, key_out)):
        for head in range(heads):
            first = (part * heads + head) * QK
            a, b = raw[:, first : first + half], raw[:, first + half : first + QK]
            out[:, head * QK : head * QK + half] = (a * cos - b * sin).astype(BF16)
            out[:, head * QK + half : (head + 1) * QK] = (b * cos + a * sin).astype(BF16)
    value_out[...] = raw[:, 2 * heads * QK :].astype(BF16)

    @pl.when(local == 0)
    def _():
        acc[...] = jnp.zeros_like(acc)

    for head in range(heads):
        rate = rates[head]
        key = key_out[:, head * QK : (head + 1) * QK].astype(F32)
        weighted = (key * key_decay(rate, chunk.count)).astype(BF16)
        state = mm_tn(weighted, value_out[:, head * HV : (head + 1) * HV])
        for slot in range(3):
            on, exponent = export_terms(meta, chunk, local, chunks, place, slot, rows)

            @pl.when(on)
            def _():
                acc[slot, head] += state * power(rate, exponent, HV)

    @pl.when(local == chunks - 1)
    def _():
        exports[...] = acc[...].astype(BF16)


def project(meta, rates, values, weight, cosine, sine):
    rows, width = values.shape[0], weight.shape[1]
    heads = width // (2 * QK + HV)
    chunks = rows // CHUNK
    table = pl.BlockSpec((CHUNK, QK // 2), lambda i: (i, 0))
    widths = (heads * QK, heads * QK, heads * HV)
    states = (3, heads, QK, HV)
    return pl.pallas_call(
        functools.partial(project_kernel, heads, rows, chunks),
        grid=(chunks,),
        in_specs=[
            smem(), smem(),
            pl.BlockSpec((CHUNK, D), lambda i: (i, 0)),
            pl.BlockSpec((D, width), lambda i: (0, 0)),
            table, table,
        ],
        out_specs=[pl.BlockSpec((CHUNK, w), lambda i: (i, 0)) for w in widths]
        + [pl.BlockSpec(states, lambda i: (0, 0, 0, 0))],
        out_shape=[jax.ShapeDtypeStruct((rows, w), BF16) for w in widths]
        + [jax.ShapeDtypeStruct(states, BF16)],
        scratch_shapes=[pltpu.VMEM(states, F32)],
        compiler_params=params(("arbitrary",)),
        name="project",
        cost_estimate=pl.CostEstimate(
            flops=2 * rows * D * width, bytes_accessed=2 * (rows + width) * D, transcendentals=0
        ),
    )(meta, rates, values, weight, cosine, sine)


def matmul_kernel(values, weight, out):
    out[...] = mm(values[...], weight[...]).astype(out.dtype)


def matmul(values, weight, kind):
    array, width, number = weight
    rows = values.shape[0]
    return pl.pallas_call(
        matmul_kernel,
        grid=(rows // CHUNK,),
        in_specs=[
            pl.BlockSpec((CHUNK, D), lambda i: (i, 0)),
            pl.BlockSpec((D, width), lambda i: (0, number)),
        ],
        out_specs=pl.BlockSpec((CHUNK, width), lambda i: (i, 0)),
        out_shape=jax.ShapeDtypeStruct((rows, width), kind),
        compiler_params=params(("arbitrary",)),
        name="matmul",
        cost_estimate=pl.CostEstimate(
            flops=2 * rows * D * width, bytes_accessed=2 * (rows + width) * D, transcendentals=0
        ),
    )(values, array)


def weight_grad_kernel(spans, *refs):
    count = len(spans)
    lefts, rights, out = refs[:count], refs[count : 2 * count], refs[2 * count]
    tile = pl.program_id(0)
    for left, right, (first, last) in zip(lefts, rights, spans):

        @pl.when((tile >= first) & (tile < last))
        def _():
            out[...] = mm_tn(left[...], right[...]).astype(BF16)


def weight_grads(pairs):
    rows = pairs[0][0].shape[0]
    wide = min(right.shape[1] for _, right in pairs)
    tall = 1024
    steps = D // tall
    spans, first = [], 0
    for _, right in pairs:
        spans.append((first, first + right.shape[1] // wide))
        first = spans[-1][1]

    def left_spec(span):
        return pl.BlockSpec(
            (rows, tall),
            lambda n, m: (
                0, jnp.where(n < span[0], 0, jnp.where(n < span[1], m, steps - 1)),
            ),
        )

    def right_spec(span):
        return pl.BlockSpec(
            (rows, wide), lambda n, m: (0, jnp.clip(n - span[0], 0, span[1] - span[0] - 1))
        )

    return pl.pallas_call(
        functools.partial(weight_grad_kernel, tuple(spans)),
        grid=(first, steps),
        in_specs=[left_spec(span) for span in spans] + [right_spec(span) for span in spans],
        out_specs=pl.BlockSpec((tall, wide), lambda n, m: (m, n)),
        out_shape=jax.ShapeDtypeStruct((D, first * wide), BF16),
        compiler_params=params(("arbitrary", "arbitrary")),
        name="weight_grads",
        cost_estimate=pl.CostEstimate(
            flops=2 * rows * D * first * wide,
            bytes_accessed=2 * D * first * wide + 4 * rows * D,
            transcendentals=0,
        ),
    )(*[left for left, _ in pairs], *[right for _, right in pairs])


def paired_grad_kernel(spans, tiles, steps, *refs):
    count = len(spans)
    lefts, rights, out = refs[:count], refs[count : 2 * count], refs[2 * count]
    made, received, send_sem, recv_sem = refs[2 * count + 1 :]
    step = pl.program_id(0)
    core = lax.axis_index("col") % 2
    partner = lax.axis_index("col") + 1 - 2 * core

    def copy(index):
        return pltpu.make_async_remote_copy(
            src_ref=made.at[index, :, 1 - core],
            dst_ref=received.at[index],
            send_sem=send_sem.at[index],
            recv_sem=recv_sem.at[index],
            device_id={"col": partner},
            device_id_type=pl.DeviceIdType.MESH,
        )

    @pl.when(step == 0)
    def _():
        barrier = pltpu.get_barrier_semaphore()
        pl.semaphore_signal(
            barrier, inc=1, device_id={"col": partner}, device_id_type=pl.DeviceIdType.MESH
        )
        pl.semaphore_wait(barrier, 1)

    for left, right, (first, last) in zip(lefts, rights, spans):

        @pl.when((step >= first * steps) & (step < last * steps))
        def _():
            total = mm_tn(left[...], right[...]).astype(BF16)
            made[step] = total.reshape(made.shape[1:])

    @pl.when(step < tiles)
    def _():
        copy(step).start()

    @pl.when(step > 0)
    def _():
        index = step - 1
        copy(index).wait()
        out[...] = (made[index, :, core].astype(F32) + received[index].astype(F32)).astype(BF16)


def paired_grads(pairs, number):
    rows = pairs[0][0].shape[0]
    wide = min(right.shape[1] for _, right in pairs)
    wide = min(wide, 512)
    tall = 1024
    steps = D // tall
    block = D // SLOTS
    depth = tall // block // 2
    spans, first = [], 0
    for _, right in pairs:
        spans.append((first, first + right.shape[1] // wide))
        first = spans[-1][1]
    tiles = first * steps

    def left_spec(span):
        def index(s):
            n, m = s // steps, s % steps
            return 0, jnp.where(n < span[0], 0, jnp.where(n < span[1], m, steps - 1))

        return pl.BlockSpec((rows, tall), index)

    def right_spec(span):
        def index(s):
            return 0, jnp.clip(s // steps - span[0], 0, span[1] - span[0] - 1)

        return pl.BlockSpec((rows, wide), index)

    def out_index(s):
        done = jnp.maximum(s - 1, 0)
        return done % steps, 0, done // steps

    result = pl.pallas_call(
        functools.partial(paired_grad_kernel, tuple(spans), tiles, steps),
        grid=(tiles + 1,),
        in_specs=[left_spec(span) for span in spans] + [right_spec(span) for span in spans],
        out_specs=pl.BlockSpec((depth, block, wide), out_index),
        out_shape=jax.ShapeDtypeStruct((SLOTS // 2, block, first * wide), BF16),
        scratch_shapes=[
            pltpu.VMEM((tiles, depth, 2, block, wide), BF16),
            pltpu.VMEM((tiles, depth, block, wide), BF16),
            pltpu.SemaphoreType.DMA((tiles,)),
            pltpu.SemaphoreType.DMA((tiles,)),
        ],
        compiler_params=pltpu.CompilerParams(
            dimension_semantics=("arbitrary",),
            collective_id=number,
            has_side_effects=True,
            vmem_limit_bytes=60 * 1024 * 1024,
        ),
        name="paired_grads",
        cost_estimate=pl.CostEstimate(
            flops=2 * rows * D * first * wide,
            bytes_accessed=2 * D * first * wide + 4 * rows * D,
            transcendentals=0,
        ),
    )(*[left for left, _ in pairs], *[right for _, right in pairs])
    return result


def column_grads(pairs, number):
    if lax.axis_size("col") != SLOTS:
        return weight_grads(pairs)
    return paired_grads(pairs, number)


def norm_pieces(row, own, from_x, from_y, far_a, far_b, gain, bias, out, average_out, inverse_out):
    block = own.shape[1]
    second = pl.program_id(0) >= pl.num_programs(0) // 2
    far = jnp.where(second, far_b[...], far_a[...])
    pieces = [piece.astype(F32) for piece in (own[...], from_x[...], from_y[...], far)]
    average = sum(jnp.sum(piece, axis=1, keepdims=True) for piece in pieces) / D
    squares = sum(jnp.sum(piece * piece, axis=1, keepdims=True) for piece in pieces) / D
    inverse = lax.rsqrt(squares - average * average + EPSILON)
    for flip, piece in enumerate(pieces):
        spot = pl.ds(pl.multiple_of((row[0] ^ flip) * block, 128), block)
        out[:, spot] = ((piece - average) * inverse * gain[:, spot] + bias[:, spot]).astype(BF16)
    average_out[...] = jnp.broadcast_to(average, average_out.shape)
    inverse_out[...] = jnp.broadcast_to(inverse, inverse_out.shape)


def up_kernel(row, *refs, joined):
    if joined:
        pieces, gain, norm_bias = refs[:5], refs[5], refs[6]
        weight, bias, grad_hidden, second_out, average_out, inverse_out = refs[7:13]
        hidden_out, grad_out, bias_out = refs[13:]
        norm_pieces(row, *pieces, gain, norm_bias, second_out, average_out, inverse_out)
        values = second_out
    else:
        values, weight, bias, grad_hidden, hidden_out, grad_out, bias_out = refs
    before = mm(values[...], weight[...]) + bias[...]
    phi = 0.5 * (1.0 + lax.erf(before * (0.5**0.5)))
    hidden_out[...] = (before * phi).astype(BF16)
    density = jnp.exp(-0.5 * before * before) * 0.3989422804014327
    grad = (grad_hidden[...].astype(F32) * (phi + before * density)).astype(BF16)
    grad_out[...] = grad

    @pl.when(pl.program_id(0) == 0)
    def _():
        bias_out[...] = jnp.zeros_like(bias_out)

    bias_out[...] += jnp.sum(grad.astype(F32), axis=0, keepdims=True)


def feed_up(pieces, row, gain, norm_bias, weight, bias, grad_hidden):
    array, width, number = weight
    joined = isinstance(pieces, tuple)
    rows = grad_hidden.shape[0]
    steps = 4
    tile = rows // steps
    block = pl.BlockSpec((tile, width), lambda i, r: (i, 0))
    vector = pl.BlockSpec((1, width), lambda i, r: (0, 0))
    wide = pl.BlockSpec((tile, D), lambda i, r: (i, 0))
    stat = pl.BlockSpec((tile, 128), lambda i, r: (i, 0))
    gains = pl.BlockSpec((1, D), lambda i, r: (0, 0))
    if joined:
        piece = pl.BlockSpec((tile, pieces[0].shape[1]), lambda i, r: (i, 0))
        far_a = pl.BlockSpec(
            (tile, pieces[0].shape[1]), lambda i, r: (jnp.minimum(i, steps // 2 - 1), 0)
        )
        far_b = pl.BlockSpec(
            (tile, pieces[0].shape[1]), lambda i, r: (jnp.maximum(i - steps // 2, 0), 0)
        )
        inputs = list(pieces) + [gain[None, :], norm_bias[None, :]]
        in_specs = [piece] * 3 + [far_a, far_b, gains, gains]
        early_specs = [wide, stat, stat]
        early_shapes = [
            jax.ShapeDtypeStruct((rows, D), BF16),
            jax.ShapeDtypeStruct((rows, 128), F32),
            jax.ShapeDtypeStruct((rows, 128), F32),
        ]
        normed = []
    else:
        normed = list(norm_wide(pieces, gain, norm_bias))
        inputs, in_specs, early_specs, early_shapes = [normed[0]], [wide], [], []
    outs = pl.pallas_call(
        functools.partial(up_kernel, joined=joined),
        grid_spec=pltpu.PrefetchScalarGridSpec(
            num_scalar_prefetch=1,
            grid=(steps,),
            in_specs=in_specs
            + [pl.BlockSpec((D, width), lambda i, r: (0, number)), vector, block],
            out_specs=early_specs + [block, block, vector],
        ),
        out_shape=early_shapes
        + [
            jax.ShapeDtypeStruct((rows, width), BF16),
            jax.ShapeDtypeStruct((rows, width), BF16),
            jax.ShapeDtypeStruct((1, width), F32),
        ],
        compiler_params=params(("arbitrary",)),
        name="feed_up",
        cost_estimate=pl.CostEstimate(
            flops=2 * rows * D * width,
            bytes_accessed=2 * (2 * rows + width) * D + 8 * rows * width,
            transcendentals=2 * rows * width,
        ),
    )(row, *inputs, array, bias[None, :], grad_hidden)
    return normed + list(outs)


PARTIAL_FLIP = (1, 3, 2, 3, 2, 1, 0, 0)
PARTIAL_HALF = (0, 0, 1, 1, 0, 1, 0, 1)


def table_lookup(table, step):
    result = jnp.int32(table[0])
    for index in range(1, len(table)):
        result = jnp.where(step == index, table[index], result)
    return result


def partial_kernel(count, row, *refs):
    values, weights = refs[:count], refs[count : 2 * count]
    outs = refs[2 * count :]
    step = pl.program_id(0)
    total = mm_nt(values[0][...], weights[0][...])
    for x, w in zip(values[1:], weights[1:]):
        total = total + mm_nt(x[...], w[...])
    for index, out in enumerate(outs):

        @pl.when(step // 2 == index)
        def _():
            out[0] = total.astype(out.dtype)


def partial_blocks(values, weights, row, first, kinds):
    rows = values[0].shape[0]
    half, block = rows // 2, D // 4
    count = len(values)
    flips = PARTIAL_FLIP[2 * first : 2 * (first + len(kinds))]
    halves = PARTIAL_HALF[2 * first : 2 * (first + len(kinds))]

    def value_spec(x):
        return pl.BlockSpec((half, x.shape[1]), lambda s, r: (table_lookup(halves, s), 0))

    def weight_spec(w):
        return pl.BlockSpec((block, w[1]), lambda s, r: (r[0] ^ table_lookup(flips, s), w[2]))

    def out_spec(index):
        return pl.BlockSpec((1, half, block), lambda s, r: (jnp.clip(s - 2 * index, 0, 1), 0, 0))

    depth = sum(x.shape[1] for x in values)
    return pl.pallas_call(
        functools.partial(partial_kernel, count),
        grid_spec=pltpu.PrefetchScalarGridSpec(
            num_scalar_prefetch=1,
            grid=(2 * len(kinds),),
            in_specs=[value_spec(x) for x in values] + [weight_spec(w) for w in weights],
            out_specs=[out_spec(index) for index in range(len(kinds))],
        ),
        out_shape=[jax.ShapeDtypeStruct((2, half, block), kind) for kind in kinds],
        compiler_params=params(("arbitrary",)),
        name="partial_blocks",
        cost_estimate=pl.CostEstimate(
            flops=rows * block * depth * 2 * len(kinds),
            bytes_accessed=(rows + D) * depth * 2 + 4 * rows * block * len(kinds),
            transcendentals=0,
        ),
    )(row, *values, *[w[0] for w in weights])


def permute_row(value, pairs):
    return lax.ppermute(value, "row", pairs)


def in_order(*values):
    return lax.optimization_barrier(values)


def reduce_row_start(values, weights, row):
    if lax.axis_size("row") != 4:
        columns = [array[:, n * width : (n + 1) * width] for array, width, n in weights]
        return sum(mm_nt(x, w) for x, w in zip(values, columns)).astype(BF16)
    return tuple(partial_blocks(values, weights, row, 0, (BF16, BF16)))


def reduce_row_finish(sends, values, weights, row, between=None):
    if lax.axis_size("row") != 4:
        total = lax.psum_scatter(sends, "row", scatter_dimension=1, tiled=True).astype(F32)
        return total, between() if between else None
    from_x = permute_row(sends[0], X_PAIRS)
    from_y = permute_row(sends[1], Y_PAIRS)
    extra = None
    if between is not None:
        extra = between()
        from_x, from_y, extra = in_order(from_x, from_y, extra)
    keep, own = partial_blocks(values, weights, row, 2, (BF16, F32))
    next_y = (keep[0].astype(F32) + from_x[1].astype(F32)).astype(BF16)
    next_x = (keep[1].astype(F32) + from_y[1].astype(F32)).astype(BF16)
    last_y = permute_row(next_y, Y_PAIRS)
    last_x = permute_row(next_x, X_PAIRS)
    first_half = own[0] + from_x[0].astype(F32) + last_y.astype(F32)
    second_half = own[1] + from_y[0].astype(F32) + last_x.astype(F32)
    return jnp.concatenate([first_half, second_half], axis=0), extra


def gather_row(value, between=None, later=None):
    if lax.axis_size("row") != 4:
        gathered = lax.all_gather(value, "row", axis=1, tiled=True)
        if later is not None:
            return gathered, later[0](later[1])
        return gathered, between() if between else None
    half = value.shape[0] // 2
    from_x = permute_row(value, X_PAIRS)
    from_y = permute_row(value, Y_PAIRS)
    extra = None
    if between is not None:
        extra = between()
        from_x, from_y, extra = in_order(from_x, from_y, extra)
    if later is not None:
        from_x, from_y, argument = in_order(from_x, from_y, later[1])
    far_a = permute_row(from_x[:half], Y_PAIRS)
    far_b = permute_row(from_y[half:], X_PAIRS)
    if later is not None:
        extra = later[0](argument)
        far_a, far_b, extra = in_order(far_a, far_b, extra)
    return (value, from_x, from_y, far_a, far_b), extra


def gather_row_small(value):
    if lax.axis_size("row") != 4:
        return lax.all_gather(value, "row", axis=1, tiled=True)
    row = lax.axis_index("row")
    pieces = jnp.stack(
        [value] + [permute_row(value, pairs) for pairs in (X_PAIRS, Y_PAIRS, D_PAIRS)]
    )
    ordered = [
        lax.dynamic_index_in_dim(pieces, row ^ place, 0, keepdims=False) for place in range(4)
    ]
    return jnp.concatenate(ordered, axis=1)


def sum_row_small(value):
    if lax.axis_size("row") != 4:
        return lax.psum(value, "row")
    first = value + permute_row(value, X_PAIRS)
    return first + permute_row(first, Y_PAIRS)


def norm_backward(grad_out, normal, inverse, gain_vector):
    scaled = grad_out * gain_vector
    sums = sum_row_small(jnp.stack([jnp.sum(scaled, axis=1), jnp.sum(scaled * normal, axis=1)]))
    means = sums / D
    grad_in = inverse * (scaled - means[0][:, None] - normal * means[1][:, None])
    return (grad_in, jnp.sum(grad_out * normal, axis=0), jnp.sum(grad_out, axis=0))


def gather_col(weight):
    return lax.all_gather(weight, "col", axis=0, tiled=True)


def scatter_col(grad):
    if grad.ndim == 2:
        return lax.psum_scatter(grad, "col", scatter_dimension=0, tiled=True).astype(F32)
    groups = [list(range(core, SLOTS, 2)) for core in range(2)]
    total = lax.psum_scatter(grad, "col", scatter_dimension=0, axis_index_groups=groups)
    return total.astype(F32)


class Exchange:
    def __init__(self, messages, send_sem, recv_sem):
        col = lax.axis_index("col")
        self.base = (col // SLOTS) * SLOTS
        self.place = col % SLOTS
        self.messages, self.send_sem, self.recv_sem = messages, send_sem, recv_sem

    def copy(self, index):
        _, target, source, destination = self.messages[index]
        return pltpu.make_async_remote_copy(
            src_ref=source,
            dst_ref=destination,
            send_sem=self.send_sem.at[index],
            recv_sem=self.recv_sem.at[index],
            device_id={"col": self.base + target},
            device_id_type=pl.DeviceIdType.MESH,
        )

    def greet(self):
        barrier = pltpu.get_barrier_semaphore()
        for step in range(1, SLOTS):
            other = self.base + (self.place + step) % SLOTS
            pl.semaphore_signal(
                barrier, inc=1, device_id={"col": other}, device_id_type=pl.DeviceIdType.MESH
            )
        pl.semaphore_wait(barrier, SLOTS - 1)

    def run(self, programs):
        for place, program in enumerate(programs):

            @pl.when(self.place == place)
            def _():
                sent = []
                for action in program:
                    if callable(action):
                        action()
                    elif action >= 0:
                        self.copy(action).start()
                        sent.append(action)
                    else:
                        self.copy(~action).wait_recv()
                for index in sent:
                    self.copy(index).wait_send()


def scaled_add(meta, rates, target, terms, rows):
    heads = target.shape[0]
    for head in range(heads):
        total = None
        for term in terms:
            if isinstance(term, tuple):
                ref, slot = term
                exponent = jnp.maximum(
                    trunk_reference(meta, jnp.int32(3), rows)
                    - trunk_reference(meta, jnp.int32(slot), rows),
                    0,
                )
                value = ref[head].astype(F32) * power(rates[head], exponent, HV)
            else:
                value = term[head].astype(F32)
            total = value if total is None else total + value
        target[head] = total.astype(BF16)


def share_kernel(rows, meta, rates, ex, sh, shift, tot, send_sem, recv_sem):
    messages = [
        (0, 2, ex.at[0], sh.at[0]),
        (0, 1, ex.at[0], sh.at[0]),
        (1, 3, ex.at[0], sh.at[1]),
        (2, 3, ex.at[0], sh.at[2]),
        (2, 3, sh.at[0], sh.at[0]),
        (3, 2, sh.at[1], sh.at[1]),
        (3, 4, ex.at[1], sh.at[4]),
        (3, 5, ex.at[2], sh.at[5]),
        (3, 4, tot, sh.at[3]),
        (4, 5, ex.at[1], sh.at[6]),
        (4, 6, ex.at[1], sh.at[6]),
        (4, 5, ex.at[2], sh.at[7]),
        (5, 7, sh.at[7], sh.at[7]),
        (4, 5, sh.at[4], sh.at[4]),
        (4, 6, sh.at[4], sh.at[4]),
        (5, 4, sh.at[5], sh.at[5]),
        (5, 7, sh.at[5], sh.at[5]),
        (4, 5, sh.at[3], sh.at[3]),
        (4, 6, sh.at[3], sh.at[3]),
        (6, 7, sh.at[6], sh.at[6]),
        (6, 7, sh.at[4], sh.at[4]),
        (6, 7, sh.at[3], sh.at[3]),
        (7, 6, sh.at[7], sh.at[7]),
        (7, 6, sh.at[5], sh.at[5]),
        (4, 5, ex.at[0], shift),
        (6, 7, ex.at[0], shift),
    ]
    exchange = Exchange(messages, send_sem, recv_sem)

    def keep_trunk():
        sh[3] = ex[0]

    def total_trunk():
        terms = [(sh.at[slot], slot) for slot in range(3)] + [ex.at[0]]
        scaled_add(meta, rates, tot, terms, rows)

    def keep_branches():
        sh[6] = ex[1]
        sh[7] = ex[2]

    exchange.greet()
    exchange.run(
        [
            [0, 1],
            [2, ~1],
            [3, ~0, 4, ~5],
            [6, 7, keep_trunk, ~2, 5, ~4, ~3, total_trunk, 8],
            [10, 11, 9, 24, keep_branches, ~6, 14, 13, ~15, ~8, 18, 17],
            [~11, 12, ~7, 16, 15, ~9, ~24, ~13, ~17],
            [25, ~10, 19, ~14, 20, ~22, ~23, ~18, 21],
            [~12, 22, ~16, 23, ~19, ~20, ~25, ~21],
        ]
    )


def vmem():
    return pl.BlockSpec(memory_space=pltpu.VMEM)


def share_states(meta, rates, exports, rows):
    heads = exports.shape[1]
    state = (heads, QK, HV)
    return pl.pallas_call(
        functools.partial(share_kernel, rows),
        in_specs=[smem(), smem(), vmem()],
        out_specs=[vmem(), vmem()],
        out_shape=[
            jax.ShapeDtypeStruct((SLOTS,) + state, BF16),
            jax.ShapeDtypeStruct(state, BF16),
        ],
        scratch_shapes=[
            pltpu.VMEM(state, BF16),
            pltpu.SemaphoreType.DMA((26,)),
            pltpu.SemaphoreType.DMA((26,)),
        ],
        compiler_params=pltpu.CompilerParams(
            collective_id=1, has_side_effects=True, vmem_limit_bytes=40 * 1024 * 1024
        ),
        name="share_states",
        cost_estimate=pl.CostEstimate(
            flops=0, bytes_accessed=100 * 1024 * 1024, transcendentals=0
        ),
    )(meta, rates, exports)


def return_kernel(rows, meta, rates, y, first, own0, own1, own2, rx, tx, send_sem, recv_sem):
    messages = [
        (7, 6, y.at[3], rx.at[0]),
        (7, 6, y.at[4], rx.at[1]),
        (7, 6, y.at[5], rx.at[2]),
        (6, 7, y.at[6], rx.at[0]),
        (6, 7, y.at[7], rx.at[1]),
        (7, 5, tx.at[0], rx.at[0]),
        (7, 5, tx.at[1], rx.at[1]),
        (6, 4, tx.at[0], rx.at[0]),
        (6, 4, tx.at[1], rx.at[1]),
        (6, 4, tx.at[2], rx.at[2]),
        (5, 4, y.at[3], rx.at[3]),
        (5, 4, y.at[4], rx.at[4]),
        (5, 4, y.at[5], rx.at[5]),
        (5, 4, tx.at[0], rx.at[6]),
        (5, 4, tx.at[1], rx.at[7]),
        (4, 3, tx.at[0], rx.at[0]),
        (4, 3, tx.at[1], own1),
        (4, 3, tx.at[2], own2),
        (2, 3, y.at[0], rx.at[1]),
        (2, 3, y.at[1], rx.at[2]),
        (3, 2, tx.at[2], own0),
        (3, 1, tx.at[1], own0),
        (3, 0, tx.at[0], rx.at[0]),
        (1, 0, y.at[0], rx.at[1]),
        (5, 4, first, own0),
        (7, 6, first, own0),
    ]
    exchange = Exchange(messages, send_sem, recv_sem)

    def add(target, *terms):
        return lambda: scaled_add(meta, rates, target, terms, rows)

    exchange.greet()
    exchange.run(
        [
            [~23, ~22, add(own0, rx.at[0], rx.at[1])],
            [23, ~21],
            [18, 19, ~20],
            [
                ~18, ~19, ~15,
                add(tx.at[0], y.at[0], rx.at[1], (rx.at[0], 0)), 22,
                add(tx.at[1], y.at[1], rx.at[2], (rx.at[0], 1)), 21,
                add(tx.at[2], y.at[2], (rx.at[0], 2)), 20,
                add(own0, rx.at[0], y.at[3]),
                ~16, ~17,
            ],
            [
                ~10, ~7, add(tx.at[0], y.at[3], rx.at[0], rx.at[3]), 15,
                ~11, ~8, add(tx.at[1], y.at[4], rx.at[1], rx.at[4]), 16,
                ~12, ~9, add(tx.at[2], y.at[5], rx.at[2], rx.at[5]), 17,
                ~13, add(own1, y.at[6], rx.at[6]),
                ~14, add(own2, y.at[7], rx.at[7]),
                ~24,
            ],
            [
                10, 11, 12, 24,
                ~5, add(tx.at[0], y.at[6], rx.at[0]), 13,
                ~6, add(tx.at[1], y.at[7], rx.at[1]), 14,
            ],
            [
                3, 4,
                ~0, add(tx.at[0], y.at[3], rx.at[0]), 7,
                ~1, add(tx.at[1], y.at[4], rx.at[1]), 8,
                ~2, add(tx.at[2], y.at[5], rx.at[2]), 9,
                ~25,
            ],
            [
                0, 1, 2, 25,
                ~3, add(tx.at[0], y.at[6], rx.at[0]), 5,
                ~4, add(tx.at[1], y.at[7], rx.at[1]), 6,
            ],
        ]
    )


def return_states(meta, rates, exports, first_state, rows):
    heads = exports.shape[1]
    state = (heads, QK, HV)
    return pl.pallas_call(
        functools.partial(return_kernel, rows),
        in_specs=[smem(), smem(), vmem(), vmem()],
        out_specs=[vmem()] * 3,
        out_shape=[jax.ShapeDtypeStruct(state, BF16)] * 3,
        scratch_shapes=[
            pltpu.VMEM((8,) + state, BF16),
            pltpu.VMEM((3,) + state, BF16),
            pltpu.SemaphoreType.DMA((26,)),
            pltpu.SemaphoreType.DMA((26,)),
        ],
        compiler_params=pltpu.CompilerParams(
            collective_id=2, has_side_effects=True, vmem_limit_bytes=40 * 1024 * 1024
        ),
        name="return_states",
        cost_estimate=pl.CostEstimate(
            flops=0, bytes_accessed=100 * 1024 * 1024, transcendentals=0
        ),
    )(meta, rates, exports, first_state)


def sum_col(value):
    size = lax.axis_size("col")
    if size != SLOTS:
        return lax.psum(value, "col")
    for flip in (1, 2, 4):
        value = value + lax.ppermute(value, "col", [(a, a ^ flip) for a in range(size)])
    return value


def sum_col_vectors(vectors, extra=None):
    col = lax.axis_index("col")
    size = lax.axis_size("col")
    parts = list(vectors) + ([extra] if extra is not None else [])
    total = sum_col(jnp.concatenate(parts).reshape(-1, 128)).reshape(-1)
    results, first = [], 0
    for vector in vectors:
        width = vector.shape[0] // size
        results.append(lax.dynamic_slice_in_dim(total, first + col * width, width, 0))
        first += vector.shape[0]
    return results, total[first:]


def token_tables(place, rows, lengths, parents):
    index = place * rows + jnp.arange(rows, dtype=jnp.int32)
    in_trunk = index < TRUNK
    beyond = jnp.maximum(index - TRUNK, 0)
    segment = jnp.where(in_trunk, 0, 1 + beyond // SEG)
    position = jnp.where(in_trunk, index, beyond % SEG)

    def lookup(table, spots):
        hits = spots[:, None] == jnp.arange(table.shape[0], dtype=jnp.int32)
        return jnp.sum(jnp.where(hits, table, 0), axis=1)

    branch = 1 + lookup(parents, jnp.clip(segment - 5, 0, 7))
    parent_length = lookup(lengths, branch)
    depth = position + jnp.where(segment >= 1, lengths[0], 0)
    depth = depth + jnp.where(segment >= 5, parent_length, 0)
    valid = (position < lookup(lengths, segment)).astype(F32)
    half = QK // 2
    frequency = 10000.0 ** (-jnp.arange(half, dtype=F32) / (half - 1))
    angles = depth.astype(F32)[:, None] * frequency[None, :]
    return valid, jnp.cos(angles), jnp.sin(angles)


def body(
    tokens,
    cotangent,
    query_weight,
    key_weight,
    value_weight,
    gate_weight,
    out_weight,
    up_weight,
    down_weight,
    first_gain,
    first_bias,
    group_gain,
    group_bias,
    second_gain,
    second_bias,
    up_bias,
    down_bias,
    segment_lengths,
    leaf_parents,
):
    rows = tokens.shape[0]
    col = lax.axis_index("col")
    row = lax.axis_index("row")
    row_ref = row.astype(jnp.int32)[None]
    place = (col % SLOTS).astype(jnp.int32)
    tree = (col // SLOTS).astype(jnp.int32)
    lengths = lax.dynamic_index_in_dim(segment_lengths, tree, 0, keepdims=False)
    parents = lax.dynamic_index_in_dim(leaf_parents, tree, 0, keepdims=False)
    meta = jnp.concatenate([lengths, parents, place[None]]).astype(jnp.int32)
    heads = query_weight.shape[1] // QK
    head_numbers = (row * heads + jnp.arange(heads, dtype=jnp.int32)).astype(F32)
    rates = jnp.log(1.0 - 2.0 ** (-5.0 - head_numbers))

    wide = heads * HV
    narrow = heads * QK
    project_full = gather_col(jnp.concatenate([query_weight, key_weight, value_weight], axis=1))
    gate_full = gather_col(gate_weight)
    out_full = gather_col(out_weight.T)
    feed_full = gather_col(jnp.concatenate([down_weight.T, up_weight], axis=1))
    query_part, key_part = (project_full, narrow, 0), (project_full, narrow, 1)
    value_part = (project_full, wide, 1)
    out_part = (out_full, wide, 0)
    down_part, up_part = (feed_full, wide, 0), (feed_full, wide, 1)

    valid, cosine, sine = token_tables(place, rows, lengths, parents)
    column = valid[:, None]
    gains = gather_row_small(jnp.stack([first_gain, first_bias, second_gain, second_bias]))
    token_pieces, _ = gather_row(tokens)
    first_wide, first_average, first_inverse = join(token_pieces, row_ref, gains[0], gains[1])
    fed_low = (cotangent.astype(F32) * column).astype(BF16)
    fed_low, first_average = lax.optimization_barrier((fed_low, first_average))

    fed_pieces, projected = gather_row(
        fed_low, lambda: project(meta, rates, first_wide, project_full, cosine, sine)
    )
    query_rot, key_rot, value_low, exports = projected
    shared, shifted = share_states(meta, rates, exports, rows)
    gate_full, shared = in_order(gate_full, shared)
    gate_part = (gate_full, wide, 0)
    gate_full, fed_pieces = in_order(gate_full, fed_pieces)
    gate_part = (gate_full, wide, 0)
    gate_raw, gated, normal, inverse, states = retain(
        meta, rates, query_rot, key_rot, value_low, first_wide, gate_part, shared, shifted,
        group_gain, group_bias,
    )

    sends = reduce_row_start([gated], [out_part], row_ref)
    attended, _ = reduce_row_finish(sends, [gated], [out_part], row_ref)
    middle = tokens.astype(F32) + attended

    def feed_gradient(pieces):
        joined = join(pieces, row_ref)
        return joined, matmul(joined, down_part, BF16)

    middle_pieces, (fed_wide, grad_hidden) = gather_row(
        middle.astype(BF16), later=(feed_gradient, fed_pieces)
    )
    second_wide, second_average, second_inverse, hidden, grad_before, up_bias_grad = feed_up(
        middle_pieces, row_ref, gains[2], gains[3], up_part, up_bias, grad_hidden
    )
    sends = reduce_row_start([grad_before], [up_part], row_ref)
    sends, hidden = in_order(sends, hidden)
    second_back, feed_partial = reduce_row_finish(
        sends,
        [grad_before],
        [up_part],
        row_ref,
        lambda: column_grads([(fed_wide, hidden), (second_wide, grad_before)], 3),
    )
    feed_grad = scatter_col(feed_partial)
    grad_fed = fed_low.astype(F32)
    down_bias_grad = jnp.sum(grad_fed, axis=0)

    second_normal = (middle - second_average[:, :1]) * second_inverse[:, :1]
    grad_middle_norm, second_gain_grad, second_bias_grad = norm_backward(
        second_back, second_normal, second_inverse[:, :1], second_gain
    )
    grad_middle = grad_fed + grad_middle_norm
    grad_pieces, fed_sends = gather_row(
        grad_middle.astype(BF16), lambda: reduce_row_start([hidden], [down_part], row_ref)
    )
    grad_wide = join(grad_pieces, row_ref)
    out_partial = column_grads([(grad_wide, gated)], 4)
    out_partial, grad_wide, feed_grad, fed_sends = in_order(
        out_partial, grad_wide, feed_grad, fed_sends
    )
    out_grad = scatter_col(out_partial)
    fed_out, gate_results = reduce_row_finish(
        fed_sends,
        [hidden],
        [down_part],
        row_ref,
        lambda: gate_back(
            meta, rates, grad_wide, out_part, gate_raw, normal, inverse, query_rot, group_gain, group_bias
        ),
    )
    fed_out = fed_out + down_bias
    layer_out = middle + fed_out
    grad_gate, grad_retained, group_gain_grad, group_bias_grad, returns, first_state = gate_results
    own = return_states(meta, rates, returns, first_state, rows)
    grad_gate, own = in_order(grad_gate, own)
    gate_partial = column_grads([(first_wide, grad_gate)], 5)
    gate_partial, own, out_grad = in_order(gate_partial, own, out_grad)
    gate_grad = scatter_col(gate_partial)
    grad_query, grad_key, grad_value = retain_back(
        meta, rates, query_rot, key_rot, value_low, grad_retained, states, cosine, sine, own
    )
    back_values = [grad_query, grad_key, grad_value, grad_gate]
    back_weights = [query_part, key_part, value_part, gate_part]
    back_values = [grad_query, grad_key, grad_value, grad_gate]
    back_weights = [query_part, key_part, value_part, gate_part]
    sends = reduce_row_start(back_values, back_weights, row_ref)
    sends, grad_value = in_order(sends, grad_value)
    first_back, project_partial = reduce_row_finish(
        sends,
        back_values,
        back_weights,
        row_ref,
        lambda: column_grads(
            [(first_wide, grad_query), (first_wide, grad_key), (first_wide, grad_value)], 6
        ),
    )
    project_partial, gate_grad, group_gain_grad = in_order(
        project_partial, gate_grad, group_gain_grad
    )
    project_grad = scatter_col(project_partial)

    first_normal = (tokens.astype(F32) - first_average[:, :1]) * first_inverse[:, :1]
    grad_first, first_gain_grad, first_bias_grad = norm_backward(
        first_back, first_normal, first_inverse[:, :1], first_gain
    )
    tokens_grad = grad_middle + grad_first

    vectors, _ = sum_col_vectors(
        (
            group_gain_grad[0],
            group_bias_grad[0],
            second_gain_grad,
            second_bias_grad,
            up_bias_grad[0],
            down_bias_grad,
        )
    )
    squares = jnp.stack(
        [
            jnp.sum(column * layer_out * layer_out),
            jnp.sum(column * attended * attended),
            jnp.sum(column * fed_out * fed_out),
        ]
    )
    last, col_squares = sum_col_vectors(
        (first_gain_grad, first_bias_grad), jnp.concatenate([squares, jnp.zeros((125,), F32)])
    )
    totals = sum_row_small(col_squares[None, :])[0, :3]
    valid_count = jnp.sum(segment_lengths).astype(F32) * D
    norm_values = jnp.sqrt(totals / valid_count)
    return (
        layer_out.astype(BF16),
        tokens_grad,
        project_grad[:, :narrow],
        project_grad[:, narrow : 2 * narrow],
        project_grad[:, 2 * narrow :],
        gate_grad,
        out_grad.T,
        feed_grad[:, wide:],
        feed_grad[:, :wide].T,
        last[0],
        last[1],
        vectors[0],
        vectors[1],
        vectors[2],
        vectors[3],
        vectors[4],
        vectors[5],
        norm_values,
    )


def solution(mesh):
    matrix, turned, vector = P("col", "row"), P("row", "col"), P("row")
    in_specs = (matrix,) * 6 + (turned, matrix, turned) + (vector,) * 8 + (P(), P())
    split = P(("row", "col"))
    out_specs = (matrix,) * 6 + (turned, matrix, turned) + (split,) * 8 + (P(),)
    return jax.shard_map(body, mesh=mesh, in_specs=in_specs, out_specs=out_specs, check_vma=False)
```

```python
import functools

import jax
import jax.numpy as jnp
from jax import lax
from jax.experimental import pallas as pl
from jax.experimental.pallas import tpu as pltpu
from jax.sharding import PartitionSpec as P

D = 2048
QK = 256
HV = 512
TRUNK = 4096
SEG = 512
TREE_LEN = TRUNK + 12 * SEG
CHUNK = 256
TRUNK_CHUNKS = TRUNK // CHUNK
SLOTS = 8
GRAD_TILE = 256

EPSILON = 1e-05
SCALE = QK**-0.5
F32 = jnp.float32
BF16 = jnp.bfloat16

X_PAIRS = [(0, 1), (1, 0), (2, 3), (3, 2)]
Y_PAIRS = [(0, 2), (2, 0), (1, 3), (3, 1)]
D_PAIRS = [(0, 3), (3, 0), (1, 2), (2, 1)]


def mm(a, b):
    return lax.dot_general(a, b, (((1,), (0,)), ((), ())), preferred_element_type=F32)


def mm_nt(a, b):
    return lax.dot_general(a, b, (((1,), (1,)), ((), ())), preferred_element_type=F32)


def mm_tn(a, b):
    return lax.dot_general(a, b, (((0,), (0,)), ((), ())), preferred_element_type=F32)


def params(semantics, limit=None):
    return pltpu.CompilerParams(
        dimension_semantics=semantics, vmem_limit_bytes=limit or 60 * 1024 * 1024
    )


def smem():
    return pl.BlockSpec(memory_space=pltpu.SMEM)


class Chunk:
    def __init__(self, meta, index):
        in_trunk = index < TRUNK_CHUNKS
        beyond = jnp.maximum(index - TRUNK_CHUNKS, 0)
        self.in_trunk = in_trunk
        self.segment = jnp.where(in_trunk, 0, 1 + beyond // 2)
        self.first = jnp.where(in_trunk, index * CHUNK, (beyond % 2) * CHUNK)
        length = meta[self.segment]
        trunk_length = meta[0]
        self.trunk_length = trunk_length
        self.length = length
        self.is_leaf = self.segment >= 5
        self.parent = meta[13 + jnp.clip(self.segment - 5, 0, 7)]
        parent_length = meta[1 + self.parent]
        self.start = jnp.where(
            in_trunk,
            self.first,
            trunk_length + self.first + jnp.where(self.is_leaf, parent_length, 0),
        )
        self.count = jnp.clip(length - self.first, 0, CHUNK)
        self.end = self.start + self.count
        self.continues = jnp.where(in_trunk, index + 1 < TRUNK_CHUNKS, beyond % 2 == 0)


def trunk_reference(meta, place, rows):
    return jnp.minimum(meta[0], jnp.minimum(rows * (place + 1), TRUNK))


def power(rate, exponent, width):
    return jnp.exp(jnp.full((1, width), exponent.astype(F32), F32) * rate)


def column_power(rate, exponents):
    return jnp.exp(exponents.astype(F32) * rate)


def token_column(width=1):
    return lax.broadcasted_iota(jnp.int32, (CHUNK, width), 0)


def decay_matrix(rate):
    t = lax.broadcasted_iota(jnp.int32, (CHUNK, CHUNK), 0)
    u = lax.broadcasted_iota(jnp.int32, (CHUNK, CHUNK), 1)
    return jnp.where(u <= t, jnp.exp((t - u).astype(F32) * rate) * SCALE, 0.0)


def valid_decay(decay, count):
    u = lax.broadcasted_iota(jnp.int32, (1, CHUNK), 1)
    return decay[...] * jnp.where(u < count, 1.0, 0.0)


def key_decay(rate, count):
    j = token_column()
    return jnp.where(j < count, column_power(rate, jnp.maximum(count - j, 0)), 0.0)


def export_terms(meta, chunk, local, chunks, place, slot, rows):
    if slot == 0:
        is_shift = ((place == 4) | (place == 6)) & (local == chunks - 1)
        exponent = jnp.where(
            chunk.in_trunk,
            jnp.maximum(trunk_reference(meta, place, rows) - chunk.end, 0),
            0,
        )
        return chunk.in_trunk | is_shift, exponent
    wanted = (place == 3) | (place == 4)
    mine = (chunk.segment % 2 == 1) if slot == 1 else (chunk.segment % 2 == 0)
    is_branch = (chunk.segment >= 1) & (chunk.segment < 5)
    exponent = jnp.where(is_branch, jnp.maximum(chunk.length - chunk.first - chunk.count, 0), 0)
    return wanted & mine & is_branch, exponent


def import_terms(meta, chunk, place, slot, rows):
    if slot < 4:
        sees = jnp.logical_not(chunk.in_trunk) | (place > slot)
        if slot < 3:
            sees = sees & (place < 4)
        return sees, jnp.maximum(chunk.start - trunk_reference(meta, jnp.int32(slot), rows), 0)
    sees = chunk.is_leaf & (chunk.parent == slot - 4)
    return sees, chunk.first


def shift_in(meta, place, chunks):
    previous = Chunk(meta, jnp.maximum(place * chunks - 1, 0))
    return (place == 5) | (place == 7), CHUNK - previous.count


def retain_kernel(
    rows, chunks, meta, rates, query, key, value, wide, weight, shared, shifted, gain, bias,
    gate_out, gated_out, normal_out, inverse_out, state_out, running, total, decay,
):
    local = pl.program_id(1)
    rate = rates[pl.program_id(0)]
    place = meta[21]
    chunk = Chunk(meta, place * chunks + local)

    @pl.when(local == 0)
    def _():
        decay[...] = decay_matrix(rate)
        running[...] = jnp.zeros_like(running)
        on, exponent = shift_in(meta, place, chunks)

        @pl.when(on)
        def _():
            running[...] = shifted[0].astype(F32) * power(rate, exponent, HV)

    incoming = running[...]
    total[...] = incoming
    for slot in range(SLOTS):
        on, exponent = import_terms(meta, chunk, place, slot, rows)

        @pl.when(on)
        def _():
            total[...] += shared[slot, 0].astype(F32) * power(rate, exponent, HV)

    state = total[...].astype(BF16)
    state_out[0, 0] = state

    q, k, v = query[...], key[...], value[...]
    scores = (mm_nt(q, k) * valid_decay(decay, chunk.count)).astype(BF16)
    own = token_column()
    reach = column_power(rate, own) * SCALE
    retained = mm(scores, v) + mm(q, state) * reach

    j = token_column()
    ahead = jnp.where(j < chunk.count, column_power(rate, CHUNK - j), 0.0)
    fresh = mm_tn((k.astype(F32) * ahead).astype(BF16), v)
    keep = jnp.where(chunk.continues, 1.0, 0.0)
    running[...] = (incoming * power(rate, jnp.int32(CHUNK), HV) + fresh) * keep

    average = jnp.mean(retained, axis=1, keepdims=True)
    centred = retained - average
    inverse = lax.rsqrt(jnp.mean(centred * centred, axis=1, keepdims=True) + EPSILON)
    normal = centred * inverse
    gate_value = mm(wide[...], weight[...])
    gate_out[...] = gate_value
    gated = (normal * gain[...] + bias[...]) * (gate_value / (1.0 + jnp.exp(-gate_value)))
    gated_out[...] = gated.astype(BF16)
    normal_out[...] = normal.astype(BF16)
    inverse_out[0] = jnp.broadcast_to(inverse, (CHUNK, 128))


def retain(meta, rates, query, key, value, inputs, weight, shared, shifted, gain, bias):
    array, _, number = weight
    rows = key.shape[0]
    heads = key.shape[1] // QK
    chunks = rows // CHUNK
    wide = pl.BlockSpec((CHUNK, HV), lambda h, c: (c, h))
    narrow = pl.BlockSpec((CHUNK, QK), lambda h, c: (c, h))
    vector = pl.BlockSpec((1, HV), lambda h, c: (0, h))
    return pl.pallas_call(
        functools.partial(retain_kernel, rows, chunks),
        grid=(heads, chunks),
        in_specs=[
            smem(), smem(), narrow, narrow, wide,
            pl.BlockSpec((CHUNK, D), lambda h, c: (c, 0)),
            pl.BlockSpec((D, HV), lambda h, c: (0, number * heads + h)),
            pl.BlockSpec((SLOTS, 1, QK, HV), lambda h, c: (0, h, 0, 0)),
            pl.BlockSpec((1, QK, HV), lambda h, c: (h, 0, 0)),
            vector, vector,
        ],
        out_specs=[
            wide, wide, wide,
            pl.BlockSpec((1, CHUNK, 128), lambda h, c: (h, c, 0)),
            pl.BlockSpec((1, 1, QK, HV), lambda h, c: (h, c, 0, 0)),
        ],
        out_shape=[
            jax.ShapeDtypeStruct((rows, heads * HV), F32),
            jax.ShapeDtypeStruct((rows, heads * HV), BF16),
            jax.ShapeDtypeStruct((rows, heads * HV), BF16),
            jax.ShapeDtypeStruct((heads, rows, 128), F32),
            jax.ShapeDtypeStruct((heads, chunks, QK, HV), BF16),
        ],
        scratch_shapes=[
            pltpu.VMEM((QK, HV), F32), pltpu.VMEM((QK, HV), F32), pltpu.VMEM((CHUNK, CHUNK), F32)
        ],
        compiler_params=params(("arbitrary", "arbitrary")),
        name="retention_forward",
        cost_estimate=pl.CostEstimate(
            flops=2 * rows * heads * (CHUNK * 768 + 2 * QK * HV + D * HV),
            bytes_accessed=rows * heads * 8192,
            transcendentals=rows * heads * 768,
        ),
    )(meta, rates, query, key, value, inputs, array, shared, shifted, gain[None, :], bias[None, :])


def gate_back_kernel(
    rows, chunks, meta, rates, wide, weight, gate, normal_in, inverse_in, query, gain, bias,
    gate_out, retained_out, gain_out, bias_out, exports, first_out, acc,
):
    local = pl.program_id(1)
    rate = rates[pl.program_id(0)]
    place = meta[21]
    chunk = Chunk(meta, place * chunks + local)
    grad_gated = mm(wide[...], weight[...])
    gate_value = gate[...].astype(F32)
    normal = normal_in[...].astype(F32)
    sigmoid = 1.0 / (1.0 + jnp.exp(-gate_value))
    normed = normal * gain[...] + bias[...]
    grad_gate = grad_gated * normed * (sigmoid * (1.0 + gate_value * (1.0 - sigmoid)))
    gate_out[...] = grad_gate.astype(BF16)
    grad_normed = grad_gated * (gate_value * sigmoid)

    @pl.when(local == 0)
    def _():
        gain_out[...] = jnp.zeros_like(gain_out)
        bias_out[...] = jnp.zeros_like(bias_out)
        acc[...] = jnp.zeros_like(acc)

    gain_out[...] += jnp.sum(grad_normed * normal, axis=0, keepdims=True)
    bias_out[...] += jnp.sum(grad_normed, axis=0, keepdims=True)
    scaled = grad_normed * gain[...]
    grad = inverse_in[0][:, :1] * (
        scaled
        - jnp.mean(scaled, axis=1, keepdims=True)
        - normal * jnp.mean(scaled * normal, axis=1, keepdims=True)
    )
    grad = grad.astype(BF16)
    retained_out[...] = grad
    reach = column_power(rate, token_column()) * SCALE
    state = mm_tn((query[...].astype(F32) * reach).astype(BF16), grad)
    for slot in range(SLOTS):
        on, exponent = import_terms(meta, chunk, place, slot, rows)

        @pl.when(on)
        def _():
            acc[slot] += state * power(rate, exponent, HV)

    @pl.when(local == 0)
    def _():
        on, exponent = shift_in(meta, place, chunks)
        scale = jnp.where(on, power(rate, exponent, HV), 0.0)
        first_out[0] = (state * scale).astype(BF16)

    @pl.when(local == chunks - 1)
    def _():
        exports[:, 0] = acc[...].astype(BF16)


def gate_back(meta, rates, wide, weight, gate, normal, inverse, query, gain, bias):
    array, width, number = weight
    first = number * (width // HV)
    rows = query.shape[0]
    heads = query.shape[1] // QK
    chunks = rows // CHUNK
    block = pl.BlockSpec((CHUNK, HV), lambda h, c: (c, h))
    vector = pl.BlockSpec((1, HV), lambda h, c: (0, h))
    return pl.pallas_call(
        functools.partial(gate_back_kernel, rows, chunks),
        grid=(heads, chunks),
        in_specs=[
            smem(), smem(),
            pl.BlockSpec((CHUNK, D), lambda h, c: (c, 0)),
            pl.BlockSpec((D, HV), lambda h, c: (0, first + h)),
            block, block,
            pl.BlockSpec((1, CHUNK, 128), lambda h, c: (h, c, 0)),
            pl.BlockSpec((CHUNK, QK), lambda h, c: (c, h)),
            vector, vector,
        ],
        out_specs=[
            block, block, vector, vector,
            pl.BlockSpec((SLOTS, 1, QK, HV), lambda h, c: (0, h, 0, 0)),
            pl.BlockSpec((1, QK, HV), lambda h, c: (h, 0, 0)),
        ],
        out_shape=[
            jax.ShapeDtypeStruct((rows, heads * HV), BF16),
            jax.ShapeDtypeStruct((rows, heads * HV), BF16),
            jax.ShapeDtypeStruct((1, heads * HV), F32),
            jax.ShapeDtypeStruct((1, heads * HV), F32),
            jax.ShapeDtypeStruct((SLOTS, heads, QK, HV), BF16),
            jax.ShapeDtypeStruct((heads, QK, HV), BF16),
        ],
        scratch_shapes=[pltpu.VMEM((SLOTS, QK, HV), F32)],
        compiler_params=params(("arbitrary", "arbitrary")),
        name="gate_backward",
        cost_estimate=pl.CostEstimate(
            flops=2 * rows * heads * HV * (D + QK),
            bytes_accessed=rows * heads * 12288,
            transcendentals=rows * heads * HV,
        ),
    )(meta, rates, wide, array, gate, normal, inverse, query, gain[None, :], bias[None, :])


def retain_back_kernel(
    rows, chunks, meta, rates, query, key, value, grad, state_in, cosine, sine, own0, own1, own2,
    query_out, key_out, value_out, running, total_ref, decay_ref,
):
    step = pl.program_id(1)
    local = chunks - 1 - step
    rate = rates[pl.program_id(0)]
    place = meta[21]
    chunk = Chunk(meta, place * chunks + local)
    before = Chunk(meta, jnp.maximum(place * chunks + local - 1, 0))

    @pl.when(step == 0)
    def _():
        decay_ref[...] = decay_matrix(rate)
        running[...] = jnp.zeros_like(running)

    later = running[...]
    total_ref[...] = later
    for slot, ref in ((0, own0), (1, own1), (2, own2)):
        on, exponent = export_terms(meta, chunk, local, chunks, place, slot, rows)

        @pl.when(on)
        def _():
            total_ref[...] += ref[0].astype(F32) * power(rate, exponent, HV)

    total = total_ref[...].astype(BF16)

    q, k, v, g = query[...], key[...], value[...], grad[...]
    decay = valid_decay(decay_ref, chunk.count)
    scores = (mm_nt(q, k) * decay).astype(BF16)
    slopes = (mm_nt(g, v) * decay).astype(BF16)
    reach = column_power(rate, token_column()) * SCALE
    toward = key_decay(rate, chunk.count)
    grad_query = mm(slopes, k) + mm_nt(g, state_in[0, 0]) * reach
    grad_key = mm_tn(slopes, q) + mm_nt(v, total) * toward
    grad_value = mm_tn(scores, g) + mm(k, total) * toward
    value_out[...] = grad_value.astype(BF16)
    cos, sin = cosine[...], sine[...]
    half = QK // 2
    for out, val in ((query_out, grad_query), (key_out, grad_key)):
        a, b = val[:, :half], val[:, half:]
        out[:, :half] = (a * cos + b * sin).astype(BF16)
        out[:, half:] = (b * cos - a * sin).astype(BF16)

    fresh = mm_tn((q.astype(F32) * reach).astype(BF16), g)
    carried = fresh + later * power(rate, chunk.count, HV)
    keep = jnp.where((local > 0) & before.continues, 1.0, 0.0)
    running[...] = carried * power(rate, CHUNK - before.count, HV) * keep


def retain_back(meta, rates, query, key, value, grad, states, cosine, sine, own):
    rows = query.shape[0]
    heads = query.shape[1] // QK
    chunks = rows // CHUNK
    last = chunks - 1
    wide = pl.BlockSpec((CHUNK, HV), lambda h, s: (last - s, h))
    narrow = pl.BlockSpec((CHUNK, QK), lambda h, s: (last - s, h))
    table = pl.BlockSpec((CHUNK, QK // 2), lambda h, s: (last - s, 0))
    state = pl.BlockSpec((1, QK, HV), lambda h, s: (h, 0, 0))
    return pl.pallas_call(
        functools.partial(retain_back_kernel, rows, chunks),
        grid=(heads, chunks),
        in_specs=[
            smem(), smem(), narrow, narrow, wide, wide,
            pl.BlockSpec((1, 1, QK, HV), lambda h, s: (h, last - s, 0, 0)),
            table, table, state, state, state,
        ],
        out_specs=[narrow, narrow, wide],
        out_shape=[
            jax.ShapeDtypeStruct((rows, heads * QK), BF16),
            jax.ShapeDtypeStruct((rows, heads * QK), BF16),
            jax.ShapeDtypeStruct((rows, heads * HV), BF16),
        ],
        scratch_shapes=[
            pltpu.VMEM((QK, HV), F32), pltpu.VMEM((QK, HV), F32), pltpu.VMEM((CHUNK, CHUNK), F32)
        ],
        compiler_params=params(("arbitrary", "arbitrary")),
        name="retention_backward",
        cost_estimate=pl.CostEstimate(
            flops=2 * rows * heads * (CHUNK * 1792 + 4 * QK * HV),
            bytes_accessed=rows * heads * 6144,
            transcendentals=rows * heads * 256,
        ),
    )(meta, rates, query, key, value, grad, states, cosine, sine, *own)


def norm_kernel(values, gain, bias, out, average_out, inverse_out):
    x = values[...].astype(F32)
    average = jnp.mean(x, axis=1, keepdims=True)
    inverse = lax.rsqrt(jnp.mean(x * x, axis=1, keepdims=True) - average * average + EPSILON)
    out[...] = ((x - average) * inverse * gain[...] + bias[...]).astype(BF16)
    average_out[...] = jnp.broadcast_to(average, average_out.shape)
    inverse_out[...] = jnp.broadcast_to(inverse, inverse_out.shape)


def norm_wide(values, gain, bias):
    rows = values.shape[0]
    block = pl.BlockSpec((CHUNK, D), lambda i: (i, 0))
    vector = pl.BlockSpec((1, D), lambda i: (0, 0))
    stat = pl.BlockSpec((CHUNK, 128), lambda i: (i, 0))
    return pl.pallas_call(
        norm_kernel,
        grid=(rows // CHUNK,),
        in_specs=[block, vector, vector],
        out_specs=[block, stat, stat],
        out_shape=[
            jax.ShapeDtypeStruct((rows, D), BF16),
            jax.ShapeDtypeStruct((rows, 128), F32),
            jax.ShapeDtypeStruct((rows, 128), F32),
        ],
        compiler_params=params(("arbitrary",)),
        name="layer_norm",
        cost_estimate=pl.CostEstimate(
            flops=8 * rows * D, bytes_accessed=4 * rows * D, transcendentals=rows
        ),
    )(values, gain[None, :], bias[None, :])


def join_kernel(row, own, from_x, from_y, far_a, far_b, *refs, norm):
    block = own.shape[1]
    second = pl.program_id(0) >= pl.num_programs(0) // 2
    spots = [
        pl.ds(pl.multiple_of((row[0] ^ flip) * block, 128), block) for flip in range(4)
    ]
    pieces = [own[...], from_x[...], from_y[...], jnp.where(second, far_b[...], far_a[...])]
    if not norm:
        for spot, piece in zip(spots, pieces):
            refs[0][:, spot] = piece
        return
    gain, bias, out, average_out, inverse_out = refs
    pieces = [piece.astype(F32) for piece in pieces]
    average = sum(jnp.sum(piece, axis=1, keepdims=True) for piece in pieces) / D
    squares = sum(jnp.sum(piece * piece, axis=1, keepdims=True) for piece in pieces) / D
    inverse = lax.rsqrt(squares - average * average + EPSILON)
    for spot, piece in zip(spots, pieces):
        out[:, spot] = ((piece - average) * inverse * gain[:, spot] + bias[:, spot]).astype(BF16)
    average_out[...] = jnp.broadcast_to(average, average_out.shape)
    inverse_out[...] = jnp.broadcast_to(inverse, inverse_out.shape)


def join(pieces, row, gain=None, bias=None):
    norm = gain is not None
    if not isinstance(pieces, tuple):
        return norm_wide(pieces, gain, bias) if norm else pieces
    rows, block = pieces[0].shape
    steps = 4
    tile = rows // steps
    piece = pl.BlockSpec((tile, block), lambda i, r: (i, 0))
    far_a = pl.BlockSpec((tile, block), lambda i, r: (jnp.minimum(i, steps // 2 - 1), 0))
    far_b = pl.BlockSpec((tile, block), lambda i, r: (jnp.maximum(i - steps // 2, 0), 0))
    vector = pl.BlockSpec((1, D), lambda i, r: (0, 0))
    wide = pl.BlockSpec((tile, D), lambda i, r: (i, 0))
    stat = pl.BlockSpec((tile, 128), lambda i, r: (i, 0))
    wide_shape = jax.ShapeDtypeStruct((rows, D), BF16)
    stat_shape = jax.ShapeDtypeStruct((rows, 128), F32)
    return pl.pallas_call(
        functools.partial(join_kernel, norm=norm),
        grid_spec=pltpu.PrefetchScalarGridSpec(
            num_scalar_prefetch=1,
            grid=(steps,),
            in_specs=[piece] * 3 + [far_a, far_b] + ([vector] * 2 if norm else []),
            out_specs=[wide, stat, stat] if norm else wide,
        ),
        out_shape=[wide_shape, stat_shape, stat_shape] if norm else wide_shape,
        compiler_params=params(("arbitrary",)),
        name="join_norm" if norm else "join",
        cost_estimate=pl.CostEstimate(
            flops=8 * rows * D, bytes_accessed=4 * rows * D, transcendentals=0
        ),
    )(row, *pieces, *((gain[None, :], bias[None, :]) if norm else ()))


def project_kernel(
    heads, rows, chunks, meta, rates, values, weight, cosine, sine,
    query_out, key_out, value_out, exports, acc,
):
    local = pl.program_id(0)
    place = meta[21]
    chunk = Chunk(meta, place * chunks + local)
    raw = mm(values[...], weight[...])
    cos, sin = cosine[...], sine[...]
    half = QK // 2
    for part, out in ((0, query_out), (1, key_out)):
        for head in range(heads):
            first = (part * heads + head) * QK
            a, b = raw[:, first : first + half], raw[:, first + half : first + QK]
            out[:, head * QK : head * QK + half] = (a * cos - b * sin).astype(BF16)
            out[:, head * QK + half : (head + 1) * QK] = (b * cos + a * sin).astype(BF16)
    value_out[...] = raw[:, 2 * heads * QK :].astype(BF16)

    @pl.when(local == 0)
    def _():
        acc[...] = jnp.zeros_like(acc)

    for head in range(heads):
        rate = rates[head]
        key = key_out[:, head * QK : (head + 1) * QK].astype(F32)
        weighted = (key * key_decay(rate, chunk.count)).astype(BF16)
        state = mm_tn(weighted, value_out[:, head * HV : (head + 1) * HV])
        for slot in range(3):
            on, exponent = export_terms(meta, chunk, local, chunks, place, slot, rows)

            @pl.when(on)
            def _():
                acc[slot, head] += state * power(rate, exponent, HV)

    @pl.when(local == chunks - 1)
    def _():
        exports[...] = acc[...].astype(BF16)


def project(meta, rates, values, weight, cosine, sine):
    rows, width = values.shape[0], weight.shape[1]
    heads = width // (2 * QK + HV)
    chunks = rows // CHUNK
    table = pl.BlockSpec((CHUNK, QK // 2), lambda i: (i, 0))
    widths = (heads * QK, heads * QK, heads * HV)
    states = (3, heads, QK, HV)
    return pl.pallas_call(
        functools.partial(project_kernel, heads, rows, chunks),
        grid=(chunks,),
        in_specs=[
            smem(), smem(),
            pl.BlockSpec((CHUNK, D), lambda i: (i, 0)),
            pl.BlockSpec((D, width), lambda i: (0, 0)),
            table, table,
        ],
        out_specs=[pl.BlockSpec((CHUNK, w), lambda i: (i, 0)) for w in widths]
        + [pl.BlockSpec(states, lambda i: (0, 0, 0, 0))],
        out_shape=[jax.ShapeDtypeStruct((rows, w), BF16) for w in widths]
        + [jax.ShapeDtypeStruct(states, BF16)],
        scratch_shapes=[pltpu.VMEM(states, F32)],
        compiler_params=params(("arbitrary",)),
        name="project",
        cost_estimate=pl.CostEstimate(
            flops=2 * rows * D * width, bytes_accessed=2 * (rows + width) * D, transcendentals=0
        ),
    )(meta, rates, values, weight, cosine, sine)


def matmul_kernel(values, weight, out):
    out[...] = mm(values[...], weight[...]).astype(out.dtype)


def matmul(values, weight, kind):
    array, width, number = weight
    rows = values.shape[0]
    return pl.pallas_call(
        matmul_kernel,
        grid=(rows // CHUNK,),
        in_specs=[
            pl.BlockSpec((CHUNK, D), lambda i: (i, 0)),
            pl.BlockSpec((D, width), lambda i: (0, number)),
        ],
        out_specs=pl.BlockSpec((CHUNK, width), lambda i: (i, 0)),
        out_shape=jax.ShapeDtypeStruct((rows, width), kind),
        compiler_params=params(("arbitrary",)),
        name="matmul",
        cost_estimate=pl.CostEstimate(
            flops=2 * rows * D * width, bytes_accessed=2 * (rows + width) * D, transcendentals=0
        ),
    )(values, array)


def weight_grad_kernel(spans, *refs):
    count = len(spans)
    lefts, rights, out = refs[:count], refs[count : 2 * count], refs[2 * count]
    tile = pl.program_id(0)
    for left, right, (first, last) in zip(lefts, rights, spans):

        @pl.when((tile >= first) & (tile < last))
        def _():
            height = 2 * GRAD_TILE

            def part(index, _):
                spot = pl.ds(pl.multiple_of(index * height, height), height)
                out[spot, :] = mm_tn(left[:, spot], right[...]).astype(BF16)
                return 0

            lax.fori_loop(0, left.shape[1] // height, part, 0)


def weight_grads(pairs):
    rows = pairs[0][0].shape[0]
    wide = min(right.shape[1] for _, right in pairs)
    tall = 1024
    steps = D // tall
    spans, first = [], 0
    for _, right in pairs:
        spans.append((first, first + right.shape[1] // wide))
        first = spans[-1][1]

    def left_spec(span):
        return pl.BlockSpec(
            (rows, tall),
            lambda n, m: (
                0, jnp.where(n < span[0], 0, jnp.where(n < span[1], m, steps - 1)),
            ),
        )

    def right_spec(span):
        return pl.BlockSpec(
            (rows, wide), lambda n, m: (0, jnp.clip(n - span[0], 0, span[1] - span[0] - 1))
        )

    return pl.pallas_call(
        functools.partial(weight_grad_kernel, tuple(spans)),
        grid=(first, steps),
        in_specs=[left_spec(span) for span in spans] + [right_spec(span) for span in spans],
        out_specs=pl.BlockSpec((tall, wide), lambda n, m: (m, n)),
        out_shape=jax.ShapeDtypeStruct((D, first * wide), BF16),
        compiler_params=params(("arbitrary", "arbitrary")),
        name="weight_grads",
        cost_estimate=pl.CostEstimate(
            flops=2 * rows * D * first * wide,
            bytes_accessed=2 * D * first * wide + 4 * rows * D,
            transcendentals=0,
        ),
    )(*[left for left, _ in pairs], *[right for _, right in pairs])


def paired_grad_kernel(spans, tiles, steps, *refs):
    count = len(spans)
    lefts, rights = refs[:count], refs[count : 2 * count]
    out, made, received, send_sem, recv_sem = refs[2 * count :]
    step = pl.program_id(0)
    core = lax.axis_index("col") % 2
    partner = lax.axis_index("col") + 1 - 2 * core

    def copy(index):
        return pltpu.make_async_remote_copy(
            src_ref=made.at[index, :, 1 - core],
            dst_ref=received.at[index],
            send_sem=send_sem.at[index],
            recv_sem=recv_sem.at[index],
            device_id={"col": partner},
            device_id_type=pl.DeviceIdType.MESH,
        )

    @pl.when(step == 0)
    def _():
        barrier = pltpu.get_barrier_semaphore()
        pl.semaphore_signal(
            barrier, inc=1, device_id={"col": partner}, device_id_type=pl.DeviceIdType.MESH
        )
        pl.semaphore_wait(barrier, 1)

    for left, right, (first, last) in zip(lefts, rights, spans):

        @pl.when((step >= first * steps) & (step < last * steps))
        def _():
            total = mm_tn(left[...], right[...]).astype(BF16)
            made[step] = total.reshape(made.shape[1:])

    @pl.when(step < tiles)
    def _():
        copy(step).start()

    @pl.when(step > 0)
    def _():
        index = step - 1
        copy(index).wait()
        out[...] = (made[index, :, core].astype(F32) + received[index].astype(F32)).astype(BF16)


def paired_grads(pairs, number):
    rows = pairs[0][0].shape[0]
    wide = min(right.shape[1] for _, right in pairs)
    wide = min(wide, 512)
    tall = 1024
    steps = D // tall
    block = D // SLOTS
    depth = tall // block // 2
    spans, first = [], 0
    for _, right in pairs:
        spans.append((first, first + right.shape[1] // wide))
        first = spans[-1][1]
    tiles = first * steps

    def left_spec(span):
        def index(s):
            n, m = s // steps, s % steps
            return 0, jnp.where(n < span[0], 0, jnp.where(n < span[1], m, steps - 1))

        return pl.BlockSpec((rows, tall), index)

    def right_spec(span):
        def index(s):
            return 0, jnp.clip(s // steps - span[0], 0, span[1] - span[0] - 1)

        return pl.BlockSpec((rows, wide), index)

    def out_index(s):
        done = jnp.maximum(s - 1, 0)
        return done % steps, 0, done // steps

    result = pl.pallas_call(
        functools.partial(paired_grad_kernel, tuple(spans), tiles, steps),
        grid=(tiles + 1,),
        in_specs=[left_spec(span) for span in spans] + [right_spec(span) for span in spans],
        out_specs=pl.BlockSpec((depth, block, wide), out_index),
        out_shape=jax.ShapeDtypeStruct((SLOTS // 2, block, first * wide), BF16),
        scratch_shapes=[
            pltpu.VMEM((tiles, depth, 2, block, wide), BF16),
            pltpu.VMEM((tiles, depth, block, wide), BF16),
            pltpu.SemaphoreType.DMA((tiles,)),
            pltpu.SemaphoreType.DMA((tiles,)),
        ],
        compiler_params=pltpu.CompilerParams(
            dimension_semantics=("arbitrary",),
            collective_id=number,
            has_side_effects=True,
            vmem_limit_bytes=60 * 1024 * 1024,
        ),
        name="paired_grads",
        cost_estimate=pl.CostEstimate(
            flops=2 * rows * D * first * wide,
            bytes_accessed=2 * D * first * wide + 4 * rows * D,
            transcendentals=0,
        ),
    )(*[left for left, _ in pairs], *[right for _, right in pairs])
    return result


def column_grads(pairs, number):
    if lax.axis_size("col") != SLOTS:
        return weight_grads(pairs)
    return paired_grads(pairs, number)


def norm_pieces(row, own, from_x, from_y, far_a, far_b, gain, bias, out, average_out, inverse_out):
    block = own.shape[1]
    second = pl.program_id(0) >= pl.num_programs(0) // 2
    far = jnp.where(second, far_b[...], far_a[...])
    pieces = [piece.astype(F32) for piece in (own[...], from_x[...], from_y[...], far)]
    average = sum(jnp.sum(piece, axis=1, keepdims=True) for piece in pieces) / D
    squares = sum(jnp.sum(piece * piece, axis=1, keepdims=True) for piece in pieces) / D
    inverse = lax.rsqrt(squares - average * average + EPSILON)
    for flip, piece in enumerate(pieces):
        spot = pl.ds(pl.multiple_of((row[0] ^ flip) * block, 128), block)
        out[:, spot] = ((piece - average) * inverse * gain[:, spot] + bias[:, spot]).astype(BF16)
    average_out[...] = jnp.broadcast_to(average, average_out.shape)
    inverse_out[...] = jnp.broadcast_to(inverse, inverse_out.shape)


def up_kernel(row, *refs, joined):
    if joined:
        pieces, gain, norm_bias = refs[:5], refs[5], refs[6]
        weight, bias, grad_hidden, scales, second_out, average_out, inverse_out = refs[7:14]
        hidden_out, grad_out, bias_out, sums_out, moved = refs[14:]
        norm_pieces(row, *pieces, gain, norm_bias, second_out, average_out, inverse_out)
        values = second_out
    else:
        values, weight, bias, grad_hidden, scales = refs[:5]
        hidden_out, grad_out, bias_out, sums_out, moved = refs[5:]
    before = mm(values[...], weight[...]) + bias[...]
    phi = 0.5 * (1.0 + lax.erf(before * (0.5**0.5)))
    hidden_out[...] = (before * phi).astype(BF16)
    density = jnp.exp(-0.5 * before * before) * 0.3989422804014327
    grad = (grad_hidden[...].astype(F32) * (phi + before * density)).astype(BF16)
    grad_out[...] = grad

    @pl.when(pl.program_id(0) == 0)
    def _():
        bias_out[...] = jnp.zeros_like(bias_out)
        parts = mm(scales[...], weight[...])
        moved[0:1] = parts[0:1] + parts[1:2]
        moved[1:2] = parts[2:3] + parts[3:4]

    wide_grad = grad.astype(F32)
    bias_out[...] += jnp.sum(wide_grad, axis=0, keepdims=True)
    plain = jnp.sum(wide_grad * moved[0:1], axis=1, keepdims=True)
    crossed = jnp.sum(wide_grad * (before - bias[...] - moved[1:2]), axis=1, keepdims=True)
    lane = lax.broadcasted_iota(jnp.int32, sums_out.shape, 1)
    sums_out[...] = jnp.where(lane == 0, plain, crossed)


def feed_up(pieces, row, gain, norm_bias, weight, bias, grad_hidden):
    array, width, number = weight
    joined = isinstance(pieces, tuple)
    rows = grad_hidden.shape[0]
    steps = 4
    tile = rows // steps
    block = pl.BlockSpec((tile, width), lambda i, r: (i, 0))
    vector = pl.BlockSpec((1, width), lambda i, r: (0, 0))
    wide = pl.BlockSpec((tile, D), lambda i, r: (i, 0))
    stat = pl.BlockSpec((tile, 128), lambda i, r: (i, 0))
    gains = pl.BlockSpec((1, D), lambda i, r: (0, 0))
    if joined:
        piece = pl.BlockSpec((tile, pieces[0].shape[1]), lambda i, r: (i, 0))
        far_a = pl.BlockSpec(
            (tile, pieces[0].shape[1]), lambda i, r: (jnp.minimum(i, steps // 2 - 1), 0)
        )
        far_b = pl.BlockSpec(
            (tile, pieces[0].shape[1]), lambda i, r: (jnp.maximum(i - steps // 2, 0), 0)
        )
        inputs = list(pieces) + [gain[None, :], norm_bias[None, :]]
        in_specs = [piece] * 3 + [far_a, far_b, gains, gains]
        early_specs = [wide, stat, stat]
        early_shapes = [
            jax.ShapeDtypeStruct((rows, D), BF16),
            jax.ShapeDtypeStruct((rows, 128), F32),
            jax.ShapeDtypeStruct((rows, 128), F32),
        ]
        normed = []
    else:
        normed = list(norm_wide(pieces, gain, norm_bias))
        inputs, in_specs, early_specs, early_shapes = [normed[0]], [wide], [], []
    scales = jnp.stack([gain, norm_bias])
    high = lax.reduce_precision(scales, 8, 7)
    low = scales - high
    rest = jnp.zeros((4, D), F32)
    scales = jnp.concatenate([high[:1], low[:1], high[1:], low[1:], rest], axis=0).astype(BF16)
    outs = pl.pallas_call(
        functools.partial(up_kernel, joined=joined),
        grid_spec=pltpu.PrefetchScalarGridSpec(
            num_scalar_prefetch=1,
            grid=(steps,),
            in_specs=in_specs
            + [
                pl.BlockSpec((D, width), lambda i, r: (0, number)), vector, block,
                pl.BlockSpec((8, D), lambda i, r: (0, 0)),
            ],
            out_specs=early_specs + [block, block, vector, stat],
            scratch_shapes=[pltpu.VMEM((8, width), F32)],
        ),
        out_shape=early_shapes
        + [
            jax.ShapeDtypeStruct((rows, width), BF16),
            jax.ShapeDtypeStruct((rows, width), BF16),
            jax.ShapeDtypeStruct((1, width), F32),
            jax.ShapeDtypeStruct((rows, 128), F32),
        ],
        compiler_params=params(("arbitrary",)),
        name="feed_up",
        cost_estimate=pl.CostEstimate(
            flops=2 * rows * D * width,
            bytes_accessed=2 * (2 * rows + width) * D + 8 * rows * width,
            transcendentals=2 * rows * width,
        ),
    )(row, *inputs, array, bias[None, :], grad_hidden, scales)
    return normed + list(outs)


PARTIAL_FLIP = (1, 3, 2, 3, 2, 1, 0, 0)
PARTIAL_HALF = (0, 0, 1, 1, 0, 1, 0, 1)


def table_lookup(table, step):
    result = jnp.int32(table[0])
    for index in range(1, len(table)):
        result = jnp.where(step == index, table[index], result)
    return result


def partial_kernel(count, row, *refs):
    values, weights = refs[:count], refs[count : 2 * count]
    outs = refs[2 * count :]
    step = pl.program_id(0)
    strip = values[0].shape[0] // 2

    def part(number, _):
        spot = pl.ds(pl.multiple_of(number * strip, strip), strip)
        total = mm_nt(values[0][spot, :], weights[0][...])
        for x, w in zip(values[1:], weights[1:]):
            total = total + mm_nt(x[spot, :], w[...])
        for index, out in enumerate(outs):

            @pl.when(step // 2 == index)
            def _():
                out[0, spot, :] = total.astype(out.dtype)

        return 0

    lax.fori_loop(0, 2, part, 0)


def partial_blocks(values, weights, row, first, kinds):
    rows = values[0].shape[0]
    half, block = rows // 2, D // 4
    count = len(values)
    flips = PARTIAL_FLIP[2 * first : 2 * (first + len(kinds))]
    halves = PARTIAL_HALF[2 * first : 2 * (first + len(kinds))]

    def value_spec(x):
        return pl.BlockSpec((half, x.shape[1]), lambda s, r: (table_lookup(halves, s), 0))

    def weight_spec(w):
        return pl.BlockSpec((block, w[1]), lambda s, r: (r[0] ^ table_lookup(flips, s), w[2]))

    def out_spec(index):
        return pl.BlockSpec((1, half, block), lambda s, r: (jnp.clip(s - 2 * index, 0, 1), 0, 0))

    depth = sum(x.shape[1] for x in values)
    return pl.pallas_call(
        functools.partial(partial_kernel, count),
        grid_spec=pltpu.PrefetchScalarGridSpec(
            num_scalar_prefetch=1,
            grid=(2 * len(kinds),),
            in_specs=[value_spec(x) for x in values] + [weight_spec(w) for w in weights],
            out_specs=[out_spec(index) for index in range(len(kinds))],
        ),
        out_shape=[jax.ShapeDtypeStruct((2, half, block), kind) for kind in kinds],
        compiler_params=params(("arbitrary",)),
        name="partial_blocks",
        cost_estimate=pl.CostEstimate(
            flops=rows * block * depth * 2 * len(kinds),
            bytes_accessed=(rows + D) * depth * 2 + 4 * rows * block * len(kinds),
            transcendentals=0,
        ),
    )(row, *values, *[w[0] for w in weights])


def permute_row(value, pairs):
    return lax.ppermute(value, "row", pairs)


def in_order(*values):
    return lax.optimization_barrier(values)


def reduce_row_start(values, weights, row):
    if lax.axis_size("row") != 4:
        columns = [array[:, n * width : (n + 1) * width] for array, width, n in weights]
        return sum(mm_nt(x, w) for x, w in zip(values, columns)).astype(BF16)
    return tuple(partial_blocks(values, weights, row, 0, (BF16, BF16)))


def reduce_row_finish(sends, values, weights, row, between=None, tied=None):
    if lax.axis_size("row") != 4:
        total = lax.psum_scatter(sends, "row", scatter_dimension=1, tiled=True).astype(F32)
        return total, between(tied) if between else None
    from_x = permute_row(sends[0], X_PAIRS)
    from_y = permute_row(sends[1], Y_PAIRS)
    keep, own = partial_blocks(values, weights, row, 2, (BF16, F32))
    extra = None
    if between is not None:
        if tied is not None:
            keep, own, tied = in_order(keep, own, tied)
        extra = between(tied)
        from_x, from_y, extra = in_order(from_x, from_y, extra)
    next_y = (keep[0].astype(F32) + from_x[1].astype(F32)).astype(BF16)
    next_x = (keep[1].astype(F32) + from_y[1].astype(F32)).astype(BF16)
    last_y = permute_row(next_y, Y_PAIRS)
    last_x = permute_row(next_x, X_PAIRS)
    first_half = own[0] + from_x[0].astype(F32) + last_y.astype(F32)
    second_half = own[1] + from_y[0].astype(F32) + last_x.astype(F32)
    return jnp.concatenate([first_half, second_half], axis=0), extra


def gather_row(value, between=None, later=None):
    if lax.axis_size("row") != 4:
        gathered = lax.all_gather(value, "row", axis=1, tiled=True)
        if later is not None:
            return gathered, later[0](later[1])
        return gathered, between() if between else None
    half = value.shape[0] // 2
    from_x = permute_row(value, X_PAIRS)
    from_y = permute_row(value, Y_PAIRS)
    extra = None
    if between is not None:
        extra = between()
        from_x, from_y, extra = in_order(from_x, from_y, extra)
    if later is not None:
        from_x, from_y, argument = in_order(from_x, from_y, later[1])
    far_a = permute_row(from_x[:half], Y_PAIRS)
    far_b = permute_row(from_y[half:], X_PAIRS)
    if later is not None:
        extra = later[0](argument)
        far_a, far_b, extra = in_order(far_a, far_b, extra)
    return (value, from_x, from_y, far_a, far_b), extra


def gather_row_small(value):
    if lax.axis_size("row") != 4:
        return lax.all_gather(value, "row", axis=1, tiled=True)
    row = lax.axis_index("row")
    pieces = jnp.stack(
        [value] + [permute_row(value, pairs) for pairs in (X_PAIRS, Y_PAIRS, D_PAIRS)]
    )
    ordered = [
        lax.dynamic_index_in_dim(pieces, row ^ place, 0, keepdims=False) for place in range(4)
    ]
    return jnp.concatenate(ordered, axis=1)


def sum_row_small(value):
    if lax.axis_size("row") != 4:
        return lax.psum(value, "row")
    first = value + permute_row(value, X_PAIRS)
    return first + permute_row(first, Y_PAIRS)


def sum_row_direct(value):
    if lax.axis_size("row") != 4:
        return lax.psum(value, "row")
    others = [permute_row(value, pairs) for pairs in (X_PAIRS, Y_PAIRS, D_PAIRS)]
    return value + others[0] + (others[1] + others[2])


def norm_backward(grad_out, normal, inverse, gain_vector, sums=None):
    scaled = grad_out * gain_vector
    if sums is None:
        sums = sum_row_small(jnp.stack([jnp.sum(scaled, axis=1), jnp.sum(scaled * normal, axis=1)]))
    means = sums / D
    grad_in = inverse * (scaled - means[0][:, None] - normal * means[1][:, None])
    return (grad_in, jnp.sum(grad_out * normal, axis=0), jnp.sum(grad_out, axis=0))


def gather_col(weight):
    return lax.all_gather(weight, "col", axis=0, tiled=True)


def scatter_col(grad):
    if grad.ndim == 2:
        return lax.psum_scatter(grad, "col", scatter_dimension=0, tiled=True).astype(F32)
    groups = [list(range(core, SLOTS, 2)) for core in range(2)]
    total = lax.psum_scatter(grad, "col", scatter_dimension=0, axis_index_groups=groups)
    return total.astype(F32)


class Exchange:
    def __init__(self, messages, send_sem, recv_sem):
        col = lax.axis_index("col")
        self.base = (col // SLOTS) * SLOTS
        self.place = col % SLOTS
        self.messages, self.send_sem, self.recv_sem = messages, send_sem, recv_sem

    def copy(self, index):
        _, target, source, destination = self.messages[index]
        return pltpu.make_async_remote_copy(
            src_ref=source,
            dst_ref=destination,
            send_sem=self.send_sem.at[index],
            recv_sem=self.recv_sem.at[index],
            device_id={"col": self.base + target},
            device_id_type=pl.DeviceIdType.MESH,
        )

    def greet(self):
        barrier = pltpu.get_barrier_semaphore()
        for step in range(1, SLOTS):
            other = self.base + (self.place + step) % SLOTS
            pl.semaphore_signal(
                barrier, inc=1, device_id={"col": other}, device_id_type=pl.DeviceIdType.MESH
            )
        pl.semaphore_wait(barrier, SLOTS - 1)

    def run(self, programs, drain=True):
        for place, program in enumerate(programs):
            if not program:
                continue

            @pl.when(self.place == place)
            def _():
                for action in program:
                    if callable(action):
                        action()
                    elif action >= 0:
                        self.copy(action).start()
                    else:
                        self.copy(~action).wait_recv()

        if drain:
            self.drain()

    def drain(self):
        for place in range(SLOTS):
            mine = [i for i, message in enumerate(self.messages) if message[0] == place]
            if mine:

                @pl.when(self.place == place)
                def _():
                    for index in mine:
                        self.copy(index).wait_send()


def scaled_add(meta, rates, target, terms, rows):
    heads = target.shape[0]
    strip = 64
    for head in range(heads):

        def add(index, _):
            spot = pl.ds(pl.multiple_of(index * strip, strip), strip)
            total = None
            for term in terms:
                if isinstance(term, tuple):
                    ref, slot = term
                    exponent = jnp.maximum(
                        trunk_reference(meta, jnp.int32(3), rows)
                        - trunk_reference(meta, jnp.int32(slot), rows),
                        0,
                    )
                    value = ref[head, spot, :].astype(F32) * power(rates[head], exponent, HV)
                else:
                    value = term[head, spot, :].astype(F32)
                total = value if total is None else total + value
            target[head, spot, :] = total.astype(BF16)
            return 0

        lax.fori_loop(0, QK // strip, add, 0)


def share_kernel(rows, meta, rates, ex, sh, shift, tot, send_sem, recv_sem):
    messages = [
        (0, 2, ex.at[0], sh.at[0]),
        (0, 1, ex.at[0], sh.at[0]),
        (1, 3, ex.at[0], sh.at[1]),
        (2, 3, ex.at[0], sh.at[2]),
        (2, 3, sh.at[0], sh.at[0]),
        (3, 2, sh.at[1], sh.at[1]),
        (3, 4, ex.at[1], sh.at[4]),
        (3, 5, ex.at[2], sh.at[5]),
        (3, 4, tot, sh.at[3]),
        (4, 5, ex.at[1], sh.at[6]),
        (4, 6, ex.at[1], sh.at[6]),
        (4, 5, ex.at[2], sh.at[7]),
        (5, 7, sh.at[7], sh.at[7]),
        (4, 5, sh.at[4], sh.at[4]),
        (4, 6, sh.at[4], sh.at[4]),
        (5, 4, sh.at[5], sh.at[5]),
        (5, 7, sh.at[5], sh.at[5]),
        (4, 5, sh.at[3], sh.at[3]),
        (4, 6, sh.at[3], sh.at[3]),
        (6, 7, sh.at[6], sh.at[6]),
        (6, 7, sh.at[4], sh.at[4]),
        (6, 7, sh.at[3], sh.at[3]),
        (7, 6, sh.at[7], sh.at[7]),
        (7, 6, sh.at[5], sh.at[5]),
        (4, 5, ex.at[0], shift),
        (6, 7, ex.at[0], shift),
    ]
    exchange = Exchange(messages, send_sem, recv_sem)

    def keep_trunk():
        sh[3] = ex[0]

    def total_trunk():
        terms = [(sh.at[slot], slot) for slot in range(3)] + [ex.at[0]]
        scaled_add(meta, rates, tot, terms, rows)

    def keep_branches():
        sh[6] = ex[1]
        sh[7] = ex[2]

    exchange.greet()
    exchange.run(
        [
            [0, 1],
            [2, ~1],
            [3, ~0, 4, ~5],
            [6, 7, keep_trunk, ~2, 5, ~4, ~3, total_trunk, 8],
            [10, 11, 9, 24, keep_branches, ~6, 14, 13, ~15, ~8, 18, 17],
            [~11, 12, ~7, 16, 15, ~9, ~24, ~13, ~17],
            [25, ~10, 19, ~14, 20, ~22, ~23, ~18, 21],
            [~12, 22, ~16, 23, ~19, ~20, ~25, ~21],
        ]
    )


def vmem():
    return pl.BlockSpec(memory_space=pltpu.VMEM)


def share_states(meta, rates, exports, rows):
    heads = exports.shape[1]
    state = (heads, QK, HV)
    return pl.pallas_call(
        functools.partial(share_kernel, rows),
        in_specs=[smem(), smem(), vmem()],
        out_specs=[vmem(), vmem()],
        out_shape=[
            jax.ShapeDtypeStruct((SLOTS,) + state, BF16),
            jax.ShapeDtypeStruct(state, BF16),
        ],
        scratch_shapes=[
            pltpu.VMEM(state, BF16),
            pltpu.SemaphoreType.DMA((26,)),
            pltpu.SemaphoreType.DMA((26,)),
        ],
        compiler_params=pltpu.CompilerParams(
            collective_id=1, has_side_effects=True, vmem_limit_bytes=40 * 1024 * 1024
        ),
        name="share_states",
        cost_estimate=pl.CostEstimate(
            flops=0, bytes_accessed=100 * 1024 * 1024, transcendentals=0
        ),
    )(meta, rates, exports)


def return_kernel(
    rows, meta, rates, y, first, left, right, own0, own1, own2, grads, rx, tx, send_sem, recv_sem
):
    messages = [
        (7, 6, y.at[3], rx.at[0]),
        (7, 6, y.at[4], rx.at[1]),
        (7, 6, y.at[5], rx.at[2]),
        (6, 7, y.at[6], rx.at[0]),
        (6, 7, y.at[7], rx.at[1]),
        (7, 5, tx.at[0], rx.at[0]),
        (7, 5, tx.at[1], rx.at[1]),
        (6, 4, tx.at[0], rx.at[0]),
        (6, 4, tx.at[1], rx.at[1]),
        (6, 4, tx.at[2], rx.at[2]),
        (5, 4, y.at[3], rx.at[3]),
        (5, 4, y.at[4], rx.at[4]),
        (5, 4, y.at[5], rx.at[5]),
        (5, 4, tx.at[0], rx.at[6]),
        (5, 4, tx.at[1], rx.at[7]),
        (4, 3, tx.at[0], rx.at[0]),
        (4, 3, tx.at[1], own1),
        (4, 3, tx.at[2], own2),
        (2, 3, y.at[0], rx.at[1]),
        (2, 3, y.at[1], rx.at[2]),
        (3, 2, tx.at[2], own0),
        (3, 1, tx.at[1], own0),
        (3, 0, tx.at[0], rx.at[0]),
        (1, 0, y.at[0], rx.at[1]),
        (5, 4, first, own0),
        (7, 6, first, own0),
    ]
    exchange = Exchange(messages, send_sem, recv_sem)

    def add(target, *terms):
        return lambda: scaled_add(meta, rates, target, terms, rows)

    def multiply(begin, end):
        def tile(index, _):
            spot = pl.ds(pl.multiple_of(index * GRAD_TILE, GRAD_TILE), GRAD_TILE)
            grads[spot, :] = mm_tn(left[:, spot], right[...]).astype(BF16)
            return 0

        lax.fori_loop(begin, end, tile, 0)

    tiles = D // GRAD_TILE
    exchange.greet()
    exchange.run([[], [23], [18, 19], [], [], [10, 11, 12, 24], [3, 4], [0, 1, 2, 25]], False)
    multiply(0, tiles // 2)
    exchange.run(
        [
            [],
            [],
            [],
            [],
            [
                ~10, ~7, add(tx.at[0], y.at[3], rx.at[0], rx.at[3]), 15,
                ~11, ~8, add(tx.at[1], y.at[4], rx.at[1], rx.at[4]), 16,
                ~12, ~9, add(tx.at[2], y.at[5], rx.at[2], rx.at[5]), 17,
                ~13, add(own1, y.at[6], rx.at[6]),
                ~14, add(own2, y.at[7], rx.at[7]),
                ~24,
            ],
            [
                ~5, add(tx.at[0], y.at[6], rx.at[0]), 13,
                ~6, add(tx.at[1], y.at[7], rx.at[1]), 14,
            ],
            [
                ~0, add(tx.at[0], y.at[3], rx.at[0]), 7,
                ~1, add(tx.at[1], y.at[4], rx.at[1]), 8,
                ~2, add(tx.at[2], y.at[5], rx.at[2]), 9,
                ~25,
            ],
            [
                ~3, add(tx.at[0], y.at[6], rx.at[0]), 5,
                ~4, add(tx.at[1], y.at[7], rx.at[1]), 6,
            ],
        ],
        False,
    )
    multiply(tiles // 2, tiles)
    exchange.run(
        [
            [~23, ~22, add(own0, rx.at[0], rx.at[1])],
            [~21],
            [~20],
            [
                ~18, ~19, ~15,
                add(tx.at[0], y.at[0], rx.at[1], (rx.at[0], 0)), 22,
                add(tx.at[1], y.at[1], rx.at[2], (rx.at[0], 1)), 21,
                add(tx.at[2], y.at[2], (rx.at[0], 2)), 20,
                add(own0, rx.at[0], y.at[3]),
                ~16, ~17,
            ],
            [],
            [],
            [],
            [],
        ],
        False,
    )
    exchange.drain()


def return_states(meta, rates, exports, first_state, left, right, rows):
    heads = exports.shape[1]
    state = (heads, QK, HV)
    return pl.pallas_call(
        functools.partial(return_kernel, rows),
        in_specs=[smem(), smem(), vmem(), vmem(), vmem(), vmem()],
        out_specs=[vmem()] * 4,
        out_shape=[jax.ShapeDtypeStruct(state, BF16)] * 3
        + [jax.ShapeDtypeStruct((D, right.shape[1]), BF16)],
        scratch_shapes=[
            pltpu.VMEM((8,) + state, BF16),
            pltpu.VMEM((3,) + state, BF16),
            pltpu.SemaphoreType.DMA((26,)),
            pltpu.SemaphoreType.DMA((26,)),
        ],
        compiler_params=pltpu.CompilerParams(
            collective_id=2, has_side_effects=True, vmem_limit_bytes=40 * 1024 * 1024
        ),
        name="return_states",
        cost_estimate=pl.CostEstimate(
            flops=0, bytes_accessed=100 * 1024 * 1024, transcendentals=0
        ),
    )(meta, rates, exports, first_state, left, right)


def sum_col(value):
    size = lax.axis_size("col")
    if size != SLOTS:
        return lax.psum(value, "col")
    for flip in (1, 2, 4):
        value = value + lax.ppermute(value, "col", [(a, a ^ flip) for a in range(size)])
    return value


def sum_col_vectors(vectors, extra=None):
    col = lax.axis_index("col")
    size = lax.axis_size("col")
    parts = list(vectors) + ([extra] if extra is not None else [])
    total = sum_col(jnp.concatenate(parts).reshape(-1, 128)).reshape(-1)
    results, first = [], 0
    for vector in vectors:
        width = vector.shape[0] // size
        results.append(lax.dynamic_slice_in_dim(total, first + col * width, width, 0))
        first += vector.shape[0]
    return results, total[first:]


def token_tables(place, rows, lengths, parents):
    index = place * rows + jnp.arange(rows, dtype=jnp.int32)
    in_trunk = index < TRUNK
    beyond = jnp.maximum(index - TRUNK, 0)
    segment = jnp.where(in_trunk, 0, 1 + beyond // SEG)
    position = jnp.where(in_trunk, index, beyond % SEG)

    def lookup(table, spots):
        hits = spots[:, None] == jnp.arange(table.shape[0], dtype=jnp.int32)
        return jnp.sum(jnp.where(hits, table, 0), axis=1)

    branch = 1 + lookup(parents, jnp.clip(segment - 5, 0, 7))
    parent_length = lookup(lengths, branch)
    depth = position + jnp.where(segment >= 1, lengths[0], 0)
    depth = depth + jnp.where(segment >= 5, parent_length, 0)
    valid = (position < lookup(lengths, segment)).astype(F32)
    half = QK // 2
    frequency = 10000.0 ** (-jnp.arange(half, dtype=F32) / (half - 1))
    angles = depth.astype(F32)[:, None] * frequency[None, :]
    return valid, jnp.cos(angles), jnp.sin(angles)


def body(
    tokens,
    cotangent,
    query_weight,
    key_weight,
    value_weight,
    gate_weight,
    out_weight,
    up_weight,
    down_weight,
    first_gain,
    first_bias,
    group_gain,
    group_bias,
    second_gain,
    second_bias,
    up_bias,
    down_bias,
    segment_lengths,
    leaf_parents,
):
    rows = tokens.shape[0]
    col = lax.axis_index("col")
    row = lax.axis_index("row")
    row_ref = row.astype(jnp.int32)[None]
    place = (col % SLOTS).astype(jnp.int32)
    tree = (col // SLOTS).astype(jnp.int32)
    lengths = lax.dynamic_index_in_dim(segment_lengths, tree, 0, keepdims=False)
    parents = lax.dynamic_index_in_dim(leaf_parents, tree, 0, keepdims=False)
    meta = jnp.concatenate([lengths, parents, place[None]]).astype(jnp.int32)
    heads = query_weight.shape[1] // QK
    head_numbers = (row * heads + jnp.arange(heads, dtype=jnp.int32)).astype(F32)
    rates = jnp.log(1.0 - 2.0 ** (-5.0 - head_numbers))

    wide = heads * HV
    narrow = heads * QK
    project_full = gather_col(jnp.concatenate([query_weight, key_weight, value_weight], axis=1))
    gate_full = gather_col(gate_weight)
    out_full = gather_col(out_weight.T)
    feed_full = gather_col(jnp.concatenate([down_weight.T, up_weight], axis=1))
    query_part, key_part = (project_full, narrow, 0), (project_full, narrow, 1)
    value_part = (project_full, wide, 1)
    out_part = (out_full, wide, 0)
    down_part, up_part = (feed_full, wide, 0), (feed_full, wide, 1)

    valid, cosine, sine = token_tables(place, rows, lengths, parents)
    column = valid[:, None]
    gains = gather_row_small(jnp.stack([first_gain, first_bias, second_gain, second_bias]))
    token_pieces, _ = gather_row(tokens)
    first_wide, first_average, first_inverse = join(token_pieces, row_ref, gains[0], gains[1])
    fed_low = (cotangent.astype(F32) * column).astype(BF16)
    fed_low, first_average = lax.optimization_barrier((fed_low, first_average))

    fed_pieces, projected = gather_row(
        fed_low, lambda: project(meta, rates, first_wide, project_full, cosine, sine)
    )
    query_rot, key_rot, value_low, exports = projected
    shared, shifted = share_states(meta, rates, exports, rows)
    gate_full, shared = in_order(gate_full, shared)
    gate_part = (gate_full, wide, 0)
    gate_full, fed_pieces = in_order(gate_full, fed_pieces)
    gate_part = (gate_full, wide, 0)
    gate_raw, gated, normal, inverse, states = retain(
        meta, rates, query_rot, key_rot, value_low, first_wide, gate_part, shared, shifted,
        group_gain, group_bias,
    )

    sends = reduce_row_start([gated], [out_part], row_ref)
    attended, _ = reduce_row_finish(sends, [gated], [out_part], row_ref)
    middle = tokens.astype(F32) + attended

    def feed_gradient(pieces):
        joined = join(pieces, row_ref)
        return joined, matmul(joined, down_part, BF16)

    middle_pieces, (fed_wide, grad_hidden) = gather_row(
        middle.astype(BF16), later=(feed_gradient, fed_pieces)
    )
    second_wide, second_average, second_inverse, hidden, grad_before, up_bias_grad, feed_sums = (
        feed_up(middle_pieces, row_ref, gains[2], gains[3], up_part, up_bias, grad_hidden)
    )
    feed_sums = sum_row_direct(feed_sums[:, :2].T)
    sends = reduce_row_start([grad_before], [up_part], row_ref)
    sends, hidden = in_order(sends, hidden)
    second_back, feed_partial = reduce_row_finish(
        sends,
        [grad_before],
        [up_part],
        row_ref,
        lambda hidden: weight_grads([(fed_wide, hidden), (second_wide, grad_before)]),
        hidden,
    )
    feed_grad = scatter_col(feed_partial)
    grad_fed = fed_low.astype(F32)
    down_bias_grad = jnp.sum(grad_fed, axis=0)

    second_normal = (middle - second_average[:, :1]) * second_inverse[:, :1]
    grad_middle_norm, second_gain_grad, second_bias_grad = norm_backward(
        second_back, second_normal, second_inverse[:, :1], second_gain, feed_sums
    )
    grad_middle = grad_fed + grad_middle_norm
    grad_pieces, fed_sends = gather_row(
        grad_middle.astype(BF16), lambda: reduce_row_start([hidden], [down_part], row_ref)
    )
    grad_wide = join(grad_pieces, row_ref)
    fed_sends, grad_wide = in_order(fed_sends, grad_wide)
    fed_out, out_partial = reduce_row_finish(
        fed_sends, [hidden], [down_part], row_ref, lambda _: column_grads([(grad_wide, gated)], 4)
    )
    fed_out = fed_out + down_bias
    layer_out = middle + fed_out
    out_partial, grad_wide, feed_grad = in_order(out_partial, grad_wide, feed_grad)
    out_grad = scatter_col(out_partial)
    grad_gate, grad_retained, group_gain_grad, group_bias_grad, returns, first_state = gate_back(
        meta, rates, grad_wide, out_part, gate_raw, normal, inverse, query_rot, group_gain, group_bias
    )
    own0, own1, own2, gate_partial = return_states(
        meta, rates, returns, first_state, first_wide, grad_gate, rows
    )
    gate_partial, own0, out_grad = in_order(gate_partial, own0, out_grad)
    own = (own0, own1, own2)
    gate_grad = scatter_col(gate_partial)
    grad_query, grad_key, grad_value = retain_back(
        meta, rates, query_rot, key_rot, value_low, grad_retained, states, cosine, sine, own
    )
    back_values = [grad_query, grad_key, grad_value, grad_gate]
    back_weights = [query_part, key_part, value_part, gate_part]
    sends = reduce_row_start(back_values, back_weights, row_ref)
    sends, grad_value = in_order(sends, grad_value)
    first_back, project_partial = reduce_row_finish(
        sends,
        back_values,
        back_weights,
        row_ref,
        lambda _: column_grads(
            [(first_wide, grad_query), (first_wide, grad_key), (first_wide, grad_value)], 6
        ),
    )
    project_partial, gate_grad = in_order(project_partial, gate_grad)
    project_grad = scatter_col(project_partial)

    first_normal = (tokens.astype(F32) - first_average[:, :1]) * first_inverse[:, :1]
    grad_first, first_gain_grad, first_bias_grad = norm_backward(
        first_back, first_normal, first_inverse[:, :1], first_gain
    )
    tokens_grad = grad_middle + grad_first

    squares = jnp.stack(
        [
            jnp.sum(column * layer_out * layer_out),
            jnp.sum(column * attended * attended),
            jnp.sum(column * fed_out * fed_out),
        ]
    )
    vectors, col_squares = sum_col_vectors(
        (
            first_gain_grad,
            first_bias_grad,
            group_gain_grad[0],
            group_bias_grad[0],
            second_gain_grad,
            second_bias_grad,
            up_bias_grad[0],
            down_bias_grad,
        ),
        jnp.concatenate([squares, jnp.zeros((125,), F32)]),
    )
    totals = sum_row_small(col_squares[None, :])[0, :3]
    valid_count = jnp.sum(segment_lengths).astype(F32) * D
    norm_values = jnp.sqrt(totals / valid_count)
    return (
        layer_out.astype(BF16),
        tokens_grad,
        project_grad[:, :narrow],
        project_grad[:, narrow : 2 * narrow],
        project_grad[:, 2 * narrow :],
        gate_grad,
        out_grad.T,
        feed_grad[:, wide:],
        feed_grad[:, :wide].T,
        *vectors,
        norm_values,
    )


def solution(mesh):
    matrix, turned, vector = P("col", "row"), P("row", "col"), P("row")
    in_specs = (matrix,) * 6 + (turned, matrix, turned) + (vector,) * 8 + (P(), P())
    split = P(("row", "col"))
    out_specs = (matrix,) * 6 + (turned, matrix, turned) + (split,) * 8 + (P(),)
    return jax.shard_map(body, mesh=mesh, in_specs=in_specs, out_specs=out_specs, check_vma=False)
```

```python
import functools

import jax
import jax.numpy as jnp
from jax import lax
from jax.experimental import pallas as pl
from jax.experimental.pallas import tpu as pltpu
from jax.sharding import PartitionSpec as P

D = 2048
QK = 256
HV = 512
TRUNK = 4096
SEG = 512
TREE_LEN = TRUNK + 12 * SEG
CHUNK = 256
TRUNK_CHUNKS = TRUNK // CHUNK
SLOTS = 8
GRAD_TILE = 256

EPSILON = 1e-05
SCALE = QK**-0.5
F32 = jnp.float32
BF16 = jnp.bfloat16

X_PAIRS = [(0, 1), (1, 0), (2, 3), (3, 2)]
Y_PAIRS = [(0, 2), (2, 0), (1, 3), (3, 1)]
D_PAIRS = [(0, 3), (3, 0), (1, 2), (2, 1)]


def mm(a, b):
    return lax.dot_general(a, b, (((1,), (0,)), ((), ())), preferred_element_type=F32)


def mm_nt(a, b):
    return lax.dot_general(a, b, (((1,), (1,)), ((), ())), preferred_element_type=F32)


def mm_tn(a, b):
    return lax.dot_general(a, b, (((0,), (0,)), ((), ())), preferred_element_type=F32)


def params(semantics, limit=None):
    return pltpu.CompilerParams(
        dimension_semantics=semantics, vmem_limit_bytes=limit or 60 * 1024 * 1024
    )


def smem():
    return pl.BlockSpec(memory_space=pltpu.SMEM)


class Chunk:
    def __init__(self, meta, index):
        in_trunk = index < TRUNK_CHUNKS
        beyond = jnp.maximum(index - TRUNK_CHUNKS, 0)
        self.in_trunk = in_trunk
        self.segment = jnp.where(in_trunk, 0, 1 + beyond // 2)
        self.first = jnp.where(in_trunk, index * CHUNK, (beyond % 2) * CHUNK)
        length = meta[self.segment]
        trunk_length = meta[0]
        self.trunk_length = trunk_length
        self.length = length
        self.is_leaf = self.segment >= 5
        self.parent = meta[13 + jnp.clip(self.segment - 5, 0, 7)]
        parent_length = meta[1 + self.parent]
        self.start = jnp.where(
            in_trunk,
            self.first,
            trunk_length + self.first + jnp.where(self.is_leaf, parent_length, 0),
        )
        self.count = jnp.clip(length - self.first, 0, CHUNK)
        self.end = self.start + self.count
        self.continues = jnp.where(in_trunk, index + 1 < TRUNK_CHUNKS, beyond % 2 == 0)


def trunk_reference(meta, place, rows):
    return jnp.minimum(meta[0], jnp.minimum(rows * (place + 1), TRUNK))


def power(rate, exponent, width):
    return jnp.exp(jnp.full((1, width), exponent.astype(F32), F32) * rate)


def column_power(rate, exponents):
    return jnp.exp(exponents.astype(F32) * rate)


def token_column(width=1):
    return lax.broadcasted_iota(jnp.int32, (CHUNK, width), 0)


def decay_matrix(rate):
    t = lax.broadcasted_iota(jnp.int32, (CHUNK, CHUNK), 0)
    u = lax.broadcasted_iota(jnp.int32, (CHUNK, CHUNK), 1)
    return jnp.where(u <= t, jnp.exp((t - u).astype(F32) * rate) * SCALE, 0.0)


def valid_decay(decay, count):
    u = lax.broadcasted_iota(jnp.int32, (1, CHUNK), 1)
    return decay[...] * jnp.where(u < count, 1.0, 0.0)


def key_decay(rate, count):
    j = token_column()
    return jnp.where(j < count, column_power(rate, jnp.maximum(count - j, 0)), 0.0)


def export_terms(meta, chunk, local, chunks, place, slot, rows):
    if slot == 0:
        is_shift = ((place == 4) | (place == 6)) & (local == chunks - 1)
        exponent = jnp.where(
            chunk.in_trunk,
            jnp.maximum(trunk_reference(meta, place, rows) - chunk.end, 0),
            0,
        )
        return chunk.in_trunk | is_shift, exponent
    wanted = (place == 3) | (place == 4)
    mine = (chunk.segment % 2 == 1) if slot == 1 else (chunk.segment % 2 == 0)
    is_branch = (chunk.segment >= 1) & (chunk.segment < 5)
    exponent = jnp.where(is_branch, jnp.maximum(chunk.length - chunk.first - chunk.count, 0), 0)
    return wanted & mine & is_branch, exponent


def import_terms(meta, chunk, place, slot, rows):
    if slot < 4:
        sees = jnp.logical_not(chunk.in_trunk) | (place > slot)
        if slot < 3:
            sees = sees & (place < 4)
        return sees, jnp.maximum(chunk.start - trunk_reference(meta, jnp.int32(slot), rows), 0)
    sees = chunk.is_leaf & (chunk.parent == slot - 4)
    return sees, chunk.first


def shift_in(meta, place, chunks):
    previous = Chunk(meta, jnp.maximum(place * chunks - 1, 0))
    return (place == 5) | (place == 7), CHUNK - previous.count


def retain_kernel(
    rows, chunks, meta, rates, query, key, value, wide, weight, shared, shifted, gain, bias,
    gate_out, gated_out, normal_out, inverse_out, state_out, running, total, decay,
):
    local = pl.program_id(1)
    rate = rates[pl.program_id(0)]
    place = meta[21]
    chunk = Chunk(meta, place * chunks + local)

    @pl.when(local == 0)
    def _():
        decay[...] = decay_matrix(rate)
        running[...] = jnp.zeros_like(running)
        on, exponent = shift_in(meta, place, chunks)

        @pl.when(on)
        def _():
            running[...] = shifted[0].astype(F32) * power(rate, exponent, HV)

    incoming = running[...]
    total[...] = incoming
    for slot in range(SLOTS):
        on, exponent = import_terms(meta, chunk, place, slot, rows)

        @pl.when(on)
        def _():
            total[...] += shared[slot, 0].astype(F32) * power(rate, exponent, HV)

    state = total[...].astype(BF16)
    state_out[0, 0] = state

    q, k, v = query[...], key[...], value[...]
    scores = (mm_nt(q, k) * valid_decay(decay, chunk.count)).astype(BF16)
    own = token_column()
    reach = column_power(rate, own) * SCALE
    retained = mm(scores, v) + mm(q, state) * reach

    j = token_column()
    ahead = jnp.where(j < chunk.count, column_power(rate, CHUNK - j), 0.0)
    fresh = mm_tn((k.astype(F32) * ahead).astype(BF16), v)
    keep = jnp.where(chunk.continues, 1.0, 0.0)
    running[...] = (incoming * power(rate, jnp.int32(CHUNK), HV) + fresh) * keep

    average = jnp.mean(retained, axis=1, keepdims=True)
    centred = retained - average
    inverse = lax.rsqrt(jnp.mean(centred * centred, axis=1, keepdims=True) + EPSILON)
    normal = centred * inverse
    gate_value = mm(wide[...], weight[...])
    gate_out[...] = gate_value
    gated = (normal * gain[...] + bias[...]) * (gate_value / (1.0 + jnp.exp(-gate_value)))
    gated_out[...] = gated.astype(BF16)
    normal_out[...] = normal.astype(BF16)
    inverse_out[0] = jnp.broadcast_to(inverse, (CHUNK, 128))


def retain(meta, rates, query, key, value, inputs, weight, shared, shifted, gain, bias):
    array, _, number = weight
    rows = key.shape[0]
    heads = key.shape[1] // QK
    chunks = rows // CHUNK
    wide = pl.BlockSpec((CHUNK, HV), lambda h, c: (c, h))
    narrow = pl.BlockSpec((CHUNK, QK), lambda h, c: (c, h))
    vector = pl.BlockSpec((1, HV), lambda h, c: (0, h))
    return pl.pallas_call(
        functools.partial(retain_kernel, rows, chunks),
        grid=(heads, chunks),
        in_specs=[
            smem(), smem(), narrow, narrow, wide,
            pl.BlockSpec((CHUNK, D), lambda h, c: (c, 0)),
            pl.BlockSpec((D, HV), lambda h, c: (0, number * heads + h)),
            pl.BlockSpec((SLOTS, 1, QK, HV), lambda h, c: (0, h, 0, 0)),
            pl.BlockSpec((1, QK, HV), lambda h, c: (h, 0, 0)),
            vector, vector,
        ],
        out_specs=[
            wide, wide, wide,
            pl.BlockSpec((1, CHUNK, 128), lambda h, c: (h, c, 0)),
            pl.BlockSpec((1, 1, QK, HV), lambda h, c: (h, c, 0, 0)),
        ],
        out_shape=[
            jax.ShapeDtypeStruct((rows, heads * HV), F32),
            jax.ShapeDtypeStruct((rows, heads * HV), BF16),
            jax.ShapeDtypeStruct((rows, heads * HV), BF16),
            jax.ShapeDtypeStruct((heads, rows, 128), F32),
            jax.ShapeDtypeStruct((heads, chunks, QK, HV), BF16),
        ],
        scratch_shapes=[
            pltpu.VMEM((QK, HV), F32), pltpu.VMEM((QK, HV), F32), pltpu.VMEM((CHUNK, CHUNK), F32)
        ],
        compiler_params=params(("arbitrary", "arbitrary")),
        name="retention_forward",
        cost_estimate=pl.CostEstimate(
            flops=2 * rows * heads * (CHUNK * 768 + 2 * QK * HV + D * HV),
            bytes_accessed=rows * heads * 8192,
            transcendentals=rows * heads * 768,
        ),
    )(meta, rates, query, key, value, inputs, array, shared, shifted, gain[None, :], bias[None, :])


def gate_back_kernel(
    rows, chunks, meta, rates, wide, weight, gate, normal_in, inverse_in, query, gain, bias,
    gate_out, retained_out, gain_out, bias_out, exports, first_out, acc,
):
    local = pl.program_id(1)
    rate = rates[pl.program_id(0)]
    place = meta[21]
    chunk = Chunk(meta, place * chunks + local)
    grad_gated = mm(wide[...], weight[...])
    gate_value = gate[...].astype(F32)
    normal = normal_in[...].astype(F32)
    sigmoid = 1.0 / (1.0 + jnp.exp(-gate_value))
    normed = normal * gain[...] + bias[...]
    grad_gate = grad_gated * normed * (sigmoid * (1.0 + gate_value * (1.0 - sigmoid)))
    gate_out[...] = grad_gate.astype(BF16)
    grad_normed = grad_gated * (gate_value * sigmoid)

    @pl.when(local == 0)
    def _():
        gain_out[...] = jnp.zeros_like(gain_out)
        bias_out[...] = jnp.zeros_like(bias_out)
        acc[...] = jnp.zeros_like(acc)

    gain_out[...] += jnp.sum(grad_normed * normal, axis=0, keepdims=True)
    bias_out[...] += jnp.sum(grad_normed, axis=0, keepdims=True)
    scaled = grad_normed * gain[...]
    grad = inverse_in[0][:, :1] * (
        scaled
        - jnp.mean(scaled, axis=1, keepdims=True)
        - normal * jnp.mean(scaled * normal, axis=1, keepdims=True)
    )
    grad = grad.astype(BF16)
    retained_out[...] = grad
    reach = column_power(rate, token_column()) * SCALE
    state = mm_tn((query[...].astype(F32) * reach).astype(BF16), grad)
    for slot in range(SLOTS):
        on, exponent = import_terms(meta, chunk, place, slot, rows)

        @pl.when(on)
        def _():
            acc[slot] += state * power(rate, exponent, HV)

    @pl.when(local == 0)
    def _():
        on, exponent = shift_in(meta, place, chunks)
        scale = jnp.where(on, power(rate, exponent, HV), 0.0)
        first_out[0] = (state * scale).astype(BF16)

    @pl.when(local == chunks - 1)
    def _():
        exports[:, 0] = acc[...].astype(BF16)


def gate_back(meta, rates, wide, weight, gate, normal, inverse, query, gain, bias):
    array, width, number = weight
    first = number * (width // HV)
    rows = query.shape[0]
    heads = query.shape[1] // QK
    chunks = rows // CHUNK
    block = pl.BlockSpec((CHUNK, HV), lambda h, c: (c, h))
    vector = pl.BlockSpec((1, HV), lambda h, c: (0, h))
    return pl.pallas_call(
        functools.partial(gate_back_kernel, rows, chunks),
        grid=(heads, chunks),
        in_specs=[
            smem(), smem(),
            pl.BlockSpec((CHUNK, D), lambda h, c: (c, 0)),
            pl.BlockSpec((D, HV), lambda h, c: (0, first + h)),
            block, block,
            pl.BlockSpec((1, CHUNK, 128), lambda h, c: (h, c, 0)),
            pl.BlockSpec((CHUNK, QK), lambda h, c: (c, h)),
            vector, vector,
        ],
        out_specs=[
            block, block, vector, vector,
            pl.BlockSpec((SLOTS, 1, QK, HV), lambda h, c: (0, h, 0, 0)),
            pl.BlockSpec((1, QK, HV), lambda h, c: (h, 0, 0)),
        ],
        out_shape=[
            jax.ShapeDtypeStruct((rows, heads * HV), BF16),
            jax.ShapeDtypeStruct((rows, heads * HV), BF16),
            jax.ShapeDtypeStruct((1, heads * HV), F32),
            jax.ShapeDtypeStruct((1, heads * HV), F32),
            jax.ShapeDtypeStruct((SLOTS, heads, QK, HV), BF16),
            jax.ShapeDtypeStruct((heads, QK, HV), BF16),
        ],
        scratch_shapes=[pltpu.VMEM((SLOTS, QK, HV), F32)],
        compiler_params=params(("arbitrary", "arbitrary")),
        name="gate_backward",
        cost_estimate=pl.CostEstimate(
            flops=2 * rows * heads * HV * (D + QK),
            bytes_accessed=rows * heads * 12288,
            transcendentals=rows * heads * HV,
        ),
    )(meta, rates, wide, array, gate, normal, inverse, query, gain[None, :], bias[None, :])


def retain_back_kernel(
    rows, chunks, meta, rates, query, key, value, grad, state_in, cosine, sine, own0, own1, own2,
    query_out, key_out, value_out, running, total_ref, decay_ref,
):
    step = pl.program_id(1)
    local = chunks - 1 - step
    rate = rates[pl.program_id(0)]
    place = meta[21]
    chunk = Chunk(meta, place * chunks + local)
    before = Chunk(meta, jnp.maximum(place * chunks + local - 1, 0))

    @pl.when(step == 0)
    def _():
        decay_ref[...] = decay_matrix(rate)
        running[...] = jnp.zeros_like(running)

    later = running[...]
    total_ref[...] = later
    for slot, ref in ((0, own0), (1, own1), (2, own2)):
        on, exponent = export_terms(meta, chunk, local, chunks, place, slot, rows)

        @pl.when(on)
        def _():
            total_ref[...] += ref[0].astype(F32) * power(rate, exponent, HV)

    total = total_ref[...].astype(BF16)

    q, k, v, g = query[...], key[...], value[...], grad[...]
    decay = valid_decay(decay_ref, chunk.count)
    scores = (mm_nt(q, k) * decay).astype(BF16)
    slopes = (mm_nt(g, v) * decay).astype(BF16)
    reach = column_power(rate, token_column()) * SCALE
    toward = key_decay(rate, chunk.count)
    grad_query = mm(slopes, k) + mm_nt(g, state_in[0, 0]) * reach
    grad_key = mm_tn(slopes, q) + mm_nt(v, total) * toward
    grad_value = mm_tn(scores, g) + mm(k, total) * toward
    value_out[...] = grad_value.astype(BF16)
    cos, sin = cosine[...], sine[...]
    half = QK // 2
    for out, val in ((query_out, grad_query), (key_out, grad_key)):
        a, b = val[:, :half], val[:, half:]
        out[:, :half] = (a * cos + b * sin).astype(BF16)
        out[:, half:] = (b * cos - a * sin).astype(BF16)

    fresh = mm_tn((q.astype(F32) * reach).astype(BF16), g)
    carried = fresh + later * power(rate, chunk.count, HV)
    keep = jnp.where((local > 0) & before.continues, 1.0, 0.0)
    running[...] = carried * power(rate, CHUNK - before.count, HV) * keep


def retain_back(meta, rates, query, key, value, grad, states, cosine, sine, own):
    rows = query.shape[0]
    heads = query.shape[1] // QK
    chunks = rows // CHUNK
    last = chunks - 1
    wide = pl.BlockSpec((CHUNK, HV), lambda h, s: (last - s, h))
    narrow = pl.BlockSpec((CHUNK, QK), lambda h, s: (last - s, h))
    table = pl.BlockSpec((CHUNK, QK // 2), lambda h, s: (last - s, 0))
    state = pl.BlockSpec((1, QK, HV), lambda h, s: (h, 0, 0))
    return pl.pallas_call(
        functools.partial(retain_back_kernel, rows, chunks),
        grid=(heads, chunks),
        in_specs=[
            smem(), smem(), narrow, narrow, wide, wide,
            pl.BlockSpec((1, 1, QK, HV), lambda h, s: (h, last - s, 0, 0)),
            table, table, state, state, state,
        ],
        out_specs=[narrow, narrow, wide],
        out_shape=[
            jax.ShapeDtypeStruct((rows, heads * QK), BF16),
            jax.ShapeDtypeStruct((rows, heads * QK), BF16),
            jax.ShapeDtypeStruct((rows, heads * HV), BF16),
        ],
        scratch_shapes=[
            pltpu.VMEM((QK, HV), F32), pltpu.VMEM((QK, HV), F32), pltpu.VMEM((CHUNK, CHUNK), F32)
        ],
        compiler_params=params(("arbitrary", "arbitrary")),
        name="retention_backward",
        cost_estimate=pl.CostEstimate(
            flops=2 * rows * heads * (CHUNK * 1792 + 4 * QK * HV),
            bytes_accessed=rows * heads * 6144,
            transcendentals=rows * heads * 256,
        ),
    )(meta, rates, query, key, value, grad, states, cosine, sine, *own)


def norm_kernel(values, gain, bias, out, average_out, inverse_out):
    x = values[...].astype(F32)
    average = jnp.mean(x, axis=1, keepdims=True)
    inverse = lax.rsqrt(jnp.mean(x * x, axis=1, keepdims=True) - average * average + EPSILON)
    out[...] = ((x - average) * inverse * gain[...] + bias[...]).astype(BF16)
    average_out[...] = jnp.broadcast_to(average, average_out.shape)
    inverse_out[...] = jnp.broadcast_to(inverse, inverse_out.shape)


def norm_wide(values, gain, bias):
    rows = values.shape[0]
    block = pl.BlockSpec((CHUNK, D), lambda i: (i, 0))
    vector = pl.BlockSpec((1, D), lambda i: (0, 0))
    stat = pl.BlockSpec((CHUNK, 128), lambda i: (i, 0))
    return pl.pallas_call(
        norm_kernel,
        grid=(rows // CHUNK,),
        in_specs=[block, vector, vector],
        out_specs=[block, stat, stat],
        out_shape=[
            jax.ShapeDtypeStruct((rows, D), BF16),
            jax.ShapeDtypeStruct((rows, 128), F32),
            jax.ShapeDtypeStruct((rows, 128), F32),
        ],
        compiler_params=params(("arbitrary",)),
        name="layer_norm",
        cost_estimate=pl.CostEstimate(
            flops=8 * rows * D, bytes_accessed=4 * rows * D, transcendentals=rows
        ),
    )(values, gain[None, :], bias[None, :])


def join_kernel(row, own, from_x, from_y, far_a, far_b, *refs, norm):
    block = own.shape[1]
    second = pl.program_id(0) >= pl.num_programs(0) // 2
    spots = [
        pl.ds(pl.multiple_of((row[0] ^ flip) * block, 128), block) for flip in range(4)
    ]
    pieces = [own[...], from_x[...], from_y[...], jnp.where(second, far_b[...], far_a[...])]
    if not norm:
        for spot, piece in zip(spots, pieces):
            refs[0][:, spot] = piece
        return
    gain, bias, out, average_out, inverse_out = refs
    pieces = [piece.astype(F32) for piece in pieces]
    average = sum(jnp.sum(piece, axis=1, keepdims=True) for piece in pieces) / D
    squares = sum(jnp.sum(piece * piece, axis=1, keepdims=True) for piece in pieces) / D
    inverse = lax.rsqrt(squares - average * average + EPSILON)
    for spot, piece in zip(spots, pieces):
        out[:, spot] = ((piece - average) * inverse * gain[:, spot] + bias[:, spot]).astype(BF16)
    average_out[...] = jnp.broadcast_to(average, average_out.shape)
    inverse_out[...] = jnp.broadcast_to(inverse, inverse_out.shape)


def join(pieces, row, gain=None, bias=None):
    norm = gain is not None
    if not isinstance(pieces, tuple):
        return norm_wide(pieces, gain, bias) if norm else pieces
    rows, block = pieces[0].shape
    steps = 4
    tile = rows // steps
    piece = pl.BlockSpec((tile, block), lambda i, r: (i, 0))
    far_a = pl.BlockSpec((tile, block), lambda i, r: (jnp.minimum(i, steps // 2 - 1), 0))
    far_b = pl.BlockSpec((tile, block), lambda i, r: (jnp.maximum(i - steps // 2, 0), 0))
    vector = pl.BlockSpec((1, D), lambda i, r: (0, 0))
    wide = pl.BlockSpec((tile, D), lambda i, r: (i, 0))
    stat = pl.BlockSpec((tile, 128), lambda i, r: (i, 0))
    wide_shape = jax.ShapeDtypeStruct((rows, D), BF16)
    stat_shape = jax.ShapeDtypeStruct((rows, 128), F32)
    return pl.pallas_call(
        functools.partial(join_kernel, norm=norm),
        grid_spec=pltpu.PrefetchScalarGridSpec(
            num_scalar_prefetch=1,
            grid=(steps,),
            in_specs=[piece] * 3 + [far_a, far_b] + ([vector] * 2 if norm else []),
            out_specs=[wide, stat, stat] if norm else wide,
        ),
        out_shape=[wide_shape, stat_shape, stat_shape] if norm else wide_shape,
        compiler_params=params(("arbitrary",)),
        name="join_norm" if norm else "join",
        cost_estimate=pl.CostEstimate(
            flops=8 * rows * D, bytes_accessed=4 * rows * D, transcendentals=0
        ),
    )(row, *pieces, *((gain[None, :], bias[None, :]) if norm else ()))


def project_kernel(
    heads, rows, chunks, meta, rates, values, weight, cosine, sine,
    query_out, key_out, value_out, exports, acc,
):
    local = pl.program_id(0)
    place = meta[21]
    chunk = Chunk(meta, place * chunks + local)
    raw = mm(values[...], weight[...])
    cos, sin = cosine[...], sine[...]
    half = QK // 2
    for part, out in ((0, query_out), (1, key_out)):
        for head in range(heads):
            first = (part * heads + head) * QK
            a, b = raw[:, first : first + half], raw[:, first + half : first + QK]
            out[:, head * QK : head * QK + half] = (a * cos - b * sin).astype(BF16)
            out[:, head * QK + half : (head + 1) * QK] = (b * cos + a * sin).astype(BF16)
    value_out[...] = raw[:, 2 * heads * QK :].astype(BF16)

    @pl.when(local == 0)
    def _():
        acc[...] = jnp.zeros_like(acc)

    for head in range(heads):
        rate = rates[head]
        key = key_out[:, head * QK : (head + 1) * QK].astype(F32)
        weighted = (key * key_decay(rate, chunk.count)).astype(BF16)
        state = mm_tn(weighted, value_out[:, head * HV : (head + 1) * HV])
        for slot in range(3):
            on, exponent = export_terms(meta, chunk, local, chunks, place, slot, rows)

            @pl.when(on)
            def _():
                acc[slot, head] += state * power(rate, exponent, HV)

    @pl.when(local == chunks - 1)
    def _():
        exports[...] = acc[...].astype(BF16)


def project(meta, rates, values, weight, cosine, sine):
    rows, width = values.shape[0], weight.shape[1]
    heads = width // (2 * QK + HV)
    chunks = rows // CHUNK
    table = pl.BlockSpec((CHUNK, QK // 2), lambda i: (i, 0))
    widths = (heads * QK, heads * QK, heads * HV)
    states = (3, heads, QK, HV)
    return pl.pallas_call(
        functools.partial(project_kernel, heads, rows, chunks),
        grid=(chunks,),
        in_specs=[
            smem(), smem(),
            pl.BlockSpec((CHUNK, D), lambda i: (i, 0)),
            pl.BlockSpec((D, width), lambda i: (0, 0)),
            table, table,
        ],
        out_specs=[pl.BlockSpec((CHUNK, w), lambda i: (i, 0)) for w in widths]
        + [pl.BlockSpec(states, lambda i: (0, 0, 0, 0))],
        out_shape=[jax.ShapeDtypeStruct((rows, w), BF16) for w in widths]
        + [jax.ShapeDtypeStruct(states, BF16)],
        scratch_shapes=[pltpu.VMEM(states, F32)],
        compiler_params=params(("arbitrary",)),
        name="project",
        cost_estimate=pl.CostEstimate(
            flops=2 * rows * D * width, bytes_accessed=2 * (rows + width) * D, transcendentals=0
        ),
    )(meta, rates, values, weight, cosine, sine)


def matmul_kernel(values, weight, out):
    out[...] = mm(values[...], weight[...]).astype(out.dtype)


def matmul(values, weight, kind):
    array, width, number = weight
    rows = values.shape[0]
    return pl.pallas_call(
        matmul_kernel,
        grid=(rows // CHUNK,),
        in_specs=[
            pl.BlockSpec((CHUNK, D), lambda i: (i, 0)),
            pl.BlockSpec((D, width), lambda i: (0, number)),
        ],
        out_specs=pl.BlockSpec((CHUNK, width), lambda i: (i, 0)),
        out_shape=jax.ShapeDtypeStruct((rows, width), kind),
        compiler_params=params(("arbitrary",)),
        name="matmul",
        cost_estimate=pl.CostEstimate(
            flops=2 * rows * D * width, bytes_accessed=2 * (rows + width) * D, transcendentals=0
        ),
    )(values, array)


def weight_grad_kernel(spans, *refs):
    count = len(spans)
    lefts, rights, out = refs[:count], refs[count : 2 * count], refs[2 * count]
    tile = pl.program_id(0)
    for left, right, (first, last) in zip(lefts, rights, spans):

        @pl.when((tile >= first) & (tile < last))
        def _():
            height = 2 * GRAD_TILE

            def part(index, _):
                spot = pl.ds(pl.multiple_of(index * height, height), height)
                out[spot, :] = mm_tn(left[:, spot], right[...]).astype(BF16)
                return 0

            lax.fori_loop(0, left.shape[1] // height, part, 0)


def weight_grads(pairs):
    rows = pairs[0][0].shape[0]
    wide = min(right.shape[1] for _, right in pairs)
    tall = 1024
    steps = D // tall
    spans, first = [], 0
    for _, right in pairs:
        spans.append((first, first + right.shape[1] // wide))
        first = spans[-1][1]

    def left_spec(span):
        return pl.BlockSpec(
            (rows, tall),
            lambda n, m: (
                0, jnp.where(n < span[0], 0, jnp.where(n < span[1], m, steps - 1)),
            ),
        )

    def right_spec(span):
        return pl.BlockSpec(
            (rows, wide), lambda n, m: (0, jnp.clip(n - span[0], 0, span[1] - span[0] - 1))
        )

    return pl.pallas_call(
        functools.partial(weight_grad_kernel, tuple(spans)),
        grid=(first, steps),
        in_specs=[left_spec(span) for span in spans] + [right_spec(span) for span in spans],
        out_specs=pl.BlockSpec((tall, wide), lambda n, m: (m, n)),
        out_shape=jax.ShapeDtypeStruct((D, first * wide), BF16),
        compiler_params=params(("arbitrary", "arbitrary")),
        name="weight_grads",
        cost_estimate=pl.CostEstimate(
            flops=2 * rows * D * first * wide,
            bytes_accessed=2 * D * first * wide + 4 * rows * D,
            transcendentals=0,
        ),
    )(*[left for left, _ in pairs], *[right for _, right in pairs])


def paired_grad_kernel(spans, tiles, steps, *refs):
    count = len(spans)
    lefts, rights = refs[:count], refs[count : 2 * count]
    out, made, received, send_sem, recv_sem = refs[2 * count :]
    step = pl.program_id(0)
    core = lax.axis_index("col") % 2
    partner = lax.axis_index("col") + 1 - 2 * core

    def copy(index):
        return pltpu.make_async_remote_copy(
            src_ref=made.at[index, :, 1 - core],
            dst_ref=received.at[index],
            send_sem=send_sem.at[index],
            recv_sem=recv_sem.at[index],
            device_id={"col": partner},
            device_id_type=pl.DeviceIdType.MESH,
        )

    @pl.when(step == 0)
    def _():
        barrier = pltpu.get_barrier_semaphore()
        pl.semaphore_signal(
            barrier, inc=1, device_id={"col": partner}, device_id_type=pl.DeviceIdType.MESH
        )
        pl.semaphore_wait(barrier, 1)

    for left, right, (first, last) in zip(lefts, rights, spans):

        @pl.when((step >= first * steps) & (step < last * steps))
        def _():
            total = mm_tn(left[...], right[...]).astype(BF16)
            made[step] = total.reshape(made.shape[1:])

    @pl.when(step < tiles)
    def _():
        copy(step).start()

    @pl.when(step > 0)
    def _():
        index = step - 1
        copy(index).wait()
        out[...] = (made[index, :, core].astype(F32) + received[index].astype(F32)).astype(BF16)


def paired_grads(pairs, number):
    rows = pairs[0][0].shape[0]
    wide = min(right.shape[1] for _, right in pairs)
    wide = min(wide, 512)
    tall = 1024
    steps = D // tall
    block = D // SLOTS
    depth = tall // block // 2
    spans, first = [], 0
    for _, right in pairs:
        spans.append((first, first + right.shape[1] // wide))
        first = spans[-1][1]
    tiles = first * steps

    def left_spec(span):
        def index(s):
            n, m = s // steps, s % steps
            return 0, jnp.where(n < span[0], 0, jnp.where(n < span[1], m, steps - 1))

        return pl.BlockSpec((rows, tall), index)

    def right_spec(span):
        def index(s):
            return 0, jnp.clip(s // steps - span[0], 0, span[1] - span[0] - 1)

        return pl.BlockSpec((rows, wide), index)

    def out_index(s):
        done = jnp.maximum(s - 1, 0)
        return done % steps, 0, done // steps

    result = pl.pallas_call(
        functools.partial(paired_grad_kernel, tuple(spans), tiles, steps),
        grid=(tiles + 1,),
        in_specs=[left_spec(span) for span in spans] + [right_spec(span) for span in spans],
        out_specs=pl.BlockSpec((depth, block, wide), out_index),
        out_shape=jax.ShapeDtypeStruct((SLOTS // 2, block, first * wide), BF16),
        scratch_shapes=[
            pltpu.VMEM((tiles, depth, 2, block, wide), BF16),
            pltpu.VMEM((tiles, depth, block, wide), BF16),
            pltpu.SemaphoreType.DMA((tiles,)),
            pltpu.SemaphoreType.DMA((tiles,)),
        ],
        compiler_params=pltpu.CompilerParams(
            dimension_semantics=("arbitrary",),
            collective_id=number,
            has_side_effects=True,
            vmem_limit_bytes=60 * 1024 * 1024,
        ),
        name="paired_grads",
        cost_estimate=pl.CostEstimate(
            flops=2 * rows * D * first * wide,
            bytes_accessed=2 * D * first * wide + 4 * rows * D,
            transcendentals=0,
        ),
    )(*[left for left, _ in pairs], *[right for _, right in pairs])
    return result


def column_grads(pairs, number):
    if lax.axis_size("col") != SLOTS:
        return weight_grads(pairs)
    return paired_grads(pairs, number)


def norm_pieces(row, own, from_x, from_y, far_a, far_b, gain, bias, out, average_out, inverse_out):
    block = own.shape[1]
    second = pl.program_id(0) >= pl.num_programs(0) // 2
    far = jnp.where(second, far_b[...], far_a[...])
    pieces = [piece.astype(F32) for piece in (own[...], from_x[...], from_y[...], far)]
    average = sum(jnp.sum(piece, axis=1, keepdims=True) for piece in pieces) / D
    squares = sum(jnp.sum(piece * piece, axis=1, keepdims=True) for piece in pieces) / D
    inverse = lax.rsqrt(squares - average * average + EPSILON)
    for flip, piece in enumerate(pieces):
        spot = pl.ds(pl.multiple_of((row[0] ^ flip) * block, 128), block)
        out[:, spot] = ((piece - average) * inverse * gain[:, spot] + bias[:, spot]).astype(BF16)
    average_out[...] = jnp.broadcast_to(average, average_out.shape)
    inverse_out[...] = jnp.broadcast_to(inverse, inverse_out.shape)


def up_kernel(row, *refs, joined):
    if joined:
        pieces, gain, norm_bias = refs[:5], refs[5], refs[6]
        weight, bias, grad_hidden, scales, second_out, average_out, inverse_out = refs[7:14]
        hidden_out, grad_out, bias_out, sums_out, moved = refs[14:]
        norm_pieces(row, *pieces, gain, norm_bias, second_out, average_out, inverse_out)
        values = second_out
    else:
        values, weight, bias, grad_hidden, scales = refs[:5]
        hidden_out, grad_out, bias_out, sums_out, moved = refs[5:]
    before = mm(values[...], weight[...]) + bias[...]
    phi = 0.5 * (1.0 + lax.erf(before * (0.5**0.5)))
    hidden_out[...] = (before * phi).astype(BF16)
    density = jnp.exp(-0.5 * before * before) * 0.3989422804014327
    grad = (grad_hidden[...].astype(F32) * (phi + before * density)).astype(BF16)
    grad_out[...] = grad

    @pl.when(pl.program_id(0) == 0)
    def _():
        bias_out[...] = jnp.zeros_like(bias_out)
        parts = mm(scales[...], weight[...])
        moved[0:1] = parts[0:1] + parts[1:2]
        moved[1:2] = parts[2:3] + parts[3:4]

    wide_grad = grad.astype(F32)
    bias_out[...] += jnp.sum(wide_grad, axis=0, keepdims=True)
    plain = jnp.sum(wide_grad * moved[0:1], axis=1, keepdims=True)
    crossed = jnp.sum(wide_grad * (before - bias[...] - moved[1:2]), axis=1, keepdims=True)
    lane = lax.broadcasted_iota(jnp.int32, sums_out.shape, 1)
    sums_out[...] = jnp.where(lane == 0, plain, crossed)


def feed_up(pieces, row, gain, norm_bias, weight, bias, grad_hidden):
    array, width, number = weight
    joined = isinstance(pieces, tuple)
    rows = grad_hidden.shape[0]
    steps = 4
    tile = rows // steps
    block = pl.BlockSpec((tile, width), lambda i, r: (i, 0))
    vector = pl.BlockSpec((1, width), lambda i, r: (0, 0))
    wide = pl.BlockSpec((tile, D), lambda i, r: (i, 0))
    stat = pl.BlockSpec((tile, 128), lambda i, r: (i, 0))
    gains = pl.BlockSpec((1, D), lambda i, r: (0, 0))
    if joined:
        piece = pl.BlockSpec((tile, pieces[0].shape[1]), lambda i, r: (i, 0))
        far_a = pl.BlockSpec(
            (tile, pieces[0].shape[1]), lambda i, r: (jnp.minimum(i, steps // 2 - 1), 0)
        )
        far_b = pl.BlockSpec(
            (tile, pieces[0].shape[1]), lambda i, r: (jnp.maximum(i - steps // 2, 0), 0)
        )
        inputs = list(pieces) + [gain[None, :], norm_bias[None, :]]
        in_specs = [piece] * 3 + [far_a, far_b, gains, gains]
        early_specs = [wide, stat, stat]
        early_shapes = [
            jax.ShapeDtypeStruct((rows, D), BF16),
            jax.ShapeDtypeStruct((rows, 128), F32),
            jax.ShapeDtypeStruct((rows, 128), F32),
        ]
        normed = []
    else:
        normed = list(norm_wide(pieces, gain, norm_bias))
        inputs, in_specs, early_specs, early_shapes = [normed[0]], [wide], [], []
    scales = jnp.stack([gain, norm_bias])
    high = lax.reduce_precision(scales, 8, 7)
    low = scales - high
    rest = jnp.zeros((4, D), F32)
    scales = jnp.concatenate([high[:1], low[:1], high[1:], low[1:], rest], axis=0).astype(BF16)
    outs = pl.pallas_call(
        functools.partial(up_kernel, joined=joined),
        grid_spec=pltpu.PrefetchScalarGridSpec(
            num_scalar_prefetch=1,
            grid=(steps,),
            in_specs=in_specs
            + [
                pl.BlockSpec((D, width), lambda i, r: (0, number)), vector, block,
                pl.BlockSpec((8, D), lambda i, r: (0, 0)),
            ],
            out_specs=early_specs + [block, block, vector, stat],
            scratch_shapes=[pltpu.VMEM((8, width), F32)],
        ),
        out_shape=early_shapes
        + [
            jax.ShapeDtypeStruct((rows, width), BF16),
            jax.ShapeDtypeStruct((rows, width), BF16),
            jax.ShapeDtypeStruct((1, width), F32),
            jax.ShapeDtypeStruct((rows, 128), F32),
        ],
        compiler_params=params(("arbitrary",)),
        name="feed_up",
        cost_estimate=pl.CostEstimate(
            flops=2 * rows * D * width,
            bytes_accessed=2 * (2 * rows + width) * D + 8 * rows * width,
            transcendentals=2 * rows * width,
        ),
    )(row, *inputs, array, bias[None, :], grad_hidden, scales)
    return normed + list(outs)


PARTIAL_FLIP = (1, 3, 2, 3, 2, 1, 0, 0)
PARTIAL_HALF = (0, 0, 1, 1, 0, 1, 0, 1)


def table_lookup(table, step):
    result = jnp.int32(table[0])
    for index in range(1, len(table)):
        result = jnp.where(step == index, table[index], result)
    return result


def partial_kernel(count, row, *refs):
    values, weights = refs[:count], refs[count : 2 * count]
    outs = refs[2 * count :]
    step = pl.program_id(0)
    strip = values[0].shape[0] // 2

    def part(number, _):
        spot = pl.ds(pl.multiple_of(number * strip, strip), strip)
        total = mm_nt(values[0][spot, :], weights[0][...])
        for x, w in zip(values[1:], weights[1:]):
            total = total + mm_nt(x[spot, :], w[...])
        for index, out in enumerate(outs):

            @pl.when(step // 2 == index)
            def _():
                out[0, spot, :] = total.astype(out.dtype)

        return 0

    lax.fori_loop(0, 2, part, 0)


def partial_blocks(values, weights, row, first, kinds):
    rows = values[0].shape[0]
    half, block = rows // 2, D // 4
    count = len(values)
    flips = PARTIAL_FLIP[2 * first : 2 * (first + len(kinds))]
    halves = PARTIAL_HALF[2 * first : 2 * (first + len(kinds))]

    def value_spec(x):
        return pl.BlockSpec((half, x.shape[1]), lambda s, r: (table_lookup(halves, s), 0))

    def weight_spec(w):
        return pl.BlockSpec((block, w[1]), lambda s, r: (r[0] ^ table_lookup(flips, s), w[2]))

    def out_spec(index):
        return pl.BlockSpec((1, half, block), lambda s, r: (jnp.clip(s - 2 * index, 0, 1), 0, 0))

    depth = sum(x.shape[1] for x in values)
    return pl.pallas_call(
        functools.partial(partial_kernel, count),
        grid_spec=pltpu.PrefetchScalarGridSpec(
            num_scalar_prefetch=1,
            grid=(2 * len(kinds),),
            in_specs=[value_spec(x) for x in values] + [weight_spec(w) for w in weights],
            out_specs=[out_spec(index) for index in range(len(kinds))],
        ),
        out_shape=[jax.ShapeDtypeStruct((2, half, block), kind) for kind in kinds],
        compiler_params=params(("arbitrary",)),
        name="partial_blocks",
        cost_estimate=pl.CostEstimate(
            flops=rows * block * depth * 2 * len(kinds),
            bytes_accessed=(rows + D) * depth * 2 + 4 * rows * block * len(kinds),
            transcendentals=0,
        ),
    )(row, *values, *[w[0] for w in weights])


def permute_row(value, pairs):
    return lax.ppermute(value, "row", pairs)


def in_order(*values):
    return lax.optimization_barrier(values)


def reduce_row_start(values, weights, row):
    if lax.axis_size("row") != 4:
        columns = [array[:, n * width : (n + 1) * width] for array, width, n in weights]
        return sum(mm_nt(x, w) for x, w in zip(values, columns)).astype(BF16)
    return tuple(partial_blocks(values, weights, row, 0, (BF16, BF16)))


def reduce_row_rest(values, weights, row):
    if lax.axis_size("row") != 4:
        return ()
    return tuple(partial_blocks(values, weights, row, 2, (BF16, F32)))


def reduce_row_finish(sends, values, weights, row, between=None, tied=None, rest=None):
    if lax.axis_size("row") != 4:
        total = lax.psum_scatter(sends, "row", scatter_dimension=1, tiled=True).astype(F32)
        return total, between(tied) if between else None
    from_x = permute_row(sends[0], X_PAIRS)
    from_y = permute_row(sends[1], Y_PAIRS)
    keep, own = rest if rest is not None else reduce_row_rest(values, weights, row)
    extra = None
    if between is not None:
        if tied is not None:
            keep, own, tied = in_order(keep, own, tied)
        extra = between(tied)
        from_x, from_y, extra = in_order(from_x, from_y, extra)
    next_y = (keep[0].astype(F32) + from_x[1].astype(F32)).astype(BF16)
    next_x = (keep[1].astype(F32) + from_y[1].astype(F32)).astype(BF16)
    last_y = permute_row(next_y, Y_PAIRS)
    last_x = permute_row(next_x, X_PAIRS)
    first_half = own[0] + from_x[0].astype(F32) + last_y.astype(F32)
    second_half = own[1] + from_y[0].astype(F32) + last_x.astype(F32)
    return jnp.concatenate([first_half, second_half], axis=0), extra


def gather_row(value, between=None, later=None):
    if lax.axis_size("row") != 4:
        gathered = lax.all_gather(value, "row", axis=1, tiled=True)
        if later is not None:
            return gathered, later[0](later[1])
        return gathered, between() if between else None
    half = value.shape[0] // 2
    from_x = permute_row(value, X_PAIRS)
    from_y = permute_row(value, Y_PAIRS)
    extra = None
    if between is not None:
        extra = between()
        from_x, from_y, extra = in_order(from_x, from_y, extra)
    if later is not None:
        from_x, from_y, argument = in_order(from_x, from_y, later[1])
    far_a = permute_row(from_x[:half], Y_PAIRS)
    far_b = permute_row(from_y[half:], X_PAIRS)
    if later is not None:
        extra = later[0](argument)
        far_a, far_b, extra = in_order(far_a, far_b, extra)
    return (value, from_x, from_y, far_a, far_b), extra


def gather_row_small(value):
    if lax.axis_size("row") != 4:
        return lax.all_gather(value, "row", axis=1, tiled=True)
    row = lax.axis_index("row")
    pieces = jnp.stack(
        [value] + [permute_row(value, pairs) for pairs in (X_PAIRS, Y_PAIRS, D_PAIRS)]
    )
    ordered = [
        lax.dynamic_index_in_dim(pieces, row ^ place, 0, keepdims=False) for place in range(4)
    ]
    return jnp.concatenate(ordered, axis=1)


def sum_row_direct(value):
    if lax.axis_size("row") != 4:
        return lax.psum(value, "row")
    others = [permute_row(value, pairs) for pairs in (X_PAIRS, Y_PAIRS, D_PAIRS)]
    return value + others[0] + (others[1] + others[2])


def norm_backward(grad_out, normal, inverse, gain_vector, sums=None):
    scaled = grad_out * gain_vector
    if sums is None:
        sums = sum_row_direct(
            jnp.stack([jnp.sum(scaled, axis=1), jnp.sum(scaled * normal, axis=1)])
        )
    means = sums / D
    grad_in = inverse * (scaled - means[0][:, None] - normal * means[1][:, None])
    return (grad_in, jnp.sum(grad_out * normal, axis=0), jnp.sum(grad_out, axis=0))


def gather_col(weight):
    return lax.all_gather(weight, "col", axis=0, tiled=True)


def scatter_col(grad):
    if grad.ndim == 2:
        return lax.psum_scatter(grad, "col", scatter_dimension=0, tiled=True).astype(F32)
    groups = [list(range(core, SLOTS, 2)) for core in range(2)]
    total = lax.psum_scatter(grad, "col", scatter_dimension=0, axis_index_groups=groups)
    return total.astype(F32)


class Exchange:
    def __init__(self, messages, send_sem, recv_sem):
        col = lax.axis_index("col")
        self.base = (col // SLOTS) * SLOTS
        self.place = col % SLOTS
        self.messages, self.send_sem, self.recv_sem = messages, send_sem, recv_sem

    def copy(self, index):
        _, target, source, destination = self.messages[index]
        return pltpu.make_async_remote_copy(
            src_ref=source,
            dst_ref=destination,
            send_sem=self.send_sem.at[index],
            recv_sem=self.recv_sem.at[index],
            device_id={"col": self.base + target},
            device_id_type=pl.DeviceIdType.MESH,
        )

    def greet(self):
        barrier = pltpu.get_barrier_semaphore()
        for step in range(1, SLOTS):
            other = self.base + (self.place + step) % SLOTS
            pl.semaphore_signal(
                barrier, inc=1, device_id={"col": other}, device_id_type=pl.DeviceIdType.MESH
            )
        pl.semaphore_wait(barrier, SLOTS - 1)

    def run(self, programs, drain=True):
        for place, program in enumerate(programs):
            if not program:
                continue

            @pl.when(self.place == place)
            def _():
                for action in program:
                    if callable(action):
                        action()
                    elif action >= 0:
                        self.copy(action).start()
                    else:
                        self.copy(~action).wait_recv()

        if drain:
            self.drain()

    def drain(self):
        for place in range(SLOTS):
            mine = [i for i, message in enumerate(self.messages) if message[0] == place]
            if mine:

                @pl.when(self.place == place)
                def _():
                    for index in mine:
                        self.copy(index).wait_send()


def scaled_add(meta, rates, target, terms, rows):
    heads = target.shape[0]
    strip = 64
    for head in range(heads):

        def add(index, _):
            spot = pl.ds(pl.multiple_of(index * strip, strip), strip)
            total = None
            for term in terms:
                if isinstance(term, tuple):
                    ref, slot = term
                    exponent = jnp.maximum(
                        trunk_reference(meta, jnp.int32(3), rows)
                        - trunk_reference(meta, jnp.int32(slot), rows),
                        0,
                    )
                    value = ref[head, spot, :].astype(F32) * power(rates[head], exponent, HV)
                else:
                    value = term[head, spot, :].astype(F32)
                total = value if total is None else total + value
            target[head, spot, :] = total.astype(BF16)
            return 0

        lax.fori_loop(0, QK // strip, add, 0)


def share_kernel(rows, meta, rates, ex, sh, shift, tot, send_sem, recv_sem):
    messages = [
        (0, 2, ex.at[0], sh.at[0]),
        (0, 1, ex.at[0], sh.at[0]),
        (1, 3, ex.at[0], sh.at[1]),
        (2, 3, ex.at[0], sh.at[2]),
        (2, 3, sh.at[0], sh.at[0]),
        (3, 2, sh.at[1], sh.at[1]),
        (3, 4, ex.at[1], sh.at[4]),
        (3, 5, ex.at[2], sh.at[5]),
        (3, 4, tot, sh.at[3]),
        (4, 5, ex.at[1], sh.at[6]),
        (4, 6, ex.at[1], sh.at[6]),
        (4, 5, ex.at[2], sh.at[7]),
        (5, 7, sh.at[7], sh.at[7]),
        (4, 5, sh.at[4], sh.at[4]),
        (4, 6, sh.at[4], sh.at[4]),
        (5, 4, sh.at[5], sh.at[5]),
        (5, 7, sh.at[5], sh.at[5]),
        (4, 5, sh.at[3], sh.at[3]),
        (4, 6, sh.at[3], sh.at[3]),
        (6, 7, sh.at[6], sh.at[6]),
        (6, 7, sh.at[4], sh.at[4]),
        (6, 7, sh.at[3], sh.at[3]),
        (7, 6, sh.at[7], sh.at[7]),
        (7, 6, sh.at[5], sh.at[5]),
        (4, 5, ex.at[0], shift),
        (6, 7, ex.at[0], shift),
    ]
    exchange = Exchange(messages, send_sem, recv_sem)

    def keep_trunk():
        sh[3] = ex[0]

    def total_trunk():
        terms = [(sh.at[slot], slot) for slot in range(3)] + [ex.at[0]]
        scaled_add(meta, rates, tot, terms, rows)

    def keep_branches():
        sh[6] = ex[1]
        sh[7] = ex[2]

    exchange.greet()
    exchange.run(
        [
            [0, 1],
            [2, ~1],
            [3, ~0, 4, ~5],
            [6, 7, keep_trunk, ~2, 5, ~4, ~3, total_trunk, 8],
            [10, 11, 9, 24, keep_branches, ~6, 14, 13, ~15, ~8, 18, 17],
            [~11, 12, ~7, 16, 15, ~9, ~24, ~13, ~17],
            [25, ~10, 19, ~14, 20, ~22, ~23, ~18, 21],
            [~12, 22, ~16, 23, ~19, ~20, ~25, ~21],
        ]
    )


def vmem():
    return pl.BlockSpec(memory_space=pltpu.VMEM)


def share_states(meta, rates, exports, rows):
    heads = exports.shape[1]
    state = (heads, QK, HV)
    return pl.pallas_call(
        functools.partial(share_kernel, rows),
        in_specs=[smem(), smem(), vmem()],
        out_specs=[vmem(), vmem()],
        out_shape=[
            jax.ShapeDtypeStruct((SLOTS,) + state, BF16),
            jax.ShapeDtypeStruct(state, BF16),
        ],
        scratch_shapes=[
            pltpu.VMEM(state, BF16),
            pltpu.SemaphoreType.DMA((26,)),
            pltpu.SemaphoreType.DMA((26,)),
        ],
        compiler_params=pltpu.CompilerParams(
            collective_id=1, has_side_effects=True, vmem_limit_bytes=40 * 1024 * 1024
        ),
        name="share_states",
        cost_estimate=pl.CostEstimate(
            flops=0, bytes_accessed=100 * 1024 * 1024, transcendentals=0
        ),
    )(meta, rates, exports)


def return_kernel(
    rows, meta, rates, y, first, left, right, own0, own1, own2, grads, rx, tx, send_sem, recv_sem
):
    messages = [
        (7, 6, y.at[3], rx.at[0]),
        (7, 6, y.at[4], rx.at[1]),
        (7, 6, y.at[5], rx.at[2]),
        (6, 7, y.at[6], rx.at[0]),
        (6, 7, y.at[7], rx.at[1]),
        (7, 5, tx.at[0], rx.at[0]),
        (7, 5, tx.at[1], rx.at[1]),
        (6, 4, tx.at[0], rx.at[0]),
        (6, 4, tx.at[1], rx.at[1]),
        (6, 4, tx.at[2], rx.at[2]),
        (5, 4, y.at[3], rx.at[3]),
        (5, 4, y.at[4], rx.at[4]),
        (5, 4, y.at[5], rx.at[5]),
        (5, 4, tx.at[0], rx.at[6]),
        (5, 4, tx.at[1], rx.at[7]),
        (4, 3, tx.at[0], rx.at[0]),
        (4, 3, tx.at[1], own1),
        (4, 3, tx.at[2], own2),
        (2, 3, y.at[0], rx.at[1]),
        (2, 3, y.at[1], rx.at[2]),
        (3, 2, tx.at[2], own0),
        (3, 1, tx.at[1], own0),
        (3, 0, tx.at[0], rx.at[0]),
        (1, 0, y.at[0], rx.at[1]),
        (5, 4, first, own0),
        (7, 6, first, own0),
    ]
    exchange = Exchange(messages, send_sem, recv_sem)

    def add(target, *terms):
        return lambda: scaled_add(meta, rates, target, terms, rows)

    def multiply(begin, end):
        def tile(index, _):
            spot = pl.ds(pl.multiple_of(index * GRAD_TILE, GRAD_TILE), GRAD_TILE)
            grads[spot, :] = mm_tn(left[:, spot], right[...]).astype(BF16)
            return 0

        lax.fori_loop(begin, end, tile, 0)

    tiles = D // GRAD_TILE
    exchange.greet()
    exchange.run([[], [23], [18, 19], [], [], [10, 11, 12, 24], [3, 4], [0, 1, 2, 25]], False)
    multiply(0, tiles // 2)
    exchange.run(
        [
            [],
            [],
            [],
            [],
            [
                ~10, ~7, add(tx.at[0], y.at[3], rx.at[0], rx.at[3]), 15,
                ~11, ~8, add(tx.at[1], y.at[4], rx.at[1], rx.at[4]), 16,
                ~12, ~9, add(tx.at[2], y.at[5], rx.at[2], rx.at[5]), 17,
                ~13, add(own1, y.at[6], rx.at[6]),
                ~14, add(own2, y.at[7], rx.at[7]),
                ~24,
            ],
            [
                ~5, add(tx.at[0], y.at[6], rx.at[0]), 13,
                ~6, add(tx.at[1], y.at[7], rx.at[1]), 14,
            ],
            [
                ~0, add(tx.at[0], y.at[3], rx.at[0]), 7,
                ~1, add(tx.at[1], y.at[4], rx.at[1]), 8,
                ~2, add(tx.at[2], y.at[5], rx.at[2]), 9,
                ~25,
            ],
            [
                ~3, add(tx.at[0], y.at[6], rx.at[0]), 5,
                ~4, add(tx.at[1], y.at[7], rx.at[1]), 6,
            ],
        ],
        False,
    )
    multiply(tiles // 2, tiles)
    exchange.run(
        [
            [~23, ~22, add(own0, rx.at[0], rx.at[1])],
            [~21],
            [~20],
            [
                ~18, ~19, ~15,
                add(tx.at[0], y.at[0], rx.at[1], (rx.at[0], 0)), 22,
                add(tx.at[1], y.at[1], rx.at[2], (rx.at[0], 1)), 21,
                add(tx.at[2], y.at[2], (rx.at[0], 2)), 20,
                add(own0, rx.at[0], y.at[3]),
                ~16, ~17,
            ],
            [],
            [],
            [],
            [],
        ],
        False,
    )
    exchange.drain()


def return_states(meta, rates, exports, first_state, left, right, rows):
    heads = exports.shape[1]
    state = (heads, QK, HV)
    return pl.pallas_call(
        functools.partial(return_kernel, rows),
        in_specs=[smem(), smem(), vmem(), vmem(), vmem(), vmem()],
        out_specs=[vmem()] * 4,
        out_shape=[jax.ShapeDtypeStruct(state, BF16)] * 3
        + [jax.ShapeDtypeStruct((D, right.shape[1]), BF16)],
        scratch_shapes=[
            pltpu.VMEM((8,) + state, BF16),
            pltpu.VMEM((3,) + state, BF16),
            pltpu.SemaphoreType.DMA((26,)),
            pltpu.SemaphoreType.DMA((26,)),
        ],
        compiler_params=pltpu.CompilerParams(
            collective_id=2, has_side_effects=True, vmem_limit_bytes=40 * 1024 * 1024
        ),
        name="return_states",
        cost_estimate=pl.CostEstimate(
            flops=0, bytes_accessed=100 * 1024 * 1024, transcendentals=0
        ),
    )(meta, rates, exports, first_state, left, right)


def sum_col(value):
    size = lax.axis_size("col")
    if size != SLOTS:
        return lax.psum(value, "col")
    for flip in (1, 2, 4):
        value = value + lax.ppermute(value, "col", [(a, a ^ flip) for a in range(size)])
    return value


def sum_col_vectors(vectors, extra=None):
    col = lax.axis_index("col")
    size = lax.axis_size("col")
    parts = list(vectors) + ([extra] if extra is not None else [])
    total = sum_col(jnp.concatenate(parts).reshape(-1, 128)).reshape(-1)
    results, first = [], 0
    for vector in vectors:
        width = vector.shape[0] // size
        results.append(lax.dynamic_slice_in_dim(total, first + col * width, width, 0))
        first += vector.shape[0]
    return results, total[first:]


def token_tables(place, rows, lengths, parents):
    index = place * rows + jnp.arange(rows, dtype=jnp.int32)
    in_trunk = index < TRUNK
    beyond = jnp.maximum(index - TRUNK, 0)
    segment = jnp.where(in_trunk, 0, 1 + beyond // SEG)
    position = jnp.where(in_trunk, index, beyond % SEG)

    def lookup(table, spots):
        hits = spots[:, None] == jnp.arange(table.shape[0], dtype=jnp.int32)
        return jnp.sum(jnp.where(hits, table, 0), axis=1)

    branch = 1 + lookup(parents, jnp.clip(segment - 5, 0, 7))
    parent_length = lookup(lengths, branch)
    depth = position + jnp.where(segment >= 1, lengths[0], 0)
    depth = depth + jnp.where(segment >= 5, parent_length, 0)
    valid = (position < lookup(lengths, segment)).astype(F32)
    half = QK // 2
    frequency = 10000.0 ** (-jnp.arange(half, dtype=F32) / (half - 1))
    angles = depth.astype(F32)[:, None] * frequency[None, :]
    return valid, jnp.cos(angles), jnp.sin(angles)


def body(
    tokens,
    cotangent,
    query_weight,
    key_weight,
    value_weight,
    gate_weight,
    out_weight,
    up_weight,
    down_weight,
    first_gain,
    first_bias,
    group_gain,
    group_bias,
    second_gain,
    second_bias,
    up_bias,
    down_bias,
    segment_lengths,
    leaf_parents,
):
    rows = tokens.shape[0]
    col = lax.axis_index("col")
    row = lax.axis_index("row")
    row_ref = row.astype(jnp.int32)[None]
    place = (col % SLOTS).astype(jnp.int32)
    tree = (col // SLOTS).astype(jnp.int32)
    lengths = lax.dynamic_index_in_dim(segment_lengths, tree, 0, keepdims=False)
    parents = lax.dynamic_index_in_dim(leaf_parents, tree, 0, keepdims=False)
    meta = jnp.concatenate([lengths, parents, place[None]]).astype(jnp.int32)
    heads = query_weight.shape[1] // QK
    head_numbers = (row * heads + jnp.arange(heads, dtype=jnp.int32)).astype(F32)
    rates = jnp.log(1.0 - 2.0 ** (-5.0 - head_numbers))

    wide = heads * HV
    narrow = heads * QK
    project_full = gather_col(jnp.concatenate([query_weight, key_weight, value_weight], axis=1))
    gate_full = gather_col(gate_weight)
    out_full = gather_col(out_weight.T)
    feed_full = gather_col(jnp.concatenate([down_weight.T, up_weight], axis=1))
    query_part, key_part = (project_full, narrow, 0), (project_full, narrow, 1)
    value_part = (project_full, wide, 1)
    out_part = (out_full, wide, 0)
    down_part, up_part = (feed_full, wide, 0), (feed_full, wide, 1)

    valid, cosine, sine = token_tables(place, rows, lengths, parents)
    column = valid[:, None]
    gains = gather_row_small(jnp.stack([first_gain, first_bias, second_gain, second_bias]))
    token_pieces, _ = gather_row(tokens)
    first_wide, first_average, first_inverse = join(token_pieces, row_ref, gains[0], gains[1])
    fed_low = (cotangent.astype(F32) * column).astype(BF16)
    fed_low, first_average = lax.optimization_barrier((fed_low, first_average))

    fed_pieces, projected = gather_row(
        fed_low, lambda: project(meta, rates, first_wide, project_full, cosine, sine)
    )
    query_rot, key_rot, value_low, exports = projected
    shared, shifted = share_states(meta, rates, exports, rows)
    gate_full, shared = in_order(gate_full, shared)
    gate_part = (gate_full, wide, 0)
    gate_full, fed_pieces = in_order(gate_full, fed_pieces)
    gate_part = (gate_full, wide, 0)
    gate_raw, gated, normal, inverse, states = retain(
        meta, rates, query_rot, key_rot, value_low, first_wide, gate_part, shared, shifted,
        group_gain, group_bias,
    )

    sends = reduce_row_start([gated], [out_part], row_ref)
    attended, _ = reduce_row_finish(sends, [gated], [out_part], row_ref)
    middle = tokens.astype(F32) + attended

    def feed_gradient(pieces):
        joined = join(pieces, row_ref)
        return joined, matmul(joined, down_part, BF16)

    middle_pieces, (fed_wide, grad_hidden) = gather_row(
        middle.astype(BF16), later=(feed_gradient, fed_pieces)
    )
    second_wide, second_average, second_inverse, hidden, grad_before, up_bias_grad, feed_sums = (
        feed_up(middle_pieces, row_ref, gains[2], gains[3], up_part, up_bias, grad_hidden)
    )
    feed_sums = sum_row_direct(feed_sums[:, :2].T)
    sends = reduce_row_start([grad_before], [up_part], row_ref)
    sends, hidden = in_order(sends, hidden)
    second_back, feed_partial = reduce_row_finish(
        sends,
        [grad_before],
        [up_part],
        row_ref,
        lambda hidden: weight_grads([(fed_wide, hidden), (second_wide, grad_before)]),
        hidden,
    )
    feed_grad = scatter_col(feed_partial)
    grad_fed = fed_low.astype(F32)
    down_bias_grad = jnp.sum(grad_fed, axis=0)

    second_normal = (middle - second_average[:, :1]) * second_inverse[:, :1]
    grad_middle_norm, second_gain_grad, second_bias_grad = norm_backward(
        second_back, second_normal, second_inverse[:, :1], second_gain, feed_sums
    )
    grad_middle = grad_fed + grad_middle_norm
    grad_pieces, (fed_sends, fed_rest) = gather_row(
        grad_middle.astype(BF16),
        lambda: (
            reduce_row_start([hidden], [down_part], row_ref),
            reduce_row_rest([hidden], [down_part], row_ref),
        ),
    )
    grad_wide = join(grad_pieces, row_ref)
    fed_sends, grad_wide = in_order(fed_sends, grad_wide)
    out_partial = column_grads([(grad_wide, gated)], 4)
    out_partial, grad_wide = in_order(out_partial, grad_wide)
    out_partial, feed_grad = in_order(out_partial, feed_grad)
    out_grad = scatter_col(out_partial)
    fed_out, gate_results = reduce_row_finish(
        fed_sends,
        [hidden],
        [down_part],
        row_ref,
        lambda _: tuple(
            gate_back(
                meta, rates, grad_wide, out_part, gate_raw, normal, inverse, query_rot, group_gain, group_bias
            )
        ),
        rest=fed_rest,
    )
    fed_out = fed_out + down_bias
    layer_out = middle + fed_out
    grad_gate, grad_retained, group_gain_grad, group_bias_grad, returns, first_state = gate_results
    own0, own1, own2, gate_partial = return_states(
        meta, rates, returns, first_state, first_wide, grad_gate, rows
    )
    gate_partial, own0, out_grad = in_order(gate_partial, own0, out_grad)
    own = (own0, own1, own2)
    gate_grad = scatter_col(gate_partial)
    grad_query, grad_key, grad_value = retain_back(
        meta, rates, query_rot, key_rot, value_low, grad_retained, states, cosine, sine, own
    )
    back_values = [grad_query, grad_key, grad_value, grad_gate]
    back_weights = [query_part, key_part, value_part, gate_part]
    sends = reduce_row_start(back_values, back_weights, row_ref)
    sends, grad_value = in_order(sends, grad_value)
    first_back, project_partial = reduce_row_finish(
        sends,
        back_values,
        back_weights,
        row_ref,
        lambda _: column_grads(
            [(first_wide, grad_query), (first_wide, grad_key), (first_wide, grad_value)], 6
        ),
    )
    project_partial, gate_grad = in_order(project_partial, gate_grad)
    project_grad = scatter_col(project_partial)

    first_normal = (tokens.astype(F32) - first_average[:, :1]) * first_inverse[:, :1]
    grad_first, first_gain_grad, first_bias_grad = norm_backward(
        first_back, first_normal, first_inverse[:, :1], first_gain
    )
    tokens_grad = grad_middle + grad_first

    squares = jnp.stack(
        [
            jnp.sum(column * layer_out * layer_out),
            jnp.sum(column * attended * attended),
            jnp.sum(column * fed_out * fed_out),
        ]
    )
    vectors, col_squares = sum_col_vectors(
        (
            first_gain_grad,
            first_bias_grad,
            group_gain_grad[0],
            group_bias_grad[0],
            second_gain_grad,
            second_bias_grad,
            up_bias_grad[0],
            down_bias_grad,
        ),
        jnp.concatenate([squares, jnp.zeros((125,), F32)]),
    )
    totals = sum_row_direct(col_squares[None, :])[0, :3]
    valid_count = jnp.sum(segment_lengths).astype(F32) * D
    norm_values = jnp.sqrt(totals / valid_count)
    return (
        layer_out.astype(BF16),
        tokens_grad,
        project_grad[:, :narrow],
        project_grad[:, narrow : 2 * narrow],
        project_grad[:, 2 * narrow :],
        gate_grad,
        out_grad.T,
        feed_grad[:, wide:],
        feed_grad[:, :wide].T,
        *vectors,
        norm_values,
    )


def solution(mesh):
    matrix, turned, vector = P("col", "row"), P("row", "col"), P("row")
    in_specs = (matrix,) * 6 + (turned, matrix, turned) + (vector,) * 8 + (P(), P())
    split = P(("row", "col"))
    out_specs = (matrix,) * 6 + (turned, matrix, turned) + (split,) * 8 + (P(),)
    return jax.shard_map(body, mesh=mesh, in_specs=in_specs, out_specs=out_specs, check_vma=False)
```

```python
import functools

import jax
import jax.numpy as jnp
from jax import lax
from jax.experimental import pallas as pl
from jax.experimental.pallas import tpu as pltpu
from jax.sharding import PartitionSpec as P

D = 2048
QK = 256
HV = 512
TRUNK = 4096
SEG = 512
TREE_LEN = TRUNK + 12 * SEG
CHUNK = 256
TRUNK_CHUNKS = TRUNK // CHUNK
SLOTS = 8
GRAD_TILE = 256

EPSILON = 1e-05
SCALE = QK**-0.5
F32 = jnp.float32
BF16 = jnp.bfloat16

X_PAIRS = [(0, 1), (1, 0), (2, 3), (3, 2)]
Y_PAIRS = [(0, 2), (2, 0), (1, 3), (3, 1)]
D_PAIRS = [(0, 3), (3, 0), (1, 2), (2, 1)]


def mm(a, b):
    return lax.dot_general(a, b, (((1,), (0,)), ((), ())), preferred_element_type=F32)


def mm_nt(a, b):
    return lax.dot_general(a, b, (((1,), (1,)), ((), ())), preferred_element_type=F32)


def mm_tn(a, b):
    return lax.dot_general(a, b, (((0,), (0,)), ((), ())), preferred_element_type=F32)


def params(semantics, limit=None):
    return pltpu.CompilerParams(
        dimension_semantics=semantics, vmem_limit_bytes=limit or 60 * 1024 * 1024
    )


def smem():
    return pl.BlockSpec(memory_space=pltpu.SMEM)


class Chunk:
    def __init__(self, meta, index):
        in_trunk = index < TRUNK_CHUNKS
        beyond = jnp.maximum(index - TRUNK_CHUNKS, 0)
        self.in_trunk = in_trunk
        self.segment = jnp.where(in_trunk, 0, 1 + beyond // 2)
        self.first = jnp.where(in_trunk, index * CHUNK, (beyond % 2) * CHUNK)
        length = meta[self.segment]
        trunk_length = meta[0]
        self.trunk_length = trunk_length
        self.length = length
        self.is_leaf = self.segment >= 5
        self.parent = meta[13 + jnp.clip(self.segment - 5, 0, 7)]
        parent_length = meta[1 + self.parent]
        self.start = jnp.where(
            in_trunk,
            self.first,
            trunk_length + self.first + jnp.where(self.is_leaf, parent_length, 0),
        )
        self.count = jnp.clip(length - self.first, 0, CHUNK)
        self.end = self.start + self.count
        self.continues = jnp.where(in_trunk, index + 1 < TRUNK_CHUNKS, beyond % 2 == 0)


def trunk_reference(meta, place, rows):
    return jnp.minimum(meta[0], jnp.minimum(rows * (place + 1), TRUNK))


def power(rate, exponent, width):
    return jnp.exp(jnp.full((1, width), exponent.astype(F32), F32) * rate)


def column_power(rate, exponents):
    return jnp.exp(exponents.astype(F32) * rate)


def token_column(width=1):
    return lax.broadcasted_iota(jnp.int32, (CHUNK, width), 0)


def decay_matrix(rate):
    t = lax.broadcasted_iota(jnp.int32, (CHUNK, CHUNK), 0)
    u = lax.broadcasted_iota(jnp.int32, (CHUNK, CHUNK), 1)
    return jnp.where(u <= t, jnp.exp((t - u).astype(F32) * rate) * SCALE, 0.0)


def valid_decay(decay, count):
    u = lax.broadcasted_iota(jnp.int32, (1, CHUNK), 1)
    return decay[...] * jnp.where(u < count, 1.0, 0.0)


def key_decay(rate, count):
    j = token_column()
    return jnp.where(j < count, column_power(rate, jnp.maximum(count - j, 0)), 0.0)


def export_terms(meta, chunk, local, chunks, place, slot, rows):
    if slot == 0:
        is_shift = ((place == 4) | (place == 6)) & (local == chunks - 1)
        exponent = jnp.where(
            chunk.in_trunk,
            jnp.maximum(trunk_reference(meta, place, rows) - chunk.end, 0),
            0,
        )
        return chunk.in_trunk | is_shift, exponent
    wanted = (place == 3) | (place == 4)
    mine = (chunk.segment % 2 == 1) if slot == 1 else (chunk.segment % 2 == 0)
    is_branch = (chunk.segment >= 1) & (chunk.segment < 5)
    exponent = jnp.where(is_branch, jnp.maximum(chunk.length - chunk.first - chunk.count, 0), 0)
    return wanted & mine & is_branch, exponent


def import_terms(meta, chunk, place, slot, rows):
    if slot < 4:
        sees = jnp.logical_not(chunk.in_trunk) | (place > slot)
        if slot < 3:
            sees = sees & (place < 4)
        return sees, jnp.maximum(chunk.start - trunk_reference(meta, jnp.int32(slot), rows), 0)
    sees = chunk.is_leaf & (chunk.parent == slot - 4)
    return sees, chunk.first


def shift_in(meta, place, chunks):
    previous = Chunk(meta, jnp.maximum(place * chunks - 1, 0))
    return (place == 5) | (place == 7), CHUNK - previous.count


def retain_kernel(
    rows, chunks, meta, rates, query, key, value, wide, weight, shared, shifted, gain, bias,
    gate_out, gated_out, normal_out, inverse_out, state_out, running, total, decay,
):
    local = pl.program_id(1)
    rate = rates[pl.program_id(0)]
    place = meta[21]
    chunk = Chunk(meta, place * chunks + local)

    @pl.when(local == 0)
    def _():
        decay[...] = decay_matrix(rate)
        running[...] = jnp.zeros_like(running)
        on, exponent = shift_in(meta, place, chunks)

        @pl.when(on)
        def _():
            running[...] = shifted[0].astype(F32) * power(rate, exponent, HV)

    incoming = running[...]
    total[...] = incoming
    for slot in range(SLOTS):
        on, exponent = import_terms(meta, chunk, place, slot, rows)

        @pl.when(on)
        def _():
            total[...] += shared[slot, 0].astype(F32) * power(rate, exponent, HV)

    state = total[...].astype(BF16)
    state_out[0, 0] = state

    q, k, v = query[...], key[...], value[...]
    scores = (mm_nt(q, k) * valid_decay(decay, chunk.count)).astype(BF16)
    own = token_column()
    reach = column_power(rate, own) * SCALE
    retained = mm(scores, v) + mm(q, state) * reach

    j = token_column()
    ahead = jnp.where(j < chunk.count, column_power(rate, CHUNK - j), 0.0)
    fresh = mm_tn((k.astype(F32) * ahead).astype(BF16), v)
    keep = jnp.where(chunk.continues, 1.0, 0.0)
    running[...] = (incoming * power(rate, jnp.int32(CHUNK), HV) + fresh) * keep

    average = jnp.mean(retained, axis=1, keepdims=True)
    centred = retained - average
    inverse = lax.rsqrt(jnp.mean(centred * centred, axis=1, keepdims=True) + EPSILON)
    normal = centred * inverse
    gate_value = mm(wide[...], weight[...])
    gate_out[...] = gate_value
    gated = (normal * gain[...] + bias[...]) * (gate_value / (1.0 + jnp.exp(-gate_value)))
    gated_out[...] = gated.astype(BF16)
    normal_out[...] = normal.astype(BF16)
    inverse_out[0] = jnp.broadcast_to(inverse, (CHUNK, 128))


def retain(meta, rates, query, key, value, inputs, weight, shared, shifted, gain, bias):
    array, _, number = weight
    rows = key.shape[0]
    heads = key.shape[1] // QK
    chunks = rows // CHUNK
    wide = pl.BlockSpec((CHUNK, HV), lambda h, c: (c, h))
    narrow = pl.BlockSpec((CHUNK, QK), lambda h, c: (c, h))
    vector = pl.BlockSpec((1, HV), lambda h, c: (0, h))
    return pl.pallas_call(
        functools.partial(retain_kernel, rows, chunks),
        grid=(heads, chunks),
        in_specs=[
            smem(), smem(), narrow, narrow, wide,
            pl.BlockSpec((CHUNK, D), lambda h, c: (c, 0)),
            pl.BlockSpec((D, HV), lambda h, c: (0, number * heads + h)),
            pl.BlockSpec((SLOTS, 1, QK, HV), lambda h, c: (0, h, 0, 0)),
            pl.BlockSpec((1, QK, HV), lambda h, c: (h, 0, 0)),
            vector, vector,
        ],
        out_specs=[
            wide, wide, wide,
            pl.BlockSpec((1, CHUNK, 128), lambda h, c: (h, c, 0)),
            pl.BlockSpec((1, 1, QK, HV), lambda h, c: (h, c, 0, 0)),
        ],
        out_shape=[
            jax.ShapeDtypeStruct((rows, heads * HV), F32),
            jax.ShapeDtypeStruct((rows, heads * HV), BF16),
            jax.ShapeDtypeStruct((rows, heads * HV), BF16),
            jax.ShapeDtypeStruct((heads, rows, 128), F32),
            jax.ShapeDtypeStruct((heads, chunks, QK, HV), BF16),
        ],
        scratch_shapes=[
            pltpu.VMEM((QK, HV), F32), pltpu.VMEM((QK, HV), F32), pltpu.VMEM((CHUNK, CHUNK), F32)
        ],
        compiler_params=params(("arbitrary", "arbitrary")),
        name="retention_forward",
        cost_estimate=pl.CostEstimate(
            flops=2 * rows * heads * (CHUNK * 768 + 2 * QK * HV + D * HV),
            bytes_accessed=rows * heads * 8192,
            transcendentals=rows * heads * 768,
        ),
    )(meta, rates, query, key, value, inputs, array, shared, shifted, gain[None, :], bias[None, :])


def gate_back_kernel(
    rows, chunks, meta, rates, wide, weight, gate, normal_in, inverse_in, query, gain, bias,
    gate_out, retained_out, gain_out, bias_out, exports, first_out, acc,
):
    local = pl.program_id(1)
    rate = rates[pl.program_id(0)]
    place = meta[21]
    chunk = Chunk(meta, place * chunks + local)
    grad_gated = mm(wide[...], weight[...])
    gate_value = gate[...].astype(F32)
    normal = normal_in[...].astype(F32)
    sigmoid = 1.0 / (1.0 + jnp.exp(-gate_value))
    normed = normal * gain[...] + bias[...]
    grad_gate = grad_gated * normed * (sigmoid * (1.0 + gate_value * (1.0 - sigmoid)))
    gate_out[...] = grad_gate.astype(BF16)
    grad_normed = grad_gated * (gate_value * sigmoid)

    @pl.when(local == 0)
    def _():
        gain_out[...] = jnp.zeros_like(gain_out)
        bias_out[...] = jnp.zeros_like(bias_out)
        acc[...] = jnp.zeros_like(acc)

    gain_out[...] += jnp.sum(grad_normed * normal, axis=0, keepdims=True)
    bias_out[...] += jnp.sum(grad_normed, axis=0, keepdims=True)
    scaled = grad_normed * gain[...]
    grad = inverse_in[0][:, :1] * (
        scaled
        - jnp.mean(scaled, axis=1, keepdims=True)
        - normal * jnp.mean(scaled * normal, axis=1, keepdims=True)
    )
    grad = grad.astype(BF16)
    retained_out[...] = grad
    reach = column_power(rate, token_column()) * SCALE
    state = mm_tn((query[...].astype(F32) * reach).astype(BF16), grad)
    for slot in range(SLOTS):
        on, exponent = import_terms(meta, chunk, place, slot, rows)

        @pl.when(on)
        def _():
            acc[slot] += state * power(rate, exponent, HV)

    @pl.when(local == 0)
    def _():
        on, exponent = shift_in(meta, place, chunks)
        scale = jnp.where(on, power(rate, exponent, HV), 0.0)
        first_out[0] = (state * scale).astype(BF16)

    @pl.when(local == chunks - 1)
    def _():
        exports[:, 0] = acc[...].astype(BF16)


def gate_back(meta, rates, wide, weight, gate, normal, inverse, query, gain, bias):
    array, width, number = weight
    first = number * (width // HV)
    rows = query.shape[0]
    heads = query.shape[1] // QK
    chunks = rows // CHUNK
    block = pl.BlockSpec((CHUNK, HV), lambda h, c: (c, h))
    vector = pl.BlockSpec((1, HV), lambda h, c: (0, h))
    return pl.pallas_call(
        functools.partial(gate_back_kernel, rows, chunks),
        grid=(heads, chunks),
        in_specs=[
            smem(), smem(),
            pl.BlockSpec((CHUNK, D), lambda h, c: (c, 0)),
            pl.BlockSpec((D, HV), lambda h, c: (0, first + h)),
            block, block,
            pl.BlockSpec((1, CHUNK, 128), lambda h, c: (h, c, 0)),
            pl.BlockSpec((CHUNK, QK), lambda h, c: (c, h)),
            vector, vector,
        ],
        out_specs=[
            block, block, vector, vector,
            pl.BlockSpec((SLOTS, 1, QK, HV), lambda h, c: (0, h, 0, 0)),
            pl.BlockSpec((1, QK, HV), lambda h, c: (h, 0, 0)),
        ],
        out_shape=[
            jax.ShapeDtypeStruct((rows, heads * HV), BF16),
            jax.ShapeDtypeStruct((rows, heads * HV), BF16),
            jax.ShapeDtypeStruct((1, heads * HV), F32),
            jax.ShapeDtypeStruct((1, heads * HV), F32),
            jax.ShapeDtypeStruct((SLOTS, heads, QK, HV), BF16),
            jax.ShapeDtypeStruct((heads, QK, HV), BF16),
        ],
        scratch_shapes=[pltpu.VMEM((SLOTS, QK, HV), F32)],
        compiler_params=params(("arbitrary", "arbitrary")),
        name="gate_backward",
        cost_estimate=pl.CostEstimate(
            flops=2 * rows * heads * HV * (D + QK),
            bytes_accessed=rows * heads * 12288,
            transcendentals=rows * heads * HV,
        ),
    )(meta, rates, wide, array, gate, normal, inverse, query, gain[None, :], bias[None, :])


def retain_back_kernel(
    rows, chunks, meta, rates, query, key, value, grad, state_in, cosine, sine, own0, own1, own2,
    query_out, key_out, value_out, running, total_ref, decay_ref,
):
    step = pl.program_id(1)
    local = chunks - 1 - step
    rate = rates[pl.program_id(0)]
    place = meta[21]
    chunk = Chunk(meta, place * chunks + local)
    before = Chunk(meta, jnp.maximum(place * chunks + local - 1, 0))

    @pl.when(step == 0)
    def _():
        decay_ref[...] = decay_matrix(rate)
        running[...] = jnp.zeros_like(running)

    later = running[...]
    total_ref[...] = later
    for slot, ref in ((0, own0), (1, own1), (2, own2)):
        on, exponent = export_terms(meta, chunk, local, chunks, place, slot, rows)

        @pl.when(on)
        def _():
            total_ref[...] += ref[0].astype(F32) * power(rate, exponent, HV)

    total = total_ref[...].astype(BF16)

    q, k, v, g = query[...], key[...], value[...], grad[...]
    decay = valid_decay(decay_ref, chunk.count)
    scores = (mm_nt(q, k) * decay).astype(BF16)
    slopes = (mm_nt(g, v) * decay).astype(BF16)
    reach = column_power(rate, token_column()) * SCALE
    toward = key_decay(rate, chunk.count)
    grad_query = mm(slopes, k) + mm_nt(g, state_in[0, 0]) * reach
    grad_key = mm_tn(slopes, q) + mm_nt(v, total) * toward
    grad_value = mm_tn(scores, g) + mm(k, total) * toward
    value_out[...] = grad_value.astype(BF16)
    cos, sin = cosine[...], sine[...]
    half = QK // 2
    for out, val in ((query_out, grad_query), (key_out, grad_key)):
        a, b = val[:, :half], val[:, half:]
        out[:, :half] = (a * cos + b * sin).astype(BF16)
        out[:, half:] = (b * cos - a * sin).astype(BF16)

    fresh = mm_tn((q.astype(F32) * reach).astype(BF16), g)
    carried = fresh + later * power(rate, chunk.count, HV)
    keep = jnp.where((local > 0) & before.continues, 1.0, 0.0)
    running[...] = carried * power(rate, CHUNK - before.count, HV) * keep


def retain_back(meta, rates, query, key, value, grad, states, cosine, sine, own):
    rows = query.shape[0]
    heads = query.shape[1] // QK
    chunks = rows // CHUNK
    last = chunks - 1
    wide = pl.BlockSpec((CHUNK, HV), lambda h, s: (last - s, h))
    narrow = pl.BlockSpec((CHUNK, QK), lambda h, s: (last - s, h))
    table = pl.BlockSpec((CHUNK, QK // 2), lambda h, s: (last - s, 0))
    state = pl.BlockSpec((1, QK, HV), lambda h, s: (h, 0, 0))
    return pl.pallas_call(
        functools.partial(retain_back_kernel, rows, chunks),
        grid=(heads, chunks),
        in_specs=[
            smem(), smem(), narrow, narrow, wide, wide,
            pl.BlockSpec((1, 1, QK, HV), lambda h, s: (h, last - s, 0, 0)),
            table, table, state, state, state,
        ],
        out_specs=[narrow, narrow, wide],
        out_shape=[
            jax.ShapeDtypeStruct((rows, heads * QK), BF16),
            jax.ShapeDtypeStruct((rows, heads * QK), BF16),
            jax.ShapeDtypeStruct((rows, heads * HV), BF16),
        ],
        scratch_shapes=[
            pltpu.VMEM((QK, HV), F32), pltpu.VMEM((QK, HV), F32), pltpu.VMEM((CHUNK, CHUNK), F32)
        ],
        compiler_params=params(("arbitrary", "arbitrary")),
        name="retention_backward",
        cost_estimate=pl.CostEstimate(
            flops=2 * rows * heads * (CHUNK * 1792 + 4 * QK * HV),
            bytes_accessed=rows * heads * 6144,
            transcendentals=rows * heads * 256,
        ),
    )(meta, rates, query, key, value, grad, states, cosine, sine, *own)


def norm_kernel(values, gain, bias, out, average_out, inverse_out):
    x = values[...].astype(F32)
    average = jnp.mean(x, axis=1, keepdims=True)
    inverse = lax.rsqrt(jnp.mean(x * x, axis=1, keepdims=True) - average * average + EPSILON)
    out[...] = ((x - average) * inverse * gain[...] + bias[...]).astype(BF16)
    average_out[...] = jnp.broadcast_to(average, average_out.shape)
    inverse_out[...] = jnp.broadcast_to(inverse, inverse_out.shape)


def norm_wide(values, gain, bias):
    rows = values.shape[0]
    block = pl.BlockSpec((CHUNK, D), lambda i: (i, 0))
    vector = pl.BlockSpec((1, D), lambda i: (0, 0))
    stat = pl.BlockSpec((CHUNK, 128), lambda i: (i, 0))
    return pl.pallas_call(
        norm_kernel,
        grid=(rows // CHUNK,),
        in_specs=[block, vector, vector],
        out_specs=[block, stat, stat],
        out_shape=[
            jax.ShapeDtypeStruct((rows, D), BF16),
            jax.ShapeDtypeStruct((rows, 128), F32),
            jax.ShapeDtypeStruct((rows, 128), F32),
        ],
        compiler_params=params(("arbitrary",)),
        name="layer_norm",
        cost_estimate=pl.CostEstimate(
            flops=8 * rows * D, bytes_accessed=4 * rows * D, transcendentals=rows
        ),
    )(values, gain[None, :], bias[None, :])


def join_kernel(row, own, from_x, from_y, far_a, far_b, *refs, norm):
    block = own.shape[1]
    second = pl.program_id(0) >= pl.num_programs(0) // 2
    spots = [
        pl.ds(pl.multiple_of((row[0] ^ flip) * block, 128), block) for flip in range(4)
    ]
    pieces = [own[...], from_x[...], from_y[...], jnp.where(second, far_b[...], far_a[...])]
    if not norm:
        for spot, piece in zip(spots, pieces):
            refs[0][:, spot] = piece
        return
    gain, bias, out, average_out, inverse_out = refs
    pieces = [piece.astype(F32) for piece in pieces]
    average = sum(jnp.sum(piece, axis=1, keepdims=True) for piece in pieces) / D
    squares = sum(jnp.sum(piece * piece, axis=1, keepdims=True) for piece in pieces) / D
    inverse = lax.rsqrt(squares - average * average + EPSILON)
    for spot, piece in zip(spots, pieces):
        out[:, spot] = ((piece - average) * inverse * gain[:, spot] + bias[:, spot]).astype(BF16)
    average_out[...] = jnp.broadcast_to(average, average_out.shape)
    inverse_out[...] = jnp.broadcast_to(inverse, inverse_out.shape)


def join(pieces, row, gain=None, bias=None):
    norm = gain is not None
    if not isinstance(pieces, tuple):
        return norm_wide(pieces, gain, bias) if norm else pieces
    rows, block = pieces[0].shape
    steps = 4
    tile = rows // steps
    piece = pl.BlockSpec((tile, block), lambda i, r: (i, 0))
    far_a = pl.BlockSpec((tile, block), lambda i, r: (jnp.minimum(i, steps // 2 - 1), 0))
    far_b = pl.BlockSpec((tile, block), lambda i, r: (jnp.maximum(i - steps // 2, 0), 0))
    vector = pl.BlockSpec((1, D), lambda i, r: (0, 0))
    wide = pl.BlockSpec((tile, D), lambda i, r: (i, 0))
    stat = pl.BlockSpec((tile, 128), lambda i, r: (i, 0))
    wide_shape = jax.ShapeDtypeStruct((rows, D), BF16)
    stat_shape = jax.ShapeDtypeStruct((rows, 128), F32)
    return pl.pallas_call(
        functools.partial(join_kernel, norm=norm),
        grid_spec=pltpu.PrefetchScalarGridSpec(
            num_scalar_prefetch=1,
            grid=(steps,),
            in_specs=[piece] * 3 + [far_a, far_b] + ([vector] * 2 if norm else []),
            out_specs=[wide, stat, stat] if norm else wide,
        ),
        out_shape=[wide_shape, stat_shape, stat_shape] if norm else wide_shape,
        compiler_params=params(("arbitrary",)),
        name="join_norm" if norm else "join",
        cost_estimate=pl.CostEstimate(
            flops=8 * rows * D, bytes_accessed=4 * rows * D, transcendentals=0
        ),
    )(row, *pieces, *((gain[None, :], bias[None, :]) if norm else ()))


def project_kernel(
    heads, rows, chunks, meta, rates, values, weight, cosine, sine,
    query_out, key_out, value_out, exports, acc,
):
    local = pl.program_id(0)
    place = meta[21]
    chunk = Chunk(meta, place * chunks + local)
    raw = mm(values[...], weight[...])
    cos, sin = cosine[...], sine[...]
    half = QK // 2
    for part, out in ((0, query_out), (1, key_out)):
        for head in range(heads):
            first = (part * heads + head) * QK
            a, b = raw[:, first : first + half], raw[:, first + half : first + QK]
            out[:, head * QK : head * QK + half] = (a * cos - b * sin).astype(BF16)
            out[:, head * QK + half : (head + 1) * QK] = (b * cos + a * sin).astype(BF16)
    value_out[...] = raw[:, 2 * heads * QK :].astype(BF16)

    @pl.when(local == 0)
    def _():
        acc[...] = jnp.zeros_like(acc)

    for head in range(heads):
        rate = rates[head]
        key = key_out[:, head * QK : (head + 1) * QK].astype(F32)
        weighted = (key * key_decay(rate, chunk.count)).astype(BF16)
        state = mm_tn(weighted, value_out[:, head * HV : (head + 1) * HV])
        for slot in range(3):
            on, exponent = export_terms(meta, chunk, local, chunks, place, slot, rows)

            @pl.when(on)
            def _():
                acc[slot, head] += state * power(rate, exponent, HV)

    @pl.when(local == chunks - 1)
    def _():
        exports[...] = acc[...].astype(BF16)


def project(meta, rates, values, weight, cosine, sine):
    rows, width = values.shape[0], weight.shape[1]
    heads = width // (2 * QK + HV)
    chunks = rows // CHUNK
    table = pl.BlockSpec((CHUNK, QK // 2), lambda i: (i, 0))
    widths = (heads * QK, heads * QK, heads * HV)
    states = (3, heads, QK, HV)
    return pl.pallas_call(
        functools.partial(project_kernel, heads, rows, chunks),
        grid=(chunks,),
        in_specs=[
            smem(), smem(),
            pl.BlockSpec((CHUNK, D), lambda i: (i, 0)),
            pl.BlockSpec((D, width), lambda i: (0, 0)),
            table, table,
        ],
        out_specs=[pl.BlockSpec((CHUNK, w), lambda i: (i, 0)) for w in widths]
        + [pl.BlockSpec(states, lambda i: (0, 0, 0, 0))],
        out_shape=[jax.ShapeDtypeStruct((rows, w), BF16) for w in widths]
        + [jax.ShapeDtypeStruct(states, BF16)],
        scratch_shapes=[pltpu.VMEM(states, F32)],
        compiler_params=params(("arbitrary",)),
        name="project",
        cost_estimate=pl.CostEstimate(
            flops=2 * rows * D * width, bytes_accessed=2 * (rows + width) * D, transcendentals=0
        ),
    )(meta, rates, values, weight, cosine, sine)


def matmul_kernel(values, weight, out):
    out[...] = mm(values[...], weight[...]).astype(out.dtype)


def matmul(values, weight, kind):
    array, width, number = weight
    rows = values.shape[0]
    return pl.pallas_call(
        matmul_kernel,
        grid=(rows // CHUNK,),
        in_specs=[
            pl.BlockSpec((CHUNK, D), lambda i: (i, 0)),
            pl.BlockSpec((D, width), lambda i: (0, number)),
        ],
        out_specs=pl.BlockSpec((CHUNK, width), lambda i: (i, 0)),
        out_shape=jax.ShapeDtypeStruct((rows, width), kind),
        compiler_params=params(("arbitrary",)),
        name="matmul",
        cost_estimate=pl.CostEstimate(
            flops=2 * rows * D * width, bytes_accessed=2 * (rows + width) * D, transcendentals=0
        ),
    )(values, array)


def weight_grad_kernel(spans, *refs):
    count = len(spans)
    lefts, rights, out = refs[:count], refs[count : 2 * count], refs[2 * count]
    tile = pl.program_id(0)
    for left, right, (first, last) in zip(lefts, rights, spans):

        @pl.when((tile >= first) & (tile < last))
        def _():
            height = 2 * GRAD_TILE

            def part(index, _):
                spot = pl.ds(pl.multiple_of(index * height, height), height)
                out[spot, :] = mm_tn(left[:, spot], right[...]).astype(BF16)
                return 0

            lax.fori_loop(0, left.shape[1] // height, part, 0)


def weight_grads(pairs):
    rows = pairs[0][0].shape[0]
    wide = min(right.shape[1] for _, right in pairs)
    tall = 1024
    steps = D // tall
    spans, first = [], 0
    for _, right in pairs:
        spans.append((first, first + right.shape[1] // wide))
        first = spans[-1][1]

    def left_spec(span):
        return pl.BlockSpec(
            (rows, tall),
            lambda n, m: (
                0, jnp.where(n < span[0], 0, jnp.where(n < span[1], m, steps - 1)),
            ),
        )

    def right_spec(span):
        return pl.BlockSpec(
            (rows, wide), lambda n, m: (0, jnp.clip(n - span[0], 0, span[1] - span[0] - 1))
        )

    return pl.pallas_call(
        functools.partial(weight_grad_kernel, tuple(spans)),
        grid=(first, steps),
        in_specs=[left_spec(span) for span in spans] + [right_spec(span) for span in spans],
        out_specs=pl.BlockSpec((tall, wide), lambda n, m: (m, n)),
        out_shape=jax.ShapeDtypeStruct((D, first * wide), BF16),
        compiler_params=params(("arbitrary", "arbitrary")),
        name="weight_grads",
        cost_estimate=pl.CostEstimate(
            flops=2 * rows * D * first * wide,
            bytes_accessed=2 * D * first * wide + 4 * rows * D,
            transcendentals=0,
        ),
    )(*[left for left, _ in pairs], *[right for _, right in pairs])


def paired_grad_kernel(spans, tiles, steps, *refs):
    count = len(spans)
    lefts, rights = refs[:count], refs[count : 2 * count]
    out, made, received, send_sem, recv_sem = refs[2 * count :]
    step = pl.program_id(0)
    core = lax.axis_index("col") % 2
    partner = lax.axis_index("col") + 1 - 2 * core

    def copy(index):
        return pltpu.make_async_remote_copy(
            src_ref=made.at[index, :, 1 - core],
            dst_ref=received.at[index],
            send_sem=send_sem.at[index],
            recv_sem=recv_sem.at[index],
            device_id={"col": partner},
            device_id_type=pl.DeviceIdType.MESH,
        )

    @pl.when(step == 0)
    def _():
        barrier = pltpu.get_barrier_semaphore()
        pl.semaphore_signal(
            barrier, inc=1, device_id={"col": partner}, device_id_type=pl.DeviceIdType.MESH
        )
        pl.semaphore_wait(barrier, 1)

    for left, right, (first, last) in zip(lefts, rights, spans):

        @pl.when((step >= first * steps) & (step < last * steps))
        def _():
            total = mm_tn(left[...], right[...]).astype(BF16)
            made[step] = total.reshape(made.shape[1:])

    @pl.when(step < tiles)
    def _():
        copy(step).start()

    @pl.when(step > 0)
    def _():
        index = step - 1
        copy(index).wait()
        out[...] = (made[index, :, core].astype(F32) + received[index].astype(F32)).astype(BF16)


def paired_grads(pairs, number):
    rows = pairs[0][0].shape[0]
    wide = min(right.shape[1] for _, right in pairs)
    wide = min(wide, 512)
    tall = 1024
    steps = D // tall
    block = D // SLOTS
    depth = tall // block // 2
    spans, first = [], 0
    for _, right in pairs:
        spans.append((first, first + right.shape[1] // wide))
        first = spans[-1][1]
    tiles = first * steps

    def left_spec(span):
        def index(s):
            n, m = s // steps, s % steps
            return 0, jnp.where(n < span[0], 0, jnp.where(n < span[1], m, steps - 1))

        return pl.BlockSpec((rows, tall), index)

    def right_spec(span):
        def index(s):
            return 0, jnp.clip(s // steps - span[0], 0, span[1] - span[0] - 1)

        return pl.BlockSpec((rows, wide), index)

    def out_index(s):
        done = jnp.maximum(s - 1, 0)
        return done % steps, 0, done // steps

    result = pl.pallas_call(
        functools.partial(paired_grad_kernel, tuple(spans), tiles, steps),
        grid=(tiles + 1,),
        in_specs=[left_spec(span) for span in spans] + [right_spec(span) for span in spans],
        out_specs=pl.BlockSpec((depth, block, wide), out_index),
        out_shape=jax.ShapeDtypeStruct((SLOTS // 2, block, first * wide), BF16),
        scratch_shapes=[
            pltpu.VMEM((tiles, depth, 2, block, wide), BF16),
            pltpu.VMEM((tiles, depth, block, wide), BF16),
            pltpu.SemaphoreType.DMA((tiles,)),
            pltpu.SemaphoreType.DMA((tiles,)),
        ],
        compiler_params=pltpu.CompilerParams(
            dimension_semantics=("arbitrary",),
            collective_id=number,
            has_side_effects=True,
            vmem_limit_bytes=60 * 1024 * 1024,
        ),
        name="paired_grads",
        cost_estimate=pl.CostEstimate(
            flops=2 * rows * D * first * wide,
            bytes_accessed=2 * D * first * wide + 4 * rows * D,
            transcendentals=0,
        ),
    )(*[left for left, _ in pairs], *[right for _, right in pairs])
    return result


def column_grads(pairs, number):
    if lax.axis_size("col") != SLOTS:
        return weight_grads(pairs)
    return paired_grads(pairs, number)


def norm_pieces(row, own, from_x, from_y, far_a, far_b, gain, bias, out, average_out, inverse_out):
    block = own.shape[1]
    second = pl.program_id(0) >= pl.num_programs(0) // 2
    far = jnp.where(second, far_b[...], far_a[...])
    pieces = [piece.astype(F32) for piece in (own[...], from_x[...], from_y[...], far)]
    average = sum(jnp.sum(piece, axis=1, keepdims=True) for piece in pieces) / D
    squares = sum(jnp.sum(piece * piece, axis=1, keepdims=True) for piece in pieces) / D
    inverse = lax.rsqrt(squares - average * average + EPSILON)
    for flip, piece in enumerate(pieces):
        spot = pl.ds(pl.multiple_of((row[0] ^ flip) * block, 128), block)
        out[:, spot] = ((piece - average) * inverse * gain[:, spot] + bias[:, spot]).astype(BF16)
    average_out[...] = jnp.broadcast_to(average, average_out.shape)
    inverse_out[...] = jnp.broadcast_to(inverse, inverse_out.shape)


def up_kernel(row, *refs, joined):
    if joined:
        pieces, gain, norm_bias = refs[:5], refs[5], refs[6]
        weight, bias, grad_hidden, scales, second_out, average_out, inverse_out = refs[7:14]
        hidden_out, grad_out, bias_out, sums_out, moved = refs[14:]
        norm_pieces(row, *pieces, gain, norm_bias, second_out, average_out, inverse_out)
        values = second_out
    else:
        values, weight, bias, grad_hidden, scales = refs[:5]
        hidden_out, grad_out, bias_out, sums_out, moved = refs[5:]
    before = mm(values[...], weight[...]) + bias[...]
    phi = 0.5 * (1.0 + lax.erf(before * (0.5**0.5)))
    hidden_out[...] = (before * phi).astype(BF16)
    density = jnp.exp(-0.5 * before * before) * 0.3989422804014327
    grad = (grad_hidden[...].astype(F32) * (phi + before * density)).astype(BF16)
    grad_out[...] = grad

    @pl.when(pl.program_id(0) == 0)
    def _():
        bias_out[...] = jnp.zeros_like(bias_out)
        parts = mm(scales[...], weight[...])
        moved[0:1] = parts[0:1] + parts[1:2]
        moved[1:2] = parts[2:3] + parts[3:4]

    wide_grad = grad.astype(F32)
    bias_out[...] += jnp.sum(wide_grad, axis=0, keepdims=True)
    plain = jnp.sum(wide_grad * moved[0:1], axis=1, keepdims=True)
    crossed = jnp.sum(wide_grad * (before - bias[...] - moved[1:2]), axis=1, keepdims=True)
    lane = lax.broadcasted_iota(jnp.int32, sums_out.shape, 1)
    sums_out[...] = jnp.where(lane == 0, plain, crossed)


def feed_up(pieces, row, gain, norm_bias, weight, bias, grad_hidden):
    array, width, number = weight
    joined = isinstance(pieces, tuple)
    rows = grad_hidden.shape[0]
    steps = 4
    tile = rows // steps
    block = pl.BlockSpec((tile, width), lambda i, r: (i, 0))
    vector = pl.BlockSpec((1, width), lambda i, r: (0, 0))
    wide = pl.BlockSpec((tile, D), lambda i, r: (i, 0))
    stat = pl.BlockSpec((tile, 128), lambda i, r: (i, 0))
    gains = pl.BlockSpec((1, D), lambda i, r: (0, 0))
    if joined:
        piece = pl.BlockSpec((tile, pieces[0].shape[1]), lambda i, r: (i, 0))
        far_a = pl.BlockSpec(
            (tile, pieces[0].shape[1]), lambda i, r: (jnp.minimum(i, steps // 2 - 1), 0)
        )
        far_b = pl.BlockSpec(
            (tile, pieces[0].shape[1]), lambda i, r: (jnp.maximum(i - steps // 2, 0), 0)
        )
        inputs = list(pieces) + [gain[None, :], norm_bias[None, :]]
        in_specs = [piece] * 3 + [far_a, far_b, gains, gains]
        early_specs = [wide, stat, stat]
        early_shapes = [
            jax.ShapeDtypeStruct((rows, D), BF16),
            jax.ShapeDtypeStruct((rows, 128), F32),
            jax.ShapeDtypeStruct((rows, 128), F32),
        ]
        normed = []
    else:
        normed = list(norm_wide(pieces, gain, norm_bias))
        inputs, in_specs, early_specs, early_shapes = [normed[0]], [wide], [], []
    scales = jnp.stack([gain, norm_bias])
    high = lax.reduce_precision(scales, 8, 7)
    low = scales - high
    rest = jnp.zeros((4, D), F32)
    scales = jnp.concatenate([high[:1], low[:1], high[1:], low[1:], rest], axis=0).astype(BF16)
    outs = pl.pallas_call(
        functools.partial(up_kernel, joined=joined),
        grid_spec=pltpu.PrefetchScalarGridSpec(
            num_scalar_prefetch=1,
            grid=(steps,),
            in_specs=in_specs
            + [
                pl.BlockSpec((D, width), lambda i, r: (0, number)), vector, block,
                pl.BlockSpec((8, D), lambda i, r: (0, 0)),
            ],
            out_specs=early_specs + [block, block, vector, stat],
            scratch_shapes=[pltpu.VMEM((8, width), F32)],
        ),
        out_shape=early_shapes
        + [
            jax.ShapeDtypeStruct((rows, width), BF16),
            jax.ShapeDtypeStruct((rows, width), BF16),
            jax.ShapeDtypeStruct((1, width), F32),
            jax.ShapeDtypeStruct((rows, 128), F32),
        ],
        compiler_params=params(("arbitrary",)),
        name="feed_up",
        cost_estimate=pl.CostEstimate(
            flops=2 * rows * D * width,
            bytes_accessed=2 * (2 * rows + width) * D + 8 * rows * width,
            transcendentals=2 * rows * width,
        ),
    )(row, *inputs, array, bias[None, :], grad_hidden, scales)
    return normed + list(outs)


PARTIAL_FLIP = (1, 3, 2, 3, 2, 1, 0, 0)
PARTIAL_HALF = (0, 0, 1, 1, 0, 1, 0, 1)


def table_lookup(table, step):
    result = jnp.int32(table[0])
    for index in range(1, len(table)):
        result = jnp.where(step == index, table[index], result)
    return result


def partial_kernel(count, row, *refs):
    values, weights = refs[:count], refs[count : 2 * count]
    outs = refs[2 * count :]
    step = pl.program_id(0)
    strip = values[0].shape[0] // 2

    def part(number, _):
        spot = pl.ds(pl.multiple_of(number * strip, strip), strip)
        total = mm_nt(values[0][spot, :], weights[0][...])
        for x, w in zip(values[1:], weights[1:]):
            total = total + mm_nt(x[spot, :], w[...])
        for index, out in enumerate(outs):

            @pl.when(step // 2 == index)
            def _():
                out[0, spot, :] = total.astype(out.dtype)

        return 0

    lax.fori_loop(0, 2, part, 0)


def partial_blocks(values, weights, row, first, kinds):
    rows = values[0].shape[0]
    half, block = rows // 2, D // 4
    count = len(values)
    flips = PARTIAL_FLIP[2 * first : 2 * (first + len(kinds))]
    halves = PARTIAL_HALF[2 * first : 2 * (first + len(kinds))]

    def value_spec(x):
        return pl.BlockSpec((half, x.shape[1]), lambda s, r: (table_lookup(halves, s), 0))

    def weight_spec(w):
        return pl.BlockSpec((block, w[1]), lambda s, r: (r[0] ^ table_lookup(flips, s), w[2]))

    def out_spec(index):
        return pl.BlockSpec((1, half, block), lambda s, r: (jnp.clip(s - 2 * index, 0, 1), 0, 0))

    depth = sum(x.shape[1] for x in values)
    return pl.pallas_call(
        functools.partial(partial_kernel, count),
        grid_spec=pltpu.PrefetchScalarGridSpec(
            num_scalar_prefetch=1,
            grid=(2 * len(kinds),),
            in_specs=[value_spec(x) for x in values] + [weight_spec(w) for w in weights],
            out_specs=[out_spec(index) for index in range(len(kinds))],
        ),
        out_shape=[jax.ShapeDtypeStruct((2, half, block), kind) for kind in kinds],
        compiler_params=params(("arbitrary",)),
        name="partial_blocks",
        cost_estimate=pl.CostEstimate(
            flops=rows * block * depth * 2 * len(kinds),
            bytes_accessed=(rows + D) * depth * 2 + 4 * rows * block * len(kinds),
            transcendentals=0,
        ),
    )(row, *values, *[w[0] for w in weights])


def permute_row(value, pairs):
    return lax.ppermute(value, "row", pairs)


def in_order(*values):
    return lax.optimization_barrier(values)


def reduce_row_start(values, weights, row):
    if lax.axis_size("row") != 4:
        columns = [array[:, n * width : (n + 1) * width] for array, width, n in weights]
        return sum(mm_nt(x, w) for x, w in zip(values, columns)).astype(BF16)
    return tuple(partial_blocks(values, weights, row, 0, (BF16, BF16)))


def reduce_row_rest(values, weights, row):
    if lax.axis_size("row") != 4:
        return ()
    return tuple(partial_blocks(values, weights, row, 2, (BF16, F32)))


def reduce_row_finish(
    sends, values, weights, row, between=None, tied=None, rest=None, delayed=False
):
    if lax.axis_size("row") != 4:
        total = lax.psum_scatter(sends, "row", scatter_dimension=1, tiled=True).astype(F32)
        extra = between(tied) if between else None
        return ((lambda first: (total, first)) if delayed else total), extra
    from_x = permute_row(sends[0], X_PAIRS)
    from_y = permute_row(sends[1], Y_PAIRS)
    keep, own = rest if rest is not None else reduce_row_rest(values, weights, row)
    extra = None
    if between is not None:
        if tied is not None:
            keep, own, tied = in_order(keep, own, tied)
        extra = between(tied)
        from_x, from_y, extra = in_order(from_x, from_y, extra)
    next_y = (keep[0].astype(F32) + from_x[1].astype(F32)).astype(BF16)
    next_x = (keep[1].astype(F32) + from_y[1].astype(F32)).astype(BF16)
    last_y = permute_row(next_y, Y_PAIRS)
    last_x = permute_row(next_x, X_PAIRS)

    def add(last_y, last_x):
        first_half = own[0] + from_x[0].astype(F32) + last_y.astype(F32)
        second_half = own[1] + from_y[0].astype(F32) + last_x.astype(F32)
        return jnp.concatenate([first_half, second_half], axis=0)

    def add_after(first):
        now_y, now_x, first = in_order(last_y, last_x, first)
        return add(now_y, now_x), first

    return (add_after if delayed else add(last_y, last_x)), extra


def gather_row(value, between=None, later=None):
    if lax.axis_size("row") != 4:
        gathered = lax.all_gather(value, "row", axis=1, tiled=True)
        if later is not None:
            return gathered, later[0](later[1])
        return gathered, between() if between else None
    half = value.shape[0] // 2
    from_x = permute_row(value, X_PAIRS)
    from_y = permute_row(value, Y_PAIRS)
    extra = None
    if between is not None:
        extra = between()
        from_x, from_y, extra = in_order(from_x, from_y, extra)
    if later is not None:
        from_x, from_y, argument = in_order(from_x, from_y, later[1])
    far_a = permute_row(from_x[:half], Y_PAIRS)
    far_b = permute_row(from_y[half:], X_PAIRS)
    if later is not None:
        extra = later[0](argument)
        far_a, far_b, extra = in_order(far_a, far_b, extra)
    return (value, from_x, from_y, far_a, far_b), extra


def gather_row_small(value):
    if lax.axis_size("row") != 4:
        return lax.all_gather(value, "row", axis=1, tiled=True)
    row = lax.axis_index("row")
    pieces = jnp.stack(
        [value] + [permute_row(value, pairs) for pairs in (X_PAIRS, Y_PAIRS, D_PAIRS)]
    )
    ordered = [
        lax.dynamic_index_in_dim(pieces, row ^ place, 0, keepdims=False) for place in range(4)
    ]
    return jnp.concatenate(ordered, axis=1)


def sum_row_direct(value):
    if lax.axis_size("row") != 4:
        return lax.psum(value, "row")
    others = [permute_row(value, pairs) for pairs in (X_PAIRS, Y_PAIRS, D_PAIRS)]
    return value + others[0] + (others[1] + others[2])


def norm_backward(grad_out, normal, inverse, gain_vector, sums=None):
    scaled = grad_out * gain_vector
    if sums is None:
        sums = sum_row_direct(
            jnp.stack([jnp.sum(scaled, axis=1), jnp.sum(scaled * normal, axis=1)])
        )
    means = sums / D
    grad_in = inverse * (scaled - means[0][:, None] - normal * means[1][:, None])
    return (grad_in, jnp.sum(grad_out * normal, axis=0), jnp.sum(grad_out, axis=0))


def gather_col(weight):
    return lax.all_gather(weight, "col", axis=0, tiled=True)


def scatter_col(grad):
    if grad.ndim == 2:
        return lax.psum_scatter(grad, "col", scatter_dimension=0, tiled=True)
    groups = [list(range(core, SLOTS, 2)) for core in range(2)]
    return lax.psum_scatter(grad, "col", scatter_dimension=0, axis_index_groups=groups)


class Exchange:
    def __init__(self, messages, send_sem, recv_sem):
        col = lax.axis_index("col")
        self.base = (col // SLOTS) * SLOTS
        self.place = col % SLOTS
        self.messages, self.send_sem, self.recv_sem = messages, send_sem, recv_sem

    def copy(self, index):
        _, target, source, destination = self.messages[index]
        return pltpu.make_async_remote_copy(
            src_ref=source,
            dst_ref=destination,
            send_sem=self.send_sem.at[index],
            recv_sem=self.recv_sem.at[index],
            device_id={"col": self.base + target},
            device_id_type=pl.DeviceIdType.MESH,
        )

    def greet(self):
        barrier = pltpu.get_barrier_semaphore()
        for step in range(1, SLOTS):
            other = self.base + (self.place + step) % SLOTS
            pl.semaphore_signal(
                barrier, inc=1, device_id={"col": other}, device_id_type=pl.DeviceIdType.MESH
            )
        pl.semaphore_wait(barrier, SLOTS - 1)

    def run(self, programs, drain=True):
        for place, program in enumerate(programs):
            if not program:
                continue

            @pl.when(self.place == place)
            def _():
                for action in program:
                    if callable(action):
                        action()
                    elif action >= 0:
                        self.copy(action).start()
                    else:
                        self.copy(~action).wait_recv()

        if drain:
            self.drain()

    def drain(self):
        for place in range(SLOTS):
            mine = [i for i, message in enumerate(self.messages) if message[0] == place]
            if mine:

                @pl.when(self.place == place)
                def _():
                    for index in mine:
                        self.copy(index).wait_send()


def scaled_add(meta, rates, target, terms, rows):
    heads = target.shape[0]
    strip = 64
    for head in range(heads):

        def add(index, _):
            spot = pl.ds(pl.multiple_of(index * strip, strip), strip)
            total = None
            for term in terms:
                if isinstance(term, tuple):
                    ref, slot = term
                    exponent = jnp.maximum(
                        trunk_reference(meta, jnp.int32(3), rows)
                        - trunk_reference(meta, jnp.int32(slot), rows),
                        0,
                    )
                    value = ref[head, spot, :].astype(F32) * power(rates[head], exponent, HV)
                else:
                    value = term[head, spot, :].astype(F32)
                total = value if total is None else total + value
            target[head, spot, :] = total.astype(BF16)
            return 0

        lax.fori_loop(0, QK // strip, add, 0)


def share_kernel(rows, meta, rates, ex, sh, shift, tot, send_sem, recv_sem):
    messages = [
        (0, 2, ex.at[0], sh.at[0]),
        (0, 1, ex.at[0], sh.at[0]),
        (1, 3, ex.at[0], sh.at[1]),
        (2, 3, ex.at[0], sh.at[2]),
        (2, 3, sh.at[0], sh.at[0]),
        (3, 2, sh.at[1], sh.at[1]),
        (3, 4, ex.at[1], sh.at[4]),
        (3, 5, ex.at[2], sh.at[5]),
        (3, 4, tot, sh.at[3]),
        (4, 5, ex.at[1], sh.at[6]),
        (4, 6, ex.at[1], sh.at[6]),
        (4, 5, ex.at[2], sh.at[7]),
        (5, 7, sh.at[7], sh.at[7]),
        (4, 5, sh.at[4], sh.at[4]),
        (4, 6, sh.at[4], sh.at[4]),
        (5, 4, sh.at[5], sh.at[5]),
        (5, 7, sh.at[5], sh.at[5]),
        (4, 5, sh.at[3], sh.at[3]),
        (4, 6, sh.at[3], sh.at[3]),
        (6, 7, sh.at[6], sh.at[6]),
        (6, 7, sh.at[4], sh.at[4]),
        (6, 7, sh.at[3], sh.at[3]),
        (7, 6, sh.at[7], sh.at[7]),
        (7, 6, sh.at[5], sh.at[5]),
        (4, 5, ex.at[0], shift),
        (6, 7, ex.at[0], shift),
    ]
    exchange = Exchange(messages, send_sem, recv_sem)

    def keep_trunk():
        sh[3] = ex[0]

    def total_trunk():
        terms = [(sh.at[slot], slot) for slot in range(3)] + [ex.at[0]]
        scaled_add(meta, rates, tot, terms, rows)

    def keep_branches():
        sh[6] = ex[1]
        sh[7] = ex[2]

    exchange.greet()
    exchange.run(
        [
            [0, 1],
            [2, ~1],
            [3, ~0, 4, ~5],
            [6, 7, keep_trunk, ~2, 5, ~4, ~3, total_trunk, 8],
            [10, 11, 9, 24, keep_branches, ~6, 14, 13, ~15, ~8, 18, 17],
            [~11, 12, ~7, 16, 15, ~9, ~24, ~13, ~17],
            [25, ~10, 19, ~14, 20, ~22, ~23, ~18, 21],
            [~12, 22, ~16, 23, ~19, ~20, ~25, ~21],
        ]
    )


def vmem():
    return pl.BlockSpec(memory_space=pltpu.VMEM)


def share_states(meta, rates, exports, rows):
    heads = exports.shape[1]
    state = (heads, QK, HV)
    return pl.pallas_call(
        functools.partial(share_kernel, rows),
        in_specs=[smem(), smem(), vmem()],
        out_specs=[vmem(), vmem()],
        out_shape=[
            jax.ShapeDtypeStruct((SLOTS,) + state, BF16),
            jax.ShapeDtypeStruct(state, BF16),
        ],
        scratch_shapes=[
            pltpu.VMEM(state, BF16),
            pltpu.SemaphoreType.DMA((26,)),
            pltpu.SemaphoreType.DMA((26,)),
        ],
        compiler_params=pltpu.CompilerParams(
            collective_id=1, has_side_effects=True, vmem_limit_bytes=40 * 1024 * 1024
        ),
        name="share_states",
        cost_estimate=pl.CostEstimate(
            flops=0, bytes_accessed=100 * 1024 * 1024, transcendentals=0
        ),
    )(meta, rates, exports)


def return_kernel(
    rows, meta, rates, y, first, left, right, own0, own1, own2, grads, rx, tx, send_sem, recv_sem
):
    messages = [
        (7, 6, y.at[3], rx.at[0]),
        (7, 6, y.at[4], rx.at[1]),
        (7, 6, y.at[5], rx.at[2]),
        (6, 7, y.at[6], rx.at[0]),
        (6, 7, y.at[7], rx.at[1]),
        (7, 5, tx.at[0], rx.at[0]),
        (7, 5, tx.at[1], rx.at[1]),
        (6, 4, tx.at[0], rx.at[0]),
        (6, 4, tx.at[1], rx.at[1]),
        (6, 4, tx.at[2], rx.at[2]),
        (5, 4, y.at[3], rx.at[3]),
        (5, 4, y.at[4], rx.at[4]),
        (5, 4, y.at[5], rx.at[5]),
        (5, 4, tx.at[0], rx.at[6]),
        (5, 4, tx.at[1], rx.at[7]),
        (4, 3, tx.at[0], rx.at[0]),
        (4, 3, tx.at[1], own1),
        (4, 3, tx.at[2], own2),
        (2, 3, y.at[0], rx.at[1]),
        (2, 3, y.at[1], rx.at[2]),
        (3, 2, tx.at[2], own0),
        (3, 1, tx.at[1], own0),
        (3, 0, tx.at[0], rx.at[0]),
        (1, 0, y.at[0], rx.at[1]),
        (5, 4, first, own0),
        (7, 6, first, own0),
    ]
    exchange = Exchange(messages, send_sem, recv_sem)

    def add(target, *terms):
        return lambda: scaled_add(meta, rates, target, terms, rows)

    def multiply(begin, end):
        def tile(index, _):
            spot = pl.ds(pl.multiple_of(index * GRAD_TILE, GRAD_TILE), GRAD_TILE)
            grads[spot, :] = mm_tn(left[:, spot], right[...]).astype(BF16)
            return 0

        lax.fori_loop(begin, end, tile, 0)

    tiles = D // GRAD_TILE
    exchange.greet()
    exchange.run([[], [23], [18, 19], [], [], [10, 11, 12, 24], [3, 4], [0, 1, 2, 25]], False)
    multiply(0, tiles // 2)
    exchange.run(
        [
            [],
            [],
            [],
            [],
            [
                ~10, ~7, add(tx.at[0], y.at[3], rx.at[0], rx.at[3]), 15,
                ~11, ~8, add(tx.at[1], y.at[4], rx.at[1], rx.at[4]), 16,
                ~12, ~9, add(tx.at[2], y.at[5], rx.at[2], rx.at[5]), 17,
                ~13, add(own1, y.at[6], rx.at[6]),
                ~14, add(own2, y.at[7], rx.at[7]),
                ~24,
            ],
            [
                ~5, add(tx.at[0], y.at[6], rx.at[0]), 13,
                ~6, add(tx.at[1], y.at[7], rx.at[1]), 14,
            ],
            [
                ~0, add(tx.at[0], y.at[3], rx.at[0]), 7,
                ~1, add(tx.at[1], y.at[4], rx.at[1]), 8,
                ~2, add(tx.at[2], y.at[5], rx.at[2]), 9,
                ~25,
            ],
            [
                ~3, add(tx.at[0], y.at[6], rx.at[0]), 5,
                ~4, add(tx.at[1], y.at[7], rx.at[1]), 6,
            ],
        ],
        False,
    )
    multiply(tiles // 2, tiles)
    exchange.run(
        [
            [~23, ~22, add(own0, rx.at[0], rx.at[1])],
            [~21],
            [~20],
            [
                ~18, ~19, ~15,
                add(tx.at[0], y.at[0], rx.at[1], (rx.at[0], 0)), 22,
                add(tx.at[1], y.at[1], rx.at[2], (rx.at[0], 1)), 21,
                add(tx.at[2], y.at[2], (rx.at[0], 2)), 20,
                add(own0, rx.at[0], y.at[3]),
                ~16, ~17,
            ],
            [],
            [],
            [],
            [],
        ],
        False,
    )
    exchange.drain()


def return_states(meta, rates, exports, first_state, left, right, rows):
    heads = exports.shape[1]
    state = (heads, QK, HV)
    return pl.pallas_call(
        functools.partial(return_kernel, rows),
        in_specs=[smem(), smem(), vmem(), vmem(), vmem(), vmem()],
        out_specs=[vmem()] * 4,
        out_shape=[jax.ShapeDtypeStruct(state, BF16)] * 3
        + [jax.ShapeDtypeStruct((D, right.shape[1]), BF16)],
        scratch_shapes=[
            pltpu.VMEM((8,) + state, BF16),
            pltpu.VMEM((3,) + state, BF16),
            pltpu.SemaphoreType.DMA((26,)),
            pltpu.SemaphoreType.DMA((26,)),
        ],
        compiler_params=pltpu.CompilerParams(
            collective_id=2, has_side_effects=True, vmem_limit_bytes=40 * 1024 * 1024
        ),
        name="return_states",
        cost_estimate=pl.CostEstimate(
            flops=0, bytes_accessed=100 * 1024 * 1024, transcendentals=0
        ),
    )(meta, rates, exports, first_state, left, right)


def sum_col(value):
    size = lax.axis_size("col")
    if size != SLOTS:
        return lax.psum(value, "col")
    for flip in (1, 2, 4):
        value = value + lax.ppermute(value, "col", [(a, a ^ flip) for a in range(size)])
    return value


def sum_col_vectors(vectors, extra=None):
    col = lax.axis_index("col")
    size = lax.axis_size("col")
    parts = list(vectors) + ([extra] if extra is not None else [])
    total = sum_col(jnp.concatenate(parts).reshape(-1, 128)).reshape(-1)
    results, first = [], 0
    for vector in vectors:
        width = vector.shape[0] // size
        results.append(lax.dynamic_slice_in_dim(total, first + col * width, width, 0))
        first += vector.shape[0]
    return results, total[first:]


def token_tables(place, rows, lengths, parents):
    index = place * rows + jnp.arange(rows, dtype=jnp.int32)
    in_trunk = index < TRUNK
    beyond = jnp.maximum(index - TRUNK, 0)
    segment = jnp.where(in_trunk, 0, 1 + beyond // SEG)
    position = jnp.where(in_trunk, index, beyond % SEG)

    def lookup(table, spots):
        hits = spots[:, None] == jnp.arange(table.shape[0], dtype=jnp.int32)
        return jnp.sum(jnp.where(hits, table, 0), axis=1)

    branch = 1 + lookup(parents, jnp.clip(segment - 5, 0, 7))
    parent_length = lookup(lengths, branch)
    depth = position + jnp.where(segment >= 1, lengths[0], 0)
    depth = depth + jnp.where(segment >= 5, parent_length, 0)
    valid = (position < lookup(lengths, segment)).astype(F32)
    half = QK // 2
    frequency = 10000.0 ** (-jnp.arange(half, dtype=F32) / (half - 1))
    angles = depth.astype(F32)[:, None] * frequency[None, :]
    return valid, jnp.cos(angles), jnp.sin(angles)


def body(
    tokens,
    cotangent,
    query_weight,
    key_weight,
    value_weight,
    gate_weight,
    out_weight,
    up_weight,
    down_weight,
    first_gain,
    first_bias,
    group_gain,
    group_bias,
    second_gain,
    second_bias,
    up_bias,
    down_bias,
    segment_lengths,
    leaf_parents,
):
    rows = tokens.shape[0]
    col = lax.axis_index("col")
    row = lax.axis_index("row")
    row_ref = row.astype(jnp.int32)[None]
    place = (col % SLOTS).astype(jnp.int32)
    tree = (col // SLOTS).astype(jnp.int32)
    lengths = lax.dynamic_index_in_dim(segment_lengths, tree, 0, keepdims=False)
    parents = lax.dynamic_index_in_dim(leaf_parents, tree, 0, keepdims=False)
    meta = jnp.concatenate([lengths, parents, place[None]]).astype(jnp.int32)
    heads = query_weight.shape[1] // QK
    head_numbers = (row * heads + jnp.arange(heads, dtype=jnp.int32)).astype(F32)
    rates = jnp.log(1.0 - 2.0 ** (-5.0 - head_numbers))

    wide = heads * HV
    narrow = heads * QK
    project_full = gather_col(jnp.concatenate([query_weight, key_weight, value_weight], axis=1))
    gate_full = gather_col(gate_weight)
    out_full = gather_col(out_weight.T)
    feed_full = gather_col(jnp.concatenate([down_weight.T, up_weight], axis=1))
    query_part, key_part = (project_full, narrow, 0), (project_full, narrow, 1)
    value_part = (project_full, wide, 1)
    out_part = (out_full, wide, 0)
    down_part, up_part = (feed_full, wide, 0), (feed_full, wide, 1)

    valid, cosine, sine = token_tables(place, rows, lengths, parents)
    column = valid[:, None]
    gains = gather_row_small(jnp.stack([first_gain, first_bias, second_gain, second_bias]))
    token_pieces, _ = gather_row(tokens)
    first_wide, first_average, first_inverse = join(token_pieces, row_ref, gains[0], gains[1])
    fed_low = (cotangent.astype(F32) * column).astype(BF16)
    fed_low, first_average = lax.optimization_barrier((fed_low, first_average))

    fed_pieces, projected = gather_row(
        fed_low, lambda: project(meta, rates, first_wide, project_full, cosine, sine)
    )
    query_rot, key_rot, value_low, exports = projected
    shared, shifted = share_states(meta, rates, exports, rows)
    gate_full, shared = in_order(gate_full, shared)
    gate_part = (gate_full, wide, 0)
    gate_full, fed_pieces = in_order(gate_full, fed_pieces)
    gate_part = (gate_full, wide, 0)
    gate_raw, gated, normal, inverse, states = retain(
        meta, rates, query_rot, key_rot, value_low, first_wide, gate_part, shared, shifted,
        group_gain, group_bias,
    )

    sends = reduce_row_start([gated], [out_part], row_ref)
    attended, _ = reduce_row_finish(sends, [gated], [out_part], row_ref)
    middle = tokens.astype(F32) + attended

    def feed_gradient(pieces):
        joined = join(pieces, row_ref)
        return joined, matmul(joined, down_part, BF16)

    middle_pieces, (fed_wide, grad_hidden) = gather_row(
        middle.astype(BF16), later=(feed_gradient, fed_pieces)
    )
    second_wide, second_average, second_inverse, hidden, grad_before, up_bias_grad, feed_sums = (
        feed_up(middle_pieces, row_ref, gains[2], gains[3], up_part, up_bias, grad_hidden)
    )
    feed_sums = sum_row_direct(feed_sums[:, :2].T)
    sends = reduce_row_start([grad_before], [up_part], row_ref)
    sends, hidden = in_order(sends, hidden)
    second_back, feed_partial = reduce_row_finish(
        sends,
        [grad_before],
        [up_part],
        row_ref,
        lambda hidden: weight_grads([(fed_wide, hidden), (second_wide, grad_before)]),
        hidden,
    )
    feed_grad = scatter_col(feed_partial)
    grad_fed = fed_low.astype(F32)
    down_bias_grad = jnp.sum(grad_fed, axis=0)

    second_normal = (middle - second_average[:, :1]) * second_inverse[:, :1]
    grad_middle_norm, second_gain_grad, second_bias_grad = norm_backward(
        second_back, second_normal, second_inverse[:, :1], second_gain, feed_sums
    )
    grad_middle = grad_fed + grad_middle_norm
    grad_pieces, (fed_sends, fed_rest) = gather_row(
        grad_middle.astype(BF16),
        lambda: (
            reduce_row_start([hidden], [down_part], row_ref),
            reduce_row_rest([hidden], [down_part], row_ref),
        ),
    )
    grad_wide = join(grad_pieces, row_ref)
    fed_sends, grad_wide = in_order(fed_sends, grad_wide)
    out_partial = column_grads([(grad_wide, gated)], 4)
    out_partial, grad_wide = in_order(out_partial, grad_wide)
    out_partial, feed_grad = in_order(out_partial, feed_grad)
    out_grad = scatter_col(out_partial)
    add_fed_out, gate_results = reduce_row_finish(
        fed_sends,
        [hidden],
        [down_part],
        row_ref,
        lambda _: tuple(
            gate_back(
                meta, rates, grad_wide, out_part, gate_raw, normal, inverse, query_rot, group_gain, group_bias
            )
        ),
        rest=fed_rest,
        delayed=True,
    )
    grad_gate, grad_retained, group_gain_grad, group_bias_grad, returns, first_state = gate_results
    own0, own1, own2, gate_partial = return_states(
        meta, rates, returns, first_state, first_wide, grad_gate, rows
    )
    gate_partial, own0, out_grad = in_order(gate_partial, own0, out_grad)
    own = (own0, own1, own2)
    gate_grad = scatter_col(gate_partial)
    grad_query, grad_key, grad_value = retain_back(
        meta, rates, query_rot, key_rot, value_low, grad_retained, states, cosine, sine, own
    )
    back_values = [grad_query, grad_key, grad_value, grad_gate]
    back_weights = [query_part, key_part, value_part, gate_part]
    sends = reduce_row_start(back_values, back_weights, row_ref)
    sends, grad_value = in_order(sends, grad_value)
    fed_out, back_rest = add_fed_out(reduce_row_rest(back_values, back_weights, row_ref))
    fed_out = fed_out + down_bias
    layer_out = middle + fed_out
    first_back, project_partial = reduce_row_finish(
        sends,
        back_values,
        back_weights,
        row_ref,
        lambda _: column_grads(
            [(first_wide, grad_query), (first_wide, grad_key), (first_wide, grad_value)], 6
        ),
        rest=back_rest,
    )
    project_partial, gate_grad = in_order(project_partial, gate_grad)
    project_grad = scatter_col(project_partial).astype(F32)
    feed_grad, out_grad, gate_grad = (
        grad.astype(F32) for grad in (feed_grad, out_grad, gate_grad)
    )

    first_normal = (tokens.astype(F32) - first_average[:, :1]) * first_inverse[:, :1]
    grad_first, first_gain_grad, first_bias_grad = norm_backward(
        first_back, first_normal, first_inverse[:, :1], first_gain
    )
    tokens_grad = grad_middle + grad_first

    squares = jnp.stack(
        [
            jnp.sum(column * layer_out * layer_out),
            jnp.sum(column * attended * attended),
            jnp.sum(column * fed_out * fed_out),
        ]
    )
    vectors, col_squares = sum_col_vectors(
        (
            first_gain_grad,
            first_bias_grad,
            group_gain_grad[0],
            group_bias_grad[0],
            second_gain_grad,
            second_bias_grad,
            up_bias_grad[0],
            down_bias_grad,
        ),
        jnp.concatenate([squares, jnp.zeros((125,), F32)]),
    )
    totals = sum_row_direct(col_squares[None, :])[0, :3]
    valid_count = jnp.sum(segment_lengths).astype(F32) * D
    norm_values = jnp.sqrt(totals / valid_count)
    return (
        layer_out.astype(BF16),
        tokens_grad,
        project_grad[:, :narrow],
        project_grad[:, narrow : 2 * narrow],
        project_grad[:, 2 * narrow :],
        gate_grad,
        out_grad.T,
        feed_grad[:, wide:],
        feed_grad[:, :wide].T,
        *vectors,
        norm_values,
    )


def solution(mesh):
    matrix, turned, vector = P("col", "row"), P("row", "col"), P("row")
    in_specs = (matrix,) * 6 + (turned, matrix, turned) + (vector,) * 8 + (P(), P())
    split = P(("row", "col"))
    out_specs = (matrix,) * 6 + (turned, matrix, turned) + (split,) * 8 + (P(),)
    return jax.shard_map(body, mesh=mesh, in_specs=in_specs, out_specs=out_specs, check_vma=False)
```

```python
import functools

import jax
import jax.numpy as jnp
from jax import lax
from jax.experimental import pallas as pl
from jax.experimental.pallas import tpu as pltpu
from jax.sharding import PartitionSpec as P

D = 2048
QK = 256
HV = 512
TRUNK = 4096
SEG = 512
TREE_LEN = TRUNK + 12 * SEG
CHUNK = 256
TRUNK_CHUNKS = TRUNK // CHUNK
SLOTS = 8
GRAD_TILE = 256

EPSILON = 1e-05
SCALE = QK**-0.5
F32 = jnp.float32
BF16 = jnp.bfloat16

X_PAIRS = [(0, 1), (1, 0), (2, 3), (3, 2)]
Y_PAIRS = [(0, 2), (2, 0), (1, 3), (3, 1)]
D_PAIRS = [(0, 3), (3, 0), (1, 2), (2, 1)]


def mm(a, b):
    return lax.dot_general(a, b, (((1,), (0,)), ((), ())), preferred_element_type=F32)


def mm_nt(a, b):
    return lax.dot_general(a, b, (((1,), (1,)), ((), ())), preferred_element_type=F32)


def mm_tn(a, b):
    return lax.dot_general(a, b, (((0,), (0,)), ((), ())), preferred_element_type=F32)


def params(semantics, limit=None):
    return pltpu.CompilerParams(
        dimension_semantics=semantics, vmem_limit_bytes=limit or 60 * 1024 * 1024
    )


def smem():
    return pl.BlockSpec(memory_space=pltpu.SMEM)


class Chunk:
    def __init__(self, meta, index):
        in_trunk = index < TRUNK_CHUNKS
        beyond = jnp.maximum(index - TRUNK_CHUNKS, 0)
        self.in_trunk = in_trunk
        self.segment = jnp.where(in_trunk, 0, 1 + beyond // 2)
        self.first = jnp.where(in_trunk, index * CHUNK, (beyond % 2) * CHUNK)
        length = meta[self.segment]
        trunk_length = meta[0]
        self.trunk_length = trunk_length
        self.length = length
        self.is_leaf = self.segment >= 5
        self.parent = meta[13 + jnp.clip(self.segment - 5, 0, 7)]
        parent_length = meta[1 + self.parent]
        self.start = jnp.where(
            in_trunk,
            self.first,
            trunk_length + self.first + jnp.where(self.is_leaf, parent_length, 0),
        )
        self.count = jnp.clip(length - self.first, 0, CHUNK)
        self.end = self.start + self.count
        self.continues = jnp.where(in_trunk, index + 1 < TRUNK_CHUNKS, beyond % 2 == 0)


def trunk_reference(meta, place, rows):
    return jnp.minimum(meta[0], jnp.minimum(rows * (place + 1), TRUNK))


def power(rate, exponent, width):
    return jnp.exp(jnp.full((1, width), exponent.astype(F32), F32) * rate)


def column_power(rate, exponents):
    return jnp.exp(exponents.astype(F32) * rate)


def token_column(width=1):
    return lax.broadcasted_iota(jnp.int32, (CHUNK, width), 0)


def decay_matrix(rate):
    t = lax.broadcasted_iota(jnp.int32, (CHUNK, CHUNK), 0)
    u = lax.broadcasted_iota(jnp.int32, (CHUNK, CHUNK), 1)
    return jnp.where(u <= t, jnp.exp((t - u).astype(F32) * rate) * SCALE, 0.0)


def valid_decay(decay, count):
    u = lax.broadcasted_iota(jnp.int32, (1, CHUNK), 1)
    return decay[...] * jnp.where(u < count, 1.0, 0.0)


def key_decay(rate, count):
    j = token_column()
    return jnp.where(j < count, column_power(rate, jnp.maximum(count - j, 0)), 0.0)


def export_terms(meta, chunk, local, chunks, place, slot, rows):
    if slot == 0:
        is_shift = ((place == 4) | (place == 6)) & (local == chunks - 1)
        exponent = jnp.where(
            chunk.in_trunk,
            jnp.maximum(trunk_reference(meta, place, rows) - chunk.end, 0),
            0,
        )
        return chunk.in_trunk | is_shift, exponent
    wanted = (place == 3) | (place == 4)
    mine = (chunk.segment % 2 == 1) if slot == 1 else (chunk.segment % 2 == 0)
    is_branch = (chunk.segment >= 1) & (chunk.segment < 5)
    exponent = jnp.where(is_branch, jnp.maximum(chunk.length - chunk.first - chunk.count, 0), 0)
    return wanted & mine & is_branch, exponent


def import_terms(meta, chunk, place, slot, rows):
    if slot < 4:
        sees = jnp.logical_not(chunk.in_trunk) | (place > slot)
        if slot < 3:
            sees = sees & (place < 4)
        return sees, jnp.maximum(chunk.start - trunk_reference(meta, jnp.int32(slot), rows), 0)
    sees = chunk.is_leaf & (chunk.parent == slot - 4)
    return sees, chunk.first


def shift_in(meta, place, chunks):
    previous = Chunk(meta, jnp.maximum(place * chunks - 1, 0))
    return (place == 5) | (place == 7), CHUNK - previous.count


def retain_kernel(
    rows, chunks, meta, rates, query, key, value, wide, weight, shared, shifted, gain, bias,
    gate_out, gated_out, normal_out, inverse_out, state_out, running, total, decay,
):
    local = pl.program_id(1)
    rate = rates[pl.program_id(0)]
    place = meta[21]
    chunk = Chunk(meta, place * chunks + local)

    @pl.when(local == 0)
    def _():
        decay[...] = decay_matrix(rate)
        running[...] = jnp.zeros_like(running)
        on, exponent = shift_in(meta, place, chunks)

        @pl.when(on)
        def _():
            running[...] = shifted[0].astype(F32) * power(rate, exponent, HV)

    incoming = running[...]
    total[...] = incoming
    for slot in range(SLOTS):
        on, exponent = import_terms(meta, chunk, place, slot, rows)

        @pl.when(on)
        def _():
            total[...] += shared[slot, 0].astype(F32) * power(rate, exponent, HV)

    state = total[...].astype(BF16)
    state_out[0, 0] = state

    q, k, v = query[...], key[...], value[...]
    scores = (mm_nt(q, k) * valid_decay(decay, chunk.count)).astype(BF16)
    own = token_column()
    reach = column_power(rate, own) * SCALE
    retained = mm(scores, v) + mm(q, state) * reach

    j = token_column()
    ahead = jnp.where(j < chunk.count, column_power(rate, CHUNK - j), 0.0)
    fresh = mm_tn((k.astype(F32) * ahead).astype(BF16), v)
    keep = jnp.where(chunk.continues, 1.0, 0.0)
    running[...] = (incoming * power(rate, jnp.int32(CHUNK), HV) + fresh) * keep

    average = jnp.mean(retained, axis=1, keepdims=True)
    centred = retained - average
    inverse = lax.rsqrt(jnp.mean(centred * centred, axis=1, keepdims=True) + EPSILON)
    normal = centred * inverse
    gate_value = mm(wide[...], weight[...])
    gate_out[...] = gate_value
    gated = (normal * gain[...] + bias[...]) * (gate_value / (1.0 + jnp.exp(-gate_value)))
    gated_out[...] = gated.astype(BF16)
    normal_out[...] = normal.astype(BF16)
    inverse_out[0] = jnp.broadcast_to(inverse, (CHUNK, 128))


def retain(meta, rates, query, key, value, inputs, weight, shared, shifted, gain, bias):
    array, _, number = weight
    rows = key.shape[0]
    heads = key.shape[1] // QK
    chunks = rows // CHUNK
    wide = pl.BlockSpec((CHUNK, HV), lambda h, c: (c, h))
    narrow = pl.BlockSpec((CHUNK, QK), lambda h, c: (c, h))
    vector = pl.BlockSpec((1, HV), lambda h, c: (0, h))
    return pl.pallas_call(
        functools.partial(retain_kernel, rows, chunks),
        grid=(heads, chunks),
        in_specs=[
            smem(), smem(), narrow, narrow, wide,
            pl.BlockSpec((CHUNK, D), lambda h, c: (c, 0)),
            pl.BlockSpec((D, HV), lambda h, c: (0, number * heads + h)),
            pl.BlockSpec((SLOTS, 1, QK, HV), lambda h, c: (0, h, 0, 0)),
            pl.BlockSpec((1, QK, HV), lambda h, c: (h, 0, 0)),
            vector, vector,
        ],
        out_specs=[
            wide, wide, wide,
            pl.BlockSpec((1, CHUNK, 128), lambda h, c: (h, c, 0)),
            pl.BlockSpec((1, 1, QK, HV), lambda h, c: (h, c, 0, 0)),
        ],
        out_shape=[
            jax.ShapeDtypeStruct((rows, heads * HV), F32),
            jax.ShapeDtypeStruct((rows, heads * HV), BF16),
            jax.ShapeDtypeStruct((rows, heads * HV), BF16),
            jax.ShapeDtypeStruct((heads, rows, 128), F32),
            jax.ShapeDtypeStruct((heads, chunks, QK, HV), BF16),
        ],
        scratch_shapes=[
            pltpu.VMEM((QK, HV), F32), pltpu.VMEM((QK, HV), F32), pltpu.VMEM((CHUNK, CHUNK), F32)
        ],
        compiler_params=params(("arbitrary", "arbitrary")),
        name="retention_forward",
        cost_estimate=pl.CostEstimate(
            flops=2 * rows * heads * (CHUNK * 768 + 2 * QK * HV + D * HV),
            bytes_accessed=rows * heads * 8192,
            transcendentals=rows * heads * 768,
        ),
    )(meta, rates, query, key, value, inputs, array, shared, shifted, gain[None, :], bias[None, :])


def gate_back_kernel(
    rows, chunks, meta, rates, wide, weight, gate, normal_in, inverse_in, query, gain, bias,
    gate_out, retained_out, gain_out, bias_out, exports, first_out, acc,
):
    local = pl.program_id(1)
    rate = rates[pl.program_id(0)]
    place = meta[21]
    chunk = Chunk(meta, place * chunks + local)
    grad_gated = mm(wide[...], weight[...])
    gate_value = gate[...].astype(F32)
    normal = normal_in[...].astype(F32)
    sigmoid = 1.0 / (1.0 + jnp.exp(-gate_value))
    normed = normal * gain[...] + bias[...]
    grad_gate = grad_gated * normed * (sigmoid * (1.0 + gate_value * (1.0 - sigmoid)))
    gate_out[...] = grad_gate.astype(BF16)
    grad_normed = grad_gated * (gate_value * sigmoid)

    @pl.when(local == 0)
    def _():
        gain_out[...] = jnp.zeros_like(gain_out)
        bias_out[...] = jnp.zeros_like(bias_out)
        acc[...] = jnp.zeros_like(acc)

    gain_out[...] += jnp.sum(grad_normed * normal, axis=0, keepdims=True)
    bias_out[...] += jnp.sum(grad_normed, axis=0, keepdims=True)
    scaled = grad_normed * gain[...]
    grad = inverse_in[0][:, :1] * (
        scaled
        - jnp.mean(scaled, axis=1, keepdims=True)
        - normal * jnp.mean(scaled * normal, axis=1, keepdims=True)
    )
    grad = grad.astype(BF16)
    retained_out[...] = grad
    reach = column_power(rate, token_column()) * SCALE
    state = mm_tn((query[...].astype(F32) * reach).astype(BF16), grad)
    for slot in range(SLOTS):
        on, exponent = import_terms(meta, chunk, place, slot, rows)

        @pl.when(on)
        def _():
            acc[slot] += state * power(rate, exponent, HV)

    @pl.when(local == 0)
    def _():
        on, exponent = shift_in(meta, place, chunks)
        scale = jnp.where(on, power(rate, exponent, HV), 0.0)
        first_out[0] = (state * scale).astype(BF16)

    @pl.when(local == chunks - 1)
    def _():
        exports[:, 0] = acc[...].astype(BF16)


def gate_back(meta, rates, wide, weight, gate, normal, inverse, query, gain, bias):
    array, width, number = weight
    first = number * (width // HV)
    rows = query.shape[0]
    heads = query.shape[1] // QK
    chunks = rows // CHUNK
    block = pl.BlockSpec((CHUNK, HV), lambda h, c: (c, h))
    vector = pl.BlockSpec((1, HV), lambda h, c: (0, h))
    return pl.pallas_call(
        functools.partial(gate_back_kernel, rows, chunks),
        grid=(heads, chunks),
        in_specs=[
            smem(), smem(),
            pl.BlockSpec((CHUNK, D), lambda h, c: (c, 0)),
            pl.BlockSpec((D, HV), lambda h, c: (0, first + h)),
            block, block,
            pl.BlockSpec((1, CHUNK, 128), lambda h, c: (h, c, 0)),
            pl.BlockSpec((CHUNK, QK), lambda h, c: (c, h)),
            vector, vector,
        ],
        out_specs=[
            block, block, vector, vector,
            pl.BlockSpec((SLOTS, 1, QK, HV), lambda h, c: (0, h, 0, 0)),
            pl.BlockSpec((1, QK, HV), lambda h, c: (h, 0, 0)),
        ],
        out_shape=[
            jax.ShapeDtypeStruct((rows, heads * HV), BF16),
            jax.ShapeDtypeStruct((rows, heads * HV), BF16),
            jax.ShapeDtypeStruct((1, heads * HV), F32),
            jax.ShapeDtypeStruct((1, heads * HV), F32),
            jax.ShapeDtypeStruct((SLOTS, heads, QK, HV), BF16),
            jax.ShapeDtypeStruct((heads, QK, HV), BF16),
        ],
        scratch_shapes=[pltpu.VMEM((SLOTS, QK, HV), F32)],
        compiler_params=params(("arbitrary", "arbitrary")),
        name="gate_backward",
        cost_estimate=pl.CostEstimate(
            flops=2 * rows * heads * HV * (D + QK),
            bytes_accessed=rows * heads * 12288,
            transcendentals=rows * heads * HV,
        ),
    )(meta, rates, wide, array, gate, normal, inverse, query, gain[None, :], bias[None, :])


def retain_back_kernel(
    rows, chunks, meta, rates, query, key, value, grad, state_in, cosine, sine, own0, own1, own2,
    query_out, key_out, value_out, running, total_ref, decay_ref,
):
    step = pl.program_id(1)
    local = chunks - 1 - step
    rate = rates[pl.program_id(0)]
    place = meta[21]
    chunk = Chunk(meta, place * chunks + local)
    before = Chunk(meta, jnp.maximum(place * chunks + local - 1, 0))

    @pl.when(step == 0)
    def _():
        decay_ref[...] = decay_matrix(rate)
        running[...] = jnp.zeros_like(running)

    later = running[...]
    total_ref[...] = later
    for slot, ref in ((0, own0), (1, own1), (2, own2)):
        on, exponent = export_terms(meta, chunk, local, chunks, place, slot, rows)

        @pl.when(on)
        def _():
            total_ref[...] += ref[0].astype(F32) * power(rate, exponent, HV)

    total = total_ref[...].astype(BF16)

    q, k, v, g = query[...], key[...], value[...], grad[...]
    decay = valid_decay(decay_ref, chunk.count)
    scores = (mm_nt(q, k) * decay).astype(BF16)
    slopes = (mm_nt(g, v) * decay).astype(BF16)
    reach = column_power(rate, token_column()) * SCALE
    toward = key_decay(rate, chunk.count)
    grad_query = mm(slopes, k) + mm_nt(g, state_in[0, 0]) * reach
    grad_key = mm_tn(slopes, q) + mm_nt(v, total) * toward
    grad_value = mm_tn(scores, g) + mm(k, total) * toward
    value_out[...] = grad_value.astype(BF16)
    cos, sin = cosine[...], sine[...]
    half = QK // 2
    for out, val in ((query_out, grad_query), (key_out, grad_key)):
        a, b = val[:, :half], val[:, half:]
        out[:, :half] = (a * cos + b * sin).astype(BF16)
        out[:, half:] = (b * cos - a * sin).astype(BF16)

    fresh = mm_tn((q.astype(F32) * reach).astype(BF16), g)
    carried = fresh + later * power(rate, chunk.count, HV)
    keep = jnp.where((local > 0) & before.continues, 1.0, 0.0)
    running[...] = carried * power(rate, CHUNK - before.count, HV) * keep


def retain_back(meta, rates, query, key, value, grad, states, cosine, sine, own):
    rows = query.shape[0]
    heads = query.shape[1] // QK
    chunks = rows // CHUNK
    last = chunks - 1
    wide = pl.BlockSpec((CHUNK, HV), lambda h, s: (last - s, h))
    narrow = pl.BlockSpec((CHUNK, QK), lambda h, s: (last - s, h))
    table = pl.BlockSpec((CHUNK, QK // 2), lambda h, s: (last - s, 0))
    state = pl.BlockSpec((1, QK, HV), lambda h, s: (h, 0, 0))
    return pl.pallas_call(
        functools.partial(retain_back_kernel, rows, chunks),
        grid=(heads, chunks),
        in_specs=[
            smem(), smem(), narrow, narrow, wide, wide,
            pl.BlockSpec((1, 1, QK, HV), lambda h, s: (h, last - s, 0, 0)),
            table, table, state, state, state,
        ],
        out_specs=[narrow, narrow, wide],
        out_shape=[
            jax.ShapeDtypeStruct((rows, heads * QK), BF16),
            jax.ShapeDtypeStruct((rows, heads * QK), BF16),
            jax.ShapeDtypeStruct((rows, heads * HV), BF16),
        ],
        scratch_shapes=[
            pltpu.VMEM((QK, HV), F32), pltpu.VMEM((QK, HV), F32), pltpu.VMEM((CHUNK, CHUNK), F32)
        ],
        compiler_params=params(("arbitrary", "arbitrary")),
        name="retention_backward",
        cost_estimate=pl.CostEstimate(
            flops=2 * rows * heads * (CHUNK * 1792 + 4 * QK * HV),
            bytes_accessed=rows * heads * 6144,
            transcendentals=rows * heads * 256,
        ),
    )(meta, rates, query, key, value, grad, states, cosine, sine, *own)


def norm_kernel(values, gain, bias, out, average_out, inverse_out):
    x = values[...].astype(F32)
    average = jnp.mean(x, axis=1, keepdims=True)
    inverse = lax.rsqrt(jnp.mean(x * x, axis=1, keepdims=True) - average * average + EPSILON)
    out[...] = ((x - average) * inverse * gain[...] + bias[...]).astype(BF16)
    average_out[...] = jnp.broadcast_to(average, average_out.shape)
    inverse_out[...] = jnp.broadcast_to(inverse, inverse_out.shape)


def norm_wide(values, gain, bias):
    rows = values.shape[0]
    block = pl.BlockSpec((CHUNK, D), lambda i: (i, 0))
    vector = pl.BlockSpec((1, D), lambda i: (0, 0))
    stat = pl.BlockSpec((CHUNK, 128), lambda i: (i, 0))
    return pl.pallas_call(
        norm_kernel,
        grid=(rows // CHUNK,),
        in_specs=[block, vector, vector],
        out_specs=[block, stat, stat],
        out_shape=[
            jax.ShapeDtypeStruct((rows, D), BF16),
            jax.ShapeDtypeStruct((rows, 128), F32),
            jax.ShapeDtypeStruct((rows, 128), F32),
        ],
        compiler_params=params(("arbitrary",)),
        name="layer_norm",
        cost_estimate=pl.CostEstimate(
            flops=8 * rows * D, bytes_accessed=4 * rows * D, transcendentals=rows
        ),
    )(values, gain[None, :], bias[None, :])


def join_kernel(row, own, from_x, from_y, far_a, far_b, *refs, norm):
    block = own.shape[1]
    second = pl.program_id(0) >= pl.num_programs(0) // 2
    spots = [
        pl.ds(pl.multiple_of((row[0] ^ flip) * block, 128), block) for flip in range(4)
    ]
    pieces = [own[...], from_x[...], from_y[...], jnp.where(second, far_b[...], far_a[...])]
    if not norm:
        for spot, piece in zip(spots, pieces):
            refs[0][:, spot] = piece
        return
    gain, bias, out, average_out, inverse_out = refs
    pieces = [piece.astype(F32) for piece in pieces]
    average = sum(jnp.sum(piece, axis=1, keepdims=True) for piece in pieces) / D
    squares = sum(jnp.sum(piece * piece, axis=1, keepdims=True) for piece in pieces) / D
    inverse = lax.rsqrt(squares - average * average + EPSILON)
    for spot, piece in zip(spots, pieces):
        out[:, spot] = ((piece - average) * inverse * gain[:, spot] + bias[:, spot]).astype(BF16)
    average_out[...] = jnp.broadcast_to(average, average_out.shape)
    inverse_out[...] = jnp.broadcast_to(inverse, inverse_out.shape)


def join(pieces, row, gain=None, bias=None):
    norm = gain is not None
    if not isinstance(pieces, tuple):
        return norm_wide(pieces, gain, bias) if norm else pieces
    rows, block = pieces[0].shape
    steps = 4
    tile = rows // steps
    piece = pl.BlockSpec((tile, block), lambda i, r: (i, 0))
    far_a = pl.BlockSpec((tile, block), lambda i, r: (jnp.minimum(i, steps // 2 - 1), 0))
    far_b = pl.BlockSpec((tile, block), lambda i, r: (jnp.maximum(i - steps // 2, 0), 0))
    vector = pl.BlockSpec((1, D), lambda i, r: (0, 0))
    wide = pl.BlockSpec((tile, D), lambda i, r: (i, 0))
    stat = pl.BlockSpec((tile, 128), lambda i, r: (i, 0))
    wide_shape = jax.ShapeDtypeStruct((rows, D), BF16)
    stat_shape = jax.ShapeDtypeStruct((rows, 128), F32)
    return pl.pallas_call(
        functools.partial(join_kernel, norm=norm),
        grid_spec=pltpu.PrefetchScalarGridSpec(
            num_scalar_prefetch=1,
            grid=(steps,),
            in_specs=[piece] * 3 + [far_a, far_b] + ([vector] * 2 if norm else []),
            out_specs=[wide, stat, stat] if norm else wide,
        ),
        out_shape=[wide_shape, stat_shape, stat_shape] if norm else wide_shape,
        compiler_params=params(("arbitrary",)),
        name="join_norm" if norm else "join",
        cost_estimate=pl.CostEstimate(
            flops=8 * rows * D, bytes_accessed=4 * rows * D, transcendentals=0
        ),
    )(row, *pieces, *((gain[None, :], bias[None, :]) if norm else ()))


def project_kernel(
    heads, rows, chunks, meta, rates, values, weight, cosine, sine,
    query_out, key_out, value_out, exports, acc,
):
    local = pl.program_id(0)
    place = meta[21]
    chunk = Chunk(meta, place * chunks + local)
    raw = mm(values[...], weight[...])
    cos, sin = cosine[...], sine[...]
    half = QK // 2
    for part, out in ((0, query_out), (1, key_out)):
        for head in range(heads):
            first = (part * heads + head) * QK
            a, b = raw[:, first : first + half], raw[:, first + half : first + QK]
            out[:, head * QK : head * QK + half] = (a * cos - b * sin).astype(BF16)
            out[:, head * QK + half : (head + 1) * QK] = (b * cos + a * sin).astype(BF16)
    value_out[...] = raw[:, 2 * heads * QK :].astype(BF16)

    @pl.when(local == 0)
    def _():
        acc[...] = jnp.zeros_like(acc)

    for head in range(heads):
        rate = rates[head]
        key = key_out[:, head * QK : (head + 1) * QK].astype(F32)
        weighted = (key * key_decay(rate, chunk.count)).astype(BF16)
        state = mm_tn(weighted, value_out[:, head * HV : (head + 1) * HV])
        for slot in range(3):
            on, exponent = export_terms(meta, chunk, local, chunks, place, slot, rows)

            @pl.when(on)
            def _():
                acc[slot, head] += state * power(rate, exponent, HV)

    @pl.when(local == chunks - 1)
    def _():
        exports[...] = acc[...].astype(BF16)


def project(meta, rates, values, weight, cosine, sine):
    rows, width = values.shape[0], weight.shape[1]
    heads = width // (2 * QK + HV)
    chunks = rows // CHUNK
    table = pl.BlockSpec((CHUNK, QK // 2), lambda i: (i, 0))
    widths = (heads * QK, heads * QK, heads * HV)
    states = (3, heads, QK, HV)
    return pl.pallas_call(
        functools.partial(project_kernel, heads, rows, chunks),
        grid=(chunks,),
        in_specs=[
            smem(), smem(),
            pl.BlockSpec((CHUNK, D), lambda i: (i, 0)),
            pl.BlockSpec((D, width), lambda i: (0, 0)),
            table, table,
        ],
        out_specs=[pl.BlockSpec((CHUNK, w), lambda i: (i, 0)) for w in widths]
        + [pl.BlockSpec(states, lambda i: (0, 0, 0, 0))],
        out_shape=[jax.ShapeDtypeStruct((rows, w), BF16) for w in widths]
        + [jax.ShapeDtypeStruct(states, BF16)],
        scratch_shapes=[pltpu.VMEM(states, F32)],
        compiler_params=params(("arbitrary",)),
        name="project",
        cost_estimate=pl.CostEstimate(
            flops=2 * rows * D * width, bytes_accessed=2 * (rows + width) * D, transcendentals=0
        ),
    )(meta, rates, values, weight, cosine, sine)


def matmul_kernel(values, weight, out):
    out[...] = mm(values[...], weight[...]).astype(out.dtype)


def matmul(values, weight, kind):
    array, width, number = weight
    rows = values.shape[0]
    return pl.pallas_call(
        matmul_kernel,
        grid=(rows // CHUNK,),
        in_specs=[
            pl.BlockSpec((CHUNK, D), lambda i: (i, 0)),
            pl.BlockSpec((D, width), lambda i: (0, number)),
        ],
        out_specs=pl.BlockSpec((CHUNK, width), lambda i: (i, 0)),
        out_shape=jax.ShapeDtypeStruct((rows, width), kind),
        compiler_params=params(("arbitrary",)),
        name="matmul",
        cost_estimate=pl.CostEstimate(
            flops=2 * rows * D * width, bytes_accessed=2 * (rows + width) * D, transcendentals=0
        ),
    )(values, array)


def weight_grad_kernel(spans, *refs):
    count = len(spans)
    lefts, rights, out = refs[:count], refs[count : 2 * count], refs[2 * count]
    tile = pl.program_id(0)
    for left, right, (first, last) in zip(lefts, rights, spans):

        @pl.when((tile >= first) & (tile < last))
        def _():
            out[...] = mm_tn(left[...], right[...]).astype(BF16)


def weight_grads(pairs):
    rows = pairs[0][0].shape[0]
    wide = min(right.shape[1] for _, right in pairs)
    tall = 1024
    steps = D // tall
    spans, first = [], 0
    for _, right in pairs:
        spans.append((first, first + right.shape[1] // wide))
        first = spans[-1][1]

    def left_spec(span):
        return pl.BlockSpec(
            (rows, tall),
            lambda n, m: (
                0, jnp.where(n < span[0], 0, jnp.where(n < span[1], m, steps - 1)),
            ),
        )

    def right_spec(span):
        return pl.BlockSpec(
            (rows, wide), lambda n, m: (0, jnp.clip(n - span[0], 0, span[1] - span[0] - 1))
        )

    return pl.pallas_call(
        functools.partial(weight_grad_kernel, tuple(spans)),
        grid=(first, steps),
        in_specs=[left_spec(span) for span in spans] + [right_spec(span) for span in spans],
        out_specs=pl.BlockSpec((tall, wide), lambda n, m: (m, n)),
        out_shape=jax.ShapeDtypeStruct((D, first * wide), BF16),
        compiler_params=params(("arbitrary", "arbitrary")),
        name="weight_grads",
        cost_estimate=pl.CostEstimate(
            flops=2 * rows * D * first * wide,
            bytes_accessed=2 * D * first * wide + 4 * rows * D,
            transcendentals=0,
        ),
    )(*[left for left, _ in pairs], *[right for _, right in pairs])


def paired_grad_kernel(spans, tiles, steps, *refs):
    count = len(spans)
    lefts, rights = refs[:count], refs[count : 2 * count]
    out, made, received, send_sem, recv_sem = refs[2 * count :]
    step = pl.program_id(0)
    core = lax.axis_index("col") % 2
    partner = lax.axis_index("col") + 1 - 2 * core

    def copy(index):
        return pltpu.make_async_remote_copy(
            src_ref=made.at[index, :, 1 - core],
            dst_ref=received.at[index],
            send_sem=send_sem.at[index],
            recv_sem=recv_sem.at[index],
            device_id={"col": partner},
            device_id_type=pl.DeviceIdType.MESH,
        )

    @pl.when(step == 0)
    def _():
        barrier = pltpu.get_barrier_semaphore()
        pl.semaphore_signal(
            barrier, inc=1, device_id={"col": partner}, device_id_type=pl.DeviceIdType.MESH
        )
        pl.semaphore_wait(barrier, 1)

    for left, right, (first, last) in zip(lefts, rights, spans):

        @pl.when((step >= first * steps) & (step < last * steps))
        def _():
            total = mm_tn(left[...], right[...]).astype(BF16)
            made[step] = total.reshape(made.shape[1:])

    @pl.when(step < tiles)
    def _():
        copy(step).start()

    @pl.when(step > 0)
    def _():
        index = step - 1
        copy(index).wait()
        out[...] = (made[index, :, core].astype(F32) + received[index].astype(F32)).astype(BF16)


def paired_grads(pairs, number):
    rows = pairs[0][0].shape[0]
    wide = min(right.shape[1] for _, right in pairs)
    wide = min(wide, 512)
    tall = 1024
    steps = D // tall
    block = D // SLOTS
    depth = tall // block // 2
    spans, first = [], 0
    for _, right in pairs:
        spans.append((first, first + right.shape[1] // wide))
        first = spans[-1][1]
    tiles = first * steps

    def left_spec(span):
        def index(s):
            n, m = s // steps, s % steps
            return 0, jnp.where(n < span[0], 0, jnp.where(n < span[1], m, steps - 1))

        return pl.BlockSpec((rows, tall), index)

    def right_spec(span):
        def index(s):
            return 0, jnp.clip(s // steps - span[0], 0, span[1] - span[0] - 1)

        return pl.BlockSpec((rows, wide), index)

    def out_index(s):
        done = jnp.maximum(s - 1, 0)
        return done % steps, 0, done // steps

    result = pl.pallas_call(
        functools.partial(paired_grad_kernel, tuple(spans), tiles, steps),
        grid=(tiles + 1,),
        in_specs=[left_spec(span) for span in spans] + [right_spec(span) for span in spans],
        out_specs=pl.BlockSpec((depth, block, wide), out_index),
        out_shape=jax.ShapeDtypeStruct((SLOTS // 2, block, first * wide), BF16),
        scratch_shapes=[
            pltpu.VMEM((tiles, depth, 2, block, wide), BF16),
            pltpu.VMEM((tiles, depth, block, wide), BF16),
            pltpu.SemaphoreType.DMA((tiles,)),
            pltpu.SemaphoreType.DMA((tiles,)),
        ],
        compiler_params=pltpu.CompilerParams(
            dimension_semantics=("arbitrary",),
            collective_id=number,
            has_side_effects=True,
            vmem_limit_bytes=60 * 1024 * 1024,
        ),
        name="paired_grads",
        cost_estimate=pl.CostEstimate(
            flops=2 * rows * D * first * wide,
            bytes_accessed=2 * D * first * wide + 4 * rows * D,
            transcendentals=0,
        ),
    )(*[left for left, _ in pairs], *[right for _, right in pairs])
    return result


def column_grads(pairs, number):
    if lax.axis_size("col") != SLOTS:
        return weight_grads(pairs)
    return paired_grads(pairs, number)


def norm_pieces(row, own, from_x, from_y, far_a, far_b, gain, bias, out, average_out, inverse_out):
    block = own.shape[1]
    second = pl.program_id(0) >= pl.num_programs(0) // 2
    far = jnp.where(second, far_b[...], far_a[...])
    pieces = [piece.astype(F32) for piece in (own[...], from_x[...], from_y[...], far)]
    average = sum(jnp.sum(piece, axis=1, keepdims=True) for piece in pieces) / D
    squares = sum(jnp.sum(piece * piece, axis=1, keepdims=True) for piece in pieces) / D
    inverse = lax.rsqrt(squares - average * average + EPSILON)
    for flip, piece in enumerate(pieces):
        spot = pl.ds(pl.multiple_of((row[0] ^ flip) * block, 128), block)
        out[:, spot] = ((piece - average) * inverse * gain[:, spot] + bias[:, spot]).astype(BF16)
    average_out[...] = jnp.broadcast_to(average, average_out.shape)
    inverse_out[...] = jnp.broadcast_to(inverse, inverse_out.shape)


def up_kernel(row, *refs, joined):
    if joined:
        pieces, gain, norm_bias = refs[:5], refs[5], refs[6]
        weight, bias, grad_hidden, scales, second_out, average_out, inverse_out = refs[7:14]
        hidden_out, grad_out, bias_out, sums_out, moved = refs[14:]
        norm_pieces(row, *pieces, gain, norm_bias, second_out, average_out, inverse_out)
        values = second_out
    else:
        values, weight, bias, grad_hidden, scales = refs[:5]
        hidden_out, grad_out, bias_out, sums_out, moved = refs[5:]
    before = mm(values[...], weight[...]) + bias[...]
    phi = 0.5 * (1.0 + lax.erf(before * (0.5**0.5)))
    hidden_out[...] = (before * phi).astype(BF16)
    density = jnp.exp(-0.5 * before * before) * 0.3989422804014327
    grad = (grad_hidden[...].astype(F32) * (phi + before * density)).astype(BF16)
    grad_out[...] = grad

    @pl.when(pl.program_id(0) == 0)
    def _():
        bias_out[...] = jnp.zeros_like(bias_out)
        parts = mm(scales[...], weight[...])
        moved[0:1] = parts[0:1] + parts[1:2]
        moved[1:2] = parts[2:3] + parts[3:4]

    wide_grad = grad.astype(F32)
    bias_out[...] += jnp.sum(wide_grad, axis=0, keepdims=True)
    plain = jnp.sum(wide_grad * moved[0:1], axis=1, keepdims=True)
    crossed = jnp.sum(wide_grad * (before - bias[...] - moved[1:2]), axis=1, keepdims=True)
    lane = lax.broadcasted_iota(jnp.int32, sums_out.shape, 1)
    sums_out[...] = jnp.where(lane == 0, plain, crossed)


def feed_up(pieces, row, gain, norm_bias, weight, bias, grad_hidden):
    array, width, number = weight
    joined = isinstance(pieces, tuple)
    rows = grad_hidden.shape[0]
    steps = 4
    tile = rows // steps
    block = pl.BlockSpec((tile, width), lambda i, r: (i, 0))
    vector = pl.BlockSpec((1, width), lambda i, r: (0, 0))
    wide = pl.BlockSpec((tile, D), lambda i, r: (i, 0))
    stat = pl.BlockSpec((tile, 128), lambda i, r: (i, 0))
    gains = pl.BlockSpec((1, D), lambda i, r: (0, 0))
    if joined:
        piece = pl.BlockSpec((tile, pieces[0].shape[1]), lambda i, r: (i, 0))
        far_a = pl.BlockSpec(
            (tile, pieces[0].shape[1]), lambda i, r: (jnp.minimum(i, steps // 2 - 1), 0)
        )
        far_b = pl.BlockSpec(
            (tile, pieces[0].shape[1]), lambda i, r: (jnp.maximum(i - steps // 2, 0), 0)
        )
        inputs = list(pieces) + [gain[None, :], norm_bias[None, :]]
        in_specs = [piece] * 3 + [far_a, far_b, gains, gains]
        early_specs = [wide, stat, stat]
        early_shapes = [
            jax.ShapeDtypeStruct((rows, D), BF16),
            jax.ShapeDtypeStruct((rows, 128), F32),
            jax.ShapeDtypeStruct((rows, 128), F32),
        ]
        normed = []
    else:
        normed = list(norm_wide(pieces, gain, norm_bias))
        inputs, in_specs, early_specs, early_shapes = [normed[0]], [wide], [], []
    scales = jnp.stack([gain, norm_bias])
    high = lax.reduce_precision(scales, 8, 7)
    low = scales - high
    rest = jnp.zeros((4, D), F32)
    scales = jnp.concatenate([high[:1], low[:1], high[1:], low[1:], rest], axis=0).astype(BF16)
    outs = pl.pallas_call(
        functools.partial(up_kernel, joined=joined),
        grid_spec=pltpu.PrefetchScalarGridSpec(
            num_scalar_prefetch=1,
            grid=(steps,),
            in_specs=in_specs
            + [
                pl.BlockSpec((D, width), lambda i, r: (0, number)), vector, block,
                pl.BlockSpec((8, D), lambda i, r: (0, 0)),
            ],
            out_specs=early_specs + [block, block, vector, stat],
            scratch_shapes=[pltpu.VMEM((8, width), F32)],
        ),
        out_shape=early_shapes
        + [
            jax.ShapeDtypeStruct((rows, width), BF16),
            jax.ShapeDtypeStruct((rows, width), BF16),
            jax.ShapeDtypeStruct((1, width), F32),
            jax.ShapeDtypeStruct((rows, 128), F32),
        ],
        compiler_params=params(("arbitrary",)),
        name="feed_up",
        cost_estimate=pl.CostEstimate(
            flops=2 * rows * D * width,
            bytes_accessed=2 * (2 * rows + width) * D + 8 * rows * width,
            transcendentals=2 * rows * width,
        ),
    )(row, *inputs, array, bias[None, :], grad_hidden, scales)
    return normed + list(outs)


PARTIAL_FLIP = (1, 3, 2, 3, 2, 1, 0, 0)
PARTIAL_HALF = (0, 0, 1, 1, 0, 1, 0, 1)


def table_lookup(table, step):
    result = jnp.int32(table[0])
    for index in range(1, len(table)):
        result = jnp.where(step == index, table[index], result)
    return result


def partial_kernel(count, row, *refs):
    values, weights = refs[:count], refs[count : 2 * count]
    outs = refs[2 * count :]
    step = pl.program_id(0)
    total = mm_nt(values[0][...], weights[0][...])
    for x, w in zip(values[1:], weights[1:]):
        total = total + mm_nt(x[...], w[...])
    for index, out in enumerate(outs):

        @pl.when(step // 2 == index)
        def _():
            out[0] = total.astype(out.dtype)


def partial_blocks(values, weights, row, first, kinds):
    rows = values[0].shape[0]
    half, block = rows // 2, D // 4
    count = len(values)
    flips = PARTIAL_FLIP[2 * first : 2 * (first + len(kinds))]
    halves = PARTIAL_HALF[2 * first : 2 * (first + len(kinds))]

    def value_spec(x):
        return pl.BlockSpec((half, x.shape[1]), lambda s, r: (table_lookup(halves, s), 0))

    def weight_spec(w):
        return pl.BlockSpec((block, w[1]), lambda s, r: (r[0] ^ table_lookup(flips, s), w[2]))

    def out_spec(index):
        return pl.BlockSpec((1, half, block), lambda s, r: (jnp.clip(s - 2 * index, 0, 1), 0, 0))

    depth = sum(x.shape[1] for x in values)
    return pl.pallas_call(
        functools.partial(partial_kernel, count),
        grid_spec=pltpu.PrefetchScalarGridSpec(
            num_scalar_prefetch=1,
            grid=(2 * len(kinds),),
            in_specs=[value_spec(x) for x in values] + [weight_spec(w) for w in weights],
            out_specs=[out_spec(index) for index in range(len(kinds))],
        ),
        out_shape=[jax.ShapeDtypeStruct((2, half, block), kind) for kind in kinds],
        compiler_params=params(("arbitrary",)),
        name="partial_blocks",
        cost_estimate=pl.CostEstimate(
            flops=rows * block * depth * 2 * len(kinds),
            bytes_accessed=(rows + D) * depth * 2 + 4 * rows * block * len(kinds),
            transcendentals=0,
        ),
    )(row, *values, *[w[0] for w in weights])


def permute_row(value, pairs):
    return lax.ppermute(value, "row", pairs)


def in_order(*values):
    return lax.optimization_barrier(values)


def reduce_row_start(values, weights, row):
    if lax.axis_size("row") != 4:
        columns = [array[:, n * width : (n + 1) * width] for array, width, n in weights]
        return sum(mm_nt(x, w) for x, w in zip(values, columns)).astype(BF16)
    return tuple(partial_blocks(values, weights, row, 0, (BF16, BF16)))


def reduce_row_rest(values, weights, row):
    if lax.axis_size("row") != 4:
        return ()
    return tuple(partial_blocks(values, weights, row, 2, (BF16, F32)))


def reduce_row_finish(
    sends, values, weights, row, between=None, tied=None, rest=None, delayed=False
):
    if lax.axis_size("row") != 4:
        total = lax.psum_scatter(sends, "row", scatter_dimension=1, tiled=True).astype(F32)
        extra = between(tied) if between else None
        return ((lambda first: (total, first)) if delayed else total), extra
    from_x = permute_row(sends[0], X_PAIRS)
    from_y = permute_row(sends[1], Y_PAIRS)
    keep, own = rest if rest is not None else reduce_row_rest(values, weights, row)
    extra = None
    if between is not None:
        if tied is not None:
            keep, own, tied = in_order(keep, own, tied)
        extra = between(tied)
        from_x, from_y, extra = in_order(from_x, from_y, extra)
    next_y = (keep[0].astype(F32) + from_x[1].astype(F32)).astype(BF16)
    next_x = (keep[1].astype(F32) + from_y[1].astype(F32)).astype(BF16)
    last_y = permute_row(next_y, Y_PAIRS)
    last_x = permute_row(next_x, X_PAIRS)

    def add(last_y, last_x):
        first_half = own[0] + from_x[0].astype(F32) + last_y.astype(F32)
        second_half = own[1] + from_y[0].astype(F32) + last_x.astype(F32)
        return jnp.concatenate([first_half, second_half], axis=0)

    def add_after(first):
        now_y, now_x, first = in_order(last_y, last_x, first)
        return add(now_y, now_x), first

    return (add_after if delayed else add(last_y, last_x)), extra


def gather_row(value, between=None, later=None):
    if lax.axis_size("row") != 4:
        gathered = lax.all_gather(value, "row", axis=1, tiled=True)
        if later is not None:
            return gathered, later[0](later[1])
        return gathered, between() if between else None
    half = value.shape[0] // 2
    from_x = permute_row(value, X_PAIRS)
    from_y = permute_row(value, Y_PAIRS)
    extra = None
    if between is not None:
        extra = between()
        from_x, from_y, extra = in_order(from_x, from_y, extra)
    if later is not None:
        from_x, from_y, argument = in_order(from_x, from_y, later[1])
    far_a = permute_row(from_x[:half], Y_PAIRS)
    far_b = permute_row(from_y[half:], X_PAIRS)
    if later is not None:
        extra = later[0](argument)
        far_a, far_b, extra = in_order(far_a, far_b, extra)
    return (value, from_x, from_y, far_a, far_b), extra


def gather_row_small(value):
    if lax.axis_size("row") != 4:
        return lax.all_gather(value, "row", axis=1, tiled=True)
    row = lax.axis_index("row")
    pieces = jnp.stack(
        [value] + [permute_row(value, pairs) for pairs in (X_PAIRS, Y_PAIRS, D_PAIRS)]
    )
    ordered = [
        lax.dynamic_index_in_dim(pieces, row ^ place, 0, keepdims=False) for place in range(4)
    ]
    return jnp.concatenate(ordered, axis=1)


def sum_row_direct(value):
    if lax.axis_size("row") != 4:
        return lax.psum(value, "row")
    others = [permute_row(value, pairs) for pairs in (X_PAIRS, Y_PAIRS, D_PAIRS)]
    return value + others[0] + (others[1] + others[2])


def norm_backward(grad_out, normal, inverse, gain_vector, sums=None):
    scaled = grad_out * gain_vector
    if sums is None:
        sums = sum_row_direct(
            jnp.stack([jnp.sum(scaled, axis=1), jnp.sum(scaled * normal, axis=1)])
        )
    means = sums / D
    grad_in = inverse * (scaled - means[0][:, None] - normal * means[1][:, None])
    return (grad_in, jnp.sum(grad_out * normal, axis=0), jnp.sum(grad_out, axis=0))


def gather_col(weight):
    return lax.all_gather(weight, "col", axis=0, tiled=True)


def scatter_col(grad):
    if grad.ndim == 2:
        return lax.psum_scatter(grad, "col", scatter_dimension=0, tiled=True)
    groups = [list(range(core, SLOTS, 2)) for core in range(2)]
    return lax.psum_scatter(grad, "col", scatter_dimension=0, axis_index_groups=groups)


class Exchange:
    def __init__(self, messages, send_sem, recv_sem):
        col = lax.axis_index("col")
        self.base = (col // SLOTS) * SLOTS
        self.place = col % SLOTS
        self.messages, self.send_sem, self.recv_sem = messages, send_sem, recv_sem

    def copy(self, index):
        _, target, source, destination = self.messages[index]
        return pltpu.make_async_remote_copy(
            src_ref=source,
            dst_ref=destination,
            send_sem=self.send_sem.at[index],
            recv_sem=self.recv_sem.at[index],
            device_id={"col": self.base + target},
            device_id_type=pl.DeviceIdType.MESH,
        )

    def greet(self):
        barrier = pltpu.get_barrier_semaphore()
        for step in range(1, SLOTS):
            other = self.base + (self.place + step) % SLOTS
            pl.semaphore_signal(
                barrier, inc=1, device_id={"col": other}, device_id_type=pl.DeviceIdType.MESH
            )
        pl.semaphore_wait(barrier, SLOTS - 1)

    def run(self, programs, drain=True):
        for place, program in enumerate(programs):
            if not program:
                continue

            @pl.when(self.place == place)
            def _():
                for action in program:
                    if callable(action):
                        action()
                    elif action >= 0:
                        self.copy(action).start()
                    else:
                        self.copy(~action).wait_recv()

        if drain:
            self.drain()

    def drain(self):
        for place in range(SLOTS):
            mine = [i for i, message in enumerate(self.messages) if message[0] == place]
            if mine:

                @pl.when(self.place == place)
                def _():
                    for index in mine:
                        self.copy(index).wait_send()


def scaled_add(meta, rates, target, terms, rows):
    heads = target.shape[0]
    strip = 64
    for head in range(heads):

        def add(index, _):
            spot = pl.ds(pl.multiple_of(index * strip, strip), strip)
            total = None
            for term in terms:
                if isinstance(term, tuple):
                    ref, slot = term
                    exponent = jnp.maximum(
                        trunk_reference(meta, jnp.int32(3), rows)
                        - trunk_reference(meta, jnp.int32(slot), rows),
                        0,
                    )
                    value = ref[head, spot, :].astype(F32) * power(rates[head], exponent, HV)
                else:
                    value = term[head, spot, :].astype(F32)
                total = value if total is None else total + value
            target[head, spot, :] = total.astype(BF16)
            return 0

        lax.fori_loop(0, QK // strip, add, 0)


def share_kernel(rows, meta, rates, ex, sh, shift, tot, send_sem, recv_sem):
    messages = [
        (0, 2, ex.at[0], sh.at[0]),
        (0, 1, ex.at[0], sh.at[0]),
        (1, 3, ex.at[0], sh.at[1]),
        (2, 3, ex.at[0], sh.at[2]),
        (2, 3, sh.at[0], sh.at[0]),
        (3, 2, sh.at[1], sh.at[1]),
        (3, 4, ex.at[1], sh.at[4]),
        (3, 5, ex.at[2], sh.at[5]),
        (3, 4, tot, sh.at[3]),
        (4, 5, ex.at[1], sh.at[6]),
        (4, 6, ex.at[1], sh.at[6]),
        (4, 5, ex.at[2], sh.at[7]),
        (5, 7, sh.at[7], sh.at[7]),
        (4, 5, sh.at[4], sh.at[4]),
        (4, 6, sh.at[4], sh.at[4]),
        (5, 4, sh.at[5], sh.at[5]),
        (5, 7, sh.at[5], sh.at[5]),
        (4, 5, sh.at[3], sh.at[3]),
        (4, 6, sh.at[3], sh.at[3]),
        (6, 7, sh.at[6], sh.at[6]),
        (6, 7, sh.at[4], sh.at[4]),
        (6, 7, sh.at[3], sh.at[3]),
        (7, 6, sh.at[7], sh.at[7]),
        (7, 6, sh.at[5], sh.at[5]),
        (4, 5, ex.at[0], shift),
        (6, 7, ex.at[0], shift),
    ]
    exchange = Exchange(messages, send_sem, recv_sem)

    def keep_trunk():
        sh[3] = ex[0]

    def total_trunk():
        terms = [(sh.at[slot], slot) for slot in range(3)] + [ex.at[0]]
        scaled_add(meta, rates, tot, terms, rows)

    def keep_branches():
        sh[6] = ex[1]
        sh[7] = ex[2]

    exchange.greet()
    exchange.run(
        [
            [0, 1],
            [2, ~1],
            [3, ~0, 4, ~5],
            [6, 7, keep_trunk, ~2, 5, ~4, ~3, total_trunk, 8],
            [10, 11, 9, 24, keep_branches, ~6, 14, 13, ~15, ~8, 18, 17],
            [~11, 12, ~7, 16, 15, ~9, ~24, ~13, ~17],
            [25, ~10, 19, ~14, 20, ~22, ~23, ~18, 21],
            [~12, 22, ~16, 23, ~19, ~20, ~25, ~21],
        ]
    )


def vmem():
    return pl.BlockSpec(memory_space=pltpu.VMEM)


def share_states(meta, rates, exports, rows):
    heads = exports.shape[1]
    state = (heads, QK, HV)
    return pl.pallas_call(
        functools.partial(share_kernel, rows),
        in_specs=[smem(), smem(), vmem()],
        out_specs=[vmem(), vmem()],
        out_shape=[
            jax.ShapeDtypeStruct((SLOTS,) + state, BF16),
            jax.ShapeDtypeStruct(state, BF16),
        ],
        scratch_shapes=[
            pltpu.VMEM(state, BF16),
            pltpu.SemaphoreType.DMA((26,)),
            pltpu.SemaphoreType.DMA((26,)),
        ],
        compiler_params=pltpu.CompilerParams(
            collective_id=1, has_side_effects=True, vmem_limit_bytes=40 * 1024 * 1024
        ),
        name="share_states",
        cost_estimate=pl.CostEstimate(
            flops=0, bytes_accessed=100 * 1024 * 1024, transcendentals=0
        ),
    )(meta, rates, exports)


def return_kernel(
    rows, meta, rates, y, first, left, right, own0, own1, own2, grads, rx, tx, send_sem, recv_sem
):
    messages = [
        (7, 6, y.at[3], rx.at[0]),
        (7, 6, y.at[4], rx.at[1]),
        (7, 6, y.at[5], rx.at[2]),
        (6, 7, y.at[6], rx.at[0]),
        (6, 7, y.at[7], rx.at[1]),
        (7, 5, tx.at[0], rx.at[0]),
        (7, 5, tx.at[1], rx.at[1]),
        (6, 4, tx.at[0], rx.at[0]),
        (6, 4, tx.at[1], rx.at[1]),
        (6, 4, tx.at[2], rx.at[2]),
        (5, 4, y.at[3], rx.at[3]),
        (5, 4, y.at[4], rx.at[4]),
        (5, 4, y.at[5], rx.at[5]),
        (5, 4, tx.at[0], rx.at[6]),
        (5, 4, tx.at[1], rx.at[7]),
        (4, 3, tx.at[0], rx.at[0]),
        (4, 3, tx.at[1], own1),
        (4, 3, tx.at[2], own2),
        (2, 3, y.at[0], rx.at[1]),
        (2, 3, y.at[1], rx.at[2]),
        (3, 2, tx.at[2], own0),
        (3, 1, tx.at[1], own0),
        (3, 0, tx.at[0], rx.at[0]),
        (1, 0, y.at[0], rx.at[1]),
        (5, 4, first, own0),
        (7, 6, first, own0),
    ]
    exchange = Exchange(messages, send_sem, recv_sem)

    def add(target, *terms):
        return lambda: scaled_add(meta, rates, target, terms, rows)

    def multiply(begin, end):
        def tile(index, _):
            spot = pl.ds(pl.multiple_of(index * GRAD_TILE, GRAD_TILE), GRAD_TILE)
            grads[spot, :] = mm_tn(left[:, spot], right[...]).astype(BF16)
            return 0

        lax.fori_loop(begin, end, tile, 0)

    tiles = D // GRAD_TILE
    exchange.greet()
    exchange.run([[], [23], [18, 19], [], [], [10, 11, 12, 24], [3, 4], [0, 1, 2, 25]], False)
    multiply(0, tiles // 2)
    exchange.run(
        [
            [],
            [],
            [],
            [],
            [
                ~10, ~7, add(tx.at[0], y.at[3], rx.at[0], rx.at[3]), 15,
                ~11, ~8, add(tx.at[1], y.at[4], rx.at[1], rx.at[4]), 16,
                ~12, ~9, add(tx.at[2], y.at[5], rx.at[2], rx.at[5]), 17,
                ~13, add(own1, y.at[6], rx.at[6]),
                ~14, add(own2, y.at[7], rx.at[7]),
                ~24,
            ],
            [
                ~5, add(tx.at[0], y.at[6], rx.at[0]), 13,
                ~6, add(tx.at[1], y.at[7], rx.at[1]), 14,
            ],
            [
                ~0, add(tx.at[0], y.at[3], rx.at[0]), 7,
                ~1, add(tx.at[1], y.at[4], rx.at[1]), 8,
                ~2, add(tx.at[2], y.at[5], rx.at[2]), 9,
                ~25,
            ],
            [
                ~3, add(tx.at[0], y.at[6], rx.at[0]), 5,
                ~4, add(tx.at[1], y.at[7], rx.at[1]), 6,
            ],
        ],
        False,
    )
    multiply(tiles // 2, tiles)
    exchange.run(
        [
            [~23, ~22, add(own0, rx.at[0], rx.at[1])],
            [~21],
            [~20],
            [
                ~18, ~19, ~15,
                add(tx.at[0], y.at[0], rx.at[1], (rx.at[0], 0)), 22,
                add(tx.at[1], y.at[1], rx.at[2], (rx.at[0], 1)), 21,
                add(tx.at[2], y.at[2], (rx.at[0], 2)), 20,
                add(own0, rx.at[0], y.at[3]),
                ~16, ~17,
            ],
            [],
            [],
            [],
            [],
        ],
        False,
    )
    exchange.drain()


def return_states(meta, rates, exports, first_state, left, right, rows):
    heads = exports.shape[1]
    state = (heads, QK, HV)
    return pl.pallas_call(
        functools.partial(return_kernel, rows),
        in_specs=[smem(), smem(), vmem(), vmem(), vmem(), vmem()],
        out_specs=[vmem()] * 4,
        out_shape=[jax.ShapeDtypeStruct(state, BF16)] * 3
        + [jax.ShapeDtypeStruct((D, right.shape[1]), BF16)],
        scratch_shapes=[
            pltpu.VMEM((8,) + state, BF16),
            pltpu.VMEM((3,) + state, BF16),
            pltpu.SemaphoreType.DMA((26,)),
            pltpu.SemaphoreType.DMA((26,)),
        ],
        compiler_params=pltpu.CompilerParams(
            collective_id=2, has_side_effects=True, vmem_limit_bytes=40 * 1024 * 1024
        ),
        name="return_states",
        cost_estimate=pl.CostEstimate(
            flops=0, bytes_accessed=100 * 1024 * 1024, transcendentals=0
        ),
    )(meta, rates, exports, first_state, left, right)


def sum_col(value):
    size = lax.axis_size("col")
    if size != SLOTS:
        return lax.psum(value, "col")
    for flip in (1, 2, 4):
        value = value + lax.ppermute(value, "col", [(a, a ^ flip) for a in range(size)])
    return value


def sum_col_vectors(vectors, extra=None):
    col = lax.axis_index("col")
    size = lax.axis_size("col")
    parts = list(vectors) + ([extra] if extra is not None else [])
    total = sum_col(jnp.concatenate(parts).reshape(-1, 128)).reshape(-1)
    results, first = [], 0
    for vector in vectors:
        width = vector.shape[0] // size
        results.append(lax.dynamic_slice_in_dim(total, first + col * width, width, 0))
        first += vector.shape[0]
    return results, total[first:]


def token_tables(place, rows, lengths, parents):
    index = place * rows + jnp.arange(rows, dtype=jnp.int32)
    in_trunk = index < TRUNK
    beyond = jnp.maximum(index - TRUNK, 0)
    segment = jnp.where(in_trunk, 0, 1 + beyond // SEG)
    position = jnp.where(in_trunk, index, beyond % SEG)

    def lookup(table, spots):
        hits = spots[:, None] == jnp.arange(table.shape[0], dtype=jnp.int32)
        return jnp.sum(jnp.where(hits, table, 0), axis=1)

    branch = 1 + lookup(parents, jnp.clip(segment - 5, 0, 7))
    parent_length = lookup(lengths, branch)
    depth = position + jnp.where(segment >= 1, lengths[0], 0)
    depth = depth + jnp.where(segment >= 5, parent_length, 0)
    valid = (position < lookup(lengths, segment)).astype(F32)
    half = QK // 2
    frequency = 10000.0 ** (-jnp.arange(half, dtype=F32) / (half - 1))
    angles = depth.astype(F32)[:, None] * frequency[None, :]
    return valid, jnp.cos(angles), jnp.sin(angles)


def body(
    tokens,
    cotangent,
    query_weight,
    key_weight,
    value_weight,
    gate_weight,
    out_weight,
    up_weight,
    down_weight,
    first_gain,
    first_bias,
    group_gain,
    group_bias,
    second_gain,
    second_bias,
    up_bias,
    down_bias,
    segment_lengths,
    leaf_parents,
):
    rows = tokens.shape[0]
    col = lax.axis_index("col")
    row = lax.axis_index("row")
    row_ref = row.astype(jnp.int32)[None]
    place = (col % SLOTS).astype(jnp.int32)
    tree = (col // SLOTS).astype(jnp.int32)
    lengths = lax.dynamic_index_in_dim(segment_lengths, tree, 0, keepdims=False)
    parents = lax.dynamic_index_in_dim(leaf_parents, tree, 0, keepdims=False)
    meta = jnp.concatenate([lengths, parents, place[None]]).astype(jnp.int32)
    heads = query_weight.shape[1] // QK
    head_numbers = (row * heads + jnp.arange(heads, dtype=jnp.int32)).astype(F32)
    rates = jnp.log(1.0 - 2.0 ** (-5.0 - head_numbers))

    wide = heads * HV
    narrow = heads * QK
    project_full = gather_col(jnp.concatenate([query_weight, key_weight, value_weight], axis=1))
    gate_full = gather_col(gate_weight)
    out_full = gather_col(out_weight.T)
    feed_full = gather_col(jnp.concatenate([down_weight.T, up_weight], axis=1))
    query_part, key_part = (project_full, narrow, 0), (project_full, narrow, 1)
    value_part = (project_full, wide, 1)
    out_part = (out_full, wide, 0)
    down_part, up_part = (feed_full, wide, 0), (feed_full, wide, 1)

    valid, cosine, sine = token_tables(place, rows, lengths, parents)
    column = valid[:, None]
    gains = gather_row_small(jnp.stack([first_gain, first_bias, second_gain, second_bias]))
    token_pieces, _ = gather_row(tokens)
    first_wide, first_average, first_inverse = join(token_pieces, row_ref, gains[0], gains[1])
    fed_low = (cotangent.astype(F32) * column).astype(BF16)
    fed_low, first_average = lax.optimization_barrier((fed_low, first_average))

    fed_pieces, projected = gather_row(
        fed_low, lambda: project(meta, rates, first_wide, project_full, cosine, sine)
    )
    query_rot, key_rot, value_low, exports = projected
    shared, shifted = share_states(meta, rates, exports, rows)
    gate_full, shared = in_order(gate_full, shared)
    gate_part = (gate_full, wide, 0)
    gate_full, fed_pieces = in_order(gate_full, fed_pieces)
    gate_part = (gate_full, wide, 0)
    gate_raw, gated, normal, inverse, states = retain(
        meta, rates, query_rot, key_rot, value_low, first_wide, gate_part, shared, shifted,
        group_gain, group_bias,
    )

    sends = reduce_row_start([gated], [out_part], row_ref)
    attended, _ = reduce_row_finish(sends, [gated], [out_part], row_ref)
    middle = tokens.astype(F32) + attended

    def feed_gradient(pieces):
        joined = join(pieces, row_ref)
        return joined, matmul(joined, down_part, BF16)

    middle_pieces, (fed_wide, grad_hidden) = gather_row(
        middle.astype(BF16), later=(feed_gradient, fed_pieces)
    )
    second_wide, second_average, second_inverse, hidden, grad_before, up_bias_grad, feed_sums = (
        feed_up(middle_pieces, row_ref, gains[2], gains[3], up_part, up_bias, grad_hidden)
    )
    feed_sums = sum_row_direct(feed_sums[:, :2].T)
    sends = reduce_row_start([grad_before], [up_part], row_ref)
    sends, hidden = in_order(sends, hidden)
    second_back, feed_partial = reduce_row_finish(
        sends,
        [grad_before],
        [up_part],
        row_ref,
        lambda hidden: weight_grads([(fed_wide, hidden), (second_wide, grad_before)]),
        hidden,
    )
    feed_grad = scatter_col(feed_partial)
    grad_fed = fed_low.astype(F32)
    down_bias_grad = jnp.sum(grad_fed, axis=0)

    second_normal = (middle - second_average[:, :1]) * second_inverse[:, :1]
    grad_middle_norm, second_gain_grad, second_bias_grad = norm_backward(
        second_back, second_normal, second_inverse[:, :1], second_gain, feed_sums
    )
    grad_middle = grad_fed + grad_middle_norm
    grad_pieces, (fed_sends, fed_rest) = gather_row(
        grad_middle.astype(BF16),
        lambda: (
            reduce_row_start([hidden], [down_part], row_ref),
            reduce_row_rest([hidden], [down_part], row_ref),
        ),
    )
    grad_wide = join(grad_pieces, row_ref)
    fed_sends, grad_wide = in_order(fed_sends, grad_wide)
    out_partial = column_grads([(grad_wide, gated)], 4)
    out_partial, grad_wide = in_order(out_partial, grad_wide)
    out_partial, feed_grad = in_order(out_partial, feed_grad)
    out_grad = scatter_col(out_partial)
    add_fed_out, gate_results = reduce_row_finish(
        fed_sends,
        [hidden],
        [down_part],
        row_ref,
        lambda _: tuple(
            gate_back(
                meta, rates, grad_wide, out_part, gate_raw, normal, inverse, query_rot, group_gain, group_bias
            )
        ),
        rest=fed_rest,
        delayed=True,
    )
    grad_gate, grad_retained, group_gain_grad, group_bias_grad, returns, first_state = gate_results
    own0, own1, own2, gate_partial = return_states(
        meta, rates, returns, first_state, first_wide, grad_gate, rows
    )
    gate_partial, own0, out_grad = in_order(gate_partial, own0, out_grad)
    own = (own0, own1, own2)
    gate_grad = scatter_col(gate_partial)
    grad_query, grad_key, grad_value = retain_back(
        meta, rates, query_rot, key_rot, value_low, grad_retained, states, cosine, sine, own
    )
    back_values = [grad_query, grad_key, grad_value, grad_gate]
    back_weights = [query_part, key_part, value_part, gate_part]
    sends = reduce_row_start(back_values, back_weights, row_ref)
    sends, grad_value = in_order(sends, grad_value)
    fed_out, back_rest = add_fed_out(reduce_row_rest(back_values, back_weights, row_ref))
    fed_out = fed_out + down_bias
    layer_out = middle + fed_out
    first_back, project_partial = reduce_row_finish(
        sends,
        back_values,
        back_weights,
        row_ref,
        lambda _: column_grads(
            [(first_wide, grad_query), (first_wide, grad_key), (first_wide, grad_value)], 6
        ),
        rest=back_rest,
    )
    project_partial, gate_grad = in_order(project_partial, gate_grad)
    project_grad = scatter_col(project_partial).astype(F32)
    feed_grad, out_grad, gate_grad = (
        grad.astype(F32) for grad in (feed_grad, out_grad, gate_grad)
    )

    first_normal = (tokens.astype(F32) - first_average[:, :1]) * first_inverse[:, :1]
    grad_first, first_gain_grad, first_bias_grad = norm_backward(
        first_back, first_normal, first_inverse[:, :1], first_gain
    )
    tokens_grad = grad_middle + grad_first

    squares = jnp.stack(
        [
            jnp.sum(column * layer_out * layer_out),
            jnp.sum(column * attended * attended),
            jnp.sum(column * fed_out * fed_out),
        ]
    )
    vectors, col_squares = sum_col_vectors(
        (
            first_gain_grad,
            first_bias_grad,
            group_gain_grad[0],
            group_bias_grad[0],
            second_gain_grad,
            second_bias_grad,
            up_bias_grad[0],
            down_bias_grad,
        ),
        jnp.concatenate([squares, jnp.zeros((125,), F32)]),
    )
    totals = sum_row_direct(col_squares[None, :])[0, :3]
    valid_count = jnp.sum(segment_lengths).astype(F32) * D
    norm_values = jnp.sqrt(totals / valid_count)
    return (
        layer_out.astype(BF16),
        tokens_grad,
        project_grad[:, :narrow],
        project_grad[:, narrow : 2 * narrow],
        project_grad[:, 2 * narrow :],
        gate_grad,
        out_grad.T,
        feed_grad[:, wide:],
        feed_grad[:, :wide].T,
        *vectors,
        norm_values,
    )


def solution(mesh):
    matrix, turned, vector = P("col", "row"), P("row", "col"), P("row")
    in_specs = (matrix,) * 6 + (turned, matrix, turned) + (vector,) * 8 + (P(), P())
    split = P(("row", "col"))
    out_specs = (matrix,) * 6 + (turned, matrix, turned) + (split,) * 8 + (P(),)
    return jax.shard_map(body, mesh=mesh, in_specs=in_specs, out_specs=out_specs, check_vma=False)
```
